32 devices in a mesh: dp: 8 (over y, x, core), tp: 4 (over z).
Axes of the slice: x: 2, y: 2, z: 4, core: 2. Of those that a mesh axis runs over, the one named last changes fastest.
Arguments:
- tokens: bfloat16 [20480, 768], P(('dp', 'tp')), may hold values from -6 to 6
- w_query: bfloat16 [768, 768], P('dp', 'tp'), may hold values from -0.3125 to 0.3125
- w_key: bfloat16 [768, 768], P('dp', 'tp'), may hold values from -0.3125 to 0.3125
- w_value: bfloat16 [768, 768], P('dp', 'tp'), may hold values from -0.21875 to 0.21875
- b_query: bfloat16 [768], P('dp'), may hold values from -3 to 3
- b_value: bfloat16 [768], P('dp'), may hold values from -3 to 3
- w_out: bfloat16 [768, 768], P('dp', 'tp'), may hold values from -0.875 to 0.875
- b_out: bfloat16 [768], P('dp'), may hold values from -3 to 3
- gain_attn: bfloat16 [768], P('dp'), may hold values from 0.25 to 1.75
- shift_attn: bfloat16 [768], P('dp'), may hold values from -3 to 3
- w_up: bfloat16 [768, 3072], P('dp', 'tp'), may hold values from -0.21875 to 0.21875
- b_up: bfloat16 [3072], P('dp'), may hold values from -3 to 3
- w_down: bfloat16 [768, 3072], P('dp', 'tp'), may hold values from -0.15625 to 0.15625
- b_down: bfloat16 [768], P('dp'), may hold values from -3 to 3
- gain_ffn: bfloat16 [768], P('dp'), may hold values from 0.25 to 1.75
- shift_ffn: bfloat16 [768], P('dp'), may hold values from -3 to 3
- lengths: int32 [16], replicated, may hold values from 1024 to 1536, as said below
- deal_order: int32 [16], replicated, may hold values from 0 to 15, as said below
- cotangent: bfloat16 [20480, 768], P(('dp', 'tp')), may hold values from -6 to 6
Outputs:
- encoder_output: bfloat16 [20480, 768], P(('dp', 'tp'))
- grad_tokens: float32 [20480, 768], P(('dp', 'tp'))
- grad_w_query: float32 [768, 768], P('dp', 'tp')
- grad_w_key: float32 [768, 768], P('dp', 'tp')
- grad_w_value: float32 [768, 768], P('dp', 'tp')
- grad_b_query: float32 [768], P('dp')
- grad_b_value: float32 [768], P('dp')
- grad_w_out: float32 [768, 768], P('dp', 'tp')
- grad_b_out: float32 [768], P('dp')
- grad_gain_attn: float32 [768], P('dp')
- grad_shift_attn: float32 [768], P('dp')
- grad_w_up: float32 [768, 3072], P('dp', 'tp')
- grad_b_up: float32 [3072], P('dp')
- grad_w_down: float32 [768, 3072], P('dp', 'tp')
- grad_b_down: float32 [768], P('dp')
- grad_gain_ffn: float32 [768], P('dp')
- grad_shift_ffn: float32 [768], P('dp')
The draws below stay inside these ranges and needn't reach their ends.
Inputs may be any that keep to these rules, and one draw needn't show every extreme that they name: Group g holds sequence deal_order[2 g] in slot 0 and deal_order[2 g + 1] in slot 1; the two lengths of a group add up to 2560, and each is at least 1024. `deal_order`: each of 0 to 15 appears once.
All inputs are finite; a program needn't handle non-finite values.
Results may differ from the reference program's by a relative error of at most 0.015.
The reference program's roundings to bfloat16 on the way count: a program that leaves them out, or rounds other values in their place, can miss the bound.
Values may be sent and summed in bfloat16 or wider, within the bound.
A program may use at most 128 MiB of HBM per device.

```python
import jax
import jax.numpy as jnp
from jax import lax

D = 768
H = 12
HD = 64
FF = 3072
SHORT_MIN = 1024
GROUP_TOK = 2560
TOKENS = 20480
SEQS = 16
N_DP = 8


def deal_helper(key):
    order = jax.random.permutation(jax.random.fold_in(key, 11), SEQS).astype(jnp.int32)
    shorter = jax.random.randint(jax.random.fold_in(key, 12), (N_DP,), SHORT_MIN, GROUP_TOK // 2 + 1, dtype=jnp.int32)
    pinned = jax.random.randint(jax.random.fold_in(key, 13), (), 0, N_DP, dtype=jnp.int32)
    shorter = jnp.where(jnp.arange(N_DP, dtype=jnp.int32) == pinned, SHORT_MIN, shorter)
    first_short = jax.random.randint(jax.random.fold_in(key, 14), (N_DP,), 0, 2, dtype=jnp.int32)
    leading = jnp.where(first_short == 1, shorter, GROUP_TOK - shorter)
    dealt = jnp.stack([leading, GROUP_TOK - leading], axis=1).reshape(SEQS)
    sizes_by_seq = jnp.zeros((SEQS,), jnp.int32).at[order].set(dealt)
    return (sizes_by_seq, order)


def draw_lengths(key, part):
    return deal_helper(key)[0]


def draw_deal_order(key, part):
    return deal_helper(key)[1]


def spiked(values, rng, source, target, blocks, factor):
    owner, partner = [(jnp.arange(values.shape[axis_at]) // (values.shape[axis_at] // blocks)).reshape([-1 if axis == axis_at else 1 for axis in range(values.ndim)]) for axis_at in (source, target)]
    chosen = jax.random.permutation(rng, blocks)[partner]
    strong = (owner == chosen) | (owner == (partner + blocks // 2) % blocks)
    return jnp.where(strong, factor * values, values)


def block_levels(rng, dims, pieces, least, largest):
    factor_of, own = 1.0, jax.random.fold_in(rng, 6)
    for dim, shards_of in pieces:
        draws = jnp.exp(jax.random.uniform(jax.random.fold_in(own, dim), (shards_of,), jnp.float32, least / len(pieces), largest / len(pieces)))
        factor_of = factor_of * jnp.repeat(draws, dims[dim] // shards_of).reshape([-1 if axis == dim else 1 for axis in range(len(dims))])
    return factor_of


def normal_values(stream_key, dims, spread, limit, shards=(), held_as=jnp.bfloat16):
    gain = block_levels(stream_key, dims, shards, -0.22, 0.18) if shards else 1.0
    drawn = jax.random.normal(stream_key, dims, jnp.float32) * spread * gain
    return jnp.minimum(jnp.maximum(drawn, -limit), limit).astype(held_as)


def noise_with(stream_key, shape, deviation, limit, split, heavy, kind=jnp.bfloat16):
    entries = deviation * jax.random.normal(stream_key, shape, jnp.float32)
    if split:
        entries = entries * block_levels(stream_key, shape, split, -0.22, 0.18)
    return jnp.clip(spiked(entries, jax.random.fold_in(stream_key, 3), *heavy), -limit, limit).astype(kind)


def setup_inputs(seed: int = 0) -> dict:
    seeds = jax.random.split(jax.random.key(seed), 20)
    return {
        "tokens": normal_values(seeds[0], (TOKENS, D), 1.0, 6.0, ((0, 32),)),
        "w_query": normal_values(seeds[1], (D, D), (D // 2) ** -0.5, 0.3125, ((0, 8), (1, 4))),
        "w_key": normal_values(seeds[2], (D, D), (D // 2) ** -0.5, 0.3125, ((0, 8), (1, 4))),
        "w_value": normal_values(seeds[3], (D, D), D ** -0.5, 0.21875, ((0, 8), (1, 4))),
        "b_query": normal_values(seeds[4], (D,), 0.5, 3.0, ((0, 8),)),
        "b_value": normal_values(seeds[5], (D,), 0.5, 3.0, ((0, 8),)),
        "w_out": normal_values(seeds[6], (D, D), (D // 16) ** -0.5, 0.875, ((0, 8), (1, 4))),
        "b_out": normal_values(seeds[7], (D,), 0.5, 3.0, ((0, 8),)),
        "gain_attn": jnp.clip(1.0 + 0.15 * jax.random.normal(seeds[8], (D,), jnp.float32), 0.25, 1.75).astype(jnp.bfloat16),
        "shift_attn": normal_values(seeds[9], (D,), 0.5, 3.0, ((0, 8),)),
        "w_up": normal_values(seeds[10], (D, FF), D ** -0.5, 0.21875, ((0, 8), (1, 4))),
        "b_up": normal_values(seeds[11], (FF,), 0.5, 3.0, ((0, 8),)),
        "w_down": normal_values(seeds[12], (D, FF), (FF // 2) ** -0.5, 0.15625, ((0, 8), (1, 4))),
        "b_down": normal_values(seeds[13], (D,), 0.5, 3.0, ((0, 8),)),
        "gain_ffn": jnp.clip(1.0 + 0.15 * jax.random.normal(seeds[14], (D,), jnp.float32), 0.25, 1.75).astype(jnp.bfloat16),
        "shift_ffn": normal_values(seeds[15], (D,), 0.5, 3.0, ((0, 8),)),
        "lengths": draw_lengths(jax.random.fold_in(seeds[19], 71), 0),
        "deal_order": draw_deal_order(jax.random.fold_in(seeds[19], 71), 0),
        "cotangent": noise_with(seeds[18], (TOKENS, D), 1.0, 6.0, ((0, 32),), (0, 1, 32, 2.75)),
    }


EPS = 1e-05
HIGH = lax.Precision.HIGHEST

@jax.custom_vjp
def low(v):
    return lax.optimization_barrier(v.astype(jnp.bfloat16)).astype(jnp.float32)

@jax.custom_vjp
def low_back(v):
    return v

def low_keep(v):
    return (low(v), None)

def low_pass(kept, grad):
    return (grad,)

def back_keep(v):
    return (v, None)

def back_low(kept, grad):
    return (low(grad),)
low.defvjp(low_keep, low_pass)
low_back.defvjp(back_keep, back_low)

def matmul(left, right):
    return jnp.dot(left, right, precision=HIGH)

def normalize_layer(resid, norm_gain, shift):
    center = resid - lax.optimization_barrier(jnp.mean(resid, axis=-1, keepdims=True))
    inverse_deviation = lax.rsqrt(lax.optimization_barrier(jnp.mean(center * center, axis=-1, keepdims=True)) + EPS)
    return center * inverse_deviation * norm_gain + shift

def attention(query_heads, key_heads, value_heads, segment):
    scale = HD ** (-0.5)
    block = min(512, GROUP_TOK)

    def one_block(inputs):
        query_block, seg_block = inputs
        scores = low_back(jnp.einsum('qhd,khd->hqk', query_block, key_heads, precision=HIGH) * scale)
        allowed = seg_block[:, None] == segment[None, :]
        scores = jnp.where(allowed[None], scores, -1e+30)
        highest = lax.optimization_barrier(jnp.max(scores, axis=-1, keepdims=True))
        raised = jnp.exp(scores - highest)
        shares = low(raised / lax.optimization_barrier(jnp.sum(raised, axis=-1, keepdims=True)))
        return jnp.einsum('hqk,khd->qhd', shares, value_heads, precision=HIGH)
    mixed = lax.map(jax.checkpoint(one_block), (query_heads.reshape(GROUP_TOK // block, block, H, HD), segment.reshape(GROUP_TOK // block, block)))
    return mixed.reshape(GROUP_TOK, D)

def group_layer(params, rows, segment):
    w_query, w_key, w_value, b_query, b_value, w_out, b_out, gain_attn, shift_attn, w_up, b_up, w_down, b_down, gain_ffn, shift_ffn = params
    query_rows = low_back(low(matmul(rows, w_query) + b_query))
    key_rows = low_back(low(matmul(rows, w_key)))
    value_rows = low_back(low(matmul(rows, w_value) + b_value))
    mixed = attention(query_rows.reshape(GROUP_TOK, H, HD), key_rows.reshape(GROUP_TOK, H, HD), value_rows.reshape(GROUP_TOK, H, HD), segment)
    mixed = low_back(low(mixed))
    attn = low_back(matmul(mixed, w_out.T) + b_out)
    normalized_rows = normalize_layer(rows + attn, gain_attn, shift_attn)
    pre_act = low_back(matmul(low(normalized_rows), w_up) + b_up)
    hidden = low(jax.nn.gelu(pre_act, approximate=False))
    ffn = low_back(matmul(hidden, w_down.T) + b_down)
    return normalize_layer(normalized_rows + ffn, gain_ffn, shift_ffn)

def reference(tokens, w_query, w_key, w_value, b_query, b_value, w_out, b_out, gain_attn, shift_attn, w_up, b_up, w_down, b_down, gain_ffn, shift_ffn, lengths, deal_order, cotangent):
    dealt = lengths[deal_order].reshape(N_DP, 2)
    segments = (jnp.arange(GROUP_TOK, dtype=jnp.int32)[None, :] >= dealt[:, :1]).astype(jnp.int32)
    floats = tuple((item.astype(jnp.float32) for item in (tokens, w_query, w_key, w_value, b_query, b_value, w_out, b_out, gain_attn, shift_attn, w_up, b_up, w_down, b_down, gain_ffn, shift_ffn)))

    def forward(all_rows, *params):

        def step(carry, inputs):
            rows, segment = inputs
            return (carry, group_layer(params, rows, segment))
        _, result = lax.scan(step, jnp.zeros((), jnp.float32), (all_rows.reshape(N_DP, GROUP_TOK, D), segments))
        return result.reshape(N_DP * GROUP_TOK, D)
    result, pullback = jax.vjp(forward, *floats)
    grads = pullback(cotangent.astype(jnp.float32))
    return (result.astype(jnp.bfloat16), grads[0], grads[1], grads[2], grads[3], grads[4], grads[5], grads[6], grads[7], grads[8], grads[9], grads[10], grads[11], grads[12], grads[13], grads[14], grads[15])
```

```python
import functools

import jax
import jax.numpy as jnp
from jax import lax
from jax.experimental import pallas as pl
from jax.experimental.pallas import tpu as pltpu
from jax.sharding import PartitionSpec as P

HD = 64
SHORT = 1024
EPS = 1e-05
SQRT_HALF = 0.7071067811865476
INV_ROOT_TAU = 0.3989422804014327
MASKED = -1e30
KEYS = 512
ROWS = 128
VMEM_MAX = 67043328
MESH = pl.DeviceIdType.MESH
F32 = jnp.float32
BF16 = jnp.bfloat16


def dot(left, right):
    return jnp.dot(left, right, preferred_element_type=F32)


def contract_last(left, right):
    return lax.dot_general(left, right, (((1,), (1,)), ((), ())), preferred_element_type=F32)


def contract_first(left, right):
    return lax.dot_general(left, right, (((0,), (0,)), ((), ())), preferred_element_type=F32)


def normalize_layer(resid):
    center = resid - jnp.mean(resid, axis=-1, keepdims=True)
    inverse_deviation = lax.rsqrt(jnp.mean(center * center, axis=-1, keepdims=True) + EPS)
    return (center * inverse_deviation, inverse_deviation)


def normalize_backward(output_gradient, xhat, inverse_deviation, gain):
    scaled_rows = output_gradient * gain
    return inverse_deviation * (
        scaled_rows
        - jnp.mean(scaled_rows, axis=-1, keepdims=True)
        - xhat * jnp.mean(scaled_rows * xhat, axis=-1, keepdims=True)
    )


def gelu_slope(pre_act):
    return (
        0.5 * (1.0 + lax.erf(pre_act * SQRT_HALF))
        + pre_act * jnp.exp(-0.5 * pre_act * pre_act) * INV_ROOT_TAU
    )


def position():
    z = lax.axis_index("tp")
    d = lax.axis_index("dp")
    core = lax.rem(d, 2)
    first = 2 + 2 * core
    second = 4 - 2 * core
    return z, d, core, first, second


def xor(d, mask):
    return d + mask * (1 - 2 * lax.rem(d // mask, 2))


def greet(z, d):
    barrier = pltpu.get_barrier_semaphore()
    for mask in (1, 2, 4):
        pl.semaphore_signal(barrier, inc=1, device_id=(xor(d, mask), z), device_id_type=MESH)
    for j in range(1, 4):
        pl.semaphore_signal(barrier, inc=1, device_id=(d, lax.rem(z + j, 4)), device_id_type=MESH)
    pl.semaphore_wait(barrier, 6)


def by_distance(z):
    low = z <= 1
    near = jnp.where(z == 0, 1, jnp.where(z == 3, 2, z - 1))
    mid = jnp.where(z == 0, 2, jnp.where(z == 3, 1, z + 1))
    far = jnp.where(low, 3, 0)
    return (z, near, mid, far)


def gather_kernel(
    own_w, own_s, own_t, w, s, t,
    wz_s, wz_r, wa_s, wa_r, wb_s, wb_r, wc_s, wc_r, tk_s, tk_r, sm_s, sm_r, lo_sem, blank, bl_sem,
):
    z, d, core, first, second = position()
    packs = own_w.shape[0]
    chunks = own_t.shape[0] // ROWS
    d1, d2 = xor(d, first), xor(d, second)
    d12 = xor(d1, second)
    pal = xor(d, 1)
    order = by_distance(z)

    def put(src, dst, send, recv, dp, tp):
        return pltpu.make_async_remote_copy(
            src_ref=src, dst_ref=dst, send_sem=send, recv_sem=recv, device_id=(dp, tp), device_id_type=MESH
        )

    greet(z, d)

    keep = [
        pltpu.make_async_copy(own_w, w.at[:, z, d], lo_sem.at[0]),
        pltpu.make_async_copy(own_s, s.at[d], lo_sem.at[1]),
        pltpu.make_async_copy(own_t, t.at[pl.ds(pl.multiple_of(z * own_t.shape[0], ROWS), own_t.shape[0])], lo_sem.at[2]),
    ]
    for copy in keep:
        copy.start()

    def along_z(p, tt, src, act):
        right = put(src, w.at[p, tt, d], wz_s.at[0, p, tt], wz_r.at[p, tt], d, jnp.minimum(z + 1, 3))
        left = put(src, w.at[p, tt, d], wz_s.at[1, p, tt], wz_r.at[p, tt], d, jnp.maximum(z - 1, 0))

        @pl.when((tt <= z) & (z < 3))
        def _():
            act(right)

        @pl.when((tt >= z) & (z > 0))
        def _():
            act(left)

    def across(p, tt, src):
        return (
            put(src, w.at[p, tt, d], wa_s.at[p, tt], wa_r.at[p, tt], d1, z),
            put(src, w.at[p, tt, d], wb_s.at[p, tt, 0], wb_r.at[p, tt, 0], d2, z),
            put(src, w.at[p, tt, d], wc_s.at[p, tt, 0], wc_r.at[p, tt, 0], pal, z),
        )

    def after_first(p, tt):
        src = w.at[p, tt, d1]
        return (
            put(src, src, wb_s.at[p, tt, 1], wb_r.at[p, tt, 1], d2, z),
            put(src, src, wc_s.at[p, tt, 1], wc_r.at[p, tt, 1], pal, z),
        )

    def after_second(p, tt, i):
        src = w.at[p, tt, d2 if i == 0 else d12]
        return put(src, src, wc_s.at[p, tt, 2 + i], wc_r.at[p, tt, 2 + i], pal, z)

    def source(p, j):
        return own_w.at[p] if j == 0 else w.at[p, order[j], d]

    def arrive(ref, sem):
        return put(ref, ref, lo_sem.at[0], sem, pal, z)

    def begin(p, j):
        if j > 0:
            arrive(w.at[p, order[j], d], wz_r.at[p, order[j]]).wait_recv()
        along_z(p, order[j], source(p, j), lambda c: c.start())
        for copy in across(p, order[j], source(p, j)):
            copy.start()

    def relay_first(p, j):
        tt = order[j]
        arrive(w.at[p, tt, d1], wa_r.at[p, tt]).wait_recv()
        for copy in after_first(p, tt):
            copy.start()

    def relay_second(p, j):
        tt = order[j]
        for i in range(2):
            arrive(w.at[p, tt, d2 if i == 0 else d12], wb_r.at[p, tt, i]).wait_recv()
            after_second(p, tt, i).start()

    def token_slice(o, i):
        return t.at[pl.ds(pl.multiple_of((o * chunks + i) * ROWS, ROWS), ROWS)]

    def token_hop(o, i, hop, step):
        src = own_t.at[pl.ds(i * ROWS, ROWS)] if hop == 0 else token_slice(o, i)
        way = 0 if step > 0 else 1
        return put(src, token_slice(o, i), tk_s.at[way, hop, i], tk_r.at[way, hop, i], d, jnp.clip(z + step, 0, 3))

    last = SHORT // ROWS

    def wanted(o, i, target, step):
        k = o * chunks + i
        if step > 0:
            return (target <= 2) | (k >= last)
        return (target >= 1) | (k < 4 * chunks - last)

    def tokens(hop, step, act):
        o = z - step * hop
        target = z + step
        valid = (o >= 0) & (o <= 3) & (target >= 0) & (target <= 3)
        ids = range(chunks) if step < 0 else reversed(range(chunks))
        for i in ids:

            @pl.when(valid & wanted(o, i, target, step))
            def _():
                act(token_hop(o, i, hop, step))

    def tokens_in(hop, step):
        o = z - step * (hop + 1)
        valid = (o >= 0) & (o <= 3) & (z - step >= 0) & (z - step <= 3)
        way = 0 if step > 0 else 1
        ids = range(chunks) if step < 0 else reversed(range(chunks))
        for i in ids:

            @pl.when(valid & wanted(o, i, z, step))
            def _():
                ref = token_slice(jnp.clip(o, 0, 3), i)
                arrive(ref, tk_r.at[way, hop, i]).wait_recv()

    def small(stage):
        if stage == 0:
            return [
                put(own_s, s.at[d], sm_s.at[0], sm_r.at[0], d1, z),
                put(own_s, s.at[d], sm_s.at[1], sm_r.at[1], d2, z),
                put(own_s, s.at[d], sm_s.at[3], sm_r.at[3], pal, z),
            ]
        if stage == 1:
            return [
                put(s.at[d1], s.at[d1], sm_s.at[2], sm_r.at[2], d2, z),
                put(s.at[d1], s.at[d1], sm_s.at[4], sm_r.at[4], pal, z),
            ]
        return [
            put(s.at[d2], s.at[d2], sm_s.at[5], sm_r.at[5], pal, z),
            put(s.at[d12], s.at[d12], sm_s.at[6], sm_r.at[6], pal, z),
        ]

    blank[...] = jnp.zeros_like(blank)

    def blanks(act):
        for i in range(last):
            rows = pl.ds(pl.multiple_of(jnp.where(z == 0, 4 * chunks - last + i, i) * ROWS, ROWS), ROWS)

            @pl.when((z == 0) | (z == 3))
            def _():
                act(pltpu.make_async_copy(blank, t.at[rows], bl_sem.at[i]))

    for p in range(packs):
        begin(p, 0)
        if p == 0:
            for copy in small(0):
                copy.start()
            for step in (1, -1):
                tokens(0, step, lambda c: c.start())
    blanks(lambda c: c.start())
    arrive(s.at[d1], sm_r.at[0]).wait_recv()
    for copy in small(1):
        copy.start()
    for p in range(packs):
        relay_first(p, 0)
    arrive(s.at[d2], sm_r.at[1]).wait_recv()
    arrive(s.at[d12], sm_r.at[2]).wait_recv()
    for copy in small(2):
        copy.start()
    for j in range(1, 4):
        for p in range(packs):
            begin(p, j)
        for p in range(packs):
            relay_second(p, j - 1)
        for p in range(packs):
            relay_first(p, j)
        if j < 3:
            for step in (1, -1):
                tokens_in(j - 1, step)
                tokens(j, step, lambda c: c.start())
    for p in range(packs):
        relay_second(p, 3)
    for step in (1, -1):
        tokens_in(2, step)
    pd, pd1, pd2, pd12 = (xor(e, 1) for e in (d, d1, d2, d12))
    for i, e in enumerate((pd, pd2, pd1, pd12)):
        arrive(s.at[e], sm_r.at[3 + i]).wait_recv()
    for p in range(packs):
        for tt in range(4):
            for i, e in enumerate((pd, pd2, pd1, pd12)):
                arrive(w.at[p, tt, e], wc_r.at[p, tt, i]).wait_recv()
    for stage in range(3):
        for copy in small(stage):
            copy.wait_send()
    for hop in range(3):
        for step in (1, -1):
            tokens(hop, step, lambda c: c.wait_send())
    for p in range(packs):
        for j in range(4):
            tt = order[j]
            along_z(p, tt, source(p, j), lambda c: c.wait_send())
            for copy in across(p, tt, source(p, j)) + after_first(p, tt):
                copy.wait_send()
            for i in range(2):
                after_second(p, tt, i).wait_send()
    for copy in keep:
        copy.wait()
    blanks(lambda c: c.wait())


def gather_all(own_w, own_s, own_t):
    packs, r, c = own_w.shape
    rows, width = own_t.shape
    chunks = rows // ROWS
    dma = pltpu.SemaphoreType.DMA
    any_ = pl.BlockSpec(memory_space=pl.ANY)
    vmem = pl.BlockSpec(memory_space=pltpu.VMEM)
    return pl.pallas_call(
        gather_kernel,
        out_shape=(
            jax.ShapeDtypeStruct((packs, 4, 8, r, c), BF16),
            jax.ShapeDtypeStruct((8,) + own_s.shape, own_s.dtype),
            jax.ShapeDtypeStruct((4 * rows, width), BF16),
        ),
        in_specs=[vmem, vmem, vmem],
        out_specs=(any_, any_, any_),
        scratch_shapes=[
            dma((2, packs, 4)),
            dma((packs, 4)),
            dma((packs, 4)),
            dma((packs, 4)),
            dma((packs, 4, 2)),
            dma((packs, 4, 2)),
            dma((packs, 4, 4)),
            dma((packs, 4, 4)),
            dma((2, 3, chunks)),
            dma((2, 3, chunks)),
            dma((7,)),
            dma((7,)),
            dma((3,)),
            pltpu.VMEM((ROWS, width), BF16),
            dma((SHORT // ROWS,)),
        ],
        compiler_params=pltpu.CompilerParams(collective_id=0, has_side_effects=True),
        name="gather_all",
    )(own_w, own_s, own_t)


def reduce_kernel(
    g, sv, dt, base, out_w, out_s, out_t,
    gk, r1, b2, r2, b3, r3, s3, b4, r4, ds, dr, sk, q1, q2, q3, c2, c3, q4,
    gk_sem, p1_s, p1_r, p2_s, p2_r, p3_s, p3_r, p4_s, p4_r, t_l, t_s, t_r, v_s, v_r,
):
    z, d, core, first, second = position()
    e_mask, f_mask = second, first
    packs = g.shape[0]
    xy = d // 2
    e, f = xor(d, e_mask) // 2, xor(d, f_mask) // 2
    ef = xor(xor(d, e_mask), f_mask) // 2
    d_e, d_f, pal = xor(d, e_mask), xor(d, f_mask), xor(d, 1)
    chunks = base.shape[0] // ROWS
    total = 4 * chunks
    edge = SHORT // ROWS

    def put(src, dst, send, recv, dp, tp):
        return pltpu.make_async_remote_copy(
            src_ref=src, dst_ref=dst, send_sem=send, recv_sem=recv, device_id=(dp, tp), device_id_type=MESH
        )

    def up(ref):
        return ref[...].astype(F32)

    greet(z, d)
    fetch = [
        [pltpu.make_async_copy(g.at[p, t, :, core], gk.at[p, t], gk_sem.at[p, t]) for t in range(4)]
        for p in range(packs)
    ]
    one = [
        [put(g.at[p, t, :, 1 - core], r1.at[p, t], p1_s.at[p, t], p1_r.at[p, t], pal, z) for t in range(4)]
        for p in range(packs)
    ]
    two = [
        [put(b2.at[p, t], r2.at[p, t], p2_s.at[p, t], p2_r.at[p, t], d_e, z) for t in range(4)]
        for p in range(packs)
    ]
    three = [
        [put(b3.at[p, t], r3.at[p, t], p3_s.at[p, t], p3_r.at[p, t], d_f, z) for t in range(4)]
        for p in range(packs)
    ]

    def four(p, t, way):
        to = jnp.minimum(z + 1, 3) if way == 0 else jnp.maximum(z - 1, 0)
        return put(b4.at[p, way, t], r4.at[p, way, t], p4_s.at[p, way, t], p4_r.at[p, way, t], d, to)

    load = pltpu.make_async_copy(dt, ds, t_l)
    load.start()
    for p in range(packs):
        for t in range(4):
            one[p][t].start()
            fetch[p][t].start()

    small = [
        put(sv.at[:, 1 - core], q1, v_s.at[0], v_r.at[0], pal, z),
        put(c2, q2, v_s.at[1], v_r.at[1], d_e, z),
        put(c3, q3, v_s.at[2], v_r.at[2], d_f, z),
    ]
    small_z = [
        put(sk, q4.at[j - 1], v_s.at[2 + j], v_r.at[2 + j], d, lax.rem(z + j, 4)) for j in range(1, 4)
    ]
    small[0].start()

    def token(k, way):
        to = jnp.minimum(z + 1, 3) if way == 0 else jnp.maximum(z - 1, 0)
        slot = k if way == 0 else jnp.where(k // chunks == to, total + k % chunks, k)
        return put(ds.at[k], dr.at[slot], t_s.at[k], t_r.at[slot], d, to)

    def token_in(k, way):
        slot = k if way == 0 else jnp.where(k // chunks == z, total + k % chunks, k)
        return put(ds.at[k], dr.at[slot], t_s.at[k], t_r.at[slot], d, z), slot

    def sends(k, way):
        o = k // chunks
        if way == 0:
            low = 0 if k < total - edge else 1
            return (z >= low) & (z < o) & (o > low)
        high = 3 if k >= edge else 2
        return (z <= high) & (z > o) & (o < high)

    def starts(k, way):
        if way == 0:
            return z == (0 if k < total - edge else 1)
        return z == (3 if k >= edge else 2)

    right_order = [k for o in (3, 2, 1) for k in range(o * chunks, (o + 1) * chunks)]
    left_order = [total - 1 - k for k in right_order]
    load.wait()
    for kr, kl in zip(right_order, left_order):
        for k, way in ((kr, 0), (kl, 1)):

            @pl.when(sends(k, way) & starts(k, way))
            def _():
                token(k, way).start()

    def forward_tokens(at):
        for k, way in [(k, 0) for k in right_order] + [(k, 1) for k in left_order]:
            pos = at if way == 0 else 3 - at

            @pl.when(sends(k, way) & jnp.logical_not(starts(k, way)) & (z == pos))
            def _():
                got, slot = token_in(k, way)
                got.wait_recv()
                ds[k] = (ds[k].astype(F32) + dr[slot].astype(F32)).astype(BF16)
                token(k, way).start()

    def stage_two(p):
        for t in range(4):
            fetch[p][t].wait()
            one[p][t].wait_recv()
            for i, x in enumerate((e, ef)):
                b2[p, t, i] = (up(gk.at[p, t, x]) + up(r1.at[p, t, x])).astype(BF16)
            two[p][t].start()

    def stage_three(p):
        for t in range(4):
            two[p][t].wait_recv()
            b3[p, t] = (up(gk.at[p, t, f]) + up(r1.at[p, t, f]) + up(r2.at[p, t, 1])).astype(BF16)
            three[p][t].start()

    def stage_kept(p):
        for t in range(4):
            three[p][t].wait_recv()
            s3[p, t] = up(gk.at[p, t, xy]) + up(r1.at[p, t, xy]) + up(r2.at[p, t, 0]) + up(r3.at[p, t])

    def stage_four(p, t, way):
        goes = (t > z) if way == 0 else (t < z)
        inner = z > 0 if way == 0 else z < 3

        @pl.when(goes & inner)
        def _():
            four(p, t, way).wait_recv()
            b4[p, way, t] = (s3[p, t] + up(r4.at[p, way, t])).astype(BF16)

        @pl.when(goes & jnp.logical_not(inner))
        def _():
            b4[p, way, t] = s3[p, t].astype(BF16)

        @pl.when(goes)
        def _():
            four(p, t, way).start()

    for p in range(packs):
        stage_two(p)
        if p == 0:
            small[0].wait_recv()
            for i, x in enumerate((e, ef)):
                c2[i] = sv[x, core] + q1[x]
            small[1].start()
    forward_tokens(1)
    for p in range(packs):
        stage_three(p)
        if p == 0:
            small[1].wait_recv()
            c3[...] = sv[f, core] + q1[f] + q2[1]
            small[2].start()
    forward_tokens(2)
    small[2].wait_recv()
    sk[...] = sv[xy, core] + q1[xy] + q2[0] + q3[...]
    for copy in small_z:
        copy.start()
    for p in range(packs):
        stage_kept(p)
        for i in range(3):
            stage_four(p, 3 - i, 0)
            stage_four(p, i, 1)
    for copy in small_z:
        copy.wait_recv()
    out_s[...] = sk[...] + q4[0] + q4[1] + q4[2]
    for i in range(chunks):
        k = z * chunks + i
        rows = pl.ds(i * ROWS, ROWS)
        out_t[rows, :] = base[rows, :]
        from_left = (z > 0) & ((z > 1) | (k < total - edge))
        from_left = from_left & ((z != 1) | (k < total - edge))
        from_right = (z < 3) & ((z < 2) | (k >= edge))

        @pl.when(from_left)
        def _():
            put(ds.at[k], dr.at[k], t_s.at[k], t_r.at[k], d, z).wait_recv()
            out_t[rows, :] += dr[k].astype(F32)

        @pl.when(from_right)
        def _():
            put(ds.at[k], dr.at[total + i], t_s.at[k], t_r.at[total + i], d, z).wait_recv()
            out_t[rows, :] += dr[total + i].astype(F32)

    for p in range(packs):
        out_w[p] = s3[p, z]

        @pl.when(z > 0)
        def _():
            four(p, z, 0).wait_recv()
            out_w[p] += up(r4.at[p, 0, z])

        @pl.when(z < 3)
        def _():
            four(p, z, 1).wait_recv()
            out_w[p] += up(r4.at[p, 1, z])

    for copy in small + small_z:
        copy.wait_send()
    for p in range(packs):
        for t in range(4):
            one[p][t].wait_send()
            two[p][t].wait_send()
            three[p][t].wait_send()
            for way in range(2):

                @pl.when((t > z) if way == 0 else (t < z))
                def _():
                    four(p, t, way).wait_send()

    for k, way in [(k, 0) for k in right_order] + [(k, 1) for k in left_order]:

        @pl.when(sends(k, way))
        def _():
            token(k, way).wait_send()


def reduce_all(g, sv, dt, base):
    packs, _, _, r, c = g.shape
    rows, width = base.shape
    chunks = rows // ROWS
    dma = pltpu.SemaphoreType.DMA
    any_ = pl.BlockSpec(memory_space=pl.ANY)
    vmem = pl.BlockSpec(memory_space=pltpu.VMEM)
    vm = pltpu.VMEM
    block, sb = (r, c), sv.shape[1:]
    return pl.pallas_call(
        reduce_kernel,
        out_shape=(
            jax.ShapeDtypeStruct((packs,) + block, F32),
            jax.ShapeDtypeStruct(sb, F32),
            jax.ShapeDtypeStruct((rows, width), F32),
        ),
        in_specs=[any_, vmem, any_, vmem],
        out_specs=(vmem, vmem, vmem),
        scratch_shapes=[
            vm((packs, 4, 4) + block, BF16),
            vm((packs, 4, 4) + block, BF16),
            vm((packs, 4, 2) + block, BF16),
            vm((packs, 4, 2) + block, BF16),
            vm((packs, 4) + block, BF16),
            vm((packs, 4) + block, BF16),
            vm((packs, 4) + block, F32),
            vm((packs, 2, 4) + block, BF16),
            vm((packs, 2, 4) + block, BF16),
            vm((4 * chunks, ROWS, width), BF16),
            vm((5 * chunks, ROWS, width), BF16),
            vm(sb, F32),
            vm((4,) + sb, F32),
            vm((2,) + sb, F32),
            vm(sb, F32),
            vm((2,) + sb, F32),
            vm(sb, F32),
            vm((3,) + sb, F32),
            dma((packs, 4)),
            dma((packs, 4)),
            dma((packs, 4)),
            dma((packs, 4)),
            dma((packs, 4)),
            dma((packs, 4)),
            dma((packs, 4)),
            dma((packs, 2, 4)),
            dma((packs, 2, 4)),
            dma(()),
            dma((4 * chunks,)),
            dma((5 * chunks,)),
            dma((6,)),
            dma((6,)),
        ],
        compiler_params=pltpu.CompilerParams(
            collective_id=1, has_side_effects=True, vmem_limit_bytes=VMEM_MAX
        ),
        name="reduce_all",
    )(
        g.reshape(packs, 4, 4, 2, r, c),
        sv.reshape((4, 2) + sb),
        dt.reshape(4 * chunks, ROWS, width),
        base,
    )


def parts_of(z, own):
    sure = SHORT - own
    low = z < 2
    return (
        (jnp.where(low, 0, own - sure), sure, jnp.where(low, 0, SHORT)),
        (jnp.where(low, sure, 0), own - sure, jnp.where(z == 3, SHORT, 0)),
    )


def over_keys(z, part, start, total, act):
    window = total - SHORT
    for c in range(window // KEYS):
        act(pl.multiple_of(start + c * KEYS, KEYS))
    if part == 1:

        @pl.when((z == 1) | (z == 2))
        def _():
            for c in range(window // KEYS, total // KEYS):
                act(c * KEYS)


def aug_rows(top, r):
    return jnp.concatenate([top.astype(BF16), jnp.zeros((128 - 16, r), BF16)], axis=0)


def pick_rows(rows, r):
    index = lax.broadcasted_iota(jnp.int32, (16, r), 0)
    out = jnp.zeros((16, r), F32)
    for i, row in enumerate(rows):
        out = jnp.where(index == i, jnp.broadcast_to(row, (16, r)), out)
    return out


def split3(x):
    hi = x.astype(BF16).astype(F32)
    mid = (x - hi).astype(BF16).astype(F32)
    return hi, mid, x - hi - mid


def padded(head_rows, half, aug, r):
    zero = jnp.zeros((HD, r), BF16)
    pair = [head_rows, zero] if half == 0 else [zero, head_rows]
    return jnp.concatenate(pair + [aug], axis=0)


def attention_kernel(qt, k, vt, ka, ma, mixed_t, lse, s, m, l, acc):
    z = lax.axis_index("tp")
    own, total = qt.shape[1], k.shape[0]
    pairs = k.shape[1] // 128
    for part, (row0, r, start) in enumerate(parts_of(z, own)):
        cols = pl.ds(pl.multiple_of(row0, 128), r)
        aug = aug_rows(pick_rows((ma[0:1, cols], ma[1:2, cols]), r), r)

        def one_pair(pair, carry):
            lanes = pl.ds(pl.multiple_of(pair * 128, 128), 128)
            for half in range(2):
                m[half, :, :r] = jnp.full((1, r), MASKED, F32)
                l[half, :, :r] = jnp.zeros((1, r), F32)
                acc[half, :, :r] = jnp.zeros((HD, r), F32)
            qs = [
                padded(qt[pl.ds(pl.multiple_of(pair * 128 + half * HD, HD), HD), cols], half, aug, r)
                for half in range(2)
            ]

            def scores(key0):
                keys = pl.ds(key0, KEYS)
                left = jnp.concatenate([k[keys, lanes], ka[keys, :]], axis=1)
                for half in range(2):
                    score = dot(left, qs[half])
                    s[half, keys, :r] = score
                    m[half, :, :r] = jnp.maximum(m[half, :, :r], jnp.max(score, axis=0, keepdims=True))

            over_keys(z, part, start, total, scores)
            tops = [m[half, :, :r] for half in range(2)]

            def mix(key0):
                keys = pl.ds(key0, KEYS)
                for half in range(2):
                    raised = jnp.exp(s[half, keys, :r] - tops[half])
                    l[half, :, :r] += jnp.sum(raised, axis=0, keepdims=True)
                    values = vt[pl.ds(pl.multiple_of(pair * 128 + half * HD, HD), HD), keys]
                    acc[half, :, :r] += dot(values, raised.astype(BF16))

            over_keys(z, part, start, total, mix)
            for half in range(2):
                sums = l[half, :, :r]
                rows = pl.ds(pl.multiple_of(pair * 128 + half * HD, HD), HD)
                mixed_t[rows, cols] = acc[half, :, :r] / sums
                lse[pair, half : half + 1, cols] = tops[half] + jnp.log(sums)
            return carry

        lax.fori_loop(0, pairs, one_pair, 0)


def attention(qt, k, vt, ka, ma):
    width, own = qt.shape
    total = k.shape[0]
    widest = max(SHORT - own, own - (SHORT - own))
    vm = pltpu.VMEM
    return pl.pallas_call(
        attention_kernel,
        out_shape=(
            jax.ShapeDtypeStruct((width, own), F32),
            jax.ShapeDtypeStruct((width // 128, 8, own), F32),
        ),
        in_specs=[pl.BlockSpec(memory_space=pltpu.VMEM)] * 5,
        out_specs=(pl.BlockSpec(memory_space=pltpu.VMEM),) * 2,
        scratch_shapes=[
            vm((2, total, widest), F32),
            vm((2, 1, widest), F32),
            vm((2, 1, widest), F32),
            vm((2, HD, widest), F32),
        ],
        compiler_params=pltpu.CompilerParams(vmem_limit_bytes=VMEM_MAX),
        name="attention",
    )(qt, k, vt, ka, ma)


def attention_back_kernel(qt, q, k, kt, v, ka, ma, mixed_t, lse, dmt, dm, dqt, dk, dv, dka, dva, dqa):
    z = lax.axis_index("tp")
    own, total = qt.shape[1], k.shape[0]
    pairs = k.shape[1] // 128

    def one_pair(pair, carry):
        lanes = pl.ds(pl.multiple_of(pair * 128, 128), 128)
        dka[...] = jnp.zeros_like(dka)
        dva[...] = jnp.zeros_like(dva)
        for part, (row0, r, start) in enumerate(parts_of(z, own)):
            cols = pl.ds(pl.multiple_of(row0, 128), r)
            qs, gs, qm, gm = [], [], [], []
            low = lax.broadcasted_iota(jnp.int32, (r, 128), 1) < HD
            for half in range(2):
                rows = pl.ds(pl.multiple_of(pair * 128 + half * HD, HD), HD)
                delta = jnp.sum(dmt[rows, cols].astype(F32) * mixed_t[rows, cols], axis=0, keepdims=True)
                total_log = lse[pair, half : half + 1, cols]
                q_aug = pick_rows((ma[0:1, cols], ma[1:2, cols]) + split3(-total_log), r)
                zero = jnp.zeros((1, r), F32)
                g_aug = pick_rows((zero, zero) + split3(-delta), r)
                qs.append(padded(qt[rows, cols], half, aug_rows(q_aug, r), r))
                gs.append(padded(dmt[rows, cols], half, aug_rows(g_aug, r), r))
                mine = low if half == 0 else jnp.logical_not(low)
                here = pl.ds(pl.multiple_of(row0, 128), r)
                qm.append(jnp.where(mine, q[here, lanes], jnp.zeros((), BF16)))
                gm.append(jnp.where(mine, dm[here, lanes], jnp.zeros((), BF16)))
                dqa[half, :, :r] = jnp.zeros((HD, r), F32)

            def step(key0):
                keys = pl.ds(key0, KEYS)
                k_left = jnp.concatenate([k[keys, lanes], ka[keys, :]], axis=1)
                v_left = jnp.concatenate([v[keys, lanes], ka[keys, :]], axis=1)
                for half in range(2):
                    share = jnp.exp(dot(k_left, qs[half]))
                    slope = (share * dot(v_left, gs[half])).astype(BF16)
                    dva[keys, :] += dot(share.astype(BF16), gm[half])
                    dka[keys, :] += dot(slope, qm[half])
                    rows = pl.ds(pl.multiple_of(pair * 128 + half * HD, HD), HD)
                    dqa[half, :, :r] += dot(kt[rows, keys], slope)

            over_keys(z, part, start, total, step)
            for half in range(2):
                rows = pl.ds(pl.multiple_of(pair * 128 + half * HD, HD), HD)
                dqt[rows, cols] = (dqa[half, :, :r] * HD ** (-0.5)).astype(BF16)
        dk[:, lanes] = dka[...].astype(BF16)
        dv[:, lanes] = dva[...].astype(BF16)
        return carry

    lax.fori_loop(0, pairs, one_pair, 0)


def attention_back(qt, q, k, kt, v, ka, ma, mixed_t, lse, dmt, dm):
    width, own = qt.shape
    total = k.shape[0]
    widest = max(SHORT - own, own - (SHORT - own))
    vm = pltpu.VMEM
    return pl.pallas_call(
        attention_back_kernel,
        out_shape=(
            jax.ShapeDtypeStruct((width, own), BF16),
            jax.ShapeDtypeStruct((total, width), BF16),
            jax.ShapeDtypeStruct((total, width), BF16),
        ),
        in_specs=[pl.BlockSpec(memory_space=pltpu.VMEM)] * 11,
        out_specs=(pl.BlockSpec(memory_space=pltpu.VMEM),) * 3,
        scratch_shapes=[
            vm((total, 128), F32),
            vm((total, 128), F32),
            vm((2, HD, widest), F32),
        ],
        compiler_params=pltpu.CompilerParams(vmem_limit_bytes=VMEM_MAX),
        name="attention_back",
    )(qt, q, k, kt, v, ka, ma, mixed_t, lse, dmt, dm)


def body(
    tokens, w_query, w_key, w_value, b_query, b_value, w_out, b_out, gain_attn, shift_attn,
    w_up, b_up, w_down, b_down, gain_ffn, shift_ffn, lengths, deal_order, cotangent,
):
    own, width = tokens.shape
    n_tp, n_dp = lax.axis_size("tp"), lax.axis_size("dp")
    z, g = lax.axis_index("tp"), lax.axis_index("dp")
    total = own * n_tp
    r, hw = w_query.shape
    direct = n_tp == 4 and n_dp == 8 and r % 16 == 0

    own_w = jnp.stack([jnp.concatenate([w_query, w_key, w_value, w_out], axis=1), w_up, w_down])
    vectors = (b_query, b_value, b_out, gain_attn, shift_attn, b_down, gain_ffn, shift_ffn, b_up)
    own_s = jnp.concatenate(vectors)
    n_small = own_s.shape[0]
    if direct:
        padded_s = jnp.pad(own_s, (0, 2048 - n_small)).reshape(16, 128)
        w, s, x = gather_all(own_w, padded_s, tokens)
        s = s.reshape(n_dp, 2048)
    else:
        w = lax.all_gather(own_w, ("tp", "dp"), axis=0).reshape((n_tp, n_dp) + own_w.shape)
        w = jnp.moveaxis(w, 2, 0)
        s = lax.all_gather(own_s, "dp", axis=0)
        x = lax.all_gather(tokens, "tp", axis=0, tiled=True)
    w = w.reshape(3, n_tp, width, w_up.shape[1])
    small = [s[:, i * r : (i + 1) * r].reshape(width).astype(F32) for i in range(8)]
    bq, bv, bo, g1, h1, bd, g2, h2 = small
    bu = s[:, 8 * r : n_small].reshape(-1).astype(F32)
    wq, wk, wv, wo = (
        w[0, :, :, i * hw : (i + 1) * hw].transpose(1, 0, 2).reshape(width, width) for i in range(4)
    )

    pair = lax.dynamic_slice_in_dim(deal_order, 2 * g, 1)
    first_len = jnp.sum(jnp.where(jnp.arange(lengths.shape[0], dtype=jnp.int32) == pair[0], lengths, 0))
    key_seg = jnp.arange(total, dtype=jnp.int32)[:, None] >= first_len
    lane = jnp.arange(128, dtype=jnp.int32)[None, :]
    ka = jnp.where(lane == 0, ~key_seg, jnp.where(lane == 1, key_seg, (lane >= 2) & (lane < 5))).astype(BF16)
    row_seg = (z * own + jnp.arange(own, dtype=jnp.int32))[None, :] >= first_len
    sub = jnp.arange(8, dtype=jnp.int32)[:, None]
    ma = jnp.where(((sub == 0) & row_seg) | ((sub == 1) & ~row_seg), MASKED, 0.0).astype(F32)

    q = (dot(tokens, wq) + bq).astype(BF16) * jnp.asarray(HD ** (-0.5), BF16)
    k = dot(x, wk).astype(BF16)
    v = (dot(x, wv) + bv).astype(BF16)
    qt = q.T
    mixed_t, lse = attention(qt, k, v.T, ka, ma)
    mixed = mixed_t.T.astype(BF16)
    first_residual = tokens.astype(F32) + contract_last(mixed, wo) + bo
    xhat1, inv1 = normalize_layer(first_residual)
    y1 = xhat1 * g1 + h1
    y1r = y1.astype(BF16)

    u = [dot(y1r, w[1, t]) + bu.reshape(n_tp, -1)[t] for t in range(n_tp)]
    hr = [jax.nn.gelu(a, approximate=False).astype(BF16) for a in u]
    ffn = sum(contract_last(hr[t], w[2, t]) for t in range(n_tp))
    xhat2, inv2 = normalize_layer(y1 + ffn + bd)
    encoder_output = (xhat2 * g2 + h2).astype(BF16)

    grad = cotangent.astype(F32)
    dr2 = normalize_backward(grad, xhat2, inv2, g2)
    dfr = dr2.astype(BF16)
    du = [(dot(dfr, w[2, t]) * gelu_slope(u[t])).astype(BF16) for t in range(n_tp)]
    dy1 = dr2 + sum(contract_last(du[t], w[1, t]) for t in range(n_tp))
    dr1 = normalize_backward(dy1, xhat1, inv1, g1)
    dar = dr1.astype(BF16)
    dm = dot(dar, wo).astype(BF16)
    dqt, dk, dv = attention_back(qt, q, k, k.T, v, ka, ma, mixed_t, lse, dm.T, dm)
    dq = dqt.T
    base = dr1 + contract_last(dq, wq)
    far = contract_last(dk, wk) + contract_last(dv, wv)
    base = base + lax.dynamic_slice_in_dim(far, z * own, own)
    dt = far.astype(BF16)
    gq, gk, gv = contract_first(tokens, dq), contract_first(x, dk), contract_first(x, dv)
    go = contract_first(dar, mixed)
    ga = jnp.stack(
        [
            jnp.concatenate([m[:, t * hw : (t + 1) * hw] for m in (gq, gk, gv, go)], axis=1)
            for t in range(n_tp)
        ]
    )
    gu = jnp.stack([contract_first(y1r, du[t]) for t in range(n_tp)])
    gd = jnp.stack([contract_first(dfr, hr[t]) for t in range(n_tp)])
    sums = [
        jnp.sum(dq, axis=0, dtype=F32),
        jnp.sum(dv, axis=0, dtype=F32),
        jnp.sum(dar, axis=0, dtype=F32),
        jnp.sum(dy1 * xhat1, axis=0),
        jnp.sum(dy1, axis=0),
        jnp.sum(dfr, axis=0, dtype=F32),
        jnp.sum(grad * xhat2, axis=0),
        jnp.sum(grad, axis=0),
    ]
    sums = [a.reshape(n_dp, r) for a in sums]
    sums.append(jnp.concatenate([jnp.sum(a, axis=0, dtype=F32) for a in du]).reshape(n_dp, -1))
    sv = jnp.concatenate(sums, axis=1)
    if direct:
        grads = jnp.stack([ga, gu, gd]).astype(BF16).reshape(3, n_tp, n_dp, r, -1)
        sv = jnp.pad(sv, ((0, 0), (0, 2048 - n_small))).reshape(n_dp, 16, 128)
        gw, gs, grad_tokens = reduce_all(grads, sv, dt, base)
        gs = gs.reshape(-1)
    else:
        grads = jnp.stack([ga, gu, gd], axis=1).reshape(n_tp, 3, n_dp, r, -1)
        grads = jnp.moveaxis(grads, 1, 2).reshape(n_tp * n_dp, 3, r, -1)
        gw = lax.psum_scatter(grads, ("tp", "dp"), scatter_dimension=0, tiled=True)[0]
        gs = lax.psum_scatter(lax.psum(sv, "tp"), "dp", scatter_dimension=0, tiled=True)[0]
        others = jnp.where(jnp.arange(total)[:, None] // own == z, jnp.zeros((), BF16), dt)
        grad_tokens = base + lax.psum_scatter(others, "tp", scatter_dimension=0, tiled=True).astype(F32)
    gs = [gs[i * r : (i + 1) * r] for i in range(8)] + [gs[8 * r : n_small]]
    a = gw[0]
    return (
        encoder_output, grad_tokens,
        a[:, :hw], a[:, hw : 2 * hw], a[:, 2 * hw : 3 * hw], gs[0], gs[1],
        a[:, 3 * hw :], gs[2], gs[3], gs[4],
        gw[1], gs[8], gw[2], gs[5], gs[6], gs[7],
    )


def solution(mesh):
    rows, block, vector = P(("dp", "tp"), None), P("dp", "tp"), P("dp")
    in_specs = (
        rows, block, block, block, vector, vector, block, vector, vector, vector,
        block, vector, block, vector, vector, vector, P(), P(), rows,
    )
    out_specs = (
        rows, rows, block, block, block, vector, vector, block, vector, vector, vector,
        block, vector, block, vector, vector, vector,
    )
    return jax.shard_map(body, mesh=mesh, in_specs=in_specs, out_specs=out_specs, check_vma=False)
```

```python
import functools

import jax
import jax.numpy as jnp
from jax import lax
from jax.experimental import pallas as pl
from jax.experimental.pallas import tpu as pltpu
from jax.sharding import PartitionSpec as P

HD = 64
SHORT = 1024
EPS = 1e-05
SQRT_HALF = 0.7071067811865476
INV_ROOT_TAU = 0.3989422804014327
MASKED = -1e30
KEYS = 512
ROWS = 128
VMEM_MAX = 67043328
MESH = pl.DeviceIdType.MESH
F32 = jnp.float32
BF16 = jnp.bfloat16


def dot(left, right):
    return jnp.dot(left, right, preferred_element_type=F32)


def contract_last(left, right):
    return lax.dot_general(left, right, (((1,), (1,)), ((), ())), preferred_element_type=F32)


def contract_first(left, right):
    return lax.dot_general(left, right, (((0,), (0,)), ((), ())), preferred_element_type=F32)


def normalize_layer(resid):
    center = resid - jnp.mean(resid, axis=-1, keepdims=True)
    inverse_deviation = lax.rsqrt(jnp.mean(center * center, axis=-1, keepdims=True) + EPS)
    return (center * inverse_deviation, inverse_deviation)


def normalize_backward(output_gradient, xhat, inverse_deviation, gain):
    scaled_rows = output_gradient * gain
    return inverse_deviation * (
        scaled_rows
        - jnp.mean(scaled_rows, axis=-1, keepdims=True)
        - xhat * jnp.mean(scaled_rows * xhat, axis=-1, keepdims=True)
    )


def gelu_slope(pre_act):
    return (
        0.5 * (1.0 + lax.erf(pre_act * SQRT_HALF))
        + pre_act * jnp.exp(-0.5 * pre_act * pre_act) * INV_ROOT_TAU
    )


def position():
    z = lax.axis_index("tp")
    d = lax.axis_index("dp")
    core = lax.rem(d, 2)
    first = 2 + 2 * core
    second = 4 - 2 * core
    return z, d, core, first, second


def xor(d, mask):
    return d + mask * (1 - 2 * lax.rem(d // mask, 2))


def greet(z, d):
    barrier = pltpu.get_barrier_semaphore()
    for mask in (1, 2, 4):
        pl.semaphore_signal(barrier, inc=1, device_id=(xor(d, mask), z), device_id_type=MESH)
    for j in range(1, 4):
        pl.semaphore_signal(barrier, inc=1, device_id=(d, lax.rem(z + j, 4)), device_id_type=MESH)
    pl.semaphore_wait(barrier, 6)


def by_distance(z):
    low = z <= 1
    near = jnp.where(z == 0, 1, jnp.where(z == 3, 2, z - 1))
    mid = jnp.where(z == 0, 2, jnp.where(z == 3, 1, z + 1))
    far = jnp.where(low, 3, 0)
    return (z, near, mid, far)


def put(src, dst, send, recv, dp, tp):
    return pltpu.make_async_remote_copy(
        src_ref=src, dst_ref=dst, send_sem=send, recv_sem=recv, device_id=(dp, tp), device_id_type=MESH
    )


def forward_kernel(
    lengths, deal, own_w, own_s, own_t,
    w, vec, bu, x_out, q_out, qt_out, k_out, v_out, kt_out, wd_out, mixed_t, lse,
    wa, s, x, q, qt, k, v, kt, vt, wd, ka, sc, m, l, acc,
    wz_s, wz_r, wa_s, wa_r, wb_s, wb_r, wc_s, wc_r, tk_s, tk_r, sm_s, sm_r, lo_sem, arr_sem, out_sem,
):
    z, d, core, first, second = position()
    packs = own_w.shape[0]
    own, width = own_t.shape
    total = 4 * own
    hw = width // 4
    chunks = own // ROWS
    d1, d2 = xor(d, first), xor(d, second)
    d12 = xor(d1, second)
    pal = xor(d, 1)
    pd, pd1, pd2, pd12 = (xor(e, 1) for e in (d, d1, d2, d12))
    order = by_distance(z)
    first_len = lengths[deal[2 * d]]

    greet(z, d)

    def block(p, tt, e):
        return wa.at[tt, e] if p == 0 else w.at[p - 1, tt, e]

    def along_z(p, tt, src, act):
        dst = block(p, tt, d)
        right = put(src, dst, wz_s.at[0, p, tt], wz_r.at[p, tt], d, jnp.minimum(z + 1, 3))
        left = put(src, dst, wz_s.at[1, p, tt], wz_r.at[p, tt], d, jnp.maximum(z - 1, 0))

        @pl.when((tt <= z) & (z < 3))
        def _():
            act(right)

        @pl.when((tt >= z) & (z > 0))
        def _():
            act(left)

    def across(p, tt, src):
        dst = block(p, tt, d)
        return (
            put(src, dst, wa_s.at[p, tt], wa_r.at[p, tt], d1, z),
            put(src, dst, wb_s.at[p, tt, 0], wb_r.at[p, tt, 0], d2, z),
            put(src, dst, wc_s.at[p, tt, 0], wc_r.at[p, tt, 0], pal, z),
        )

    def after_first(p, tt):
        src = block(p, tt, d1)
        return (
            put(src, src, wb_s.at[p, tt, 1], wb_r.at[p, tt, 1], d2, z),
            put(src, src, wc_s.at[p, tt, 1], wc_r.at[p, tt, 1], pal, z),
        )

    def after_second(p, tt, i):
        src = block(p, tt, d2 if i == 0 else d12)
        return put(src, src, wc_s.at[p, tt, 2 + i], wc_r.at[p, tt, 2 + i], pal, z)

    def source(p, j):
        return own_w.at[p] if j == 0 else block(p, order[j], d)

    def arrive(ref, sem):
        put(ref, ref, arr_sem, sem, pal, z).wait_recv()

    def begin(p, j):
        if j > 0:
            arrive(block(p, order[j], d), wz_r.at[p, order[j]])
        along_z(p, order[j], source(p, j), lambda c: c.start())
        for copy in across(p, order[j], source(p, j)):
            copy.start()

    def relay_first(p, j):
        tt = order[j]
        arrive(block(p, tt, d1), wa_r.at[p, tt])
        for copy in after_first(p, tt):
            copy.start()

    def relay_second(p, j):
        tt = order[j]
        for i in range(2):
            arrive(block(p, tt, d2 if i == 0 else d12), wb_r.at[p, tt, i])
            after_second(p, tt, i).start()

    def from_pal(p):
        for tt in range(4):
            for i, e in enumerate((pd, pd2, pd1, pd12)):
                arrive(block(p, tt, e), wc_r.at[p, tt, i])

    def sent(p):
        for j in range(4):
            tt = order[j]
            along_z(p, tt, source(p, j), lambda c: c.wait_send())
            for copy in across(p, tt, source(p, j)) + after_first(p, tt):
                copy.wait_send()
            for i in range(2):
                after_second(p, tt, i).wait_send()

    def token_slice(o, i):
        return x.at[pl.ds(pl.multiple_of((o * chunks + i) * ROWS, ROWS), ROWS)]

    def token_hop(o, i, hop, step):
        src = own_t.at[pl.ds(i * ROWS, ROWS)] if hop == 0 else token_slice(o, i)
        way = 0 if step > 0 else 1
        return put(src, token_slice(o, i), tk_s.at[way, hop, i], tk_r.at[way, hop, i], d, jnp.clip(z + step, 0, 3))

    last = SHORT // ROWS

    def wanted(o, i, target, step):
        n = o * chunks + i
        if step > 0:
            return (target <= 2) | (n >= last)
        return (target >= 1) | (n < 4 * chunks - last)

    def chunk_ids(step):
        return range(chunks) if step < 0 else reversed(range(chunks))

    def tokens(hop, step, act):
        o, target = z - step * hop, z + step
        valid = (o >= 0) & (o <= 3) & (target >= 0) & (target <= 3)
        for i in chunk_ids(step):

            @pl.when(valid & wanted(o, i, target, step))
            def _():
                act(token_hop(o, i, hop, step))

    def tokens_on(hop, step, onward):
        o, target = z - step * (hop + 1), z + step
        valid = (o >= 0) & (o <= 3) & (z - step >= 0) & (z - step <= 3)
        way = 0 if step > 0 else 1
        for i in chunk_ids(step):

            @pl.when(valid & wanted(o, i, z, step))
            def _():
                arrive(token_slice(jnp.clip(o, 0, 3), i), tk_r.at[way, hop, i])

            if onward:

                @pl.when(valid & (target >= 0) & (target <= 3) & wanted(o, i, target, step))
                def _():
                    token_hop(o, i, hop + 1, step).start()

    def small(stage):
        if stage == 0:
            return [
                put(own_s, s.at[d], sm_s.at[0], sm_r.at[0], d1, z),
                put(own_s, s.at[d], sm_s.at[1], sm_r.at[1], d2, z),
                put(own_s, s.at[d], sm_s.at[3], sm_r.at[3], pal, z),
            ]
        if stage == 1:
            return [
                put(s.at[d1], s.at[d1], sm_s.at[2], sm_r.at[2], d2, z),
                put(s.at[d1], s.at[d1], sm_s.at[4], sm_r.at[4], pal, z),
            ]
        return [
            put(s.at[d2], s.at[d2], sm_s.at[5], sm_r.at[5], pal, z),
            put(s.at[d12], s.at[d12], sm_s.at[6], sm_r.at[6], pal, z),
        ]

    begin(0, 0)
    for copy in small(0):
        copy.start()
    s[d] = own_s[...]
    wa[z, d] = own_w[0]
    mine = pl.ds(pl.multiple_of(z * own, ROWS), own)
    x[mine, :] = own_t[...]
    keep = pltpu.make_async_copy(own_w.at[pl.ds(1, packs - 1)], w.at[:, z, d], lo_sem)
    keep.start()

    @pl.when(z == 0)
    def _():
        x[total - SHORT :, :] = jnp.zeros((SHORT, width), BF16)

    @pl.when(z == 3)
    def _():
        x[:SHORT, :] = jnp.zeros((SHORT, width), BF16)

    lane = lax.broadcasted_iota(jnp.int32, (own, 128), 1)
    for i in range(4):
        late = lax.broadcasted_iota(jnp.int32, (own, 128), 0) + i * own >= first_len
        ones = jnp.where((lane >= 2) & (lane < 5), 1.0, 0.0)
        flags = jnp.where(lane == 0, jnp.where(late, 0.0, 1.0), jnp.where(lane == 1, jnp.where(late, 1.0, 0.0), ones))
        ka[pl.ds(i * own, own), :] = flags.astype(BF16)

    relay_first(0, 0)
    begin(0, 1)
    for step in (1, -1):
        tokens(0, step, lambda c: c.start())
    relay_second(0, 0)
    relay_first(0, 1)
    arrive(s.at[d1], sm_r.at[0])
    for copy in small(1):
        copy.start()
    begin(0, 2)
    relay_second(0, 1)
    relay_first(0, 2)
    begin(0, 3)
    relay_second(0, 2)
    relay_first(0, 3)
    for p in range(1, packs):
        begin(p, 0)
    arrive(s.at[d2], sm_r.at[1])
    arrive(s.at[d12], sm_r.at[2])
    for copy in small(2):
        copy.start()
    relay_second(0, 3)
    for i, e in enumerate((pd, pd2, pd1, pd12)):
        arrive(s.at[e], sm_r.at[3 + i])
    r = width // 8
    for e in range(8):
        piece = s[e].astype(F32)
        vec[0:8, e * r : (e + 1) * r] = piece[0:8, 0:r]
        for j in range(hw * 2 // 128):
            col = e * hw * 2 + j * 128
            bu[0:1, col : col + 128] = piece[8 + j : 9 + j, :]
    from_pal(0)
    for tt in range(4):
        rows = wa[tt].reshape(width, width)
        for i in range(4):
            wd[i, :, tt * hw : (tt + 1) * hw] = rows[:, i * hw : (i + 1) * hw]
    wd_copy = pltpu.make_async_copy(wd, wd_out, out_sem.at[0])
    wd_copy.start()

    tile = 256

    def q_tile(n, carry):
        lanes = pl.ds(pl.multiple_of(n * tile, tile), tile)
        rows = (dot(own_t[...], wd[0, :, lanes]) + vec[0:1, lanes]).astype(BF16) * jnp.asarray(HD ** (-0.5), BF16)
        q[:, lanes] = rows
        qt[lanes, :] = rows.T
        return carry

    def project(o):
        rows = pl.ds(pl.multiple_of(o * own, ROWS), own)

        def kv_tile(n, carry):
            lanes = pl.ds(pl.multiple_of(n * tile, tile), tile)
            keys = dot(x[rows, :], wd[1, :, lanes]).astype(BF16)
            k[rows, lanes] = keys
            kt[lanes, rows] = keys.T
            values = (dot(x[rows, :], wd[2, :, lanes]) + vec[1:2, lanes]).astype(BF16)
            v[rows, lanes] = values
            vt[lanes, rows] = values.T
            return carry

        lax.fori_loop(0, width // tile, kv_tile, 0)

    lax.fori_loop(0, width // tile, q_tile, 0)
    project(z)
    for step in (1, -1):
        tokens_on(0, step, True)
    for p in range(1, packs):
        relay_first(p, 0)

    @pl.when(z > 0)
    def _():
        project(jnp.maximum(z - 1, 0))

    for p in range(1, packs):
        begin(p, 1)

    @pl.when(z < 3)
    def _():
        project(jnp.minimum(z + 1, 3))

    for p in range(1, packs):
        relay_second(p, 0)
        relay_first(p, 1)
    for step in (1, -1):
        tokens_on(1, step, False)
    for p in range(1, packs):
        begin(p, 2)
    project(jnp.where(z == 0, 2, jnp.where(z == 1, 3, z - 2)))
    outs = [
        pltpu.make_async_copy(a, b, out_sem.at[1 + i])
        for i, (a, b) in enumerate(((x, x_out), (q, q_out), (qt, qt_out), (k, k_out), (v, v_out), (kt, kt_out)))
    ]
    for copy in outs:
        copy.start()

    def both(act, j):
        def run():
            for p in range(1, packs):
                act(p, j)

        return run

    def seq(*runs):
        def run():
            for one in runs:
                one()

        return run

    between = {
        (0, 0): both(relay_second, 1),
        (0, 1): both(relay_first, 2),
        (0, 2): both(begin, 3),
        (0, 4): both(relay_second, 2),
        (1, 0): both(relay_first, 3),
        (1, 4): both(relay_second, 3),
    }
    pairs = width // 128
    for part, (row0, n, start) in enumerate(parts_of(z, own)):
        cols = pl.ds(pl.multiple_of(row0, 128), n)
        late = lax.broadcasted_iota(jnp.int32, (1, n), 1) + (z * own + row0) >= first_len
        masks = (jnp.where(late, MASKED, 0.0), jnp.where(late, 0.0, MASKED))
        aug = aug_rows(pick_rows(masks, n), n)

        def one_pair(pair, carry):
            for (at, i), run in between.items():
                if at == part:

                    @pl.when(pair == i)
                    def _():
                        run()

            attend_pair(z, part, start, pair, cols, n, aug, qt, k, vt, ka, mixed_t, lse, sc, m, l, acc)
            return carry

        lax.fori_loop(0, pairs, one_pair, 0)

    for p in range(1, packs):
        from_pal(p)
    for stage in range(3):
        for copy in small(stage):
            copy.wait_send()
    for hop in range(2):
        for step in (1, -1):
            tokens(hop, step, lambda c: c.wait_send())
    for p in range(packs):
        sent(p)
    keep.wait()
    wd_copy.wait()
    for copy in outs:
        copy.wait()


def attend_pair(z, part, start, pair, cols, n, aug, qt, k, vt, ka, mixed_t, lse, s, m, l, acc):
    total = k.shape[0]
    lanes = pl.ds(pl.multiple_of(pair * 128, 128), 128)
    for half in range(2):
        m[half, :, :n] = jnp.full((1, n), MASKED, F32)
        l[half, :, :n] = jnp.zeros((1, n), F32)
        acc[half, :, :n] = jnp.zeros((HD, n), F32)
    qs = [padded(qt[pl.ds(pl.multiple_of(pair * 128 + half * HD, HD), HD), cols], half, aug, n) for half in range(2)]

    def scores(key0):
        keys = pl.ds(key0, KEYS)
        left = jnp.concatenate([k[keys, lanes], ka[keys, :]], axis=1)
        for half in range(2):
            score = dot(left, qs[half])
            s[half, keys, :n] = score
            m[half, :, :n] = jnp.maximum(m[half, :, :n], jnp.max(score, axis=0, keepdims=True))

    over_keys(z, part, start, total, scores)
    tops = [m[half, :, :n] for half in range(2)]

    def mix(key0):
        keys = pl.ds(key0, KEYS)
        for half in range(2):
            raised = jnp.exp(s[half, keys, :n] - tops[half])
            l[half, :, :n] += jnp.sum(raised, axis=0, keepdims=True)
            values = vt[pl.ds(pl.multiple_of(pair * 128 + half * HD, HD), HD), keys]
            acc[half, :, :n] += dot(values, raised.astype(BF16))

    over_keys(z, part, start, total, mix)
    for half in range(2):
        sums = l[half, :, :n]
        rows = pl.ds(pl.multiple_of(pair * 128 + half * HD, HD), HD)
        mixed_t[rows, cols] = acc[half, :, :n] / sums
        lse[pair, half : half + 1, cols] = tops[half] + jnp.log(sums)


def forward_all(lengths, deal, own_w, own_s, own_t):
    packs, r, c = own_w.shape
    own, width = own_t.shape
    total = 4 * own
    chunks = own // ROWS
    widest = max(SHORT - own, own - (SHORT - own))
    dma, vm = pltpu.SemaphoreType.DMA, pltpu.VMEM
    any_ = pl.BlockSpec(memory_space=pl.ANY)
    vmem = pl.BlockSpec(memory_space=pltpu.VMEM)
    smem = pl.BlockSpec(memory_space=pltpu.SMEM)
    shape = jax.ShapeDtypeStruct
    return pl.pallas_call(
        forward_kernel,
        out_shape=(
            shape((packs - 1, 4, 8, r, c), BF16),
            shape((8, width), F32),
            shape((1, 4 * c), F32),
            shape((total, width), BF16),
            shape((own, width), BF16),
            shape((width, own), BF16),
            shape((total, width), BF16),
            shape((total, width), BF16),
            shape((width, total), BF16),
            shape((4, width, width), BF16),
            shape((width, own), F32),
            shape((width // 128, 8, own), F32),
        ),
        in_specs=[smem, smem, vmem, vmem, vmem],
        out_specs=(any_, vmem, vmem) + (any_,) * 7 + (vmem, vmem),
        scratch_shapes=[
            vm((4, 8, r, c), BF16),
            vm((8, 16, 128), BF16),
            vm((total, width), BF16),
            vm((own, width), BF16),
            vm((width, own), BF16),
            vm((total, width), BF16),
            vm((total, width), BF16),
            vm((width, total), BF16),
            vm((width, total), BF16),
            vm((4, width, width), BF16),
            vm((total, 128), BF16),
            vm((2, total, widest), F32),
            vm((2, 1, widest), F32),
            vm((2, 1, widest), F32),
            vm((2, HD, widest), F32),
            dma((2, packs, 4)),
            dma((packs, 4)),
            dma((packs, 4)),
            dma((packs, 4)),
            dma((packs, 4, 2)),
            dma((packs, 4, 2)),
            dma((packs, 4, 4)),
            dma((packs, 4, 4)),
            dma((2, 2, chunks)),
            dma((2, 2, chunks)),
            dma((7,)),
            dma((7,)),
            dma(()),
            dma(()),
            dma((7,)),
        ],
        compiler_params=pltpu.CompilerParams(
            collective_id=0, has_side_effects=True, vmem_limit_bytes=VMEM_MAX
        ),
        name="forward_all",
    )(lengths, deal, own_w, own_s, own_t)


def reduce_kernel(
    g, sv, dt, base, out_w, out_s, out_t,
    gk, r1, b2, r2, b3, r3, s3, b4, r4, ds, dr, sk, q1, q2, q3, c2, c3, q4,
    gk_sem, p1_s, p1_r, p2_s, p2_r, p3_s, p3_r, p4_s, p4_r, t_l, t_s, t_r, v_s, v_r,
):
    z, d, core, first, second = position()
    e_mask, f_mask = second, first
    packs = g.shape[0]
    xy = d // 2
    e, f = xor(d, e_mask) // 2, xor(d, f_mask) // 2
    ef = xor(xor(d, e_mask), f_mask) // 2
    d_e, d_f, pal = xor(d, e_mask), xor(d, f_mask), xor(d, 1)
    chunks = base.shape[0] // ROWS
    total = 4 * chunks
    edge = SHORT // ROWS

    def up(ref):
        return ref[...].astype(F32)

    greet(z, d)
    fetch = [
        [pltpu.make_async_copy(g.at[p, t, :, core], gk.at[p, t], gk_sem.at[p, t]) for t in range(4)]
        for p in range(packs)
    ]
    one = [
        [put(g.at[p, t, :, 1 - core], r1.at[p, t], p1_s.at[p, t], p1_r.at[p, t], pal, z) for t in range(4)]
        for p in range(packs)
    ]
    two = [
        [put(b2.at[p, t], r2.at[p, t], p2_s.at[p, t], p2_r.at[p, t], d_e, z) for t in range(4)]
        for p in range(packs)
    ]
    three = [
        [put(b3.at[p, t], r3.at[p, t], p3_s.at[p, t], p3_r.at[p, t], d_f, z) for t in range(4)]
        for p in range(packs)
    ]

    def four(p, t, way):
        to = jnp.minimum(z + 1, 3) if way == 0 else jnp.maximum(z - 1, 0)
        return put(b4.at[p, way, t], r4.at[p, way, t], p4_s.at[p, way, t], p4_r.at[p, way, t], d, to)

    load = pltpu.make_async_copy(dt, ds, t_l)
    load.start()
    for p in range(packs):
        for t in range(4):
            one[p][t].start()
            fetch[p][t].start()

    small = [
        put(sv.at[:, 1 - core], q1, v_s.at[0], v_r.at[0], pal, z),
        put(c2, q2, v_s.at[1], v_r.at[1], d_e, z),
        put(c3, q3, v_s.at[2], v_r.at[2], d_f, z),
    ]
    small_z = [
        put(sk, q4.at[j - 1], v_s.at[2 + j], v_r.at[2 + j], d, lax.rem(z + j, 4)) for j in range(1, 4)
    ]
    small[0].start()

    def token(k, way):
        to = jnp.minimum(z + 1, 3) if way == 0 else jnp.maximum(z - 1, 0)
        slot = k if way == 0 else jnp.where(k // chunks == to, total + k % chunks, k)
        return put(ds.at[k], dr.at[slot], t_s.at[k], t_r.at[slot], d, to)

    def token_in(k, way):
        slot = k if way == 0 else jnp.where(k // chunks == z, total + k % chunks, k)
        return put(ds.at[k], dr.at[slot], t_s.at[k], t_r.at[slot], d, z), slot

    def sends(k, way):
        o = k // chunks
        if way == 0:
            low = 0 if k < total - edge else 1
            return (z >= low) & (z < o) & (o > low)
        high = 3 if k >= edge else 2
        return (z <= high) & (z > o) & (o < high)

    def starts(k, way):
        if way == 0:
            return z == (0 if k < total - edge else 1)
        return z == (3 if k >= edge else 2)

    right_order = [k for o in (3, 2, 1) for k in range(o * chunks, (o + 1) * chunks)]
    left_order = [total - 1 - k for k in right_order]
    load.wait()
    for kr, kl in zip(right_order, left_order):
        for k, way in ((kr, 0), (kl, 1)):

            @pl.when(sends(k, way) & starts(k, way))
            def _():
                token(k, way).start()

    def forward_tokens(at):
        for k, way in [(k, 0) for k in right_order] + [(k, 1) for k in left_order]:
            pos = at if way == 0 else 3 - at

            @pl.when(sends(k, way) & jnp.logical_not(starts(k, way)) & (z == pos))
            def _():
                got, slot = token_in(k, way)
                got.wait_recv()
                ds[k] = (ds[k].astype(F32) + dr[slot].astype(F32)).astype(BF16)
                token(k, way).start()

    def stage_two(p):
        for t in range(4):
            fetch[p][t].wait()
            one[p][t].wait_recv()
            for i, x in enumerate((e, ef)):
                b2[p, t, i] = (up(gk.at[p, t, x]) + up(r1.at[p, t, x])).astype(BF16)
            two[p][t].start()

    def stage_three(p):
        for t in range(4):
            two[p][t].wait_recv()
            b3[p, t] = (up(gk.at[p, t, f]) + up(r1.at[p, t, f]) + up(r2.at[p, t, 1])).astype(BF16)
            three[p][t].start()

    def stage_kept(p):
        for t in range(4):
            three[p][t].wait_recv()
            s3[p, t] = up(gk.at[p, t, xy]) + up(r1.at[p, t, xy]) + up(r2.at[p, t, 0]) + up(r3.at[p, t])

    def stage_four(p, t, way):
        goes = (t > z) if way == 0 else (t < z)
        inner = z > 0 if way == 0 else z < 3

        @pl.when(goes & inner)
        def _():
            four(p, t, way).wait_recv()
            b4[p, way, t] = (s3[p, t] + up(r4.at[p, way, t])).astype(BF16)

        @pl.when(goes & jnp.logical_not(inner))
        def _():
            b4[p, way, t] = s3[p, t].astype(BF16)

        @pl.when(goes)
        def _():
            four(p, t, way).start()

    for p in range(packs):
        stage_two(p)
        if p == 0:
            small[0].wait_recv()
            for i, x in enumerate((e, ef)):
                c2[i] = sv[x, core] + q1[x]
            small[1].start()
    forward_tokens(1)
    for p in range(packs):
        stage_three(p)
        if p == 0:
            small[1].wait_recv()
            c3[...] = sv[f, core] + q1[f] + q2[1]
            small[2].start()
    forward_tokens(2)
    small[2].wait_recv()
    sk[...] = sv[xy, core] + q1[xy] + q2[0] + q3[...]
    for copy in small_z:
        copy.start()
    for p in range(packs):
        stage_kept(p)
        for i in range(3):
            stage_four(p, 3 - i, 0)
            stage_four(p, i, 1)
    for copy in small_z:
        copy.wait_recv()
    out_s[...] = sk[...] + q4[0] + q4[1] + q4[2]
    for i in range(chunks):
        k = z * chunks + i
        rows = pl.ds(i * ROWS, ROWS)
        out_t[rows, :] = base[rows, :]
        from_left = (z > 0) & ((z > 1) | (k < total - edge))
        from_left = from_left & ((z != 1) | (k < total - edge))
        from_right = (z < 3) & ((z < 2) | (k >= edge))

        @pl.when(from_left)
        def _():
            put(ds.at[k], dr.at[k], t_s.at[k], t_r.at[k], d, z).wait_recv()
            out_t[rows, :] += dr[k].astype(F32)

        @pl.when(from_right)
        def _():
            put(ds.at[k], dr.at[total + i], t_s.at[k], t_r.at[total + i], d, z).wait_recv()
            out_t[rows, :] += dr[total + i].astype(F32)

    for p in range(packs):
        out_w[p] = s3[p, z]

        @pl.when(z > 0)
        def _():
            four(p, z, 0).wait_recv()
            out_w[p] += up(r4.at[p, 0, z])

        @pl.when(z < 3)
        def _():
            four(p, z, 1).wait_recv()
            out_w[p] += up(r4.at[p, 1, z])

    for copy in small + small_z:
        copy.wait_send()
    for p in range(packs):
        for t in range(4):
            one[p][t].wait_send()
            two[p][t].wait_send()
            three[p][t].wait_send()
            for way in range(2):

                @pl.when((t > z) if way == 0 else (t < z))
                def _():
                    four(p, t, way).wait_send()

    for k, way in [(k, 0) for k in right_order] + [(k, 1) for k in left_order]:

        @pl.when(sends(k, way))
        def _():
            token(k, way).wait_send()


def reduce_all(g, sv, dt, base):
    packs, _, _, r, c = g.shape
    rows, width = base.shape
    chunks = rows // ROWS
    dma = pltpu.SemaphoreType.DMA
    any_ = pl.BlockSpec(memory_space=pl.ANY)
    vmem = pl.BlockSpec(memory_space=pltpu.VMEM)
    vm = pltpu.VMEM
    block, sb = (r, c), sv.shape[1:]
    return pl.pallas_call(
        reduce_kernel,
        out_shape=(
            jax.ShapeDtypeStruct((packs,) + block, F32),
            jax.ShapeDtypeStruct(sb, F32),
            jax.ShapeDtypeStruct((rows, width), F32),
        ),
        in_specs=[any_, vmem, any_, vmem],
        out_specs=(vmem, vmem, vmem),
        scratch_shapes=[
            vm((packs, 4, 4) + block, BF16),
            vm((packs, 4, 4) + block, BF16),
            vm((packs, 4, 2) + block, BF16),
            vm((packs, 4, 2) + block, BF16),
            vm((packs, 4) + block, BF16),
            vm((packs, 4) + block, BF16),
            vm((packs, 4) + block, F32),
            vm((packs, 2, 4) + block, BF16),
            vm((packs, 2, 4) + block, BF16),
            vm((4 * chunks, ROWS, width), BF16),
            vm((5 * chunks, ROWS, width), BF16),
            vm(sb, F32),
            vm((4,) + sb, F32),
            vm((2,) + sb, F32),
            vm(sb, F32),
            vm((2,) + sb, F32),
            vm(sb, F32),
            vm((3,) + sb, F32),
            dma((packs, 4)),
            dma((packs, 4)),
            dma((packs, 4)),
            dma((packs, 4)),
            dma((packs, 4)),
            dma((packs, 4)),
            dma((packs, 4)),
            dma((packs, 2, 4)),
            dma((packs, 2, 4)),
            dma(()),
            dma((4 * chunks,)),
            dma((5 * chunks,)),
            dma((6,)),
            dma((6,)),
        ],
        compiler_params=pltpu.CompilerParams(
            collective_id=1, has_side_effects=True, vmem_limit_bytes=VMEM_MAX
        ),
        name="reduce_all",
    )(
        g.reshape(packs, 4, 4, 2, r, c),
        sv.reshape((4, 2) + sb),
        dt.reshape(4 * chunks, ROWS, width),
        base,
    )


def parts_of(z, own):
    sure = SHORT - own
    low = z < 2
    return (
        (jnp.where(low, 0, own - sure), sure, jnp.where(low, 0, SHORT)),
        (jnp.where(low, sure, 0), own - sure, jnp.where(z == 3, SHORT, 0)),
    )


def over_keys(z, part, start, total, act):
    window = total - SHORT
    for c in range(window // KEYS):
        act(pl.multiple_of(start + c * KEYS, KEYS))
    if part == 1:

        @pl.when((z == 1) | (z == 2))
        def _():
            for c in range(window // KEYS, total // KEYS):
                act(c * KEYS)


def aug_rows(top, r):
    return jnp.concatenate([top.astype(BF16), jnp.zeros((128 - 16, r), BF16)], axis=0)


def pick_rows(rows, r):
    index = lax.broadcasted_iota(jnp.int32, (16, r), 0)
    out = jnp.zeros((16, r), F32)
    for i, row in enumerate(rows):
        out = jnp.where(index == i, jnp.broadcast_to(row, (16, r)), out)
    return out


def split3(x):
    hi = x.astype(BF16).astype(F32)
    mid = (x - hi).astype(BF16).astype(F32)
    return hi, mid, x - hi - mid


def padded(head_rows, half, aug, r):
    zero = jnp.zeros((HD, r), BF16)
    pair = [head_rows, zero] if half == 0 else [zero, head_rows]
    return jnp.concatenate(pair + [aug], axis=0)


def attention_kernel(qt, k, vt, ka, ma, mixed_t, lse, s, m, l, acc):
    z = lax.axis_index("tp")
    own = qt.shape[1]
    for part, (row0, n, start) in enumerate(parts_of(z, own)):
        cols = pl.ds(pl.multiple_of(row0, 128), n)
        aug = aug_rows(pick_rows((ma[0:1, cols], ma[1:2, cols]), n), n)

        def one_pair(pair, carry):
            attend_pair(z, part, start, pair, cols, n, aug, qt, k, vt, ka, mixed_t, lse, s, m, l, acc)
            return carry

        lax.fori_loop(0, k.shape[1] // 128, one_pair, 0)


def attention(qt, k, vt, ka, ma):
    width, own = qt.shape
    total = k.shape[0]
    widest = max(SHORT - own, own - (SHORT - own))
    vm = pltpu.VMEM
    return pl.pallas_call(
        attention_kernel,
        out_shape=(
            jax.ShapeDtypeStruct((width, own), F32),
            jax.ShapeDtypeStruct((width // 128, 8, own), F32),
        ),
        in_specs=[pl.BlockSpec(memory_space=pltpu.VMEM)] * 5,
        out_specs=(pl.BlockSpec(memory_space=pltpu.VMEM),) * 2,
        scratch_shapes=[
            vm((2, total, widest), F32),
            vm((2, 1, widest), F32),
            vm((2, 1, widest), F32),
            vm((2, HD, widest), F32),
        ],
        compiler_params=pltpu.CompilerParams(vmem_limit_bytes=VMEM_MAX),
        name="attention",
    )(qt, k, vt, ka, ma)


def attention_back_kernel(qt, q, k, kt, v, ka, ma, mixed_t, lse, dmt, dm, dqt, dk, dv, dka, dva, dqa):
    z = lax.axis_index("tp")
    own, total = qt.shape[1], k.shape[0]
    pairs = k.shape[1] // 128

    def one_pair(pair, carry):
        lanes = pl.ds(pl.multiple_of(pair * 128, 128), 128)
        dka[...] = jnp.zeros_like(dka)
        dva[...] = jnp.zeros_like(dva)
        for part, (row0, r, start) in enumerate(parts_of(z, own)):
            cols = pl.ds(pl.multiple_of(row0, 128), r)
            qs, gs, qm, gm = [], [], [], []
            low = lax.broadcasted_iota(jnp.int32, (r, 128), 1) < HD
            for half in range(2):
                rows = pl.ds(pl.multiple_of(pair * 128 + half * HD, HD), HD)
                delta = jnp.sum(dmt[rows, cols].astype(F32) * mixed_t[rows, cols], axis=0, keepdims=True)
                total_log = lse[pair, half : half + 1, cols]
                q_aug = pick_rows((ma[0:1, cols], ma[1:2, cols]) + split3(-total_log), r)
                zero = jnp.zeros((1, r), F32)
                g_aug = pick_rows((zero, zero) + split3(-delta), r)
                qs.append(padded(qt[rows, cols], half, aug_rows(q_aug, r), r))
                gs.append(padded(dmt[rows, cols], half, aug_rows(g_aug, r), r))
                mine = low if half == 0 else jnp.logical_not(low)
                here = pl.ds(pl.multiple_of(row0, 128), r)
                qm.append(jnp.where(mine, q[here, lanes], jnp.zeros((), BF16)))
                gm.append(jnp.where(mine, dm[here, lanes], jnp.zeros((), BF16)))
                dqa[half, :, :r] = jnp.zeros((HD, r), F32)

            def step(key0):
                keys = pl.ds(key0, KEYS)
                k_left = jnp.concatenate([k[keys, lanes], ka[keys, :]], axis=1)
                v_left = jnp.concatenate([v[keys, lanes], ka[keys, :]], axis=1)
                for half in range(2):
                    share = jnp.exp(dot(k_left, qs[half]))
                    slope = (share * dot(v_left, gs[half])).astype(BF16)
                    dva[keys, :] += dot(share.astype(BF16), gm[half])
                    dka[keys, :] += dot(slope, qm[half])
                    rows = pl.ds(pl.multiple_of(pair * 128 + half * HD, HD), HD)
                    dqa[half, :, :r] += dot(kt[rows, keys], slope)

            over_keys(z, part, start, total, step)
            for half in range(2):
                rows = pl.ds(pl.multiple_of(pair * 128 + half * HD, HD), HD)
                dqt[rows, cols] = (dqa[half, :, :r] * HD ** (-0.5)).astype(BF16)
        dk[:, lanes] = dka[...].astype(BF16)
        dv[:, lanes] = dva[...].astype(BF16)
        return carry

    lax.fori_loop(0, pairs, one_pair, 0)


def attention_back(qt, q, k, kt, v, ka, ma, mixed_t, lse, dmt, dm):
    width, own = qt.shape
    total = k.shape[0]
    widest = max(SHORT - own, own - (SHORT - own))
    vm = pltpu.VMEM
    return pl.pallas_call(
        attention_back_kernel,
        out_shape=(
            jax.ShapeDtypeStruct((width, own), BF16),
            jax.ShapeDtypeStruct((total, width), BF16),
            jax.ShapeDtypeStruct((total, width), BF16),
        ),
        in_specs=[pl.BlockSpec(memory_space=pltpu.VMEM)] * 11,
        out_specs=(pl.BlockSpec(memory_space=pltpu.VMEM),) * 3,
        scratch_shapes=[
            vm((total, 128), F32),
            vm((total, 128), F32),
            vm((2, HD, widest), F32),
        ],
        compiler_params=pltpu.CompilerParams(vmem_limit_bytes=VMEM_MAX),
        name="attention_back",
    )(qt, q, k, kt, v, ka, ma, mixed_t, lse, dmt, dm)


def body(
    tokens, w_query, w_key, w_value, b_query, b_value, w_out, b_out, gain_attn, shift_attn,
    w_up, b_up, w_down, b_down, gain_ffn, shift_ffn, lengths, deal_order, cotangent,
):
    own, width = tokens.shape
    n_tp, n_dp = lax.axis_size("tp"), lax.axis_size("dp")
    z, g = lax.axis_index("tp"), lax.axis_index("dp")
    total = own * n_tp
    r, hw = w_query.shape
    direct = n_tp == 4 and n_dp == 8 and r % 16 == 0

    own_w = jnp.stack([jnp.concatenate([w_query, w_key, w_value, w_out], axis=1), w_up, w_down])
    vectors = (b_query, b_value, b_out, gain_attn, shift_attn, b_down, gain_ffn, shift_ffn, b_up)
    n_small = 8 * r + b_up.shape[0]
    if direct:
        lines = [jnp.pad(a, (0, 128 - r)) for a in vectors[:8]] + [b_up, jnp.zeros((5 * 128,), BF16)]
        own_s = jnp.concatenate(lines).reshape(16, 128)
        w, vec, bu, x, q, qt, k, v, kt, wd, mixed_t, lse = forward_all(lengths, deal_order, own_w, own_s, tokens)
        w = w.reshape(2, n_tp, width, w_up.shape[1])
        bu = bu.reshape(-1)
        wq, wk, wv, wo = (wd[i] for i in range(4))
        bq, bv, bo, g1, h1, bd, g2, h2 = (vec[i] for i in range(8))
    else:
        w = lax.all_gather(own_w, ("tp", "dp"), axis=0).reshape((n_tp, n_dp) + own_w.shape)
        w = jnp.moveaxis(w, 2, 0).reshape(3, n_tp, width, w_up.shape[1])
        s = lax.all_gather(jnp.concatenate(vectors), "dp", axis=0)
        x = lax.all_gather(tokens, "tp", axis=0, tiled=True)
        small = [s[:, i * r : (i + 1) * r].reshape(width).astype(F32) for i in range(8)]
        bq, bv, bo, g1, h1, bd, g2, h2 = small
        bu = s[:, 8 * r : n_small].reshape(-1).astype(F32)
        wq, wk, wv, wo = (
            w[0, :, :, i * hw : (i + 1) * hw].transpose(1, 0, 2).reshape(width, width) for i in range(4)
        )
        w = w[1:]
        q = (dot(tokens, wq) + bq).astype(BF16) * jnp.asarray(HD ** (-0.5), BF16)
        k = dot(x, wk).astype(BF16)
        v = (dot(x, wv) + bv).astype(BF16)
        qt, kt = q.T, k.T

    pair = lax.dynamic_slice_in_dim(deal_order, 2 * g, 1)
    first_len = jnp.sum(jnp.where(jnp.arange(lengths.shape[0], dtype=jnp.int32) == pair[0], lengths, 0))
    key_seg = jnp.arange(total, dtype=jnp.int32)[:, None] >= first_len
    lane = jnp.arange(128, dtype=jnp.int32)[None, :]
    ka = jnp.where(lane == 0, ~key_seg, jnp.where(lane == 1, key_seg, (lane >= 2) & (lane < 5))).astype(BF16)
    row_seg = (z * own + jnp.arange(own, dtype=jnp.int32))[None, :] >= first_len
    sub = jnp.arange(8, dtype=jnp.int32)[:, None]
    ma = jnp.where(((sub == 0) & row_seg) | ((sub == 1) & ~row_seg), MASKED, 0.0).astype(F32)

    if not direct:
        mixed_t, lse = attention(qt, k, v.T, ka, ma)
    mixed = mixed_t.T.astype(BF16)
    first_residual = tokens.astype(F32) + contract_last(mixed, wo) + bo
    xhat1, inv1 = normalize_layer(first_residual)
    y1 = xhat1 * g1 + h1
    y1r = y1.astype(BF16)

    u = [dot(y1r, w[0, t]) + bu.reshape(n_tp, -1)[t] for t in range(n_tp)]
    hr = [jax.nn.gelu(a, approximate=False).astype(BF16) for a in u]
    ffn = sum(contract_last(hr[t], w[1, t]) for t in range(n_tp))
    xhat2, inv2 = normalize_layer(y1 + ffn + bd)
    encoder_output = (xhat2 * g2 + h2).astype(BF16)

    grad = cotangent.astype(F32)
    dr2 = normalize_backward(grad, xhat2, inv2, g2)
    dfr = dr2.astype(BF16)
    du = [(dot(dfr, w[1, t]) * gelu_slope(u[t])).astype(BF16) for t in range(n_tp)]
    dy1 = dr2 + sum(contract_last(du[t], w[0, t]) for t in range(n_tp))
    dr1 = normalize_backward(dy1, xhat1, inv1, g1)
    dar = dr1.astype(BF16)
    dm = dot(dar, wo).astype(BF16)
    dqt, dk, dv = attention_back(qt, q, k, kt, v, ka, ma, mixed_t, lse, dm.T, dm)
    dq = dqt.T
    base = dr1 + contract_last(dq, wq)
    far = contract_last(dk, wk) + contract_last(dv, wv)
    base = base + lax.dynamic_slice_in_dim(far, z * own, own)
    dt = far.astype(BF16)
    gq, gk, gv = contract_first(tokens, dq), contract_first(x, dk), contract_first(x, dv)
    go = contract_first(dar, mixed)
    ga = jnp.stack(
        [
            jnp.concatenate([m[:, t * hw : (t + 1) * hw] for m in (gq, gk, gv, go)], axis=1)
            for t in range(n_tp)
        ]
    )
    gu = jnp.stack([contract_first(y1r, du[t]) for t in range(n_tp)])
    gd = jnp.stack([contract_first(dfr, hr[t]) for t in range(n_tp)])
    sums = [
        jnp.sum(dq, axis=0, dtype=F32),
        jnp.sum(dv, axis=0, dtype=F32),
        jnp.sum(dar, axis=0, dtype=F32),
        jnp.sum(dy1 * xhat1, axis=0),
        jnp.sum(dy1, axis=0),
        jnp.sum(dfr, axis=0, dtype=F32),
        jnp.sum(grad * xhat2, axis=0),
        jnp.sum(grad, axis=0),
    ]
    sums = [a.reshape(n_dp, r) for a in sums]
    sums.append(jnp.concatenate([jnp.sum(a, axis=0, dtype=F32) for a in du]).reshape(n_dp, -1))
    sv = jnp.concatenate(sums, axis=1)
    if direct:
        grads = jnp.stack([ga, gu, gd]).astype(BF16).reshape(3, n_tp, n_dp, r, -1)
        sv = jnp.pad(sv, ((0, 0), (0, 2048 - n_small))).reshape(n_dp, 16, 128)
        gw, gs, grad_tokens = reduce_all(grads, sv, dt, base)
        gs = gs.reshape(-1)
    else:
        grads = jnp.stack([ga, gu, gd], axis=1).reshape(n_tp, 3, n_dp, r, -1)
        grads = jnp.moveaxis(grads, 1, 2).reshape(n_tp * n_dp, 3, r, -1)
        gw = lax.psum_scatter(grads, ("tp", "dp"), scatter_dimension=0, tiled=True)[0]
        gs = lax.psum_scatter(lax.psum(sv, "tp"), "dp", scatter_dimension=0, tiled=True)[0]
        others = jnp.where(jnp.arange(total)[:, None] // own == z, jnp.zeros((), BF16), dt)
        grad_tokens = base + lax.psum_scatter(others, "tp", scatter_dimension=0, tiled=True).astype(F32)
    gs = [gs[i * r : (i + 1) * r] for i in range(8)] + [gs[8 * r : n_small]]
    a = gw[0]
    return (
        encoder_output, grad_tokens,
        a[:, :hw], a[:, hw : 2 * hw], a[:, 2 * hw : 3 * hw], gs[0], gs[1],
        a[:, 3 * hw :], gs[2], gs[3], gs[4],
        gw[1], gs[8], gw[2], gs[5], gs[6], gs[7],
    )


def solution(mesh):
    rows, block, vector = P(("dp", "tp"), None), P("dp", "tp"), P("dp")
    in_specs = (
        rows, block, block, block, vector, vector, block, vector, vector, vector,
        block, vector, block, vector, vector, vector, P(), P(), rows,
    )
    out_specs = (
        rows, rows, block, block, block, vector, vector, block, vector, vector, vector,
        block, vector, block, vector, vector, vector,
    )
    return jax.shard_map(body, mesh=mesh, in_specs=in_specs, out_specs=out_specs, check_vma=False)
```

```python
import functools

import jax
import jax.numpy as jnp
from jax import lax
from jax.experimental import pallas as pl
from jax.experimental.pallas import tpu as pltpu
from jax.sharding import PartitionSpec as P

HD = 64
SHORT = 1024
EPS = 1e-05
SQRT_HALF = 0.7071067811865476
INV_ROOT_TAU = 0.3989422804014327
MASKED = -1e30
KEYS = 512
ROWS = 128
VMEM_MAX = 67043328
MESH = pl.DeviceIdType.MESH
F32 = jnp.float32
BF16 = jnp.bfloat16


def dot(left, right):
    return jnp.dot(left, right, preferred_element_type=F32)


def contract_last(left, right):
    return lax.dot_general(left, right, (((1,), (1,)), ((), ())), preferred_element_type=F32)


def contract_first(left, right):
    return lax.dot_general(left, right, (((0,), (0,)), ((), ())), preferred_element_type=F32)


def normalize_layer(resid):
    center = resid - jnp.mean(resid, axis=-1, keepdims=True)
    inverse_deviation = lax.rsqrt(jnp.mean(center * center, axis=-1, keepdims=True) + EPS)
    return (center * inverse_deviation, inverse_deviation)


def normalize_backward(output_gradient, xhat, inverse_deviation, gain):
    scaled_rows = output_gradient * gain
    return inverse_deviation * (
        scaled_rows
        - jnp.mean(scaled_rows, axis=-1, keepdims=True)
        - xhat * jnp.mean(scaled_rows * xhat, axis=-1, keepdims=True)
    )


def gelu_slope(pre_act):
    return (
        0.5 * (1.0 + lax.erf(pre_act * SQRT_HALF))
        + pre_act * jnp.exp(-0.5 * pre_act * pre_act) * INV_ROOT_TAU
    )


def position():
    z = lax.axis_index("tp")
    d = lax.axis_index("dp")
    core = lax.rem(d, 2)
    first = 2 + 2 * core
    second = 4 - 2 * core
    return z, d, core, first, second


def xor(d, mask):
    return d + mask * (1 - 2 * lax.rem(d // mask, 2))


def greet(z, d):
    barrier = pltpu.get_barrier_semaphore()
    for mask in (1, 2, 4):
        pl.semaphore_signal(barrier, inc=1, device_id=(xor(d, mask), z), device_id_type=MESH)
    for j in range(1, 4):
        pl.semaphore_signal(barrier, inc=1, device_id=(d, lax.rem(z + j, 4)), device_id_type=MESH)
    pl.semaphore_wait(barrier, 6)


def by_distance(z):
    low = z <= 1
    near = jnp.where(z == 0, 1, jnp.where(z == 3, 2, z - 1))
    mid = jnp.where(z == 0, 2, jnp.where(z == 3, 1, z + 1))
    far = jnp.where(low, 3, 0)
    return (z, near, mid, far)


def put(src, dst, send, recv, dp, tp):
    return pltpu.make_async_remote_copy(
        src_ref=src, dst_ref=dst, send_sem=send, recv_sem=recv, device_id=(dp, tp), device_id_type=MESH
    )


def forward_kernel(
    lengths, deal, own_w, own_s, own_t,
    w, vec, bu, x_out, q_out, qt_out, k_out, v_out, kt_out, wd_out, mixed_t, lse,
    wa, s, x, q, qt, k, v, kt, vt, wd, ka, sc, m, l, acc,
    wz_s, wz_r, wa_s, wa_r, wb_s, wb_r, wc_s, wc_r, tk_s, tk_r, sm_s, sm_r, lo_sem, arr_sem, out_sem,
):
    z, d, core, first, second = position()
    packs = own_w.shape[0]
    own, width = own_t.shape
    total = 4 * own
    hw = width // 4
    chunks = own // ROWS
    d1, d2 = xor(d, first), xor(d, second)
    d12 = xor(d1, second)
    pal = xor(d, 1)
    pd, pd1, pd2, pd12 = (xor(e, 1) for e in (d, d1, d2, d12))
    order = by_distance(z)
    first_len = lengths[deal[2 * d]]

    greet(z, d)

    def block(p, tt, e):
        return wa.at[tt, e] if p == 0 else w.at[p - 1, tt, e]

    def along_z(p, tt, src, act):
        dst = block(p, tt, d)
        right = put(src, dst, wz_s.at[0, p, tt], wz_r.at[p, tt], d, jnp.minimum(z + 1, 3))
        left = put(src, dst, wz_s.at[1, p, tt], wz_r.at[p, tt], d, jnp.maximum(z - 1, 0))

        @pl.when((tt <= z) & (z < 3))
        def _():
            act(right)

        @pl.when((tt >= z) & (z > 0))
        def _():
            act(left)

    def across(p, tt, src):
        dst = block(p, tt, d)
        return (
            put(src, dst, wa_s.at[p, tt], wa_r.at[p, tt], d1, z),
            put(src, dst, wb_s.at[p, tt, 0], wb_r.at[p, tt, 0], d2, z),
            put(src, dst, wc_s.at[p, tt, 0], wc_r.at[p, tt, 0], pal, z),
        )

    def after_first(p, tt):
        src = block(p, tt, d1)
        return (
            put(src, src, wb_s.at[p, tt, 1], wb_r.at[p, tt, 1], d2, z),
            put(src, src, wc_s.at[p, tt, 1], wc_r.at[p, tt, 1], pal, z),
        )

    def after_second(p, tt, i):
        src = block(p, tt, d2 if i == 0 else d12)
        return put(src, src, wc_s.at[p, tt, 2 + i], wc_r.at[p, tt, 2 + i], pal, z)

    def source(p, j):
        return own_w.at[p] if j == 0 else block(p, order[j], d)

    def arrive(ref, sem):
        put(ref, ref, arr_sem, sem, pal, z).wait_recv()

    def begin(p, j):
        if j > 0:
            arrive(block(p, order[j], d), wz_r.at[p, order[j]])
        along_z(p, order[j], source(p, j), lambda c: c.start())
        for copy in across(p, order[j], source(p, j)):
            copy.start()

    def relay_first(p, j):
        tt = order[j]
        arrive(block(p, tt, d1), wa_r.at[p, tt])
        for copy in after_first(p, tt):
            copy.start()

    def relay_second(p, j):
        tt = order[j]
        for i in range(2):
            arrive(block(p, tt, d2 if i == 0 else d12), wb_r.at[p, tt, i])
            after_second(p, tt, i).start()

    def from_pal(p):
        for tt in range(4):
            for i, e in enumerate((pd, pd2, pd1, pd12)):
                arrive(block(p, tt, e), wc_r.at[p, tt, i])

    def sent(p):
        for j in range(4):
            tt = order[j]
            along_z(p, tt, source(p, j), lambda c: c.wait_send())
            for copy in across(p, tt, source(p, j)) + after_first(p, tt):
                copy.wait_send()
            for i in range(2):
                after_second(p, tt, i).wait_send()

    def token_slice(o, i):
        return x.at[pl.ds(pl.multiple_of((o * chunks + i) * ROWS, ROWS), ROWS)]

    def token_hop(o, i, hop, step):
        src = own_t.at[pl.ds(i * ROWS, ROWS)] if hop == 0 else token_slice(o, i)
        way = 0 if step > 0 else 1
        return put(src, token_slice(o, i), tk_s.at[way, hop, i], tk_r.at[way, hop, i], d, jnp.clip(z + step, 0, 3))

    last = SHORT // ROWS

    def wanted(o, i, target, step):
        n = o * chunks + i
        if step > 0:
            return (target <= 2) | (n >= last)
        return (target >= 1) | (n < 4 * chunks - last)

    def chunk_ids(step):
        return range(chunks) if step < 0 else reversed(range(chunks))

    def tokens(hop, step, act):
        o, target = z - step * hop, z + step
        valid = (o >= 0) & (o <= 3) & (target >= 0) & (target <= 3)
        for i in chunk_ids(step):

            @pl.when(valid & wanted(o, i, target, step))
            def _():
                act(token_hop(o, i, hop, step))

    def tokens_on(hop, step, onward):
        o, target = z - step * (hop + 1), z + step
        valid = (o >= 0) & (o <= 3) & (z - step >= 0) & (z - step <= 3)
        way = 0 if step > 0 else 1
        for i in chunk_ids(step):

            @pl.when(valid & wanted(o, i, z, step))
            def _():
                arrive(token_slice(jnp.clip(o, 0, 3), i), tk_r.at[way, hop, i])

            if onward:

                @pl.when(valid & (target >= 0) & (target <= 3) & wanted(o, i, target, step))
                def _():
                    token_hop(o, i, hop + 1, step).start()

    def small(stage):
        if stage == 0:
            return [
                put(own_s, s.at[d], sm_s.at[0], sm_r.at[0], d1, z),
                put(own_s, s.at[d], sm_s.at[1], sm_r.at[1], d2, z),
                put(own_s, s.at[d], sm_s.at[3], sm_r.at[3], pal, z),
            ]
        if stage == 1:
            return [
                put(s.at[d1], s.at[d1], sm_s.at[2], sm_r.at[2], d2, z),
                put(s.at[d1], s.at[d1], sm_s.at[4], sm_r.at[4], pal, z),
            ]
        return [
            put(s.at[d2], s.at[d2], sm_s.at[5], sm_r.at[5], pal, z),
            put(s.at[d12], s.at[d12], sm_s.at[6], sm_r.at[6], pal, z),
        ]

    begin(0, 0)
    for copy in small(0):
        copy.start()
    s[d] = own_s[...]
    wa[z, d] = own_w[0]
    mine = pl.ds(pl.multiple_of(z * own, ROWS), own)
    x[mine, :] = own_t[...]
    keep = pltpu.make_async_copy(own_w.at[pl.ds(1, packs - 1)], w.at[:, z, d], lo_sem)
    keep.start()

    @pl.when(z == 0)
    def _():
        x[total - SHORT :, :] = jnp.zeros((SHORT, width), BF16)

    @pl.when(z == 3)
    def _():
        x[:SHORT, :] = jnp.zeros((SHORT, width), BF16)

    lane = lax.broadcasted_iota(jnp.int32, (own, 128), 1)
    for i in range(4):
        late = lax.broadcasted_iota(jnp.int32, (own, 128), 0) + i * own >= first_len
        ones = jnp.where((lane >= 2) & (lane < 5), 1.0, 0.0)
        flags = jnp.where(lane == 0, jnp.where(late, 0.0, 1.0), jnp.where(lane == 1, jnp.where(late, 1.0, 0.0), ones))
        ka[pl.ds(i * own, own), :] = flags.astype(BF16)

    relay_first(0, 0)
    begin(0, 1)
    for step in (1, -1):
        tokens(0, step, lambda c: c.start())
    relay_second(0, 0)
    relay_first(0, 1)
    arrive(s.at[d1], sm_r.at[0])
    for copy in small(1):
        copy.start()
    begin(0, 2)
    relay_second(0, 1)
    relay_first(0, 2)
    begin(0, 3)
    relay_second(0, 2)
    relay_first(0, 3)
    for p in range(1, packs):
        begin(p, 0)
    arrive(s.at[d2], sm_r.at[1])
    arrive(s.at[d12], sm_r.at[2])
    for copy in small(2):
        copy.start()
    relay_second(0, 3)
    for i, e in enumerate((pd, pd2, pd1, pd12)):
        arrive(s.at[e], sm_r.at[3 + i])
    r = width // 8
    for e in range(8):
        piece = s[e].astype(F32)
        vec[0:8, e * r : (e + 1) * r] = piece[0:8, 0:r]
        for j in range(hw * 2 // 128):
            col = e * hw * 2 + j * 128
            bu[0:1, col : col + 128] = piece[8 + j : 9 + j, :]
    from_pal(0)
    for tt in range(4):
        rows = wa[tt].reshape(width, width)
        for i in range(4):
            wd[i, :, tt * hw : (tt + 1) * hw] = rows[:, i * hw : (i + 1) * hw]
    wd_copy = pltpu.make_async_copy(wd, wd_out, out_sem.at[0])
    wd_copy.start()

    tile = 256

    def q_tile(n, carry):
        lanes = pl.ds(pl.multiple_of(n * tile, tile), tile)
        rows = (dot(own_t[...], wd[0, :, lanes]) + vec[0:1, lanes]).astype(BF16) * jnp.asarray(HD ** (-0.5), BF16)
        q[:, lanes] = rows
        qt[lanes, :] = rows.T
        return carry

    def project(o):
        rows = pl.ds(pl.multiple_of(o * own, ROWS), own)

        def kv_tile(n, carry):
            lanes = pl.ds(pl.multiple_of(n * tile, tile), tile)
            keys = dot(x[rows, :], wd[1, :, lanes]).astype(BF16)
            k[rows, lanes] = keys
            kt[lanes, rows] = keys.T
            values = (dot(x[rows, :], wd[2, :, lanes]) + vec[1:2, lanes]).astype(BF16)
            v[rows, lanes] = values
            vt[lanes, rows] = values.T
            return carry

        lax.fori_loop(0, width // tile, kv_tile, 0)

    lax.fori_loop(0, width // tile, q_tile, 0)
    project(z)
    for step in (1, -1):
        tokens_on(0, step, True)
    for p in range(1, packs):
        relay_first(p, 0)

    @pl.when(z > 0)
    def _():
        project(jnp.maximum(z - 1, 0))

    for p in range(1, packs):
        begin(p, 1)

    @pl.when(z < 3)
    def _():
        project(jnp.minimum(z + 1, 3))

    for p in range(1, packs):
        relay_second(p, 0)
        relay_first(p, 1)
    for step in (1, -1):
        tokens_on(1, step, False)
    for p in range(1, packs):
        begin(p, 2)
    project(jnp.where(z == 0, 2, jnp.where(z == 1, 3, z - 2)))
    outs = [
        pltpu.make_async_copy(a, b, out_sem.at[1 + i])
        for i, (a, b) in enumerate(((x, x_out), (q, q_out), (qt, qt_out), (k, k_out), (v, v_out), (kt, kt_out)))
    ]
    for copy in outs:
        copy.start()

    def both(act, j):
        def run():
            for p in range(1, packs):
                act(p, j)

        return run

    def seq(*runs):
        def run():
            for one in runs:
                one()

        return run

    between = {
        (0, 0): both(relay_second, 1),
        (0, 1): both(relay_first, 2),
        (0, 2): both(begin, 3),
        (0, 4): both(relay_second, 2),
        (1, 0): both(relay_first, 3),
        (1, 4): both(relay_second, 3),
    }
    pairs = width // 128
    for part, (row0, n, start) in enumerate(parts_of(z, own)):
        cols = pl.ds(pl.multiple_of(row0, 128), n)
        late = lax.broadcasted_iota(jnp.int32, (1, n), 1) + (z * own + row0) >= first_len
        masks = (jnp.where(late, MASKED, 0.0), jnp.where(late, 0.0, MASKED))
        aug = aug_rows(pick_rows(masks, n), n)

        def one_pair(pair, carry):
            for (at, i), run in between.items():
                if at == part:

                    @pl.when(pair == i)
                    def _():
                        run()

            attend_pair(z, part, start, pair, cols, n, aug, qt, k, vt, ka, mixed_t, lse, sc, m, l, acc)
            return carry

        lax.fori_loop(0, pairs, one_pair, 0)

    for p in range(1, packs):
        from_pal(p)
    for stage in range(3):
        for copy in small(stage):
            copy.wait_send()
    for hop in range(2):
        for step in (1, -1):
            tokens(hop, step, lambda c: c.wait_send())
    for p in range(packs):
        sent(p)
    keep.wait()
    wd_copy.wait()
    for copy in outs:
        copy.wait()


def attend_pair(z, part, start, pair, cols, n, aug, qt, k, vt, ka, mixed_t, lse, s, m, l, acc):
    total = k.shape[0]
    lanes = pl.ds(pl.multiple_of(pair * 128, 128), 128)
    for half in range(2):
        m[half, :, :n] = jnp.full((1, n), MASKED, F32)
        l[half, :, :n] = jnp.zeros((1, n), F32)
        acc[half, :, :n] = jnp.zeros((HD, n), F32)
    qs = [padded(qt[pl.ds(pl.multiple_of(pair * 128 + half * HD, HD), HD), cols], half, aug, n) for half in range(2)]

    def scores(key0):
        keys = pl.ds(key0, KEYS)
        left = jnp.concatenate([k[keys, lanes], ka[keys, :]], axis=1)
        for half in range(2):
            score = dot(left, qs[half])
            s[half, keys, :n] = score
            m[half, :, :n] = jnp.maximum(m[half, :, :n], jnp.max(score, axis=0, keepdims=True))

    over_keys(z, part, start, total, scores)
    tops = [m[half, :, :n] for half in range(2)]

    def mix(key0):
        keys = pl.ds(key0, KEYS)
        for half in range(2):
            raised = jnp.exp(s[half, keys, :n] - tops[half])
            l[half, :, :n] += jnp.sum(raised, axis=0, keepdims=True)
            values = vt[pl.ds(pl.multiple_of(pair * 128 + half * HD, HD), HD), keys]
            acc[half, :, :n] += dot(values, raised.astype(BF16))

    over_keys(z, part, start, total, mix)
    for half in range(2):
        sums = l[half, :, :n]
        rows = pl.ds(pl.multiple_of(pair * 128 + half * HD, HD), HD)
        mixed_t[rows, cols] = acc[half, :, :n] / sums
        lse[pair, half : half + 1, cols] = tops[half] + jnp.log(sums)


def forward_all(lengths, deal, own_w, own_s, own_t):
    packs, r, c = own_w.shape
    own, width = own_t.shape
    total = 4 * own
    chunks = own // ROWS
    widest = max(SHORT - own, own - (SHORT - own))
    dma, vm = pltpu.SemaphoreType.DMA, pltpu.VMEM
    any_ = pl.BlockSpec(memory_space=pl.ANY)
    vmem = pl.BlockSpec(memory_space=pltpu.VMEM)
    smem = pl.BlockSpec(memory_space=pltpu.SMEM)
    shape = jax.ShapeDtypeStruct
    return pl.pallas_call(
        forward_kernel,
        out_shape=(
            shape((packs - 1, 4, 8, r, c), BF16),
            shape((8, width), F32),
            shape((1, 4 * c), F32),
            shape((total, width), BF16),
            shape((own, width), BF16),
            shape((width, own), BF16),
            shape((total, width), BF16),
            shape((total, width), BF16),
            shape((width, total), BF16),
            shape((4, width, width), BF16),
            shape((width, own), F32),
            shape((width // 128, 8, own), F32),
        ),
        in_specs=[smem, smem, vmem, vmem, vmem],
        out_specs=(any_, vmem, vmem) + (any_,) * 7 + (vmem, vmem),
        scratch_shapes=[
            vm((4, 8, r, c), BF16),
            vm((8, 16, 128), BF16),
            vm((total, width), BF16),
            vm((own, width), BF16),
            vm((width, own), BF16),
            vm((total, width), BF16),
            vm((total, width), BF16),
            vm((width, total), BF16),
            vm((width, total), BF16),
            vm((4, width, width), BF16),
            vm((total, 128), BF16),
            vm((2, total, widest), F32),
            vm((2, 1, widest), F32),
            vm((2, 1, widest), F32),
            vm((2, HD, widest), F32),
            dma((2, packs, 4)),
            dma((packs, 4)),
            dma((packs, 4)),
            dma((packs, 4)),
            dma((packs, 4, 2)),
            dma((packs, 4, 2)),
            dma((packs, 4, 4)),
            dma((packs, 4, 4)),
            dma((2, 2, chunks)),
            dma((2, 2, chunks)),
            dma((7,)),
            dma((7,)),
            dma(()),
            dma(()),
            dma((7,)),
        ],
        compiler_params=pltpu.CompilerParams(
            collective_id=0, has_side_effects=True, vmem_limit_bytes=VMEM_MAX
        ),
        name="forward_all",
    )(lengths, deal, own_w, own_s, own_t)


def up(ref):
    return ref[...].astype(F32)


class Sums:
    def __init__(self, z, d, core, e_mask, f_mask, give, mine, ready, bufs, sems):
        self.z, self.d, self.give, self.mine, self.ready = z, d, give, mine, ready
        self.r1, self.b2, self.r2, self.b3, self.r3, self.s3, self.b4, self.r4 = bufs
        self.sems = sems
        self.xy = d // 2
        self.e, self.f = xor(d, e_mask) // 2, xor(d, f_mask) // 2
        self.ef = xor(xor(d, e_mask), f_mask) // 2
        self.d_e, self.d_f, self.pal = xor(d, e_mask), xor(d, f_mask), xor(d, 1)

    def one(self, p, t):
        return put(self.give(p, t), self.r1.at[p, t], self.sems[0].at[p, t], self.sems[1].at[p, t], self.pal, self.z)

    def two(self, p, t):
        return put(self.b2.at[p, t], self.r2.at[p, t], self.sems[2].at[p, t], self.sems[3].at[p, t], self.d_e, self.z)

    def three(self, p, t):
        return put(self.b3.at[p, t], self.r3.at[p, t], self.sems[4].at[p, t], self.sems[5].at[p, t], self.d_f, self.z)

    def four(self, p, t, way):
        to = jnp.minimum(self.z + 1, 3) if way == 0 else jnp.maximum(self.z - 1, 0)
        return put(
            self.b4.at[p, way, t], self.r4.at[p, way, t],
            self.sems[6].at[p, way, t], self.sems[7].at[p, way, t], self.d, to,
        )

    def at_two(self, p, t):
        self.ready(p, t)
        self.one(p, t).wait_recv()
        for i, x in enumerate((self.e, self.ef)):
            self.b2[p, t, i] = (self.mine(p, t, x) + up(self.r1.at[p, t, x])).astype(BF16)
        self.two(p, t).start()

    def at_three(self, p, t):
        self.two(p, t).wait_recv()
        f = self.f
        self.b3[p, t] = (self.mine(p, t, f) + up(self.r1.at[p, t, f]) + up(self.r2.at[p, t, 1])).astype(BF16)
        self.three(p, t).start()

    def at_kept(self, p, t):
        self.three(p, t).wait_recv()
        xy = self.xy
        self.s3[p, t] = self.mine(p, t, xy) + up(self.r1.at[p, t, xy]) + up(self.r2.at[p, t, 0]) + up(self.r3.at[p, t])

    def at_four(self, p, t, step):
        for way in range(2):
            pos = step if way == 0 else 3 - step
            if not (t > pos if way == 0 else t < pos):
                continue

            @pl.when(self.z == pos)
            def _():
                if step == 0:
                    self.b4[p, way, t] = self.s3[p, t].astype(BF16)
                else:
                    self.four(p, t, way).wait_recv()
                    self.b4[p, way, t] = (self.s3[p, t] + up(self.r4.at[p, way, t])).astype(BF16)
                self.four(p, t, way).start()

    def result(self, p, out):
        z = self.z
        out[...] = self.s3[p, z]

        @pl.when(z > 0)
        def _():
            self.four(p, z, 0).wait_recv()
            out[...] += up(self.r4.at[p, 0, z])

        @pl.when(z < 3)
        def _():
            self.four(p, z, 1).wait_recv()
            out[...] += up(self.r4.at[p, 1, z])

    def drain(self, p):
        for t in range(4):
            self.one(p, t).wait_send()
            self.two(p, t).wait_send()
            self.three(p, t).wait_send()
            for way in range(2):

                @pl.when((t > self.z) if way == 0 else (t < self.z))
                def _():
                    self.four(p, t, way).wait_send()


def sum_buffers(packs, block):
    vm = pltpu.VMEM
    return [
        vm((packs, 4, 4) + block, BF16),
        vm((packs, 4, 2) + block, BF16),
        vm((packs, 4, 2) + block, BF16),
        vm((packs, 4) + block, BF16),
        vm((packs, 4) + block, BF16),
        vm((packs, 4) + block, F32),
        vm((packs, 2, 4) + block, BF16),
        vm((packs, 2, 4) + block, BF16),
    ]


def sum_semaphores(packs):
    dma = pltpu.SemaphoreType.DMA
    return [dma((packs, 4))] * 6 + [dma((packs, 2, 4))] * 2


def finish_kernel(
    dqt, dk, dv, x, dar, mixed_t, wd, dr1, vecs, bup,
    out_w, out_s, out_t,
    xt, dart, dq, mixed, gp, sv, ds, dr, sk, q1, q2, q3, c2, c3, q4,
    r1, b2, r2, b3, r3, s3, b4, r4,
    p1_s, p1_r, p2_s, p2_r, p3_s, p3_r, p4_s, p4_r, t_s, t_r, v_s, v_r,
):
    z, d, core, first, second = position()
    own, width = out_t.shape
    chunks = own // ROWS
    total = 4 * chunks
    edge = SHORT // ROWS
    hw = width // 4
    r = width // 8
    greet(z, d)

    def token(k, way):
        to = jnp.minimum(z + 1, 3) if way == 0 else jnp.maximum(z - 1, 0)
        slot = k if way == 0 else jnp.where(k // chunks == to, total + k % chunks, k)
        return put(ds.at[k], dr.at[slot], t_s.at[k], t_r.at[slot], d, to)

    def token_in(k, way):
        slot = k if way == 0 else jnp.where(k // chunks == z, total + k % chunks, k)
        return put(ds.at[k], dr.at[slot], t_s.at[k], t_r.at[slot], d, z), slot

    def sends(k, way):
        o = k // chunks
        if way == 0:
            low = jnp.where(k < total - edge, 0, 1)
            return (z >= low) & (z < o) & (o > low)
        high = jnp.where(k >= edge, 3, 2)
        return (z <= high) & (z > o) & (o < high)

    def starts(k, way):
        if way == 0:
            return z == jnp.where(k < total - edge, 0, 1)
        return z == jnp.where(k >= edge, 3, 2)

    def pick(a, b, c, e):
        return jnp.where(z == 0, a, jnp.where(z == 1, b, jnp.where(z == 2, c, e)))

    tile = 256

    def far_shard(o, mine):
        rows = pl.ds(pl.multiple_of(o * own, ROWS), own)

        def one_tile(n, carry):
            lanes = pl.ds(pl.multiple_of(n * tile, tile), tile)
            far = contract_last(dk[rows, :], wd[1, lanes, :]) + contract_last(dv[rows, :], wd[2, lanes, :])
            if mine:
                out_t[:, lanes] = dr1[:, lanes] + far
            else:
                ds[pl.ds(o * chunks, chunks), :, lanes] = far.reshape(chunks, ROWS, tile).astype(BF16)
            return carry

        lax.fori_loop(0, width // tile, one_tile, 0)

    def far_and_send(j, carry):
        o = jnp.where(j == 0, pick(2, 3, 0, 1), jnp.where(j == 1, pick(1, 2, 1, 2), pick(3, 0, 3, 0)))

        @pl.when((j < 2) | (z == 1) | (z == 2))
        def _():
            far_shard(o, False)

        for i in range(chunks):
            for way in range(2):
                k = o * chunks + i

                @pl.when(sends(k, way) & starts(k, way))
                def _():
                    token(k, way).start()

        return carry

    lax.fori_loop(0, 3, far_and_send, 0)

    right_order = [k for o in (3, 2, 1) for k in range(o * chunks, (o + 1) * chunks)]
    left_order = [total - 1 - k for k in right_order]

    def forward_tokens(at):
        for k, way in [(k, 0) for k in right_order] + [(k, 1) for k in left_order]:
            pos = at if way == 0 else 3 - at
            passes = (at < k // chunks) if way == 0 else (3 - at > k // chunks)
            begins = (0 if k < total - edge else 1) if way == 0 else (3 if k >= edge else 2)
            if not passes or (begins >= pos if way == 0 else begins <= pos):
                continue

            @pl.when(z == pos)
            def _():
                got, slot = token_in(k, way)
                got.wait_recv()
                ds[k] = (ds[k].astype(F32) + dr[slot].astype(F32)).astype(BF16)
                token(k, way).start()

    def flip(i, carry):
        cols = pl.ds(pl.multiple_of(i * ROWS, ROWS), ROWS)
        xt[:, cols] = x[cols, :].T
        return carry

    lax.fori_loop(0, total, flip, 0)

    def flip_own(i, carry):
        cols = pl.ds(pl.multiple_of(i * ROWS, ROWS), ROWS)
        dart[:, cols] = dar[cols, :].T
        dq[cols, :] = dqt[:, cols].T
        mixed[cols, :] = mixed_t[:, cols].T.astype(BF16)
        return carry

    lax.fori_loop(0, chunks, flip_own, 0)

    def give(p, t):
        return gp.at[t, :, 1 - core]

    def mine(p, t, at):
        return gp[t, at, core].astype(F32)

    sums = Sums(
        z, d, core, second, first, give, mine, lambda p, t: None,
        (r1, b2, r2, b3, r3, s3, b4, r4), (p1_s, p1_r, p2_s, p2_r, p3_s, p3_r, p4_s, p4_r),
    )
    here = pl.ds(pl.multiple_of(z * own, ROWS), own)
    half = width // 2

    def weights(th):
        lanes = pl.ds(th * half, half)

        def rows_of(m, carry):
            rows = pl.ds(pl.multiple_of(m * half, ROWS), half)
            parts = (
                lambda: dot(xt[rows, here], dq[:, lanes]),
                lambda: dot(xt[rows, :], dk[:, lanes]),
                lambda: dot(xt[rows, :], dv[:, lanes]),
                lambda: dot(dart[rows, :], mixed[:, lanes]),
            )
            for i, part in enumerate(parts):
                got = part().astype(BF16)
                for h in range(2):
                    block = got[:, h * hw : (h + 1) * hw].reshape(2, 2, r, hw)
                    gp[2 * th + h, pl.ds(2 * m, 2), :, :, i * hw : (i + 1) * hw] = block
            return carry

        lax.fori_loop(0, 2, rows_of, 0)
        for t in (2 * th, 2 * th + 1):
            sums.one(0, t).start()

    weights(0)
    forward_tokens(1)
    weights(1)

    ones = jnp.ones((8, 4 * own), BF16)
    index = lax.broadcasted_iota(jnp.int32, (8, width), 0)
    small_rows = jnp.where(index == 0, dot(ones[:, :own], dq[...]), jnp.where(index == 1, dot(ones, dv[...]), vecs[...]))
    pad = jnp.zeros((8, 128 - r), F32)
    for i in range(8):
        sv[i // 2, i % 2, 0:8, :] = jnp.concatenate([small_rows[:, i * r : (i + 1) * r], pad], axis=1)
        wide = [bup[:, (i * 3 + j) * 128 : (i * 3 + j + 1) * 128] for j in range(3)]
        sv[i // 2, i % 2, 8:16, :] = jnp.concatenate(wide + [jnp.zeros((5, 128), F32)], axis=0)
    small = [
        put(sv.at[:, 1 - core], q1, v_s.at[0], v_r.at[0], sums.pal, z),
        put(c2, q2, v_s.at[1], v_r.at[1], sums.d_e, z),
        put(c3, q3, v_s.at[2], v_r.at[2], sums.d_f, z),
    ]
    small_z = [
        put(sk, q4.at[j - 1], v_s.at[2 + j], v_r.at[2 + j], d, lax.rem(z + j, 4)) for j in range(1, 4)
    ]
    small[0].start()
    for t in range(4):
        sums.at_two(0, t)
    forward_tokens(2)

    far_shard(z, True)

    def query_tile(n, carry):
        lanes = pl.ds(pl.multiple_of(n * tile, tile), tile)
        out_t[:, lanes] += contract_last(dq[...], wd[0, lanes, :])
        return carry

    lax.fori_loop(0, width // tile, query_tile, 0)
    small[0].wait_recv()
    for i, at in enumerate((sums.e, sums.ef)):
        c2[i] = sv[at, core] + q1[at]
    small[1].start()
    for t in range(4):
        sums.at_three(0, t)
    small[1].wait_recv()
    c3[...] = sv[sums.f, core] + q1[sums.f] + q2[1]
    small[2].start()
    for t in range(4):
        sums.at_kept(0, t)
    for step in range(3):
        for t in range(4):
            sums.at_four(0, t, step)
        if step == 0:
            small[2].wait_recv()
            sk[...] = sv[sums.xy, core] + q1[sums.xy] + q2[0] + q3[...]
            for copy in small_z:
                copy.start()
    for i in range(chunks):
        k = z * chunks + i
        rows = pl.ds(i * ROWS, ROWS)
        from_left = (z > 0) & ((z == 1) & (k < total - edge) | (z > 1))
        from_right = (z < 3) & ((z == 2) & (k >= edge) | (z < 2))

        @pl.when(from_left)
        def _():
            put(ds.at[k], dr.at[k], t_s.at[k], t_r.at[k], d, z).wait_recv()
            out_t[rows, :] += dr[k].astype(F32)

        @pl.when(from_right)
        def _():
            put(ds.at[k], dr.at[total + i], t_s.at[k], t_r.at[total + i], d, z).wait_recv()
            out_t[rows, :] += dr[total + i].astype(F32)

    for copy in small_z:
        copy.wait_recv()
    out_s[...] = sk[...] + q4[0] + q4[1] + q4[2]
    sums.result(0, out_w)
    for copy in small + small_z:
        copy.wait_send()
    sums.drain(0)
    for k in range(total):
        for way in range(2):

            @pl.when(sends(k, way))
            def _():
                token(k, way).wait_send()


def finish(dqt, dk, dv, x, dar, mixed_t, wd, dr1, vecs, bup):
    own, width = dr1.shape
    r = width // 8
    chunks = own // ROWS
    total = 4 * own
    dma, vm = pltpu.SemaphoreType.DMA, pltpu.VMEM
    vmem = pl.BlockSpec(memory_space=pltpu.VMEM)
    block, sb = (r, width), (16, 128)
    return pl.pallas_call(
        finish_kernel,
        out_shape=(
            jax.ShapeDtypeStruct(block, F32),
            jax.ShapeDtypeStruct(sb, F32),
            jax.ShapeDtypeStruct((own, width), F32),
        ),
        in_specs=[vmem] * 10,
        out_specs=(vmem, vmem, vmem),
        scratch_shapes=[
            vm((width, total), BF16),
            vm((width, own), BF16),
            vm((own, width), BF16),
            vm((own, width), BF16),
            vm((4, 4, 2) + block, BF16),
            vm((4, 2) + sb, F32),
            vm((4 * chunks, ROWS, width), BF16),
            vm((5 * chunks, ROWS, width), BF16),
            vm(sb, F32),
            vm((4,) + sb, F32),
            vm((2,) + sb, F32),
            vm(sb, F32),
            vm((2,) + sb, F32),
            vm(sb, F32),
            vm((3,) + sb, F32),
            *sum_buffers(1, block),
            *sum_semaphores(1),
            dma((4 * chunks,)),
            dma((5 * chunks,)),
            dma((6,)),
            dma((6,)),
        ],
        compiler_params=pltpu.CompilerParams(
            collective_id=1, has_side_effects=True, vmem_limit_bytes=VMEM_MAX
        ),
        name="finish",
    )(dqt, dk, dv, x, dar, mixed_t, wd, dr1, vecs, bup)


def parts_of(z, own):
    sure = SHORT - own
    low = z < 2
    return (
        (jnp.where(low, 0, own - sure), sure, jnp.where(low, 0, SHORT)),
        (jnp.where(low, sure, 0), own - sure, jnp.where(z == 3, SHORT, 0)),
    )


def over_keys(z, part, start, total, act):
    window = total - SHORT
    for c in range(window // KEYS):
        act(pl.multiple_of(start + c * KEYS, KEYS))
    if part == 1:

        @pl.when((z == 1) | (z == 2))
        def _():
            for c in range(window // KEYS, total // KEYS):
                act(c * KEYS)


def aug_rows(top, r):
    return jnp.concatenate([top.astype(BF16), jnp.zeros((128 - 16, r), BF16)], axis=0)


def pick_rows(rows, r):
    index = lax.broadcasted_iota(jnp.int32, (16, r), 0)
    out = jnp.zeros((16, r), F32)
    for i, row in enumerate(rows):
        out = jnp.where(index == i, jnp.broadcast_to(row, (16, r)), out)
    return out


def split3(x):
    hi = x.astype(BF16).astype(F32)
    mid = (x - hi).astype(BF16).astype(F32)
    return hi, mid, x - hi - mid


def padded(head_rows, half, aug, r):
    zero = jnp.zeros((HD, r), BF16)
    pair = [head_rows, zero] if half == 0 else [zero, head_rows]
    return jnp.concatenate(pair + [aug], axis=0)


def attention_kernel(qt, k, vt, ka, ma, mixed_t, lse, s, m, l, acc):
    z = lax.axis_index("tp")
    own = qt.shape[1]
    for part, (row0, n, start) in enumerate(parts_of(z, own)):
        cols = pl.ds(pl.multiple_of(row0, 128), n)
        aug = aug_rows(pick_rows((ma[0:1, cols], ma[1:2, cols]), n), n)

        def one_pair(pair, carry):
            attend_pair(z, part, start, pair, cols, n, aug, qt, k, vt, ka, mixed_t, lse, s, m, l, acc)
            return carry

        lax.fori_loop(0, k.shape[1] // 128, one_pair, 0)


def attention(qt, k, vt, ka, ma):
    width, own = qt.shape
    total = k.shape[0]
    widest = max(SHORT - own, own - (SHORT - own))
    vm = pltpu.VMEM
    return pl.pallas_call(
        attention_kernel,
        out_shape=(
            jax.ShapeDtypeStruct((width, own), F32),
            jax.ShapeDtypeStruct((width // 128, 8, own), F32),
        ),
        in_specs=[pl.BlockSpec(memory_space=pltpu.VMEM)] * 5,
        out_specs=(pl.BlockSpec(memory_space=pltpu.VMEM),) * 2,
        scratch_shapes=[
            vm((2, total, widest), F32),
            vm((2, 1, widest), F32),
            vm((2, 1, widest), F32),
            vm((2, HD, widest), F32),
        ],
        compiler_params=pltpu.CompilerParams(vmem_limit_bytes=VMEM_MAX),
        name="attention",
    )(qt, k, vt, ka, ma)


def back_pair(z, pair, pause, qt, q, k, kt, v, ka, ma, mixed_t, lse, dmt, dm, dqt, dk, dv, dka, dva, dqa):
    own, total = qt.shape[1], k.shape[0]
    lanes = pl.ds(pl.multiple_of(pair * 128, 128), 128)
    dka[...] = jnp.zeros_like(dka)
    dva[...] = jnp.zeros_like(dva)
    for part, (row0, r, start) in enumerate(parts_of(z, own)):
        pause(part)
        cols = pl.ds(pl.multiple_of(row0, 128), r)
        qs, gs, qm, gm = [], [], [], []
        low = lax.broadcasted_iota(jnp.int32, (r, 128), 1) < HD
        for half in range(2):
            rows = pl.ds(pl.multiple_of(pair * 128 + half * HD, HD), HD)
            delta = jnp.sum(dmt[rows, cols].astype(F32) * mixed_t[rows, cols], axis=0, keepdims=True)
            total_log = lse[pair, half : half + 1, cols]
            q_aug = pick_rows((ma[0:1, cols], ma[1:2, cols]) + split3(-total_log), r)
            zero = jnp.zeros((1, r), F32)
            g_aug = pick_rows((zero, zero) + split3(-delta), r)
            qs.append(padded(qt[rows, cols], half, aug_rows(q_aug, r), r))
            gs.append(padded(dmt[rows, cols], half, aug_rows(g_aug, r), r))
            mine = low if half == 0 else jnp.logical_not(low)
            here = pl.ds(pl.multiple_of(row0, 128), r)
            qm.append(jnp.where(mine, q[here, lanes], jnp.zeros((), BF16)))
            gm.append(jnp.where(mine, dm[here, lanes], jnp.zeros((), BF16)))
            dqa[half, :, :r] = jnp.zeros((HD, r), F32)

        def step(key0):
            keys = pl.ds(key0, KEYS)
            k_left = jnp.concatenate([k[keys, lanes], ka[keys, :]], axis=1)
            v_left = jnp.concatenate([v[keys, lanes], ka[keys, :]], axis=1)
            for half in range(2):
                share = jnp.exp(dot(k_left, qs[half]))
                slope = (share * dot(v_left, gs[half])).astype(BF16)
                dva[keys, :] += dot(share.astype(BF16), gm[half])
                dka[keys, :] += dot(slope, qm[half])
                rows = pl.ds(pl.multiple_of(pair * 128 + half * HD, HD), HD)
                dqa[half, :, :r] += dot(kt[rows, keys], slope)

        over_keys(z, part, start, total, step)
        for half in range(2):
            rows = pl.ds(pl.multiple_of(pair * 128 + half * HD, HD), HD)
            dqt[rows, cols] = (dqa[half, :, :r] * HD ** (-0.5)).astype(BF16)
    dk[:, lanes] = dka[...].astype(BF16)
    dv[:, lanes] = dva[...].astype(BF16)


def attention_back_kernel(*refs):
    z = lax.axis_index("tp")

    def one_pair(pair, carry):
        back_pair(z, pair, lambda part: None, *refs)
        return carry

    lax.fori_loop(0, refs[2].shape[1] // 128, one_pair, 0)


def back_sums_kernel(qt, q, k, kt, v, ka, ma, mixed_t, lse, dmt, dm, *refs):
    g = (refs[0:4], refs[4:8])
    dqt, dk, dv, out_u, out_d, dka, dva, dqa, gk, *bufs = refs[8:]
    bufs, (gk_sem, *sems) = bufs[:8], bufs[8:]
    z, d, core, first, second = position()
    greet(z, d)

    def fetch(p, t):
        return pltpu.make_async_copy(g[p][t].at[:, core], gk.at[p, t], gk_sem.at[p, t])

    sums = Sums(
        z, d, core, second, first,
        lambda p, t: g[p][t].at[:, 1 - core],
        lambda p, t, at: up(gk.at[p, t, at]),
        lambda p, t: fetch(p, t).wait(),
        bufs, sems,
    )
    for p in range(2):
        for t in range(4):
            sums.one(p, t).start()
            fetch(p, t).start()

    def each(act, *units):
        def run():
            for p, t in units:
                act(p, t)

        return run

    def kept_and_four(p):
        def run():
            for t in range(4):
                sums.at_kept(p, t)
                sums.at_four(p, t, 0)

        return run

    def four(p, step):
        return each(lambda p, t: sums.at_four(p, t, step), *[(p, t) for t in range(4)])

    packs = [[(p, t) for t in range(4)] for p in range(2)]
    between = {
        (1, 0): each(sums.at_two, *packs[0]),
        (1, 1): each(sums.at_two, *packs[1]),
        (2, 1): each(sums.at_three, *packs[0][:2]),
        (3, 0): each(sums.at_three, *packs[0][2:]),
        (3, 1): each(sums.at_three, *packs[1][:2]),
        (4, 0): each(sums.at_three, *packs[1][2:]),
        (4, 1): kept_and_four(0),
        (5, 0): four(0, 1),
        (5, 1): kept_and_four(1),
    }

    def one_pair(pair, carry):
        def pause(part):
            for (i, at), run in between.items():
                if at == part:

                    @pl.when(pair == i)
                    def _():
                        run()

        back_pair(z, pair, pause, qt, q, k, kt, v, ka, ma, mixed_t, lse, dmt, dm, dqt, dk, dv, dka, dva, dqa)
        return carry

    lax.fori_loop(0, k.shape[1] // 128, one_pair, 0)
    for p, step in ((0, 2), (1, 1), (1, 2)):
        four(p, step)()
    sums.result(0, out_u)
    sums.result(1, out_d)
    for p in range(2):
        sums.drain(p)


def back_shapes(own, total, width):
    widest = max(SHORT - own, own - (SHORT - own))
    vm = pltpu.VMEM
    outs = (
        jax.ShapeDtypeStruct((width, own), BF16),
        jax.ShapeDtypeStruct((total, width), BF16),
        jax.ShapeDtypeStruct((total, width), BF16),
    )
    return outs, [vm((total, 128), F32), vm((total, 128), F32), vm((2, HD, widest), F32)]


def attention_back(*args):
    (width, own), total = args[0].shape, args[2].shape[0]
    outs, scratch = back_shapes(own, total, width)
    return pl.pallas_call(
        attention_back_kernel,
        out_shape=outs,
        in_specs=[pl.BlockSpec(memory_space=pltpu.VMEM)] * 11,
        out_specs=(pl.BlockSpec(memory_space=pltpu.VMEM),) * 3,
        scratch_shapes=scratch,
        compiler_params=pltpu.CompilerParams(vmem_limit_bytes=VMEM_MAX),
        name="attention_back",
    )(*args)


def back_sums(args, gu, gd):
    (width, own), total = args[0].shape, args[2].shape[0]
    outs, scratch = back_shapes(own, total, width)
    block = (width // 8, gu[0].shape[1])
    g = [a.reshape((4, 2) + block) for a in (*gu, *gd)]
    vmem = pl.BlockSpec(memory_space=pltpu.VMEM)
    return pl.pallas_call(
        back_sums_kernel,
        out_shape=outs + (jax.ShapeDtypeStruct(block, F32),) * 2,
        in_specs=[vmem] * 11 + [pl.BlockSpec(memory_space=pl.ANY)] * 8,
        out_specs=(vmem,) * 5,
        scratch_shapes=[
            *scratch,
            pltpu.VMEM((2, 4, 4) + block, BF16),
            *sum_buffers(2, block),
            pltpu.SemaphoreType.DMA((2, 4)),
            *sum_semaphores(2),
        ],
        compiler_params=pltpu.CompilerParams(
            collective_id=2, has_side_effects=True, vmem_limit_bytes=VMEM_MAX
        ),
        name="back_sums",
    )(*args, *g)


def body(
    tokens, w_query, w_key, w_value, b_query, b_value, w_out, b_out, gain_attn, shift_attn,
    w_up, b_up, w_down, b_down, gain_ffn, shift_ffn, lengths, deal_order, cotangent,
):
    own, width = tokens.shape
    n_tp, n_dp = lax.axis_size("tp"), lax.axis_size("dp")
    z, g = lax.axis_index("tp"), lax.axis_index("dp")
    total = own * n_tp
    r, hw = w_query.shape
    direct = n_tp == 4 and n_dp == 8 and r % 16 == 0

    own_w = jnp.stack([jnp.concatenate([w_query, w_key, w_value, w_out], axis=1), w_up, w_down])
    vectors = (b_query, b_value, b_out, gain_attn, shift_attn, b_down, gain_ffn, shift_ffn, b_up)
    n_small = 8 * r + b_up.shape[0]
    if direct:
        narrow = jnp.pad(jnp.concatenate(vectors[:8]).reshape(8, r), ((0, 0), (0, 128 - r)))
        own_s = jnp.concatenate([narrow, jnp.pad(b_up.reshape(-1, 128), ((0, 5), (0, 0)))])
        w, vec, bu, x, q, qt, k, v, kt, wd, mixed_t, lse = forward_all(lengths, deal_order, own_w, own_s, tokens)
        w = w.reshape(2, n_tp, width, w_up.shape[1])
        bu = bu.reshape(-1)
        wq, wk, wv, wo = (wd[i] for i in range(4))
        bq, bv, bo, g1, h1, bd, g2, h2 = (vec[i] for i in range(8))
    else:
        w = lax.all_gather(own_w, ("tp", "dp"), axis=0).reshape((n_tp, n_dp) + own_w.shape)
        w = jnp.moveaxis(w, 2, 0).reshape(3, n_tp, width, w_up.shape[1])
        s = lax.all_gather(jnp.concatenate(vectors), "dp", axis=0)
        x = lax.all_gather(tokens, "tp", axis=0, tiled=True)
        small = [s[:, i * r : (i + 1) * r].reshape(width).astype(F32) for i in range(8)]
        bq, bv, bo, g1, h1, bd, g2, h2 = small
        bu = s[:, 8 * r : n_small].reshape(-1).astype(F32)
        wq, wk, wv, wo = (
            w[0, :, :, i * hw : (i + 1) * hw].transpose(1, 0, 2).reshape(width, width) for i in range(4)
        )
        w = w[1:]
        q = (dot(tokens, wq) + bq).astype(BF16) * jnp.asarray(HD ** (-0.5), BF16)
        k = dot(x, wk).astype(BF16)
        v = (dot(x, wv) + bv).astype(BF16)
        qt, kt = q.T, k.T

    pair = lax.dynamic_slice_in_dim(deal_order, 2 * g, 1)
    first_len = jnp.sum(jnp.where(jnp.arange(lengths.shape[0], dtype=jnp.int32) == pair[0], lengths, 0))
    key_seg = jnp.arange(total, dtype=jnp.int32)[:, None] >= first_len
    lane = jnp.arange(128, dtype=jnp.int32)[None, :]
    ka = jnp.where(lane == 0, ~key_seg, jnp.where(lane == 1, key_seg, (lane >= 2) & (lane < 5))).astype(BF16)
    row_seg = (z * own + jnp.arange(own, dtype=jnp.int32))[None, :] >= first_len
    sub = jnp.arange(8, dtype=jnp.int32)[:, None]
    ma = jnp.where(((sub == 0) & row_seg) | ((sub == 1) & ~row_seg), MASKED, 0.0).astype(F32)

    if not direct:
        mixed_t, lse = attention(qt, k, v.T, ka, ma)
    mixed = mixed_t.T.astype(BF16)
    first_residual = tokens.astype(F32) + contract_last(mixed, wo) + bo
    xhat1, inv1 = normalize_layer(first_residual)
    y1 = xhat1 * g1 + h1
    y1r = y1.astype(BF16)

    u = [dot(y1r, w[0, t]) + bu.reshape(n_tp, -1)[t] for t in range(n_tp)]
    hr = [jax.nn.gelu(a, approximate=False).astype(BF16) for a in u]
    ffn = sum(contract_last(hr[t], w[1, t]) for t in range(n_tp))
    xhat2, inv2 = normalize_layer(y1 + ffn + bd)
    encoder_output = (xhat2 * g2 + h2).astype(BF16)

    grad = cotangent.astype(F32)
    dr2 = normalize_backward(grad, xhat2, inv2, g2)
    dfr = dr2.astype(BF16)
    du = [(dot(dfr, w[1, t]) * gelu_slope(u[t])).astype(BF16) for t in range(n_tp)]
    dy1 = dr2 + sum(contract_last(du[t], w[0, t]) for t in range(n_tp))
    dr1 = normalize_backward(dy1, xhat1, inv1, g1)
    dar = dr1.astype(BF16)
    dm = dot(dar, wo).astype(BF16)
    gu = [contract_first(y1r, du[t]) for t in range(n_tp)]
    gd = [contract_first(dfr, hr[t]) for t in range(n_tp)]
    row_sums = [
        jnp.sum(dar, axis=0, dtype=F32),
        jnp.sum(dy1 * xhat1, axis=0),
        jnp.sum(dy1, axis=0),
        jnp.sum(dfr, axis=0, dtype=F32),
        jnp.sum(grad * xhat2, axis=0),
        jnp.sum(grad, axis=0),
    ]
    wide_sum = jnp.concatenate([jnp.sum(a, axis=0, dtype=F32) for a in du])
    back_args = (qt, q, k, kt, v, ka, ma, mixed_t, lse, dm.T, dm)
    if direct:
        gu, gd = [a.astype(BF16) for a in gu], [a.astype(BF16) for a in gd]
        dqt, dk, dv, g_up, g_down = back_sums(back_args, gu, gd)
        vecs = jnp.stack([jnp.zeros((width,), F32)] * 2 + row_sums)
        a, gs, grad_tokens = finish(dqt, dk, dv, x, dar, mixed_t, wd, dr1, vecs, wide_sum.reshape(1, -1))
        gs = [gs[i, :r] for i in range(8)] + [gs[8:11].reshape(-1)]
    else:
        dqt, dk, dv = attention_back(*back_args)
        dq = dqt.T
        base = dr1 + contract_last(dq, wq)
        far = contract_last(dk, wk) + contract_last(dv, wv)
        base = base + lax.dynamic_slice_in_dim(far, z * own, own)
        dt = far.astype(BF16)
        gq, gk, gv = contract_first(tokens, dq), contract_first(x, dk), contract_first(x, dv)
        go = contract_first(dar, mixed)
        ga = jnp.stack(
            [
                jnp.concatenate([m[:, t * hw : (t + 1) * hw] for m in (gq, gk, gv, go)], axis=1)
                for t in range(n_tp)
            ]
        )
        sums = [jnp.sum(dq, axis=0, dtype=F32), jnp.sum(dv, axis=0, dtype=F32)] + row_sums
        sums = [a.reshape(n_dp, r) for a in sums]
        sv = jnp.concatenate(sums + [wide_sum.reshape(n_dp, -1)], axis=1)
        grads = jnp.stack([ga, jnp.stack(gu), jnp.stack(gd)], axis=1).reshape(n_tp, 3, n_dp, r, -1)
        grads = jnp.moveaxis(grads, 1, 2).reshape(n_tp * n_dp, 3, r, -1)
        gw = lax.psum_scatter(grads, ("tp", "dp"), scatter_dimension=0, tiled=True)[0]
        gs = lax.psum_scatter(lax.psum(sv, "tp"), "dp", scatter_dimension=0, tiled=True)[0]
        others = jnp.where(jnp.arange(total)[:, None] // own == z, jnp.zeros((), BF16), dt)
        grad_tokens = base + lax.psum_scatter(others, "tp", scatter_dimension=0, tiled=True).astype(F32)
        gs = [gs[i * r : (i + 1) * r] for i in range(8)] + [gs[8 * r : n_small]]
        a, g_up, g_down = gw[0], gw[1], gw[2]
    return (
        encoder_output, grad_tokens,
        a[:, :hw], a[:, hw : 2 * hw], a[:, 2 * hw : 3 * hw], gs[0], gs[1],
        a[:, 3 * hw :], gs[2], gs[3], gs[4],
        g_up, gs[8], g_down, gs[5], gs[6], gs[7],
    )


def solution(mesh):
    rows, block, vector = P(("dp", "tp"), None), P("dp", "tp"), P("dp")
    in_specs = (
        rows, block, block, block, vector, vector, block, vector, vector, vector,
        block, vector, block, vector, vector, vector, P(), P(), rows,
    )
    out_specs = (
        rows, rows, block, block, block, vector, vector, block, vector, vector, vector,
        block, vector, block, vector, vector, vector,
    )
    return jax.shard_map(body, mesh=mesh, in_specs=in_specs, out_specs=out_specs, check_vma=False)
```

```python
import functools

import jax
import jax.numpy as jnp
from jax import lax
from jax.experimental import pallas as pl
from jax.experimental.pallas import tpu as pltpu
from jax.sharding import PartitionSpec as P

HD = 64
SHORT = 1024
EPS = 1e-05
SQRT_HALF = 0.7071067811865476
INV_ROOT_TAU = 0.3989422804014327
MASKED = -1e30
KEYS = 512
ROWS = 128
VMEM_MAX = 67043328
MESH = pl.DeviceIdType.MESH
F32 = jnp.float32
BF16 = jnp.bfloat16


def dot(left, right):
    return jnp.dot(left, right, preferred_element_type=F32)


def contract_last(left, right):
    return lax.dot_general(left, right, (((1,), (1,)), ((), ())), preferred_element_type=F32)


def contract_first(left, right):
    return lax.dot_general(left, right, (((0,), (0,)), ((), ())), preferred_element_type=F32)


def normalize_layer(resid):
    center = resid - jnp.mean(resid, axis=-1, keepdims=True)
    inverse_deviation = lax.rsqrt(jnp.mean(center * center, axis=-1, keepdims=True) + EPS)
    return (center * inverse_deviation, inverse_deviation)


def normalize_backward(output_gradient, xhat, inverse_deviation, gain):
    scaled_rows = output_gradient * gain
    return inverse_deviation * (
        scaled_rows
        - jnp.mean(scaled_rows, axis=-1, keepdims=True)
        - xhat * jnp.mean(scaled_rows * xhat, axis=-1, keepdims=True)
    )


def gelu_slope(pre_act):
    return (
        0.5 * (1.0 + lax.erf(pre_act * SQRT_HALF))
        + pre_act * jnp.exp(-0.5 * pre_act * pre_act) * INV_ROOT_TAU
    )


def position():
    z = lax.axis_index("tp")
    d = lax.axis_index("dp")
    core = lax.rem(d, 2)
    first = 2 + 2 * core
    second = 4 - 2 * core
    return z, d, core, first, second


def xor(d, mask):
    return d + mask * (1 - 2 * lax.rem(d // mask, 2))


def greet(z, d):
    barrier = pltpu.get_barrier_semaphore()
    for mask in (1, 2, 4):
        pl.semaphore_signal(barrier, inc=1, device_id=(xor(d, mask), z), device_id_type=MESH)
    for j in range(1, 4):
        pl.semaphore_signal(barrier, inc=1, device_id=(d, lax.rem(z + j, 4)), device_id_type=MESH)
    pl.semaphore_wait(barrier, 6)


def by_distance(z):
    low = z <= 1
    near = jnp.where(z == 0, 1, jnp.where(z == 3, 2, z - 1))
    mid = jnp.where(z == 0, 2, jnp.where(z == 3, 1, z + 1))
    far = jnp.where(low, 3, 0)
    return (z, near, mid, far)


def put(src, dst, send, recv, dp, tp):
    return pltpu.make_async_remote_copy(
        src_ref=src, dst_ref=dst, send_sem=send, recv_sem=recv, device_id=(dp, tp), device_id_type=MESH
    )


def forward_kernel(
    lengths, deal, own_w, own_s, own_t,
    w, vec, bu, xt_out, q_out, qt_out, k_out, v_out, kt_out, wd_out, mixed_t, lse,
    wa, s, x, xt, q, qt, k, v, kt, vt, wd, ka, sc, m, l, acc,
    wz_s, wz_r, wa_s, wa_r, wb_s, wb_r, wc_s, wc_r, tk_s, tk_r, sm_s, sm_r, lo_sem, arr_sem, out_sem,
):
    z, d, core, first, second = position()
    packs = own_w.shape[0]
    own, width = own_t.shape
    total = 4 * own
    hw = width // 4
    chunks = own // ROWS
    d1, d2 = xor(d, first), xor(d, second)
    d12 = xor(d1, second)
    pal = xor(d, 1)
    pd, pd1, pd2, pd12 = (xor(e, 1) for e in (d, d1, d2, d12))
    order = by_distance(z)
    first_len = lengths[deal[2 * d]]

    greet(z, d)

    def block(p, tt, e):
        return wa.at[tt, e] if p == 0 else w.at[p - 1, tt, e]

    def along_z(p, tt, src, act):
        dst = block(p, tt, d)
        right = put(src, dst, wz_s.at[0, p, tt], wz_r.at[p, tt], d, jnp.minimum(z + 1, 3))
        left = put(src, dst, wz_s.at[1, p, tt], wz_r.at[p, tt], d, jnp.maximum(z - 1, 0))

        @pl.when((tt <= z) & (z < 3))
        def _():
            act(right)

        @pl.when((tt >= z) & (z > 0))
        def _():
            act(left)

    def across(p, tt, src):
        dst = block(p, tt, d)
        return (
            put(src, dst, wa_s.at[p, tt], wa_r.at[p, tt], d1, z),
            put(src, dst, wb_s.at[p, tt, 0], wb_r.at[p, tt, 0], d2, z),
            put(src, dst, wc_s.at[p, tt, 0], wc_r.at[p, tt, 0], pal, z),
        )

    def after_first(p, tt):
        src = block(p, tt, d1)
        return (
            put(src, src, wb_s.at[p, tt, 1], wb_r.at[p, tt, 1], d2, z),
            put(src, src, wc_s.at[p, tt, 1], wc_r.at[p, tt, 1], pal, z),
        )

    def after_second(p, tt, i):
        src = block(p, tt, d2 if i == 0 else d12)
        return put(src, src, wc_s.at[p, tt, 2 + i], wc_r.at[p, tt, 2 + i], pal, z)

    def source(p, j):
        return own_w.at[p] if j == 0 else block(p, order[j], d)

    def arrive(ref, sem):
        put(ref, ref, arr_sem, sem, pal, z).wait_recv()

    def begin_z(p, j):
        if j > 0:
            arrive(block(p, order[j], d), wz_r.at[p, order[j]])
        along_z(p, order[j], source(p, j), lambda c: c.start())

    def begin_xy(p, j):
        for copy in across(p, order[j], source(p, j)):
            copy.start()

    def begin(p, j):
        begin_z(p, j)
        begin_xy(p, j)

    def relay_first(p, j):
        tt = order[j]
        arrive(block(p, tt, d1), wa_r.at[p, tt])
        for copy in after_first(p, tt):
            copy.start()

    def relay_second(p, j):
        tt = order[j]
        for i in range(2):
            arrive(block(p, tt, d2 if i == 0 else d12), wb_r.at[p, tt, i])
            after_second(p, tt, i).start()

    def from_pal(p):
        for tt in range(4):
            for i, e in enumerate((pd, pd2, pd1, pd12)):
                arrive(block(p, tt, e), wc_r.at[p, tt, i])

    def sent(p):
        for j in range(4):
            tt = order[j]
            along_z(p, tt, source(p, j), lambda c: c.wait_send())
            for copy in across(p, tt, source(p, j)) + after_first(p, tt):
                copy.wait_send()
            for i in range(2):
                after_second(p, tt, i).wait_send()

    def token_slice(o, i):
        return x.at[pl.ds(pl.multiple_of((o * chunks + i) * ROWS, ROWS), ROWS)]

    def token_hop(o, i, hop, step):
        src = own_t.at[pl.ds(i * ROWS, ROWS)] if hop == 0 else token_slice(o, i)
        way = 0 if step > 0 else 1
        return put(src, token_slice(o, i), tk_s.at[way, hop, i], tk_r.at[way, hop, i], d, jnp.clip(z + step, 0, 3))

    last = SHORT // ROWS

    def wanted(o, i, target, step):
        n = o * chunks + i
        if step > 0:
            return (target <= 2) | (n >= last)
        return (target >= 1) | (n < 4 * chunks - last)

    def chunk_ids(step):
        return list(range(chunks))[:: -step]

    def tokens(hop, step, act, which=slice(None)):
        o, target = z - step * hop, z + step
        valid = (o >= 0) & (o <= 3) & (target >= 0) & (target <= 3)
        for i in chunk_ids(step)[which]:

            @pl.when(valid & wanted(o, i, target, step))
            def _():
                act(token_hop(o, i, hop, step))

    def tokens_on(hop, step, onward):
        o, target = z - step * (hop + 1), z + step
        valid = (o >= 0) & (o <= 3) & (z - step >= 0) & (z - step <= 3)
        way = 0 if step > 0 else 1
        for i in chunk_ids(step):

            @pl.when(valid & wanted(o, i, z, step))
            def _():
                arrive(token_slice(jnp.clip(o, 0, 3), i), tk_r.at[way, hop, i])

            if onward:

                @pl.when(valid & (target >= 0) & (target <= 3) & wanted(o, i, target, step))
                def _():
                    token_hop(o, i, hop + 1, step).start()

    def small(stage):
        if stage == 0:
            return [
                put(own_s, s.at[d], sm_s.at[0], sm_r.at[0], d1, z),
                put(own_s, s.at[d], sm_s.at[1], sm_r.at[1], d2, z),
                put(own_s, s.at[d], sm_s.at[3], sm_r.at[3], pal, z),
            ]
        if stage == 1:
            return [
                put(s.at[d1], s.at[d1], sm_s.at[2], sm_r.at[2], d2, z),
                put(s.at[d1], s.at[d1], sm_s.at[4], sm_r.at[4], pal, z),
            ]
        return [
            put(s.at[d2], s.at[d2], sm_s.at[5], sm_r.at[5], pal, z),
            put(s.at[d12], s.at[d12], sm_s.at[6], sm_r.at[6], pal, z),
        ]

    def own_tokens(*which):
        for step in (1, -1):
            tokens(0, step, lambda c: c.start(), slice(*which))

    begin(0, 0)
    for copy in small(0):
        copy.start()
    own_tokens(0, 1)
    s[d] = own_s[...]
    wa[z, d] = own_w[0]
    mine = pl.ds(pl.multiple_of(z * own, ROWS), own)
    x[mine, :] = own_t[...]
    keep = pltpu.make_async_copy(own_w.at[pl.ds(1, packs - 1)], w.at[:, z, d], lo_sem)
    keep.start()

    @pl.when(z == 0)
    def _():
        x[total - SHORT :, :] = jnp.zeros((SHORT, width), BF16)
        xt[:, total - SHORT :] = jnp.zeros((width, SHORT), BF16)

    @pl.when(z == 3)
    def _():
        x[:SHORT, :] = jnp.zeros((SHORT, width), BF16)
        xt[:, :SHORT] = jnp.zeros((width, SHORT), BF16)

    begin(0, 1)
    relay_first(0, 0)
    own_tokens(1, 2)
    begin(0, 2)
    relay_second(0, 0)
    relay_first(0, 1)
    for p in range(1, packs):
        begin_z(p, 0)
    begin(0, 3)
    own_tokens(2, chunks)
    relay_second(0, 1)
    relay_first(0, 2)
    begin_xy(1, 0)
    arrive(s.at[d1], sm_r.at[0])
    for copy in small(1):
        copy.start()
    relay_second(0, 2)
    relay_first(0, 3)
    for p in range(2, packs):
        begin_xy(p, 0)
    arrive(s.at[d2], sm_r.at[1])
    arrive(s.at[d12], sm_r.at[2])
    for copy in small(2):
        copy.start()
    for p in range(1, packs):
        begin(p, 1)
    lane = lax.broadcasted_iota(jnp.int32, (own, 128), 1)
    for i in range(4):
        late = lax.broadcasted_iota(jnp.int32, (own, 128), 0) + i * own >= first_len
        ones = jnp.where((lane >= 2) & (lane < 5), 1.0, 0.0)
        flags = jnp.where(lane == 0, jnp.where(late, 0.0, 1.0), jnp.where(lane == 1, jnp.where(late, 1.0, 0.0), ones))
        ka[pl.ds(i * own, own), :] = flags.astype(BF16)

    relay_second(0, 3)
    for i, e in enumerate((pd, pd2, pd1, pd12)):
        arrive(s.at[e], sm_r.at[3 + i])
    r = width // 8
    for e in range(8):
        piece = s[e].astype(F32)
        vec[0:8, e * r : (e + 1) * r] = piece[0:8, 0:r]
        for j in range(hw * 2 // 128):
            col = e * hw * 2 + j * 128
            bu[0:1, col : col + 128] = piece[8 + j : 9 + j, :]
    from_pal(0)
    for tt in range(4):
        rows = wa[tt].reshape(width, width)
        for i in range(4):
            wd[i, :, tt * hw : (tt + 1) * hw] = rows[:, i * hw : (i + 1) * hw]
    wd_copy = pltpu.make_async_copy(wd, wd_out, out_sem.at[0])
    wd_copy.start()

    tile = 256

    def q_tile(n, carry):
        lanes = pl.ds(pl.multiple_of(n * tile, tile), tile)
        rows = (dot(own_t[...], wd[0, :, lanes]) + vec[0:1, lanes]).astype(BF16) * jnp.asarray(HD ** (-0.5), BF16)
        q[:, lanes] = rows
        qt[lanes, :] = rows.T
        return carry

    def project(o):
        rows = pl.ds(pl.multiple_of(o * own, ROWS), own)

        def kv_tile(n, carry):
            lanes = pl.ds(pl.multiple_of(n * tile, tile), tile)
            keys = dot(x[rows, :], wd[1, :, lanes]).astype(BF16)
            k[rows, lanes] = keys
            kt[lanes, rows] = keys.T
            values = (dot(x[rows, :], wd[2, :, lanes]) + vec[1:2, lanes]).astype(BF16)
            v[rows, lanes] = values
            vt[lanes, rows] = values.T
            xt[lanes, rows] = x[rows, lanes].T
            return carry

        lax.fori_loop(0, width // tile, kv_tile, 0)

    def project_far():
        for step in (1, -1):
            tokens_on(1, step, False)
        project(jnp.where(z == 0, 2, jnp.where(z == 1, 3, z - 2)))

    middle = (z == 1) | (z == 2)
    lax.fori_loop(0, width // tile, q_tile, 0)
    project(z)
    for p in range(1, packs):
        relay_first(p, 0)
    for step in (1, -1):
        tokens_on(0, step, True)

    @pl.when(z > 0)
    def _():
        project(jnp.maximum(z - 1, 0))

    for p in range(1, packs):
        begin(p, 2)
    for p in range(1, packs):
        relay_second(p, 0)
        relay_first(p, 1)

    @pl.when(z < 3)
    def _():
        project(jnp.minimum(z + 1, 3))

    @pl.when(jnp.logical_not(middle))
    def _():
        project_far()

    for p in range(1, packs):
        begin(p, 3)

    def both(act, j):
        def run():
            for p in range(1, packs):
                act(p, j)

        return run

    between = {
        (0, 1): both(relay_second, 1),
        (0, 2): both(relay_first, 2),
        (0, 5): both(relay_second, 2),
        (1, 0): both(relay_first, 3),
        (1, 4): both(relay_second, 3),
    }
    outs = [
        pltpu.make_async_copy(a, b, out_sem.at[1 + i])
        for i, (a, b) in enumerate(((xt, xt_out), (q, q_out), (qt, qt_out), (k, k_out), (v, v_out), (kt, kt_out)))
    ]
    pairs = width // 128
    for part, (row0, n, start) in enumerate(parts_of(z, own)):
        if part == 1:

            @pl.when(middle)
            def _():
                project_far()

            for copy in outs:
                copy.start()
        cols = pl.ds(pl.multiple_of(row0, 128), n)
        late = lax.broadcasted_iota(jnp.int32, (1, n), 1) + (z * own + row0) >= first_len
        masks = (jnp.where(late, MASKED, 0.0), jnp.where(late, 0.0, MASKED))
        aug = aug_rows(pick_rows(masks, n), n)

        def one_pair(pair, carry):
            for (at, i), run in between.items():
                if at == part:

                    @pl.when(pair == i)
                    def _():
                        run()

            attend_pair(z, part, start, pair, cols, n, aug, qt, k, vt, ka, mixed_t, lse, sc, m, l, acc)
            return carry

        lax.fori_loop(0, pairs, one_pair, 0)

    for p in range(1, packs):
        from_pal(p)
    for stage in range(3):
        for copy in small(stage):
            copy.wait_send()
    for hop in range(2):
        for step in (1, -1):
            tokens(hop, step, lambda c: c.wait_send())
    for p in range(packs):
        sent(p)
    keep.wait()
    wd_copy.wait()
    for copy in outs:
        copy.wait()


def attend_pair(z, part, start, pair, cols, n, aug, qt, k, vt, ka, mixed_t, lse, s, m, l, acc):
    total = k.shape[0]
    lanes = pl.ds(pl.multiple_of(pair * 128, 128), 128)
    for half in range(2):
        m[half, :, :n] = jnp.full((1, n), MASKED, F32)
        l[half, :, :n] = jnp.zeros((1, n), F32)
        acc[half, :, :n] = jnp.zeros((HD, n), F32)
    qs = [padded(qt[pl.ds(pl.multiple_of(pair * 128 + half * HD, HD), HD), cols], half, aug, n) for half in range(2)]

    def scores(key0):
        keys = pl.ds(key0, KEYS)
        left = jnp.concatenate([k[keys, lanes], ka[keys, :]], axis=1)
        for half in range(2):
            score = dot(left, qs[half])
            s[half, keys, :n] = score
            m[half, :, :n] = jnp.maximum(m[half, :, :n], jnp.max(score, axis=0, keepdims=True))

    over_keys(z, part, start, total, scores)
    tops = [m[half, :, :n] for half in range(2)]

    def mix(key0):
        keys = pl.ds(key0, KEYS)
        for half in range(2):
            raised = jnp.exp(s[half, keys, :n] - tops[half])
            l[half, :, :n] += jnp.sum(raised, axis=0, keepdims=True)
            values = vt[pl.ds(pl.multiple_of(pair * 128 + half * HD, HD), HD), keys]
            acc[half, :, :n] += dot(values, raised.astype(BF16))

    over_keys(z, part, start, total, mix)
    for half in range(2):
        sums = l[half, :, :n]
        rows = pl.ds(pl.multiple_of(pair * 128 + half * HD, HD), HD)
        mixed_t[rows, cols] = acc[half, :, :n] / sums
        lse[pair, half : half + 1, cols] = tops[half] + jnp.log(sums)


def forward_all(lengths, deal, own_w, own_s, own_t):
    packs, r, c = own_w.shape
    own, width = own_t.shape
    total = 4 * own
    chunks = own // ROWS
    widest = max(SHORT - own, own - (SHORT - own))
    dma, vm = pltpu.SemaphoreType.DMA, pltpu.VMEM
    any_ = pl.BlockSpec(memory_space=pl.ANY)
    vmem = pl.BlockSpec(memory_space=pltpu.VMEM)
    smem = pl.BlockSpec(memory_space=pltpu.SMEM)
    shape = jax.ShapeDtypeStruct
    return pl.pallas_call(
        forward_kernel,
        out_shape=(
            shape((packs - 1, 4, 8, r, c), BF16),
            shape((8, width), F32),
            shape((1, 4 * c), F32),
            shape((width, total), BF16),
            shape((own, width), BF16),
            shape((width, own), BF16),
            shape((total, width), BF16),
            shape((total, width), BF16),
            shape((width, total), BF16),
            shape((4, width, width), BF16),
            shape((width, own), F32),
            shape((width // 128, 8, own), F32),
        ),
        in_specs=[smem, smem, vmem, vmem, vmem],
        out_specs=(any_, vmem, vmem) + (any_,) * 7 + (vmem, vmem),
        scratch_shapes=[
            vm((4, 8, r, c), BF16),
            vm((8, 16, 128), BF16),
            vm((total, width), BF16),
            vm((width, total), BF16),
            vm((own, width), BF16),
            vm((width, own), BF16),
            vm((total, width), BF16),
            vm((total, width), BF16),
            vm((width, total), BF16),
            vm((width, total), BF16),
            vm((4, width, width), BF16),
            vm((total, 128), BF16),
            vm((2, total, widest), F32),
            vm((2, 1, widest), F32),
            vm((2, 1, widest), F32),
            vm((2, HD, widest), F32),
            dma((2, packs, 4)),
            dma((packs, 4)),
            dma((packs, 4)),
            dma((packs, 4)),
            dma((packs, 4, 2)),
            dma((packs, 4, 2)),
            dma((packs, 4, 4)),
            dma((packs, 4, 4)),
            dma((2, 2, chunks)),
            dma((2, 2, chunks)),
            dma((7,)),
            dma((7,)),
            dma(()),
            dma(()),
            dma((7,)),
        ],
        compiler_params=pltpu.CompilerParams(
            collective_id=0, has_side_effects=True, vmem_limit_bytes=VMEM_MAX
        ),
        name="forward_all",
    )(lengths, deal, own_w, own_s, own_t)


def up(ref):
    return ref[...].astype(F32)


class Sums:
    def __init__(self, z, d, core, e_mask, f_mask, give, mine, ready, bufs, sems):
        self.z, self.d, self.give, self.mine, self.ready = z, d, give, mine, ready
        self.r1, self.b2, self.r2, self.b3, self.r3, self.s3, self.b4, self.r4 = bufs
        self.sems = sems
        self.xy = d // 2
        self.e, self.f = xor(d, e_mask) // 2, xor(d, f_mask) // 2
        self.ef = xor(xor(d, e_mask), f_mask) // 2
        self.d_e, self.d_f, self.pal = xor(d, e_mask), xor(d, f_mask), xor(d, 1)

    def one(self, p, t):
        return put(self.give(p, t), self.r1.at[p, t], self.sems[0].at[p, t], self.sems[1].at[p, t], self.pal, self.z)

    def two(self, p, t):
        return put(self.b2.at[p, t], self.r2.at[p, t], self.sems[2].at[p, t], self.sems[3].at[p, t], self.d_e, self.z)

    def three(self, p, t):
        return put(self.b3.at[p, t], self.r3.at[p, t], self.sems[4].at[p, t], self.sems[5].at[p, t], self.d_f, self.z)

    def four(self, p, t, way):
        to = jnp.minimum(self.z + 1, 3) if way == 0 else jnp.maximum(self.z - 1, 0)
        return put(
            self.b4.at[p, way, t], self.r4.at[p, way, t],
            self.sems[6].at[p, way, t], self.sems[7].at[p, way, t], self.d, to,
        )

    def at_two(self, p, t):
        self.ready(p, t)
        self.one(p, t).wait_recv()
        for i, x in enumerate((self.e, self.ef)):
            self.b2[p, t, i] = (self.mine(p, t, x) + up(self.r1.at[p, t, x])).astype(BF16)
        self.two(p, t).start()

    def at_three(self, p, t):
        self.two(p, t).wait_recv()
        f = self.f
        self.b3[p, t] = (self.mine(p, t, f) + up(self.r1.at[p, t, f]) + up(self.r2.at[p, t, 1])).astype(BF16)
        self.three(p, t).start()

    def at_kept(self, p, t):
        self.three(p, t).wait_recv()
        xy = self.xy
        self.s3[p, t] = self.mine(p, t, xy) + up(self.r1.at[p, t, xy]) + up(self.r2.at[p, t, 0]) + up(self.r3.at[p, t])

    def at_four(self, p, t, step):
        for way in range(2):
            pos = step if way == 0 else 3 - step
            if not (t > pos if way == 0 else t < pos):
                continue

            @pl.when(self.z == pos)
            def _():
                if step == 0:
                    self.b4[p, way, t] = self.s3[p, t].astype(BF16)
                else:
                    self.four(p, t, way).wait_recv()
                    self.b4[p, way, t] = (self.s3[p, t] + up(self.r4.at[p, way, t])).astype(BF16)
                self.four(p, t, way).start()

    def result(self, p, out):
        z = self.z
        out[...] = self.s3[p, z]

        @pl.when(z > 0)
        def _():
            self.four(p, z, 0).wait_recv()
            out[...] += up(self.r4.at[p, 0, z])

        @pl.when(z < 3)
        def _():
            self.four(p, z, 1).wait_recv()
            out[...] += up(self.r4.at[p, 1, z])

    def drain(self, p):
        for t in range(4):
            self.one(p, t).wait_send()
            self.two(p, t).wait_send()
            self.three(p, t).wait_send()
            for way in range(2):

                @pl.when((t > self.z) if way == 0 else (t < self.z))
                def _():
                    self.four(p, t, way).wait_send()


def sum_buffers(packs, block):
    vm = pltpu.VMEM
    return [
        vm((packs, 4, 4) + block, BF16),
        vm((packs, 4, 2) + block, BF16),
        vm((packs, 4, 2) + block, BF16),
        vm((packs, 4) + block, BF16),
        vm((packs, 4) + block, BF16),
        vm((packs, 4) + block, F32),
        vm((packs, 2, 4) + block, BF16),
        vm((packs, 2, 4) + block, BF16),
    ]


def sum_semaphores(packs):
    dma = pltpu.SemaphoreType.DMA
    return [dma((packs, 4))] * 6 + [dma((packs, 2, 4))] * 2


def finish_kernel(
    dqt, dk, dv, xt, dar, mixed_t, wd, dr1, vecs, bup,
    out_w, out_s, out_t,
    dart, dq, mixed, gp, sv, ds, dr, sk, q1, q2, q3, c2, c3, q4,
    r1, b2, r2, b3, r3, s3, b4, r4,
    p1_s, p1_r, p2_s, p2_r, p3_s, p3_r, p4_s, p4_r, t_s, t_r, v_s, v_r,
):
    z, d, core, first, second = position()
    own, width = out_t.shape
    chunks = own // ROWS
    total = 4 * chunks
    edge = SHORT // ROWS
    hw = width // 4
    r = width // 8
    greet(z, d)

    def token(k, way):
        to = jnp.minimum(z + 1, 3) if way == 0 else jnp.maximum(z - 1, 0)
        slot = k if way == 0 else jnp.where(k // chunks == to, total + k % chunks, k)
        return put(ds.at[k], dr.at[slot], t_s.at[k], t_r.at[slot], d, to)

    def token_in(k, way):
        slot = k if way == 0 else jnp.where(k // chunks == z, total + k % chunks, k)
        return put(ds.at[k], dr.at[slot], t_s.at[k], t_r.at[slot], d, z), slot

    def sends(k, way):
        o = k // chunks
        if way == 0:
            low = jnp.where(k < total - edge, 0, 1)
            return (z >= low) & (z < o) & (o > low)
        high = jnp.where(k >= edge, 3, 2)
        return (z <= high) & (z > o) & (o < high)

    def starts(k, way):
        if way == 0:
            return z == jnp.where(k < total - edge, 0, 1)
        return z == jnp.where(k >= edge, 3, 2)

    def pick(a, b, c, e):
        return jnp.where(z == 0, a, jnp.where(z == 1, b, jnp.where(z == 2, c, e)))

    tile = 256

    def far_shard(o, mine):
        rows = pl.ds(pl.multiple_of(o * own, ROWS), own)

        def one_tile(n, carry):
            lanes = pl.ds(pl.multiple_of(n * tile, tile), tile)
            far = contract_last(dk[rows, :], wd[1, lanes, :]) + contract_last(dv[rows, :], wd[2, lanes, :])
            if mine:
                out_t[:, lanes] = dr1[:, lanes] + far
            else:
                ds[pl.ds(o * chunks, chunks), :, lanes] = far.reshape(chunks, ROWS, tile).astype(BF16)
            return carry

        lax.fori_loop(0, width // tile, one_tile, 0)

    def far_and_send(j):
        o = pick(*((2, 3, 0, 1), (1, 2, 1, 2), (3, 0, 3, 0))[j])

        @pl.when((j < 2) | (z == 1) | (z == 2))
        def _():
            far_shard(o, False)

        for i in range(chunks):
            for way in range(2):
                k = o * chunks + i

                @pl.when(sends(k, way) & starts(k, way))
                def _():
                    token(k, way).start()

    far_and_send(0)

    right_order = [k for o in (3, 2, 1) for k in range(o * chunks, (o + 1) * chunks)]
    left_order = [total - 1 - k for k in right_order]

    def forward_tokens(at):
        for k, way in [(k, 0) for k in right_order] + [(k, 1) for k in left_order]:
            pos = at if way == 0 else 3 - at
            passes = (at < k // chunks) if way == 0 else (3 - at > k // chunks)
            begins = (0 if k < total - edge else 1) if way == 0 else (3 if k >= edge else 2)
            if not passes or (begins >= pos if way == 0 else begins <= pos):
                continue

            @pl.when(z == pos)
            def _():
                got, slot = token_in(k, way)
                got.wait_recv()
                ds[k] = (ds[k].astype(F32) + dr[slot].astype(F32)).astype(BF16)
                token(k, way).start()

    def flip_own(i, carry):
        cols = pl.ds(pl.multiple_of(i * ROWS, ROWS), ROWS)
        dart[:, cols] = dar[cols, :].T
        dq[cols, :] = dqt[:, cols].T
        mixed[cols, :] = mixed_t[:, cols].T.astype(BF16)
        return carry

    lax.fori_loop(0, chunks, flip_own, 0)

    def give(p, t):
        return gp.at[t, :, 1 - core]

    def mine(p, t, at):
        return gp[t, at, core].astype(F32)

    sums = Sums(
        z, d, core, second, first, give, mine, lambda p, t: None,
        (r1, b2, r2, b3, r3, s3, b4, r4), (p1_s, p1_r, p2_s, p2_r, p3_s, p3_r, p4_s, p4_r),
    )
    here = pl.ds(pl.multiple_of(z * own, ROWS), own)
    half = width // 2

    def weights(th):
        lanes = pl.ds(th * half, half)

        def rows_of(m, carry):
            rows = pl.ds(pl.multiple_of(m * half, ROWS), half)
            parts = (
                lambda: dot(xt[rows, here], dq[:, lanes]),
                lambda: dot(xt[rows, :], dk[:, lanes]),
                lambda: dot(xt[rows, :], dv[:, lanes]),
                lambda: dot(dart[rows, :], mixed[:, lanes]),
            )
            for i, part in enumerate(parts):
                got = part().astype(BF16)
                for h in range(2):
                    block = got[:, h * hw : (h + 1) * hw].reshape(2, 2, r, hw)
                    gp[2 * th + h, pl.ds(2 * m, 2), :, :, i * hw : (i + 1) * hw] = block
            return carry

        lax.fori_loop(0, 2, rows_of, 0)
        for t in (2 * th, 2 * th + 1):
            sums.one(0, t).start()

    weights(0)
    weights(1)
    for t in (0, 1):
        sums.at_two(0, t)
    far_and_send(1)
    forward_tokens(1)
    for t in (2, 3):
        sums.at_two(0, t)
    far_and_send(2)
    forward_tokens(2)

    ones = jnp.ones((8, 4 * own), BF16)
    index = lax.broadcasted_iota(jnp.int32, (8, width), 0)
    small_rows = jnp.where(index == 0, dot(ones[:, :own], dq[...]), jnp.where(index == 1, dot(ones, dv[...]), vecs[...]))
    pad = jnp.zeros((8, 128 - r), F32)
    for i in range(8):
        sv[i // 2, i % 2, 0:8, :] = jnp.concatenate([small_rows[:, i * r : (i + 1) * r], pad], axis=1)
        wide = [bup[:, (i * 3 + j) * 128 : (i * 3 + j + 1) * 128] for j in range(3)]
        sv[i // 2, i % 2, 8:16, :] = jnp.concatenate(wide + [jnp.zeros((5, 128), F32)], axis=0)
    small = [
        put(sv.at[:, 1 - core], q1, v_s.at[0], v_r.at[0], sums.pal, z),
        put(c2, q2, v_s.at[1], v_r.at[1], sums.d_e, z),
        put(c3, q3, v_s.at[2], v_r.at[2], sums.d_f, z),
    ]
    small_z = [
        put(sk, q4.at[j - 1], v_s.at[2 + j], v_r.at[2 + j], d, lax.rem(z + j, 4)) for j in range(1, 4)
    ]
    small[0].start()
    far_shard(z, True)

    def query_tile(n, carry):
        lanes = pl.ds(pl.multiple_of(n * tile, tile), tile)
        out_t[:, lanes] += contract_last(dq[...], wd[0, lanes, :])
        return carry

    lax.fori_loop(0, width // tile, query_tile, 0)
    small[0].wait_recv()
    for i, at in enumerate((sums.e, sums.ef)):
        c2[i] = sv[at, core] + q1[at]
    small[1].start()
    for t in range(4):
        sums.at_three(0, t)
    small[1].wait_recv()
    c3[...] = sv[sums.f, core] + q1[sums.f] + q2[1]
    small[2].start()
    for t in range(4):
        sums.at_kept(0, t)
    for step in range(3):
        for t in range(4):
            sums.at_four(0, t, step)
        if step == 0:
            small[2].wait_recv()
            sk[...] = sv[sums.xy, core] + q1[sums.xy] + q2[0] + q3[...]
            for copy in small_z:
                copy.start()
    for i in range(chunks):
        k = z * chunks + i
        rows = pl.ds(i * ROWS, ROWS)
        from_left = (z > 0) & ((z == 1) & (k < total - edge) | (z > 1))
        from_right = (z < 3) & ((z == 2) & (k >= edge) | (z < 2))

        @pl.when(from_left)
        def _():
            put(ds.at[k], dr.at[k], t_s.at[k], t_r.at[k], d, z).wait_recv()
            out_t[rows, :] += dr[k].astype(F32)

        @pl.when(from_right)
        def _():
            put(ds.at[k], dr.at[total + i], t_s.at[k], t_r.at[total + i], d, z).wait_recv()
            out_t[rows, :] += dr[total + i].astype(F32)

    for copy in small_z:
        copy.wait_recv()
    out_s[...] = sk[...] + q4[0] + q4[1] + q4[2]
    sums.result(0, out_w)
    for copy in small + small_z:
        copy.wait_send()
    sums.drain(0)
    for k in range(total):
        for way in range(2):

            @pl.when(sends(k, way))
            def _():
                token(k, way).wait_send()


def finish(dqt, dk, dv, xt, dar, mixed_t, wd, dr1, vecs, bup):
    own, width = dr1.shape
    r = width // 8
    chunks = own // ROWS
    dma, vm = pltpu.SemaphoreType.DMA, pltpu.VMEM
    vmem = pl.BlockSpec(memory_space=pltpu.VMEM)
    block, sb = (r, width), (16, 128)
    return pl.pallas_call(
        finish_kernel,
        out_shape=(
            jax.ShapeDtypeStruct(block, F32),
            jax.ShapeDtypeStruct(sb, F32),
            jax.ShapeDtypeStruct((own, width), F32),
        ),
        in_specs=[vmem] * 10,
        out_specs=(vmem, vmem, vmem),
        scratch_shapes=[
            vm((width, own), BF16),
            vm((own, width), BF16),
            vm((own, width), BF16),
            vm((4, 4, 2) + block, BF16),
            vm((4, 2) + sb, F32),
            vm((4 * chunks, ROWS, width), BF16),
            vm((5 * chunks, ROWS, width), BF16),
            vm(sb, F32),
            vm((4,) + sb, F32),
            vm((2,) + sb, F32),
            vm(sb, F32),
            vm((2,) + sb, F32),
            vm(sb, F32),
            vm((3,) + sb, F32),
            *sum_buffers(1, block),
            *sum_semaphores(1),
            dma((4 * chunks,)),
            dma((5 * chunks,)),
            dma((6,)),
            dma((6,)),
        ],
        compiler_params=pltpu.CompilerParams(
            collective_id=1, has_side_effects=True, vmem_limit_bytes=VMEM_MAX
        ),
        name="finish",
    )(dqt, dk, dv, xt, dar, mixed_t, wd, dr1, vecs, bup)


def parts_of(z, own):
    sure = SHORT - own
    low = z < 2
    return (
        (jnp.where(low, 0, own - sure), sure, jnp.where(low, 0, SHORT)),
        (jnp.where(low, sure, 0), own - sure, jnp.where(z == 3, SHORT, 0)),
    )


def over_keys(z, part, start, total, act):
    window = total - SHORT
    for c in range(window // KEYS):
        act(pl.multiple_of(start + c * KEYS, KEYS))
    if part == 1:

        @pl.when((z == 1) | (z == 2))
        def _():
            for c in range(window // KEYS, total // KEYS):
                act(c * KEYS)


def aug_rows(top, r):
    return jnp.concatenate([top.astype(BF16), jnp.zeros((128 - 16, r), BF16)], axis=0)


def pick_rows(rows, r):
    index = lax.broadcasted_iota(jnp.int32, (16, r), 0)
    out = jnp.zeros((16, r), F32)
    for i, row in enumerate(rows):
        out = jnp.where(index == i, jnp.broadcast_to(row, (16, r)), out)
    return out


def split3(x):
    hi = x.astype(BF16).astype(F32)
    mid = (x - hi).astype(BF16).astype(F32)
    return hi, mid, x - hi - mid


def padded(head_rows, half, aug, r):
    zero = jnp.zeros((HD, r), BF16)
    pair = [head_rows, zero] if half == 0 else [zero, head_rows]
    return jnp.concatenate(pair + [aug], axis=0)


def attention_kernel(qt, k, vt, ka, ma, mixed_t, lse, s, m, l, acc):
    z = lax.axis_index("tp")
    own = qt.shape[1]
    for part, (row0, n, start) in enumerate(parts_of(z, own)):
        cols = pl.ds(pl.multiple_of(row0, 128), n)
        aug = aug_rows(pick_rows((ma[0:1, cols], ma[1:2, cols]), n), n)

        def one_pair(pair, carry):
            attend_pair(z, part, start, pair, cols, n, aug, qt, k, vt, ka, mixed_t, lse, s, m, l, acc)
            return carry

        lax.fori_loop(0, k.shape[1] // 128, one_pair, 0)


def attention(qt, k, vt, ka, ma):
    width, own = qt.shape
    total = k.shape[0]
    widest = max(SHORT - own, own - (SHORT - own))
    vm = pltpu.VMEM
    return pl.pallas_call(
        attention_kernel,
        out_shape=(
            jax.ShapeDtypeStruct((width, own), F32),
            jax.ShapeDtypeStruct((width // 128, 8, own), F32),
        ),
        in_specs=[pl.BlockSpec(memory_space=pltpu.VMEM)] * 5,
        out_specs=(pl.BlockSpec(memory_space=pltpu.VMEM),) * 2,
        scratch_shapes=[
            vm((2, total, widest), F32),
            vm((2, 1, widest), F32),
            vm((2, 1, widest), F32),
            vm((2, HD, widest), F32),
        ],
        compiler_params=pltpu.CompilerParams(vmem_limit_bytes=VMEM_MAX),
        name="attention",
    )(qt, k, vt, ka, ma)


def back_pair(z, pair, pause, qt, q, k, kt, v, ka, ma, mixed_t, lse, dmt, dm, dqt, dk, dv, dka, dva, dqa):
    own, total = qt.shape[1], k.shape[0]
    lanes = pl.ds(pl.multiple_of(pair * 128, 128), 128)
    dka[...] = jnp.zeros_like(dka)
    dva[...] = jnp.zeros_like(dva)
    for part, (row0, r, start) in enumerate(parts_of(z, own)):
        pause(part)
        cols = pl.ds(pl.multiple_of(row0, 128), r)
        qs, gs, qm, gm = [], [], [], []
        low = lax.broadcasted_iota(jnp.int32, (r, 128), 1) < HD
        for half in range(2):
            rows = pl.ds(pl.multiple_of(pair * 128 + half * HD, HD), HD)
            delta = jnp.sum(dmt[rows, cols].astype(F32) * mixed_t[rows, cols], axis=0, keepdims=True)
            total_log = lse[pair, half : half + 1, cols]
            q_aug = pick_rows((ma[0:1, cols], ma[1:2, cols]) + split3(-total_log), r)
            zero = jnp.zeros((1, r), F32)
            g_aug = pick_rows((zero, zero) + split3(-delta), r)
            qs.append(padded(qt[rows, cols], half, aug_rows(q_aug, r), r))
            gs.append(padded(dmt[rows, cols], half, aug_rows(g_aug, r), r))
            mine = low if half == 0 else jnp.logical_not(low)
            here = pl.ds(pl.multiple_of(row0, 128), r)
            qm.append(jnp.where(mine, q[here, lanes], jnp.zeros((), BF16)))
            gm.append(jnp.where(mine, dm[here, lanes], jnp.zeros((), BF16)))
            dqa[half, :, :r] = jnp.zeros((HD, r), F32)

        def step(key0):
            keys = pl.ds(key0, KEYS)
            k_left = jnp.concatenate([k[keys, lanes], ka[keys, :]], axis=1)
            v_left = jnp.concatenate([v[keys, lanes], ka[keys, :]], axis=1)
            for half in range(2):
                share = jnp.exp(dot(k_left, qs[half]))
                slope = (share * dot(v_left, gs[half])).astype(BF16)
                dva[keys, :] += dot(share.astype(BF16), gm[half])
                dka[keys, :] += dot(slope, qm[half])
                rows = pl.ds(pl.multiple_of(pair * 128 + half * HD, HD), HD)
                dqa[half, :, :r] += dot(kt[rows, keys], slope)

        over_keys(z, part, start, total, step)
        for half in range(2):
            rows = pl.ds(pl.multiple_of(pair * 128 + half * HD, HD), HD)
            dqt[rows, cols] = (dqa[half, :, :r] * HD ** (-0.5)).astype(BF16)
    dk[:, lanes] = dka[...].astype(BF16)
    dv[:, lanes] = dva[...].astype(BF16)


def attention_back_kernel(*refs):
    z = lax.axis_index("tp")

    def one_pair(pair, carry):
        back_pair(z, pair, lambda part: None, *refs)
        return carry

    lax.fori_loop(0, refs[2].shape[1] // 128, one_pair, 0)


def back_sums_kernel(qt, q, k, kt, v, ka, ma, mixed_t, lse, dmt, dm, *refs):
    g = (refs[0:4], refs[4:8])
    dqt, dk, dv, out_u, out_d, dka, dva, dqa, gk, *bufs = refs[8:]
    bufs, (gk_sem, *sems) = bufs[:8], bufs[8:]
    z, d, core, first, second = position()
    greet(z, d)

    def fetch(p, t):
        return pltpu.make_async_copy(g[p][t].at[:, core], gk.at[p, t], gk_sem.at[p, t])

    sums = Sums(
        z, d, core, second, first,
        lambda p, t: g[p][t].at[:, 1 - core],
        lambda p, t, at: up(gk.at[p, t, at]),
        lambda p, t: fetch(p, t).wait(),
        bufs, sems,
    )
    for p in range(2):
        for t in range(4):
            sums.one(p, t).start()
            fetch(p, t).start()

    def each(act, *units):
        def run():
            for p, t in units:
                act(p, t)

        return run

    def kept_and_four(p):
        def run():
            for t in range(4):
                sums.at_kept(p, t)
                sums.at_four(p, t, 0)

        return run

    def four(p, step):
        return each(lambda p, t: sums.at_four(p, t, step), *[(p, t) for t in range(4)])

    packs = [[(p, t) for t in range(4)] for p in range(2)]
    between = {
        (0, 1): each(sums.at_two, *packs[0]),
        (1, 0): each(sums.at_two, *packs[1]),
        (2, 1): each(sums.at_three, *packs[0][:2]),
        (3, 0): each(sums.at_three, *packs[0][2:]),
        (4, 1): kept_and_four(0),
        (5, 0): lambda: (each(sums.at_three, *packs[1][:2])(), four(0, 1)()),
        (5, 1): lambda: (each(sums.at_three, *packs[1][2:])(), four(0, 2)()),
    }

    def one_pair(pair, carry):
        def pause(part):
            for (i, at), run in between.items():
                if at == part:

                    @pl.when(pair == i)
                    def _():
                        run()

        back_pair(z, pair, pause, qt, q, k, kt, v, ka, ma, mixed_t, lse, dmt, dm, dqt, dk, dv, dka, dva, dqa)
        return carry

    lax.fori_loop(0, k.shape[1] // 128, one_pair, 0)
    kept_and_four(1)()
    for step in (1, 2):
        four(1, step)()
    sums.result(0, out_u)
    sums.result(1, out_d)
    for p in range(2):
        sums.drain(p)


def back_shapes(own, total, width):
    widest = max(SHORT - own, own - (SHORT - own))
    vm = pltpu.VMEM
    outs = (
        jax.ShapeDtypeStruct((width, own), BF16),
        jax.ShapeDtypeStruct((total, width), BF16),
        jax.ShapeDtypeStruct((total, width), BF16),
    )
    return outs, [vm((total, 128), F32), vm((total, 128), F32), vm((2, HD, widest), F32)]


def attention_back(*args):
    (width, own), total = args[0].shape, args[2].shape[0]
    outs, scratch = back_shapes(own, total, width)
    return pl.pallas_call(
        attention_back_kernel,
        out_shape=outs,
        in_specs=[pl.BlockSpec(memory_space=pltpu.VMEM)] * 11,
        out_specs=(pl.BlockSpec(memory_space=pltpu.VMEM),) * 3,
        scratch_shapes=scratch,
        compiler_params=pltpu.CompilerParams(vmem_limit_bytes=VMEM_MAX),
        name="attention_back",
    )(*args)


def back_sums(args, gu, gd):
    (width, own), total = args[0].shape, args[2].shape[0]
    outs, scratch = back_shapes(own, total, width)
    block = (width // 8, gu[0].shape[1])
    g = [a.reshape((4, 2) + block) for a in (*gu, *gd)]
    vmem = pl.BlockSpec(memory_space=pltpu.VMEM)
    return pl.pallas_call(
        back_sums_kernel,
        out_shape=outs + (jax.ShapeDtypeStruct(block, F32),) * 2,
        in_specs=[vmem] * 11 + [pl.BlockSpec(memory_space=pl.ANY)] * 8,
        out_specs=(vmem,) * 5,
        scratch_shapes=[
            *scratch,
            pltpu.VMEM((2, 4, 4) + block, BF16),
            *sum_buffers(2, block),
            pltpu.SemaphoreType.DMA((2, 4)),
            *sum_semaphores(2),
        ],
        compiler_params=pltpu.CompilerParams(
            collective_id=2, has_side_effects=True, vmem_limit_bytes=VMEM_MAX
        ),
        name="back_sums",
    )(*args, *g)


def body(
    tokens, w_query, w_key, w_value, b_query, b_value, w_out, b_out, gain_attn, shift_attn,
    w_up, b_up, w_down, b_down, gain_ffn, shift_ffn, lengths, deal_order, cotangent,
):
    own, width = tokens.shape
    n_tp, n_dp = lax.axis_size("tp"), lax.axis_size("dp")
    z, g = lax.axis_index("tp"), lax.axis_index("dp")
    total = own * n_tp
    r, hw = w_query.shape
    direct = n_tp == 4 and n_dp == 8 and r % 16 == 0

    own_w = jnp.stack([jnp.concatenate([w_query, w_key, w_value, w_out], axis=1), w_up, w_down])
    vectors = (b_query, b_value, b_out, gain_attn, shift_attn, b_down, gain_ffn, shift_ffn, b_up)
    n_small = 8 * r + b_up.shape[0]
    if direct:
        line = jnp.arange(8, dtype=jnp.int32)[:, None]
        narrow = jnp.zeros((8, r), BF16)
        for i, a in enumerate(vectors[:8]):
            narrow = jnp.where(line == i, a[None, :], narrow)
        narrow = jnp.pad(narrow, ((0, 0), (0, 128 - r)))
        own_s = jnp.concatenate([narrow, jnp.pad(b_up.reshape(-1, 128), ((0, 5), (0, 0)))])
        w, vec, bu, xt, q, qt, k, v, kt, wd, mixed_t, lse = forward_all(lengths, deal_order, own_w, own_s, tokens)
        w = w.reshape(2, n_tp, width, w_up.shape[1])
        bu = bu.reshape(-1)
        wq, wk, wv, wo = (wd[i] for i in range(4))
        bq, bv, bo, g1, h1, bd, g2, h2 = (vec[i] for i in range(8))
    else:
        w = lax.all_gather(own_w, ("tp", "dp"), axis=0).reshape((n_tp, n_dp) + own_w.shape)
        w = jnp.moveaxis(w, 2, 0).reshape(3, n_tp, width, w_up.shape[1])
        s = lax.all_gather(jnp.concatenate(vectors), "dp", axis=0)
        x = lax.all_gather(tokens, "tp", axis=0, tiled=True)
        small = [s[:, i * r : (i + 1) * r].reshape(width).astype(F32) for i in range(8)]
        bq, bv, bo, g1, h1, bd, g2, h2 = small
        bu = s[:, 8 * r : n_small].reshape(-1).astype(F32)
        wq, wk, wv, wo = (
            w[0, :, :, i * hw : (i + 1) * hw].transpose(1, 0, 2).reshape(width, width) for i in range(4)
        )
        w = w[1:]
        q = (dot(tokens, wq) + bq).astype(BF16) * jnp.asarray(HD ** (-0.5), BF16)
        k = dot(x, wk).astype(BF16)
        v = (dot(x, wv) + bv).astype(BF16)
        qt, kt = q.T, k.T

    pair = lax.dynamic_slice_in_dim(deal_order, 2 * g, 1)
    first_len = jnp.sum(jnp.where(jnp.arange(lengths.shape[0], dtype=jnp.int32) == pair[0], lengths, 0))
    key_seg = jnp.arange(total, dtype=jnp.int32)[:, None] >= first_len
    lane = jnp.arange(128, dtype=jnp.int32)[None, :]
    ka = jnp.where(lane == 0, ~key_seg, jnp.where(lane == 1, key_seg, (lane >= 2) & (lane < 5))).astype(BF16)
    row_seg = (z * own + jnp.arange(own, dtype=jnp.int32))[None, :] >= first_len
    sub = jnp.arange(8, dtype=jnp.int32)[:, None]
    ma = jnp.where(((sub == 0) & row_seg) | ((sub == 1) & ~row_seg), MASKED, 0.0).astype(F32)

    if not direct:
        mixed_t, lse = attention(qt, k, v.T, ka, ma)
    mixed = mixed_t.T.astype(BF16)
    first_residual = tokens.astype(F32) + contract_last(mixed, wo) + bo
    xhat1, inv1 = normalize_layer(first_residual)
    y1 = xhat1 * g1 + h1
    y1r = y1.astype(BF16)

    u = [dot(y1r, w[0, t]) + bu.reshape(n_tp, -1)[t] for t in range(n_tp)]
    hr = [jax.nn.gelu(a, approximate=False).astype(BF16) for a in u]
    ffn = sum(contract_last(hr[t], w[1, t]) for t in range(n_tp))
    xhat2, inv2 = normalize_layer(y1 + ffn + bd)
    encoder_output = (xhat2 * g2 + h2).astype(BF16)

    grad = cotangent.astype(F32)
    dr2 = normalize_backward(grad, xhat2, inv2, g2)
    dfr = dr2.astype(BF16)
    du = [(dot(dfr, w[1, t]) * gelu_slope(u[t])).astype(BF16) for t in range(n_tp)]
    dy1 = dr2 + sum(contract_last(du[t], w[0, t]) for t in range(n_tp))
    dr1 = normalize_backward(dy1, xhat1, inv1, g1)
    dar = dr1.astype(BF16)
    dm = dot(dar, wo).astype(BF16)
    gu = [contract_first(y1r, du[t]) for t in range(n_tp)]
    gd = [contract_first(dfr, hr[t]) for t in range(n_tp)]
    row_sums = [
        jnp.sum(dar, axis=0, dtype=F32),
        jnp.sum(dy1 * xhat1, axis=0),
        jnp.sum(dy1, axis=0),
        jnp.sum(dfr, axis=0, dtype=F32),
        jnp.sum(grad * xhat2, axis=0),
        jnp.sum(grad, axis=0),
    ]
    wide_sum = jnp.concatenate([jnp.sum(a, axis=0, dtype=F32) for a in du])
    back_args = (qt, q, k, kt, v, ka, ma, mixed_t, lse, dm.T, dm)
    if direct:
        gu, gd = [a.astype(BF16) for a in gu], [a.astype(BF16) for a in gd]
        dqt, dk, dv, g_up, g_down = back_sums(back_args, gu, gd)
        vecs = jnp.stack([jnp.zeros((width,), F32)] * 2 + row_sums)
        a, gs, grad_tokens = finish(dqt, dk, dv, xt, dar, mixed_t, wd, dr1, vecs, wide_sum.reshape(1, -1))
        gs = [gs[i, :r] for i in range(8)] + [gs[8:11].reshape(-1)]
    else:
        dqt, dk, dv = attention_back(*back_args)
        dq = dqt.T
        base = dr1 + contract_last(dq, wq)
        far = contract_last(dk, wk) + contract_last(dv, wv)
        base = base + lax.dynamic_slice_in_dim(far, z * own, own)
        dt = far.astype(BF16)
        gq, gk, gv = contract_first(tokens, dq), contract_first(x, dk), contract_first(x, dv)
        go = contract_first(dar, mixed)
        ga = jnp.stack(
            [
                jnp.concatenate([m[:, t * hw : (t + 1) * hw] for m in (gq, gk, gv, go)], axis=1)
                for t in range(n_tp)
            ]
        )
        sums = [jnp.sum(dq, axis=0, dtype=F32), jnp.sum(dv, axis=0, dtype=F32)] + row_sums
        sums = [a.reshape(n_dp, r) for a in sums]
        sv = jnp.concatenate(sums + [wide_sum.reshape(n_dp, -1)], axis=1)
        grads = jnp.stack([ga, jnp.stack(gu), jnp.stack(gd)], axis=1).reshape(n_tp, 3, n_dp, r, -1)
        grads = jnp.moveaxis(grads, 1, 2).reshape(n_tp * n_dp, 3, r, -1)
        gw = lax.psum_scatter(grads, ("tp", "dp"), scatter_dimension=0, tiled=True)[0]
        gs = lax.psum_scatter(lax.psum(sv, "tp"), "dp", scatter_dimension=0, tiled=True)[0]
        others = jnp.where(jnp.arange(total)[:, None] // own == z, jnp.zeros((), BF16), dt)
        grad_tokens = base + lax.psum_scatter(others, "tp", scatter_dimension=0, tiled=True).astype(F32)
        gs = [gs[i * r : (i + 1) * r] for i in range(8)] + [gs[8 * r : n_small]]
        a, g_up, g_down = gw[0], gw[1], gw[2]
    return (
        encoder_output, grad_tokens,
        a[:, :hw], a[:, hw : 2 * hw], a[:, 2 * hw : 3 * hw], gs[0], gs[1],
        a[:, 3 * hw :], gs[2], gs[3], gs[4],
        g_up, gs[8], g_down, gs[5], gs[6], gs[7],
    )


def solution(mesh):
    rows, block, vector = P(("dp", "tp"), None), P("dp", "tp"), P("dp")
    in_specs = (
        rows, block, block, block, vector, vector, block, vector, vector, vector,
        block, vector, block, vector, vector, vector, P(), P(), rows,
    )
    out_specs = (
        rows, rows, block, block, block, vector, vector, block, vector, vector, vector,
        block, vector, block, vector, vector, vector,
    )
    return jax.shard_map(body, mesh=mesh, in_specs=in_specs, out_specs=out_specs, check_vma=False)
```

```python
import functools

import jax
import jax.numpy as jnp
from jax import lax
from jax.experimental import pallas as pl
from jax.experimental.pallas import tpu as pltpu
from jax.sharding import PartitionSpec as P

HD = 64
SHORT = 1024
EPS = 1e-05
SQRT_HALF = 0.7071067811865476
INV_ROOT_TAU = 0.3989422804014327
MASKED = -1e30
KEYS = 512
ROWS = 128
VMEM_MAX = 67043328
MESH = pl.DeviceIdType.MESH
F32 = jnp.float32
BF16 = jnp.bfloat16


def dot(left, right):
    return jnp.dot(left, right, preferred_element_type=F32)


def contract_last(left, right):
    return lax.dot_general(left, right, (((1,), (1,)), ((), ())), preferred_element_type=F32)


def contract_first(left, right):
    return lax.dot_general(left, right, (((0,), (0,)), ((), ())), preferred_element_type=F32)


def normalize_layer(resid):
    center = resid - jnp.mean(resid, axis=-1, keepdims=True)
    inverse_deviation = lax.rsqrt(jnp.mean(center * center, axis=-1, keepdims=True) + EPS)
    return (center * inverse_deviation, inverse_deviation)


def normalize_backward(output_gradient, xhat, inverse_deviation, gain):
    scaled_rows = output_gradient * gain
    return inverse_deviation * (
        scaled_rows
        - jnp.mean(scaled_rows, axis=-1, keepdims=True)
        - xhat * jnp.mean(scaled_rows * xhat, axis=-1, keepdims=True)
    )


def gelu_slope(pre_act):
    return (
        0.5 * (1.0 + lax.erf(pre_act * SQRT_HALF))
        + pre_act * jnp.exp(-0.5 * pre_act * pre_act) * INV_ROOT_TAU
    )


def position():
    z = lax.axis_index("tp")
    d = lax.axis_index("dp")
    core = lax.rem(d, 2)
    first = 2 + 2 * core
    second = 4 - 2 * core
    return z, d, core, first, second


def xor(d, mask):
    return d + mask * (1 - 2 * lax.rem(d // mask, 2))


def greet(z, d):
    barrier = pltpu.get_barrier_semaphore()
    for mask in (1, 2, 4):
        pl.semaphore_signal(barrier, inc=1, device_id=(xor(d, mask), z), device_id_type=MESH)
    for j in range(1, 4):
        pl.semaphore_signal(barrier, inc=1, device_id=(d, lax.rem(z + j, 4)), device_id_type=MESH)
    pl.semaphore_wait(barrier, 6)


def by_distance(z):
    low = z <= 1
    near = jnp.where(z == 0, 1, jnp.where(z == 3, 2, z - 1))
    mid = jnp.where(z == 0, 2, jnp.where(z == 3, 1, z + 1))
    far = jnp.where(low, 3, 0)
    return (z, near, mid, far)


def put(src, dst, send, recv, dp, tp):
    return pltpu.make_async_remote_copy(
        src_ref=src, dst_ref=dst, send_sem=send, recv_sem=recv, device_id=(dp, tp), device_id_type=MESH
    )


def forward_kernel(
    lengths, deal, own_w, own_s, own_t,
    w, vec, bu, xt_out, q_out, qt_out, k_out, v_out, kt_out, wd_out, ka_out, mixed_t, lse, ma,
    wa, s, x, xt, q, qt, k, v, kt, vt, wd, ka, sc, m, l, acc,
    wz_s, wz_r, wa_s, wa_r, wb_s, wb_r, wc_s, wc_r, tk_s, tk_r, sm_s, sm_r, lo_sem, arr_sem, out_sem,
):
    z, d, core, first, second = position()
    packs = own_w.shape[0]
    own, width = own_t.shape
    total = 4 * own
    hw = width // 4
    chunks = own // ROWS
    d1, d2 = xor(d, first), xor(d, second)
    d12 = xor(d1, second)
    pal = xor(d, 1)
    pd, pd1, pd2, pd12 = (xor(e, 1) for e in (d, d1, d2, d12))
    order = by_distance(z)
    first_len = lengths[deal[2 * d]]

    greet(z, d)

    def block(p, tt, e):
        return wa.at[tt, e] if p == 0 else w.at[p - 1, tt, e]

    def along_z(p, tt, src, act):
        dst = block(p, tt, d)
        right = put(src, dst, wz_s.at[0, p, tt], wz_r.at[p, tt], d, jnp.minimum(z + 1, 3))
        left = put(src, dst, wz_s.at[1, p, tt], wz_r.at[p, tt], d, jnp.maximum(z - 1, 0))

        @pl.when((tt <= z) & (z < 3))
        def _():
            act(right)

        @pl.when((tt >= z) & (z > 0))
        def _():
            act(left)

    def across(p, tt, src):
        dst = block(p, tt, d)
        return (
            put(src, dst, wa_s.at[p, tt], wa_r.at[p, tt], d1, z),
            put(src, dst, wb_s.at[p, tt, 0], wb_r.at[p, tt, 0], d2, z),
            put(src, dst, wc_s.at[p, tt, 0], wc_r.at[p, tt, 0], pal, z),
        )

    def after_first(p, tt):
        src = block(p, tt, d1)
        return (
            put(src, src, wb_s.at[p, tt, 1], wb_r.at[p, tt, 1], d2, z),
            put(src, src, wc_s.at[p, tt, 1], wc_r.at[p, tt, 1], pal, z),
        )

    def after_second(p, tt, i):
        src = block(p, tt, d2 if i == 0 else d12)
        return put(src, src, wc_s.at[p, tt, 2 + i], wc_r.at[p, tt, 2 + i], pal, z)

    def source(p, j):
        return own_w.at[p] if j == 0 else block(p, order[j], d)

    def arrive(ref, sem):
        put(ref, ref, arr_sem, sem, pal, z).wait_recv()

    def begin_z(p, j):
        if j > 0:
            arrive(block(p, order[j], d), wz_r.at[p, order[j]])
        along_z(p, order[j], source(p, j), lambda c: c.start())

    def begin_xy(p, j):
        for copy in across(p, order[j], source(p, j)):
            copy.start()

    def begin(p, j):
        begin_z(p, j)
        begin_xy(p, j)

    def relay_first(p, j):
        tt = order[j]
        arrive(block(p, tt, d1), wa_r.at[p, tt])
        for copy in after_first(p, tt):
            copy.start()

    def relay_second(p, j):
        tt = order[j]
        for i in range(2):
            arrive(block(p, tt, d2 if i == 0 else d12), wb_r.at[p, tt, i])
            after_second(p, tt, i).start()

    def from_pal(p):
        for tt in range(4):
            for i, e in enumerate((pd, pd2, pd1, pd12)):
                arrive(block(p, tt, e), wc_r.at[p, tt, i])

    def sent(p):
        for j in range(4):
            tt = order[j]
            along_z(p, tt, source(p, j), lambda c: c.wait_send())
            for copy in across(p, tt, source(p, j)) + after_first(p, tt):
                copy.wait_send()
            for i in range(2):
                after_second(p, tt, i).wait_send()

    def token_slice(o, i):
        return x.at[pl.ds(pl.multiple_of((o * chunks + i) * ROWS, ROWS), ROWS)]

    def token_hop(o, i, hop, step):
        src = own_t.at[pl.ds(i * ROWS, ROWS)] if hop == 0 else token_slice(o, i)
        way = 0 if step > 0 else 1
        return put(src, token_slice(o, i), tk_s.at[way, hop, i], tk_r.at[way, hop, i], d, jnp.clip(z + step, 0, 3))

    last = SHORT // ROWS

    def wanted(o, i, target, step):
        n = o * chunks + i
        if step > 0:
            return (target <= 2) | (n >= last)
        return (target >= 1) | (n < 4 * chunks - last)

    def chunk_ids(step):
        return list(range(chunks))[:: -step]

    def tokens(hop, step, act, which=slice(None)):
        o, target = z - step * hop, z + step
        valid = (o >= 0) & (o <= 3) & (target >= 0) & (target <= 3)
        for i in chunk_ids(step)[which]:

            @pl.when(valid & wanted(o, i, target, step))
            def _():
                act(token_hop(o, i, hop, step))

    def tokens_on(hop, step, onward):
        o, target = z - step * (hop + 1), z + step
        valid = (o >= 0) & (o <= 3) & (z - step >= 0) & (z - step <= 3)
        way = 0 if step > 0 else 1
        for i in chunk_ids(step):

            @pl.when(valid & wanted(o, i, z, step))
            def _():
                arrive(token_slice(jnp.clip(o, 0, 3), i), tk_r.at[way, hop, i])

            if onward:

                @pl.when(valid & (target >= 0) & (target <= 3) & wanted(o, i, target, step))
                def _():
                    token_hop(o, i, hop + 1, step).start()

    def small(stage):
        if stage == 0:
            return [
                put(own_s, s.at[d], sm_s.at[0], sm_r.at[0], d1, z),
                put(own_s, s.at[d], sm_s.at[1], sm_r.at[1], d2, z),
                put(own_s, s.at[d], sm_s.at[3], sm_r.at[3], pal, z),
            ]
        if stage == 1:
            return [
                put(s.at[d1], s.at[d1], sm_s.at[2], sm_r.at[2], d2, z),
                put(s.at[d1], s.at[d1], sm_s.at[4], sm_r.at[4], pal, z),
            ]
        return [
            put(s.at[d2], s.at[d2], sm_s.at[5], sm_r.at[5], pal, z),
            put(s.at[d12], s.at[d12], sm_s.at[6], sm_r.at[6], pal, z),
        ]

    def own_tokens(*which):
        for step in (1, -1):
            tokens(0, step, lambda c: c.start(), slice(*which))

    begin(0, 0)
    for copy in small(0):
        copy.start()
    own_tokens(0, 1)
    s[d] = own_s[...]
    wa[z, d] = own_w[0]
    mine = pl.ds(pl.multiple_of(z * own, ROWS), own)
    x[mine, :] = own_t[...]
    keep = pltpu.make_async_copy(own_w.at[pl.ds(1, packs - 1)], w.at[:, z, d], lo_sem)
    keep.start()

    @pl.when(z == 0)
    def _():
        x[total - SHORT :, :] = jnp.zeros((SHORT, width), BF16)
        xt[:, total - SHORT :] = jnp.zeros((width, SHORT), BF16)

    @pl.when(z == 3)
    def _():
        x[:SHORT, :] = jnp.zeros((SHORT, width), BF16)
        xt[:, :SHORT] = jnp.zeros((width, SHORT), BF16)

    begin(0, 1)
    relay_first(0, 0)
    own_tokens(1, 2)
    begin(0, 2)
    relay_second(0, 0)
    relay_first(0, 1)
    for p in range(1, packs):
        begin_z(p, 0)
    begin(0, 3)
    own_tokens(2, chunks)
    relay_second(0, 1)
    relay_first(0, 2)
    begin_xy(1, 0)
    arrive(s.at[d1], sm_r.at[0])
    for copy in small(1):
        copy.start()
    relay_second(0, 2)
    relay_first(0, 3)
    for p in range(2, packs):
        begin_xy(p, 0)
    arrive(s.at[d2], sm_r.at[1])
    arrive(s.at[d12], sm_r.at[2])
    for copy in small(2):
        copy.start()
    for p in range(1, packs):
        begin(p, 1)
    lane = lax.broadcasted_iota(jnp.int32, (own, 128), 1)
    for i in range(4):
        late = lax.broadcasted_iota(jnp.int32, (own, 128), 0) + i * own >= first_len
        ones = jnp.where((lane >= 2) & (lane < 5), 1.0, 0.0)
        flags = jnp.where(lane == 0, jnp.where(late, 0.0, 1.0), jnp.where(lane == 1, jnp.where(late, 1.0, 0.0), ones))
        ka[pl.ds(i * own, own), :] = flags.astype(BF16)

    relay_second(0, 3)
    for i, e in enumerate((pd, pd2, pd1, pd12)):
        arrive(s.at[e], sm_r.at[3 + i])
    r = width // 8
    for e in range(8):
        piece = s[e].astype(F32)
        vec[0:8, e * r : (e + 1) * r] = piece[0:8, 0:r]
        for j in range(hw * 2 // 128):
            col = e * hw * 2 + j * 128
            bu[0:1, col : col + 128] = piece[8 + j : 9 + j, :]
    from_pal(0)
    for tt in range(4):
        rows = wa[tt].reshape(width, width)
        for i in range(4):
            wd[i, :, tt * hw : (tt + 1) * hw] = rows[:, i * hw : (i + 1) * hw]
    wd_copy = pltpu.make_async_copy(wd, wd_out, out_sem.at[0])
    wd_copy.start()

    tile = 256

    def q_tile(n, carry):
        lanes = pl.ds(pl.multiple_of(n * tile, tile), tile)
        rows = (dot(own_t[...], wd[0, :, lanes]) + vec[0:1, lanes]).astype(BF16) * jnp.asarray(HD ** (-0.5), BF16)
        q[:, lanes] = rows
        qt[lanes, :] = rows.T
        return carry

    def project(o):
        rows = pl.ds(pl.multiple_of(o * own, ROWS), own)

        def kv_tile(n, carry):
            lanes = pl.ds(pl.multiple_of(n * tile, tile), tile)
            keys = dot(x[rows, :], wd[1, :, lanes]).astype(BF16)
            k[rows, lanes] = keys
            kt[lanes, rows] = keys.T
            values = (dot(x[rows, :], wd[2, :, lanes]) + vec[1:2, lanes]).astype(BF16)
            v[rows, lanes] = values
            vt[lanes, rows] = values.T
            xt[lanes, rows] = x[rows, lanes].T
            return carry

        lax.fori_loop(0, width // tile, kv_tile, 0)

    def project_far():
        for step in (1, -1):
            tokens_on(1, step, False)
        project(jnp.where(z == 0, 2, jnp.where(z == 1, 3, z - 2)))

    middle = (z == 1) | (z == 2)
    lax.fori_loop(0, width // tile, q_tile, 0)
    project(z)
    for p in range(1, packs):
        relay_first(p, 0)
    for step in (1, -1):
        tokens_on(0, step, True)

    @pl.when(z > 0)
    def _():
        project(jnp.maximum(z - 1, 0))

    for p in range(1, packs):
        begin(p, 2)
    for p in range(1, packs):
        relay_second(p, 0)
        relay_first(p, 1)

    @pl.when(z < 3)
    def _():
        project(jnp.minimum(z + 1, 3))

    @pl.when(jnp.logical_not(middle))
    def _():
        project_far()

    for p in range(1, packs):
        begin(p, 3)

    def both(act, j):
        def run():
            for p in range(1, packs):
                act(p, j)

        return run

    between = {
        (0, 1): both(relay_second, 1),
        (0, 2): both(relay_first, 2),
        (0, 5): both(relay_second, 2),
        (1, 0): both(relay_first, 3),
        (1, 4): both(relay_second, 3),
    }
    late = lax.broadcasted_iota(jnp.int32, (8, own), 1) + z * own >= first_len
    sub = lax.broadcasted_iota(jnp.int32, (8, own), 0)
    away = jnp.where(sub == 0, jnp.where(late, MASKED, 0.0), jnp.where(sub == 1, jnp.where(late, 0.0, MASKED), 0.0))
    ma[...] = away
    outs = [
        pltpu.make_async_copy(a, b, out_sem.at[1 + i])
        for i, (a, b) in enumerate(
            ((xt, xt_out), (q, q_out), (qt, qt_out), (k, k_out), (v, v_out), (kt, kt_out), (ka, ka_out))
        )
    ]
    pairs = width // 128
    for part, (row0, n, start) in enumerate(parts_of(z, own)):
        if part == 1:

            @pl.when(middle)
            def _():
                project_far()

            for copy in outs:
                copy.start()
        cols = pl.ds(pl.multiple_of(row0, 128), n)
        late = lax.broadcasted_iota(jnp.int32, (1, n), 1) + (z * own + row0) >= first_len
        masks = (jnp.where(late, MASKED, 0.0), jnp.where(late, 0.0, MASKED))
        aug = aug_rows(pick_rows(masks, n), n)

        def one_pair(pair, carry):
            for (at, i), run in between.items():
                if at == part:

                    @pl.when(pair == i)
                    def _():
                        run()

            attend_pair(z, part, start, pair, cols, n, aug, qt, k, vt, ka, mixed_t, lse, sc, m, l, acc)
            return carry

        lax.fori_loop(0, pairs, one_pair, 0)

    for p in range(1, packs):
        from_pal(p)
    for stage in range(3):
        for copy in small(stage):
            copy.wait_send()
    for hop in range(2):
        for step in (1, -1):
            tokens(hop, step, lambda c: c.wait_send())
    for p in range(packs):
        sent(p)
    keep.wait()
    wd_copy.wait()
    for copy in outs:
        copy.wait()


def attend_pair(z, part, start, pair, cols, n, aug, qt, k, vt, ka, mixed_t, lse, s, m, l, acc):
    total = k.shape[0]
    lanes = pl.ds(pl.multiple_of(pair * 128, 128), 128)
    for half in range(2):
        m[half, :, :n] = jnp.full((1, n), MASKED, F32)
        l[half, :, :n] = jnp.zeros((1, n), F32)
        acc[half, :, :n] = jnp.zeros((HD, n), F32)
    qs = [padded(qt[pl.ds(pl.multiple_of(pair * 128 + half * HD, HD), HD), cols], half, aug, n) for half in range(2)]

    def scores(key0):
        keys = pl.ds(key0, KEYS)
        left = jnp.concatenate([k[keys, lanes], ka[keys, :]], axis=1)
        for half in range(2):
            score = dot(left, qs[half])
            s[half, keys, :n] = score
            m[half, :, :n] = jnp.maximum(m[half, :, :n], jnp.max(score, axis=0, keepdims=True))

    over_keys(z, part, start, total, scores)
    tops = [m[half, :, :n] for half in range(2)]

    def mix(key0):
        keys = pl.ds(key0, KEYS)
        for half in range(2):
            raised = jnp.exp(s[half, keys, :n] - tops[half])
            l[half, :, :n] += jnp.sum(raised, axis=0, keepdims=True)
            values = vt[pl.ds(pl.multiple_of(pair * 128 + half * HD, HD), HD), keys]
            acc[half, :, :n] += dot(values, raised.astype(BF16))

    over_keys(z, part, start, total, mix)
    for half in range(2):
        sums = l[half, :, :n]
        rows = pl.ds(pl.multiple_of(pair * 128 + half * HD, HD), HD)
        mixed_t[rows, cols] = acc[half, :, :n] / sums
        lse[pair, half : half + 1, cols] = tops[half] + jnp.log(sums)


def forward_all(lengths, deal, own_w, own_s, own_t):
    packs, r, c = own_w.shape
    own, width = own_t.shape
    total = 4 * own
    chunks = own // ROWS
    widest = max(SHORT - own, own - (SHORT - own))
    dma, vm = pltpu.SemaphoreType.DMA, pltpu.VMEM
    any_ = pl.BlockSpec(memory_space=pl.ANY)
    vmem = pl.BlockSpec(memory_space=pltpu.VMEM)
    smem = pl.BlockSpec(memory_space=pltpu.SMEM)
    shape = jax.ShapeDtypeStruct
    return pl.pallas_call(
        forward_kernel,
        out_shape=(
            shape((packs - 1, 4, 8, r, c), BF16),
            shape((8, width), F32),
            shape((1, 4 * c), F32),
            shape((width, total), BF16),
            shape((own, width), BF16),
            shape((width, own), BF16),
            shape((total, width), BF16),
            shape((total, width), BF16),
            shape((width, total), BF16),
            shape((4, width, width), BF16),
            shape((total, 128), BF16),
            shape((width, own), F32),
            shape((width // 128, 8, own), F32),
            shape((8, own), F32),
        ),
        in_specs=[smem, smem, vmem, vmem, vmem],
        out_specs=(any_, vmem, vmem) + (any_,) * 8 + (vmem, vmem, vmem),
        scratch_shapes=[
            vm((4, 8, r, c), BF16),
            vm((8, 16, 128), BF16),
            vm((total, width), BF16),
            vm((width, total), BF16),
            vm((own, width), BF16),
            vm((width, own), BF16),
            vm((total, width), BF16),
            vm((total, width), BF16),
            vm((width, total), BF16),
            vm((width, total), BF16),
            vm((4, width, width), BF16),
            vm((total, 128), BF16),
            vm((2, total, widest), F32),
            vm((2, 1, widest), F32),
            vm((2, 1, widest), F32),
            vm((2, HD, widest), F32),
            dma((2, packs, 4)),
            dma((packs, 4)),
            dma((packs, 4)),
            dma((packs, 4)),
            dma((packs, 4, 2)),
            dma((packs, 4, 2)),
            dma((packs, 4, 4)),
            dma((packs, 4, 4)),
            dma((2, 2, chunks)),
            dma((2, 2, chunks)),
            dma((7,)),
            dma((7,)),
            dma(()),
            dma(()),
            dma((8,)),
        ],
        compiler_params=pltpu.CompilerParams(
            collective_id=0, has_side_effects=True, vmem_limit_bytes=VMEM_MAX
        ),
        name="forward_all",
    )(lengths, deal, own_w, own_s, own_t)


def up(ref):
    return ref[...].astype(F32)


class Sums:
    def __init__(self, z, d, core, e_mask, f_mask, give, mine, ready, bufs, sems):
        self.z, self.d, self.give, self.mine, self.ready = z, d, give, mine, ready
        self.r1, self.b2, self.r2, self.b3, self.r3, self.s3, self.b4, self.r4 = bufs
        self.sems = sems
        self.xy = d // 2
        self.e, self.f = xor(d, e_mask) // 2, xor(d, f_mask) // 2
        self.ef = xor(xor(d, e_mask), f_mask) // 2
        self.d_e, self.d_f, self.pal = xor(d, e_mask), xor(d, f_mask), xor(d, 1)

    def one(self, p, t):
        return put(self.give(p, t), self.r1.at[p, t], self.sems[0].at[p, t], self.sems[1].at[p, t], self.pal, self.z)

    def two(self, p, t):
        return put(self.b2.at[p, t], self.r2.at[p, t], self.sems[2].at[p, t], self.sems[3].at[p, t], self.d_e, self.z)

    def three(self, p, t):
        return put(self.b3.at[p, t], self.r3.at[p, t], self.sems[4].at[p, t], self.sems[5].at[p, t], self.d_f, self.z)

    def four(self, p, t, way):
        to = jnp.minimum(self.z + 1, 3) if way == 0 else jnp.maximum(self.z - 1, 0)
        return put(
            self.b4.at[p, way, t], self.r4.at[p, way, t],
            self.sems[6].at[p, way, t], self.sems[7].at[p, way, t], self.d, to,
        )

    def at_two(self, p, t):
        self.ready(p, t)
        self.one(p, t).wait_recv()
        for i, x in enumerate((self.e, self.ef)):
            self.b2[p, t, i] = (self.mine(p, t, x) + up(self.r1.at[p, t, x])).astype(BF16)
        self.two(p, t).start()

    def at_three(self, p, t):
        self.two(p, t).wait_recv()
        f = self.f
        self.b3[p, t] = (self.mine(p, t, f) + up(self.r1.at[p, t, f]) + up(self.r2.at[p, t, 1])).astype(BF16)
        self.three(p, t).start()

    def at_kept(self, p, t):
        self.three(p, t).wait_recv()
        xy = self.xy
        self.s3[p, t] = self.mine(p, t, xy) + up(self.r1.at[p, t, xy]) + up(self.r2.at[p, t, 0]) + up(self.r3.at[p, t])

    def at_four(self, p, t, step):
        for way in range(2):
            pos = step if way == 0 else 3 - step
            if not (t > pos if way == 0 else t < pos):
                continue

            @pl.when(self.z == pos)
            def _():
                if step == 0:
                    self.b4[p, way, t] = self.s3[p, t].astype(BF16)
                else:
                    self.four(p, t, way).wait_recv()
                    self.b4[p, way, t] = (self.s3[p, t] + up(self.r4.at[p, way, t])).astype(BF16)
                self.four(p, t, way).start()

    def result(self, p, out):
        z = self.z
        out[...] = self.s3[p, z]

        @pl.when(z > 0)
        def _():
            self.four(p, z, 0).wait_recv()
            out[...] += up(self.r4.at[p, 0, z])

        @pl.when(z < 3)
        def _():
            self.four(p, z, 1).wait_recv()
            out[...] += up(self.r4.at[p, 1, z])

    def drain(self, p):
        for t in range(4):
            self.one(p, t).wait_send()
            self.two(p, t).wait_send()
            self.three(p, t).wait_send()
            for way in range(2):

                @pl.when((t > self.z) if way == 0 else (t < self.z))
                def _():
                    self.four(p, t, way).wait_send()


def sum_buffers(packs, block):
    vm = pltpu.VMEM
    return [
        vm((packs, 4, 4) + block, BF16),
        vm((packs, 4, 2) + block, BF16),
        vm((packs, 4, 2) + block, BF16),
        vm((packs, 4) + block, BF16),
        vm((packs, 4) + block, BF16),
        vm((packs, 4) + block, F32),
        vm((packs, 2, 4) + block, BF16),
        vm((packs, 2, 4) + block, BF16),
    ]


def sum_semaphores(packs):
    dma = pltpu.SemaphoreType.DMA
    return [dma((packs, 4))] * 6 + [dma((packs, 2, 4))] * 2


def finish_kernel(
    dqt, dk, dv, xt, dar, mixed_t, wd, dr1, vecs, bup,
    out_w, out_s, out_t,
    dart, dq, mixed, gp, sv, ds, dr, sk, q1, q2, q3, c2, c3, q4,
    r1, b2, r2, b3, r3, s3, b4, r4,
    p1_s, p1_r, p2_s, p2_r, p3_s, p3_r, p4_s, p4_r, t_s, t_r, v_s, v_r,
):
    z, d, core, first, second = position()
    own, width = out_t.shape
    chunks = own // ROWS
    total = 4 * chunks
    edge = SHORT // ROWS
    hw = width // 4
    r = width // 8
    greet(z, d)

    def token(k, way):
        to = jnp.minimum(z + 1, 3) if way == 0 else jnp.maximum(z - 1, 0)
        slot = k if way == 0 else jnp.where(k // chunks == to, total + k % chunks, k)
        return put(ds.at[k], dr.at[slot], t_s.at[k], t_r.at[slot], d, to)

    def token_in(k, way):
        slot = k if way == 0 else jnp.where(k // chunks == z, total + k % chunks, k)
        return put(ds.at[k], dr.at[slot], t_s.at[k], t_r.at[slot], d, z), slot

    def sends(k, way):
        o = k // chunks
        if way == 0:
            low = jnp.where(k < total - edge, 0, 1)
            return (z >= low) & (z < o) & (o > low)
        high = jnp.where(k >= edge, 3, 2)
        return (z <= high) & (z > o) & (o < high)

    def starts(k, way):
        if way == 0:
            return z == jnp.where(k < total - edge, 0, 1)
        return z == jnp.where(k >= edge, 3, 2)

    def pick(a, b, c, e):
        return jnp.where(z == 0, a, jnp.where(z == 1, b, jnp.where(z == 2, c, e)))

    tile = 256

    def far_shard(o, mine):
        rows = pl.ds(pl.multiple_of(o * own, ROWS), own)

        def one_tile(n, carry):
            lanes = pl.ds(pl.multiple_of(n * tile, tile), tile)
            far = contract_last(dk[rows, :], wd[1, lanes, :]) + contract_last(dv[rows, :], wd[2, lanes, :])
            if mine:
                out_t[:, lanes] = dr1[:, lanes] + far
            else:
                ds[pl.ds(o * chunks, chunks), :, lanes] = far.reshape(chunks, ROWS, tile).astype(BF16)
            return carry

        lax.fori_loop(0, width // tile, one_tile, 0)

    def far_and_send(j):
        o = pick(*((2, 3, 0, 1), (1, 2, 1, 2), (3, 0, 3, 0))[j])

        @pl.when((j < 2) | (z == 1) | (z == 2))
        def _():
            far_shard(o, False)

        for i in range(chunks):
            for way in range(2):
                k = o * chunks + i

                @pl.when(sends(k, way) & starts(k, way))
                def _():
                    token(k, way).start()

    far_and_send(0)

    right_order = [k for o in (3, 2, 1) for k in range(o * chunks, (o + 1) * chunks)]
    left_order = [total - 1 - k for k in right_order]

    def forward_tokens(at):
        for k, way in [(k, 0) for k in right_order] + [(k, 1) for k in left_order]:
            pos = at if way == 0 else 3 - at
            passes = (at < k // chunks) if way == 0 else (3 - at > k // chunks)
            begins = (0 if k < total - edge else 1) if way == 0 else (3 if k >= edge else 2)
            if not passes or (begins >= pos if way == 0 else begins <= pos):
                continue

            @pl.when(z == pos)
            def _():
                got, slot = token_in(k, way)
                got.wait_recv()
                ds[k] = (ds[k].astype(F32) + dr[slot].astype(F32)).astype(BF16)
                token(k, way).start()

    def flip_own(i, carry):
        cols = pl.ds(pl.multiple_of(i * ROWS, ROWS), ROWS)
        dart[:, cols] = dar[cols, :].T
        dq[cols, :] = dqt[:, cols].T
        mixed[cols, :] = mixed_t[:, cols].T.astype(BF16)
        return carry

    lax.fori_loop(0, chunks, flip_own, 0)

    def give(p, t):
        return gp.at[t, :, 1 - core]

    def mine(p, t, at):
        return gp[t, at, core].astype(F32)

    sums = Sums(
        z, d, core, second, first, give, mine, lambda p, t: None,
        (r1, b2, r2, b3, r3, s3, b4, r4), (p1_s, p1_r, p2_s, p2_r, p3_s, p3_r, p4_s, p4_r),
    )
    here = pl.ds(pl.multiple_of(z * own, ROWS), own)
    half = width // 2

    def weights(th):
        lanes = pl.ds(th * half, half)

        def rows_of(m, carry):
            rows = pl.ds(pl.multiple_of(m * half, ROWS), half)
            parts = (
                lambda: dot(xt[rows, here], dq[:, lanes]),
                lambda: dot(xt[rows, :], dk[:, lanes]),
                lambda: dot(xt[rows, :], dv[:, lanes]),
                lambda: dot(dart[rows, :], mixed[:, lanes]),
            )
            for i, part in enumerate(parts):
                got = part().astype(BF16)
                for h in range(2):
                    block = got[:, h * hw : (h + 1) * hw].reshape(2, 2, r, hw)
                    gp[2 * th + h, pl.ds(2 * m, 2), :, :, i * hw : (i + 1) * hw] = block
            return carry

        lax.fori_loop(0, 2, rows_of, 0)
        for t in (2 * th, 2 * th + 1):
            sums.one(0, t).start()

    weights(0)
    weights(1)
    for t in (0, 1):
        sums.at_two(0, t)
    far_and_send(1)
    forward_tokens(1)
    for t in (2, 3):
        sums.at_two(0, t)
    far_and_send(2)
    forward_tokens(2)

    ones = jnp.ones((8, 4 * own), BF16)
    index = lax.broadcasted_iota(jnp.int32, (8, width), 0)
    small_rows = jnp.where(index == 0, dot(ones[:, :own], dq[...]), jnp.where(index == 1, dot(ones, dv[...]), vecs[...]))
    pad = jnp.zeros((8, 128 - r), F32)
    for i in range(8):
        sv[i // 2, i % 2, 0:8, :] = jnp.concatenate([small_rows[:, i * r : (i + 1) * r], pad], axis=1)
        wide = [bup[:, (i * 3 + j) * 128 : (i * 3 + j + 1) * 128] for j in range(3)]
        sv[i // 2, i % 2, 8:16, :] = jnp.concatenate(wide + [jnp.zeros((5, 128), F32)], axis=0)
    small = [
        put(sv.at[:, 1 - core], q1, v_s.at[0], v_r.at[0], sums.pal, z),
        put(c2, q2, v_s.at[1], v_r.at[1], sums.d_e, z),
        put(c3, q3, v_s.at[2], v_r.at[2], sums.d_f, z),
    ]
    small_z = [
        put(sk, q4.at[j - 1], v_s.at[2 + j], v_r.at[2 + j], d, lax.rem(z + j, 4)) for j in range(1, 4)
    ]
    small[0].start()
    far_shard(z, True)

    def query_tile(n, carry):
        lanes = pl.ds(pl.multiple_of(n * tile, tile), tile)
        out_t[:, lanes] += contract_last(dq[...], wd[0, lanes, :])
        return carry

    lax.fori_loop(0, width // tile, query_tile, 0)
    small[0].wait_recv()
    for i, at in enumerate((sums.e, sums.ef)):
        c2[i] = sv[at, core] + q1[at]
    small[1].start()
    for t in range(4):
        sums.at_three(0, t)
    small[1].wait_recv()
    c3[...] = sv[sums.f, core] + q1[sums.f] + q2[1]
    small[2].start()
    for t in range(4):
        sums.at_kept(0, t)
    for step in range(3):
        for t in range(4):
            sums.at_four(0, t, step)
        if step == 0:
            small[2].wait_recv()
            sk[...] = sv[sums.xy, core] + q1[sums.xy] + q2[0] + q3[...]
            for copy in small_z:
                copy.start()
    for i in range(chunks):
        k = z * chunks + i
        rows = pl.ds(i * ROWS, ROWS)
        from_left = (z > 0) & ((z == 1) & (k < total - edge) | (z > 1))
        from_right = (z < 3) & ((z == 2) & (k >= edge) | (z < 2))

        @pl.when(from_left)
        def _():
            put(ds.at[k], dr.at[k], t_s.at[k], t_r.at[k], d, z).wait_recv()
            out_t[rows, :] += dr[k].astype(F32)

        @pl.when(from_right)
        def _():
            put(ds.at[k], dr.at[total + i], t_s.at[k], t_r.at[total + i], d, z).wait_recv()
            out_t[rows, :] += dr[total + i].astype(F32)

    for copy in small_z:
        copy.wait_recv()
    out_s[...] = sk[...] + q4[0] + q4[1] + q4[2]
    sums.result(0, out_w)
    for copy in small + small_z:
        copy.wait_send()
    sums.drain(0)
    for k in range(total):
        for way in range(2):

            @pl.when(sends(k, way))
            def _():
                token(k, way).wait_send()


def finish(dqt, dk, dv, xt, dar, mixed_t, wd, dr1, vecs, bup):
    own, width = dr1.shape
    r = width // 8
    chunks = own // ROWS
    dma, vm = pltpu.SemaphoreType.DMA, pltpu.VMEM
    vmem = pl.BlockSpec(memory_space=pltpu.VMEM)
    block, sb = (r, width), (16, 128)
    return pl.pallas_call(
        finish_kernel,
        out_shape=(
            jax.ShapeDtypeStruct(block, F32),
            jax.ShapeDtypeStruct(sb, F32),
            jax.ShapeDtypeStruct((own, width), F32),
        ),
        in_specs=[vmem] * 10,
        out_specs=(vmem, vmem, vmem),
        scratch_shapes=[
            vm((width, own), BF16),
            vm((own, width), BF16),
            vm((own, width), BF16),
            vm((4, 4, 2) + block, BF16),
            vm((4, 2) + sb, F32),
            vm((4 * chunks, ROWS, width), BF16),
            vm((5 * chunks, ROWS, width), BF16),
            vm(sb, F32),
            vm((4,) + sb, F32),
            vm((2,) + sb, F32),
            vm(sb, F32),
            vm((2,) + sb, F32),
            vm(sb, F32),
            vm((3,) + sb, F32),
            *sum_buffers(1, block),
            *sum_semaphores(1),
            dma((4 * chunks,)),
            dma((5 * chunks,)),
            dma((6,)),
            dma((6,)),
        ],
        compiler_params=pltpu.CompilerParams(
            collective_id=1, has_side_effects=True, vmem_limit_bytes=VMEM_MAX
        ),
        name="finish",
    )(dqt, dk, dv, xt, dar, mixed_t, wd, dr1, vecs, bup)


def parts_of(z, own):
    sure = SHORT - own
    low = z < 2
    return (
        (jnp.where(low, 0, own - sure), sure, jnp.where(low, 0, SHORT)),
        (jnp.where(low, sure, 0), own - sure, jnp.where(z == 3, SHORT, 0)),
    )


def over_keys(z, part, start, total, act):
    window = total - SHORT
    for c in range(window // KEYS):
        act(pl.multiple_of(start + c * KEYS, KEYS))
    if part == 1:

        @pl.when((z == 1) | (z == 2))
        def _():
            for c in range(window // KEYS, total // KEYS):
                act(c * KEYS)


def aug_rows(top, r):
    return jnp.concatenate([top.astype(BF16), jnp.zeros((128 - 16, r), BF16)], axis=0)


def pick_rows(rows, r):
    index = lax.broadcasted_iota(jnp.int32, (16, r), 0)
    out = jnp.zeros((16, r), F32)
    for i, row in enumerate(rows):
        out = jnp.where(index == i, jnp.broadcast_to(row, (16, r)), out)
    return out


def split3(x):
    hi = x.astype(BF16).astype(F32)
    mid = (x - hi).astype(BF16).astype(F32)
    return hi, mid, x - hi - mid


def padded(head_rows, half, aug, r):
    zero = jnp.zeros((HD, r), BF16)
    pair = [head_rows, zero] if half == 0 else [zero, head_rows]
    return jnp.concatenate(pair + [aug], axis=0)


def attention_kernel(qt, k, vt, ka, ma, mixed_t, lse, s, m, l, acc):
    z = lax.axis_index("tp")
    own = qt.shape[1]
    for part, (row0, n, start) in enumerate(parts_of(z, own)):
        cols = pl.ds(pl.multiple_of(row0, 128), n)
        aug = aug_rows(pick_rows((ma[0:1, cols], ma[1:2, cols]), n), n)

        def one_pair(pair, carry):
            attend_pair(z, part, start, pair, cols, n, aug, qt, k, vt, ka, mixed_t, lse, s, m, l, acc)
            return carry

        lax.fori_loop(0, k.shape[1] // 128, one_pair, 0)


def attention(qt, k, vt, ka, ma):
    width, own = qt.shape
    total = k.shape[0]
    widest = max(SHORT - own, own - (SHORT - own))
    vm = pltpu.VMEM
    return pl.pallas_call(
        attention_kernel,
        out_shape=(
            jax.ShapeDtypeStruct((width, own), F32),
            jax.ShapeDtypeStruct((width // 128, 8, own), F32),
        ),
        in_specs=[pl.BlockSpec(memory_space=pltpu.VMEM)] * 5,
        out_specs=(pl.BlockSpec(memory_space=pltpu.VMEM),) * 2,
        scratch_shapes=[
            vm((2, total, widest), F32),
            vm((2, 1, widest), F32),
            vm((2, 1, widest), F32),
            vm((2, HD, widest), F32),
        ],
        compiler_params=pltpu.CompilerParams(vmem_limit_bytes=VMEM_MAX),
        name="attention",
    )(qt, k, vt, ka, ma)


def back_pair(z, pair, pause, qt, q, k, kt, v, ka, ma, mixed_t, lse, dmt, dm, dqt, dk, dv, dka, dva, dqa):
    own, total = qt.shape[1], k.shape[0]
    lanes = pl.ds(pl.multiple_of(pair * 128, 128), 128)
    dka[...] = jnp.zeros_like(dka)
    dva[...] = jnp.zeros_like(dva)
    for part, (row0, r, start) in enumerate(parts_of(z, own)):
        pause(part)
        cols = pl.ds(pl.multiple_of(row0, 128), r)
        qs, gs, qm, gm = [], [], [], []
        low = lax.broadcasted_iota(jnp.int32, (r, 128), 1) < HD
        for half in range(2):
            rows = pl.ds(pl.multiple_of(pair * 128 + half * HD, HD), HD)
            delta = jnp.sum(dmt[rows, cols].astype(F32) * mixed_t[rows, cols], axis=0, keepdims=True)
            total_log = lse[pair, half : half + 1, cols]
            q_aug = pick_rows((ma[0:1, cols], ma[1:2, cols]) + split3(-total_log), r)
            zero = jnp.zeros((1, r), F32)
            g_aug = pick_rows((zero, zero) + split3(-delta), r)
            qs.append(padded(qt[rows, cols], half, aug_rows(q_aug, r), r))
            gs.append(padded(dmt[rows, cols], half, aug_rows(g_aug, r), r))
            mine = low if half == 0 else jnp.logical_not(low)
            here = pl.ds(pl.multiple_of(row0, 128), r)
            qm.append(jnp.where(mine, q[here, lanes], jnp.zeros((), BF16)))
            gm.append(jnp.where(mine, dm[here, lanes], jnp.zeros((), BF16)))
            dqa[half, :, :r] = jnp.zeros((HD, r), F32)

        def step(key0):
            keys = pl.ds(key0, KEYS)
            k_left = jnp.concatenate([k[keys, lanes], ka[keys, :]], axis=1)
            v_left = jnp.concatenate([v[keys, lanes], ka[keys, :]], axis=1)
            for half in range(2):
                share = jnp.exp(dot(k_left, qs[half]))
                slope = (share * dot(v_left, gs[half])).astype(BF16)
                dva[keys, :] += dot(share.astype(BF16), gm[half])
                dka[keys, :] += dot(slope, qm[half])
                rows = pl.ds(pl.multiple_of(pair * 128 + half * HD, HD), HD)
                dqa[half, :, :r] += dot(kt[rows, keys], slope)

        over_keys(z, part, start, total, step)
        for half in range(2):
            rows = pl.ds(pl.multiple_of(pair * 128 + half * HD, HD), HD)
            dqt[rows, cols] = (dqa[half, :, :r] * HD ** (-0.5)).astype(BF16)
    dk[:, lanes] = dka[...].astype(BF16)
    dv[:, lanes] = dva[...].astype(BF16)


def attention_back_kernel(*refs):
    z = lax.axis_index("tp")

    def one_pair(pair, carry):
        back_pair(z, pair, lambda part: None, *refs)
        return carry

    lax.fori_loop(0, refs[2].shape[1] // 128, one_pair, 0)


def back_sums_kernel(qt, q, k, kt, v, ka, ma, mixed_t, lse, dmt, dm, *refs):
    g = (refs[0:4], refs[4:8])
    dqt, dk, dv, out_u, out_d, dka, dva, dqa, gk, *bufs = refs[8:]
    bufs, (gk_sem, *sems) = bufs[:8], bufs[8:]
    z, d, core, first, second = position()
    greet(z, d)

    def fetch(p, t):
        return pltpu.make_async_copy(g[p][t].at[:, core], gk.at[p, t], gk_sem.at[p, t])

    sums = Sums(
        z, d, core, second, first,
        lambda p, t: g[p][t].at[:, 1 - core],
        lambda p, t, at: up(gk.at[p, t, at]),
        lambda p, t: fetch(p, t).wait(),
        bufs, sems,
    )
    for p in range(2):
        for t in range(4):
            sums.one(p, t).start()
            fetch(p, t).start()

    def each(act, *units):
        def run():
            for p, t in units:
                act(p, t)

        return run

    def kept_and_four(p):
        def run():
            for t in range(4):
                sums.at_kept(p, t)
                sums.at_four(p, t, 0)

        return run

    def four(p, step):
        return each(lambda p, t: sums.at_four(p, t, step), *[(p, t) for t in range(4)])

    packs = [[(p, t) for t in range(4)] for p in range(2)]
    between = {
        (0, 1): each(sums.at_two, *packs[0]),
        (1, 0): each(sums.at_two, *packs[1]),
        (2, 1): each(sums.at_three, *packs[0][:2]),
        (3, 0): each(sums.at_three, *packs[0][2:]),
        (4, 1): kept_and_four(0),
        (5, 0): lambda: (each(sums.at_three, *packs[1][:2])(), four(0, 1)()),
        (5, 1): lambda: (each(sums.at_three, *packs[1][2:])(), four(0, 2)()),
    }

    def one_pair(pair, carry):
        def pause(part):
            for (i, at), run in between.items():
                if at == part:

                    @pl.when(pair == i)
                    def _():
                        run()

        back_pair(z, pair, pause, qt, q, k, kt, v, ka, ma, mixed_t, lse, dmt, dm, dqt, dk, dv, dka, dva, dqa)
        return carry

    lax.fori_loop(0, k.shape[1] // 128, one_pair, 0)
    kept_and_four(1)()
    for step in (1, 2):
        four(1, step)()
    sums.result(0, out_u)
    sums.result(1, out_d)
    for p in range(2):
        sums.drain(p)


def back_shapes(own, total, width):
    widest = max(SHORT - own, own - (SHORT - own))
    vm = pltpu.VMEM
    outs = (
        jax.ShapeDtypeStruct((width, own), BF16),
        jax.ShapeDtypeStruct((total, width), BF16),
        jax.ShapeDtypeStruct((total, width), BF16),
    )
    return outs, [vm((total, 128), F32), vm((total, 128), F32), vm((2, HD, widest), F32)]


def attention_back(*args):
    (width, own), total = args[0].shape, args[2].shape[0]
    outs, scratch = back_shapes(own, total, width)
    return pl.pallas_call(
        attention_back_kernel,
        out_shape=outs,
        in_specs=[pl.BlockSpec(memory_space=pltpu.VMEM)] * 11,
        out_specs=(pl.BlockSpec(memory_space=pltpu.VMEM),) * 3,
        scratch_shapes=scratch,
        compiler_params=pltpu.CompilerParams(vmem_limit_bytes=VMEM_MAX),
        name="attention_back",
    )(*args)


def back_sums(args, gu, gd):
    (width, own), total = args[0].shape, args[2].shape[0]
    outs, scratch = back_shapes(own, total, width)
    block = (width // 8, gu[0].shape[1])
    g = [a.reshape((4, 2) + block) for a in (*gu, *gd)]
    vmem = pl.BlockSpec(memory_space=pltpu.VMEM)
    return pl.pallas_call(
        back_sums_kernel,
        out_shape=outs + (jax.ShapeDtypeStruct(block, F32),) * 2,
        in_specs=[vmem] * 11 + [pl.BlockSpec(memory_space=pl.ANY)] * 8,
        out_specs=(vmem,) * 5,
        scratch_shapes=[
            *scratch,
            pltpu.VMEM((2, 4, 4) + block, BF16),
            *sum_buffers(2, block),
            pltpu.SemaphoreType.DMA((2, 4)),
            *sum_semaphores(2),
        ],
        compiler_params=pltpu.CompilerParams(
            collective_id=2, has_side_effects=True, vmem_limit_bytes=VMEM_MAX
        ),
        name="back_sums",
    )(*args, *g)


def norms_kernel(
    tok, mixed_t, vec, bu, cot, wd, w,
    enc, dr1, dar, dm, dmt, vecs, wide, *refs,
):
    gu, gd = refs[0:4], refs[4:8]
    wo, wu, wn, mixed, y1r, hr, slope, du, dfr, y1t, dft, stage, w_sem, o_sem = refs[8:]
    own, width = tok.shape
    n_tp = wu.shape[0]
    loads = [[pltpu.make_async_copy(w.at[i, t], b.at[t], w_sem.at[i, t]) for t in range(n_tp)] for i, b in enumerate((wu, wn))]
    load_o = pltpu.make_async_copy(wd.at[3], wo, w_sem.at[2, 0])
    load_o.start()
    for t in range(n_tp):
        for i in range(2):
            loads[i][t].start()
    vecs[...] = jnp.zeros_like(vecs)
    half = own // 2

    def flip_mixed(i, carry):
        cols = pl.ds(pl.multiple_of(i * ROWS, ROWS), ROWS)
        mixed[cols, :] = mixed_t[:, cols].T.astype(BF16)
        return carry

    lax.fori_loop(0, own // ROWS, flip_mixed, 0)
    load_o.wait()
    for t in range(n_tp):
        for i in range(2):
            loads[i][t].wait()

    def row_tile(i, carry):
        rows = pl.ds(pl.multiple_of(i * half, 64), half)

        def add(index, value):
            vecs[index : index + 1, :] += jnp.sum(value, axis=0, keepdims=True)

        xhat1, inv1 = normalize_layer(tok[rows, :].astype(F32) + contract_last(mixed[rows, :], wo[...]) + vec[2:3, :])
        y1 = xhat1 * vec[3:4, :] + vec[4:5, :]
        y1b = y1.astype(BF16)
        y1r[rows, :] = y1b
        total = y1 + vec[5:6, :]
        for t in range(n_tp):
            u = dot(y1b, wu[t]) + bu[:, t * width : (t + 1) * width]
            below = 0.5 * (1.0 + lax.erf(u * SQRT_HALF))
            h = (u * below).astype(BF16)
            hr[t, rows, :] = h
            slope[t] = below + u * jnp.exp(-0.5 * u * u) * INV_ROOT_TAU
            total = total + contract_last(h, wn[t])
        xhat2, inv2 = normalize_layer(total)
        enc[rows, :] = (xhat2 * vec[6:7, :] + vec[7:8, :]).astype(BF16)
        grad = cot[rows, :].astype(F32)
        add(6, grad * xhat2)
        add(7, grad)
        dr2 = normalize_backward(grad, xhat2, inv2, vec[6:7, :])
        dfb = dr2.astype(BF16)
        dfr[rows, :] = dfb
        add(5, dfb.astype(F32))
        dy1 = dr2
        for t in range(n_tp):
            back = (dot(dfb, wn[t]) * slope[t]).astype(BF16)
            du[t, rows, :] = back
            dy1 = dy1 + contract_last(back, wu[t])
        add(3, dy1 * xhat1)
        add(4, dy1)
        first = normalize_backward(dy1, xhat1, inv1, vec[3:4, :])
        dr1[rows, :] = first
        dab = first.astype(BF16)
        dar[rows, :] = dab
        add(2, dab.astype(F32))
        dm[rows, :] = dot(dab, wo[...]).astype(BF16)
        return carry

    lax.fori_loop(0, 2, row_tile, 0)

    def flip(i, carry):
        cols = pl.ds(pl.multiple_of(i * ROWS, ROWS), ROWS)
        dft[:, cols] = dfr[cols, :].T
        y1t[:, cols] = y1r[cols, :].T
        dmt[:, cols] = dm[cols, :].T
        return carry

    lax.fori_loop(0, own // ROWS, flip, 0)
    tile = 256
    ones = jnp.ones((8, own), BF16)

    def store(i, t):
        return pltpu.make_async_copy(stage.at[i, t], (gd, gu)[i][t], o_sem.at[i, t])

    for t in range(n_tp):

        def one_tile(n, carry):
            lanes = pl.ds(pl.multiple_of(n * tile, tile), tile)
            stage[0, t, :, lanes] = dot(dft[...], hr[t, :, lanes]).astype(BF16)
            stage[1, t, :, lanes] = dot(y1t[...], du[t, :, lanes]).astype(BF16)
            wide[0:1, pl.ds(pl.multiple_of(t * width + n * tile, tile), tile)] = dot(ones, du[t, :, lanes])[0:1, :]
            return carry

        lax.fori_loop(0, width // tile, one_tile, 0)
        for i in range(2):
            store(i, t).start()
    for t in range(n_tp):
        for i in range(2):
            store(i, t).wait()


def norms(tok, mixed_t, vec, bu, cot, wd, w):
    own, width = tok.shape
    dma, vm = pltpu.SemaphoreType.DMA, pltpu.VMEM
    any_ = pl.BlockSpec(memory_space=pl.ANY)
    vmem = pl.BlockSpec(memory_space=pltpu.VMEM)
    shape = jax.ShapeDtypeStruct
    square = (width, width)
    return pl.pallas_call(
        norms_kernel,
        out_shape=(
            shape((own, width), BF16),
            shape((own, width), F32),
            shape((own, width), BF16),
            shape((own, width), BF16),
            shape((width, own), BF16),
            shape((8, width), F32),
            shape((1, 4 * width), F32),
        )
        + (shape(square, BF16),) * 8,
        in_specs=[vmem] * 5 + [any_] * 2,
        out_specs=(vmem,) * 7 + (any_,) * 8,
        scratch_shapes=[
            vm(square, BF16),
            vm((4,) + square, BF16),
            vm((4,) + square, BF16),
            vm((own, width), BF16),
            vm((own, width), BF16),
            vm((4, own, width), BF16),
            vm((4, own // 2, width), F32),
            vm((4, own, width), BF16),
            vm((own, width), BF16),
            vm((width, own), BF16),
            vm((width, own), BF16),
            vm((2, 4) + square, BF16),
            dma((3, 4)),
            dma((2, 4)),
        ],
        compiler_params=pltpu.CompilerParams(vmem_limit_bytes=VMEM_MAX),
        name="norms",
    )(tok, mixed_t, vec, bu, cot, wd, w)


def body(
    tokens, w_query, w_key, w_value, b_query, b_value, w_out, b_out, gain_attn, shift_attn,
    w_up, b_up, w_down, b_down, gain_ffn, shift_ffn, lengths, deal_order, cotangent,
):
    own, width = tokens.shape
    n_tp, n_dp = lax.axis_size("tp"), lax.axis_size("dp")
    z, g = lax.axis_index("tp"), lax.axis_index("dp")
    total = own * n_tp
    r, hw = w_query.shape
    direct = n_tp == 4 and n_dp == 8 and r % 16 == 0

    own_w = jnp.stack([jnp.concatenate([w_query, w_key, w_value, w_out], axis=1), w_up, w_down])
    vectors = (b_query, b_value, b_out, gain_attn, shift_attn, b_down, gain_ffn, shift_ffn, b_up)
    n_small = 8 * r + b_up.shape[0]
    if direct:
        line = jnp.arange(8, dtype=jnp.int32)[:, None]
        narrow = jnp.zeros((8, r), BF16)
        for i, a in enumerate(vectors[:8]):
            narrow = jnp.where(line == i, a[None, :], narrow)
        narrow = jnp.pad(narrow, ((0, 0), (0, 128 - r)))
        own_s = jnp.concatenate([narrow, jnp.pad(b_up.reshape(-1, 128), ((0, 5), (0, 0)))])
        w, vec, bu, xt, q, qt, k, v, kt, wd, ka, mixed_t, lse, ma = forward_all(lengths, deal_order, own_w, own_s, tokens)
        w = w.reshape(2, n_tp, width, w_up.shape[1])
        encoder_output, dr1, dar, dm, dmt, vecs, wide_sum, *gw = norms(tokens, mixed_t, vec, bu, cotangent, wd, w)
        args = (qt, q, k, kt, v, ka, ma, mixed_t, lse, dmt, dm)
        dqt, dk, dv, g_up, g_down = back_sums(args, gw[:4], gw[4:])
        a, gs, grad_tokens = finish(dqt, dk, dv, xt, dar, mixed_t, wd, dr1, vecs, wide_sum)
        gs = [gs[i, :r] for i in range(8)] + [gs[8:11].reshape(-1)]
    else:
        w = lax.all_gather(own_w, ("tp", "dp"), axis=0).reshape((n_tp, n_dp) + own_w.shape)
        w = jnp.moveaxis(w, 2, 0).reshape(3, n_tp, width, w_up.shape[1])
        s = lax.all_gather(jnp.concatenate(vectors), "dp", axis=0)
        x = lax.all_gather(tokens, "tp", axis=0, tiled=True)
        small = [s[:, i * r : (i + 1) * r].reshape(width).astype(F32) for i in range(8)]
        bq, bv, bo, g1, h1, bd, g2, h2 = small
        bu = s[:, 8 * r : n_small].reshape(-1).astype(F32)
        wq, wk, wv, wo = (
            w[0, :, :, i * hw : (i + 1) * hw].transpose(1, 0, 2).reshape(width, width) for i in range(4)
        )
        w = w[1:]
        q = (dot(tokens, wq) + bq).astype(BF16) * jnp.asarray(HD ** (-0.5), BF16)
        k = dot(x, wk).astype(BF16)
        v = (dot(x, wv) + bv).astype(BF16)
        qt, kt = q.T, k.T

        pair = lax.dynamic_slice_in_dim(deal_order, 2 * g, 1)
        first_len = jnp.sum(jnp.where(jnp.arange(lengths.shape[0], dtype=jnp.int32) == pair[0], lengths, 0))
        key_seg = jnp.arange(total, dtype=jnp.int32)[:, None] >= first_len
        lane = jnp.arange(128, dtype=jnp.int32)[None, :]
        ka = jnp.where(lane == 0, ~key_seg, jnp.where(lane == 1, key_seg, (lane >= 2) & (lane < 5))).astype(BF16)
        row_seg = (z * own + jnp.arange(own, dtype=jnp.int32))[None, :] >= first_len
        sub = jnp.arange(8, dtype=jnp.int32)[:, None]
        ma = jnp.where(((sub == 0) & row_seg) | ((sub == 1) & ~row_seg), MASKED, 0.0).astype(F32)

        mixed_t, lse = attention(qt, k, v.T, ka, ma)
        mixed = mixed_t.T.astype(BF16)
        first_residual = tokens.astype(F32) + contract_last(mixed, wo) + bo
        xhat1, inv1 = normalize_layer(first_residual)
        y1 = xhat1 * g1 + h1
        y1r = y1.astype(BF16)

        u = [dot(y1r, w[0, t]) + bu.reshape(n_tp, -1)[t] for t in range(n_tp)]
        hr = [jax.nn.gelu(a, approximate=False).astype(BF16) for a in u]
        ffn = sum(contract_last(hr[t], w[1, t]) for t in range(n_tp))
        xhat2, inv2 = normalize_layer(y1 + ffn + bd)
        encoder_output = (xhat2 * g2 + h2).astype(BF16)

        grad = cotangent.astype(F32)
        dr2 = normalize_backward(grad, xhat2, inv2, g2)
        dfr = dr2.astype(BF16)
        du = [(dot(dfr, w[1, t]) * gelu_slope(u[t])).astype(BF16) for t in range(n_tp)]
        dy1 = dr2 + sum(contract_last(du[t], w[0, t]) for t in range(n_tp))
        dr1 = normalize_backward(dy1, xhat1, inv1, g1)
        dar = dr1.astype(BF16)
        dm = dot(dar, wo).astype(BF16)
        gu = [contract_first(y1r, du[t]) for t in range(n_tp)]
        gd = [contract_first(dfr, hr[t]) for t in range(n_tp)]
        row_sums = [
            jnp.sum(dar, axis=0, dtype=F32),
            jnp.sum(dy1 * xhat1, axis=0),
            jnp.sum(dy1, axis=0),
            jnp.sum(dfr, axis=0, dtype=F32),
            jnp.sum(grad * xhat2, axis=0),
            jnp.sum(grad, axis=0),
        ]
        wide_sum = jnp.concatenate([jnp.sum(a, axis=0, dtype=F32) for a in du])
        back_args = (qt, q, k, kt, v, ka, ma, mixed_t, lse, dm.T, dm)
        dqt, dk, dv = attention_back(*back_args)
        dq = dqt.T
        base = dr1 + contract_last(dq, wq)
        far = contract_last(dk, wk) + contract_last(dv, wv)
        base = base + lax.dynamic_slice_in_dim(far, z * own, own)
        dt = far.astype(BF16)
        gq, gk, gv = contract_first(tokens, dq), contract_first(x, dk), contract_first(x, dv)
        go = contract_first(dar, mixed)
        ga = jnp.stack(
            [
                jnp.concatenate([m[:, t * hw : (t + 1) * hw] for m in (gq, gk, gv, go)], axis=1)
                for t in range(n_tp)
            ]
        )
        sums = [jnp.sum(dq, axis=0, dtype=F32), jnp.sum(dv, axis=0, dtype=F32)] + row_sums
        sums = [a.reshape(n_dp, r) for a in sums]
        sv = jnp.concatenate(sums + [wide_sum.reshape(n_dp, -1)], axis=1)
        grads = jnp.stack([ga, jnp.stack(gu), jnp.stack(gd)], axis=1).reshape(n_tp, 3, n_dp, r, -1)
        grads = jnp.moveaxis(grads, 1, 2).reshape(n_tp * n_dp, 3, r, -1)
        gw = lax.psum_scatter(grads, ("tp", "dp"), scatter_dimension=0, tiled=True)[0]
        gs = lax.psum_scatter(lax.psum(sv, "tp"), "dp", scatter_dimension=0, tiled=True)[0]
        others = jnp.where(jnp.arange(total)[:, None] // own == z, jnp.zeros((), BF16), dt)
        grad_tokens = base + lax.psum_scatter(others, "tp", scatter_dimension=0, tiled=True).astype(F32)
        gs = [gs[i * r : (i + 1) * r] for i in range(8)] + [gs[8 * r : n_small]]
        a, g_up, g_down = gw[0], gw[1], gw[2]
    return (
        encoder_output, grad_tokens,
        a[:, :hw], a[:, hw : 2 * hw], a[:, 2 * hw : 3 * hw], gs[0], gs[1],
        a[:, 3 * hw :], gs[2], gs[3], gs[4],
        g_up, gs[8], g_down, gs[5], gs[6], gs[7],
    )


def solution(mesh):
    rows, block, vector = P(("dp", "tp"), None), P("dp", "tp"), P("dp")
    in_specs = (
        rows, block, block, block, vector, vector, block, vector, vector, vector,
        block, vector, block, vector, vector, vector, P(), P(), rows,
    )
    out_specs = (
        rows, rows, block, block, block, vector, vector, block, vector, vector, vector,
        block, vector, block, vector, vector, vector,
    )
    return jax.shard_map(body, mesh=mesh, in_specs=in_specs, out_specs=out_specs, check_vma=False)
```

```python
import functools

import jax
import jax.numpy as jnp
from jax import lax
from jax.experimental import pallas as pl
from jax.experimental.pallas import tpu as pltpu
from jax.sharding import PartitionSpec as P

HD = 64
SHORT = 1024
EPS = 1e-05
SQRT_HALF = 0.7071067811865476
INV_ROOT_TAU = 0.3989422804014327
MASKED = -1e30
KEYS = 512
ROWS = 128
VMEM_MAX = 67043328
MESH = pl.DeviceIdType.MESH
F32 = jnp.float32
BF16 = jnp.bfloat16


def dot(left, right):
    return jnp.dot(left, right, preferred_element_type=F32)


def contract_last(left, right):
    return lax.dot_general(left, right, (((1,), (1,)), ((), ())), preferred_element_type=F32)


def contract_first(left, right):
    return lax.dot_general(left, right, (((0,), (0,)), ((), ())), preferred_element_type=F32)


def normalize_layer(resid):
    center = resid - jnp.mean(resid, axis=-1, keepdims=True)
    inverse_deviation = lax.rsqrt(jnp.mean(center * center, axis=-1, keepdims=True) + EPS)
    return (center * inverse_deviation, inverse_deviation)


def normalize_backward(output_gradient, xhat, inverse_deviation, gain):
    scaled_rows = output_gradient * gain
    return inverse_deviation * (
        scaled_rows
        - jnp.mean(scaled_rows, axis=-1, keepdims=True)
        - xhat * jnp.mean(scaled_rows * xhat, axis=-1, keepdims=True)
    )


def gelu_slope(pre_act):
    return (
        0.5 * (1.0 + lax.erf(pre_act * SQRT_HALF))
        + pre_act * jnp.exp(-0.5 * pre_act * pre_act) * INV_ROOT_TAU
    )


def position():
    z = lax.axis_index("tp")
    d = lax.axis_index("dp")
    core = lax.rem(d, 2)
    first = 2 + 2 * core
    second = 4 - 2 * core
    return z, d, core, first, second


def xor(d, mask):
    return d + mask * (1 - 2 * lax.rem(d // mask, 2))


def greet(z, d):
    barrier = pltpu.get_barrier_semaphore()
    for mask in (1, 2, 4):
        pl.semaphore_signal(barrier, inc=1, device_id=(xor(d, mask), z), device_id_type=MESH)
    for j in range(1, 4):
        pl.semaphore_signal(barrier, inc=1, device_id=(d, lax.rem(z + j, 4)), device_id_type=MESH)
    pl.semaphore_wait(barrier, 6)


def by_distance(z):
    low = z <= 1
    near = jnp.where(z == 0, 1, jnp.where(z == 1, 0, jnp.where(z == 2, 3, 2)))
    mid = jnp.where(low, 2, 1)
    far = jnp.where(low, 3, 0)
    return (z, near, mid, far)


def put(src, dst, send, recv, dp, tp):
    return pltpu.make_async_remote_copy(
        src_ref=src, dst_ref=dst, send_sem=send, recv_sem=recv, device_id=(dp, tp), device_id_type=MESH
    )


def forward_kernel(
    lengths, deal, own_w, own_s, own_t,
    w, vec, bu, xt_out, q_out, qt_out, k_out, v_out, kt_out, wd_out, ka_out, mixed_t, lse, ma,
    wa, s, x, xt, q, qt, k, v, kt, vt, wd, ka, sc, m, l, acc,
    wz_s, wz_r, wa_s, wa_r, wb_s, wb_r, wc_s, wc_r, tk_s, tk_r, sm_s, sm_r, lo_sem, arr_sem, out_sem,
):
    z, d, core, first, second = position()
    packs = own_w.shape[0]
    own, width = own_t.shape
    total = 4 * own
    hw = width // 4
    chunks = own // ROWS
    d1, d2 = xor(d, first), xor(d, second)
    d12 = xor(d1, second)
    pal = xor(d, 1)
    pd, pd1, pd2, pd12 = (xor(e, 1) for e in (d, d1, d2, d12))
    order = by_distance(z)
    first_len = lengths[deal[2 * d]]

    greet(z, d)

    def block(p, tt, e):
        return wa.at[tt, e] if p == 0 else w.at[p - 1, tt, e]

    def along_z(p, tt, src, act):
        dst = block(p, tt, d)
        right = put(src, dst, wz_s.at[0, p, tt], wz_r.at[p, tt], d, jnp.minimum(z + 1, 3))
        left = put(src, dst, wz_s.at[1, p, tt], wz_r.at[p, tt], d, jnp.maximum(z - 1, 0))

        @pl.when((tt <= z) & (z < 3))
        def _():
            act(right)

        @pl.when((tt >= z) & (z > 0))
        def _():
            act(left)

    def across(p, tt, src):
        dst = block(p, tt, d)
        return (
            put(src, dst, wa_s.at[p, tt], wa_r.at[p, tt], d1, z),
            put(src, dst, wb_s.at[p, tt, 0], wb_r.at[p, tt, 0], d2, z),
            put(src, dst, wc_s.at[p, tt, 0], wc_r.at[p, tt, 0], pal, z),
        )

    def after_first(p, tt):
        src = block(p, tt, d1)
        return (
            put(src, src, wb_s.at[p, tt, 1], wb_r.at[p, tt, 1], d2, z),
            put(src, src, wc_s.at[p, tt, 1], wc_r.at[p, tt, 1], pal, z),
        )

    def after_second(p, tt, i):
        src = block(p, tt, d2 if i == 0 else d12)
        return put(src, src, wc_s.at[p, tt, 2 + i], wc_r.at[p, tt, 2 + i], pal, z)

    def source(p, j):
        return own_w.at[p] if j == 0 else block(p, order[j], d)

    def arrive(ref, sem):
        put(ref, ref, arr_sem, sem, pal, z).wait_recv()

    def begin_z(p, j):
        if j > 0:
            arrive(block(p, order[j], d), wz_r.at[p, order[j]])
        along_z(p, order[j], source(p, j), lambda c: c.start())

    def begin_xy(p, j):
        for copy in across(p, order[j], source(p, j)):
            copy.start()

    def begin(p, j):
        begin_z(p, j)
        begin_xy(p, j)

    def relay_first(p, j):
        tt = order[j]
        arrive(block(p, tt, d1), wa_r.at[p, tt])
        for copy in after_first(p, tt):
            copy.start()

    def relay_second(p, j):
        tt = order[j]
        for i in range(2):
            arrive(block(p, tt, d2 if i == 0 else d12), wb_r.at[p, tt, i])
            after_second(p, tt, i).start()

    def from_pal(p):
        for tt in range(4):
            for i, e in enumerate((pd, pd2, pd1, pd12)):
                arrive(block(p, tt, e), wc_r.at[p, tt, i])

    def sent(p):
        for j in range(4):
            tt = order[j]
            along_z(p, tt, source(p, j), lambda c: c.wait_send())
            for copy in across(p, tt, source(p, j)) + after_first(p, tt):
                copy.wait_send()
            for i in range(2):
                after_second(p, tt, i).wait_send()

    def token_slice(o, i):
        return x.at[pl.ds(pl.multiple_of((o * chunks + i) * ROWS, ROWS), ROWS)]

    def token_hop(o, i, hop, step):
        src = own_t.at[pl.ds(i * ROWS, ROWS)] if hop == 0 else token_slice(o, i)
        way = 0 if step > 0 else 1
        return put(src, token_slice(o, i), tk_s.at[way, hop, i], tk_r.at[way, hop, i], d, jnp.clip(z + step, 0, 3))

    last = SHORT // ROWS

    def wanted(o, i, target, step):
        n = o * chunks + i
        if step > 0:
            return (target <= 2) | (n >= last)
        return (target >= 1) | (n < 4 * chunks - last)

    def chunk_ids(step):
        return list(range(chunks))[:: -step]

    def tokens(hop, step, act, which=slice(None)):
        o, target = z - step * hop, z + step
        valid = (o >= 0) & (o <= 3) & (target >= 0) & (target <= 3)
        for i in chunk_ids(step)[which]:

            @pl.when(valid & wanted(o, i, target, step))
            def _():
                act(token_hop(o, i, hop, step))

    def tokens_on(hop, step, onward):
        o, target = z - step * (hop + 1), z + step
        valid = (o >= 0) & (o <= 3) & (z - step >= 0) & (z - step <= 3)
        way = 0 if step > 0 else 1
        for i in chunk_ids(step):

            @pl.when(valid & wanted(o, i, z, step))
            def _():
                arrive(token_slice(jnp.clip(o, 0, 3), i), tk_r.at[way, hop, i])

            if onward:

                @pl.when(valid & (target >= 0) & (target <= 3) & wanted(o, i, target, step))
                def _():
                    token_hop(o, i, hop + 1, step).start()

    def small(stage):
        if stage == 0:
            return [
                put(own_s, s.at[d], sm_s.at[0], sm_r.at[0], d1, z),
                put(own_s, s.at[d], sm_s.at[1], sm_r.at[1], d2, z),
                put(own_s, s.at[d], sm_s.at[3], sm_r.at[3], pal, z),
            ]
        if stage == 1:
            return [
                put(s.at[d1], s.at[d1], sm_s.at[2], sm_r.at[2], d2, z),
                put(s.at[d1], s.at[d1], sm_s.at[4], sm_r.at[4], pal, z),
            ]
        return [
            put(s.at[d2], s.at[d2], sm_s.at[5], sm_r.at[5], pal, z),
            put(s.at[d12], s.at[d12], sm_s.at[6], sm_r.at[6], pal, z),
        ]

    def own_tokens(*which):
        for step in (1, -1):
            tokens(0, step, lambda c: c.start(), slice(*which))

    begin(0, 0)
    for copy in small(0):
        copy.start()
    own_tokens(0, 1)
    s[d] = own_s[...]
    wa[z, d] = own_w[0]
    mine = pl.ds(pl.multiple_of(z * own, ROWS), own)
    x[mine, :] = own_t[...]
    keep = pltpu.make_async_copy(own_w.at[pl.ds(1, packs - 1)], w.at[:, z, d], lo_sem)
    keep.start()

    @pl.when(z == 0)
    def _():
        x[total - SHORT :, :] = jnp.zeros((SHORT, width), BF16)
        xt[:, total - SHORT :] = jnp.zeros((width, SHORT), BF16)

    @pl.when(z == 3)
    def _():
        x[:SHORT, :] = jnp.zeros((SHORT, width), BF16)
        xt[:, :SHORT] = jnp.zeros((width, SHORT), BF16)

    begin(0, 1)
    relay_first(0, 0)
    own_tokens(1, 2)
    begin(0, 2)
    relay_second(0, 0)
    relay_first(0, 1)
    for p in range(1, packs):
        begin_z(p, 0)
    begin(0, 3)
    own_tokens(2, chunks)
    relay_second(0, 1)
    relay_first(0, 2)
    begin_xy(1, 0)
    arrive(s.at[d1], sm_r.at[0])
    for copy in small(1):
        copy.start()
    relay_second(0, 2)
    relay_first(0, 3)
    for p in range(2, packs):
        begin_xy(p, 0)
    arrive(s.at[d2], sm_r.at[1])
    arrive(s.at[d12], sm_r.at[2])
    for copy in small(2):
        copy.start()
    for p in range(1, packs):
        begin(p, 1)
    lane = lax.broadcasted_iota(jnp.int32, (own, 128), 1)
    for i in range(4):
        late = lax.broadcasted_iota(jnp.int32, (own, 128), 0) + i * own >= first_len
        ones = jnp.where((lane >= 2) & (lane < 5), 1.0, 0.0)
        flags = jnp.where(lane == 0, jnp.where(late, 0.0, 1.0), jnp.where(lane == 1, jnp.where(late, 1.0, 0.0), ones))
        ka[pl.ds(i * own, own), :] = flags.astype(BF16)

    relay_second(0, 3)
    for i, e in enumerate((pd, pd2, pd1, pd12)):
        arrive(s.at[e], sm_r.at[3 + i])
    r = width // 8
    for e in range(8):
        piece = s[e].astype(F32)
        vec[0:8, e * r : (e + 1) * r] = piece[0:8, 0:r]
        for j in range(hw * 2 // 128):
            col = e * hw * 2 + j * 128
            bu[0:1, col : col + 128] = piece[8 + j : 9 + j, :]
    from_pal(0)
    for tt in range(4):
        rows = wa[tt].reshape(width, width)
        for i in range(4):
            wd[i, :, tt * hw : (tt + 1) * hw] = rows[:, i * hw : (i + 1) * hw]
    wd_copy = pltpu.make_async_copy(wd, wd_out, out_sem.at[0])
    wd_copy.start()

    tile = 256

    def q_tile(n, carry):
        lanes = pl.ds(pl.multiple_of(n * tile, tile), tile)
        rows = (dot(own_t[...], wd[0, :, lanes]) + vec[0:1, lanes]).astype(BF16) * jnp.asarray(HD ** (-0.5), BF16)
        q[:, lanes] = rows
        qt[lanes, :] = rows.T
        return carry

    def project(o):
        rows = pl.ds(pl.multiple_of(o * own, ROWS), own)

        def kv_tile(n, carry):
            lanes = pl.ds(pl.multiple_of(n * tile, tile), tile)
            keys = dot(x[rows, :], wd[1, :, lanes]).astype(BF16)
            k[rows, lanes] = keys
            kt[lanes, rows] = keys.T
            values = (dot(x[rows, :], wd[2, :, lanes]) + vec[1:2, lanes]).astype(BF16)
            v[rows, lanes] = values
            vt[lanes, rows] = values.T
            xt[lanes, rows] = x[rows, lanes].T
            return carry

        lax.fori_loop(0, width // tile, kv_tile, 0)

    def project_far():
        for step in (1, -1):
            tokens_on(1, step, False)
        project(jnp.where(z == 0, 2, jnp.where(z == 1, 3, z - 2)))

    middle = (z == 1) | (z == 2)
    lax.fori_loop(0, width // tile, q_tile, 0)
    project(z)
    for p in range(1, packs):
        relay_first(p, 0)
    for step in (1, -1):
        tokens_on(0, step, True)

    @pl.when(z > 0)
    def _():
        project(jnp.maximum(z - 1, 0))

    for p in range(1, packs):
        begin(p, 2)
    for p in range(1, packs):
        relay_second(p, 0)
        relay_first(p, 1)

    @pl.when(z < 3)
    def _():
        project(jnp.minimum(z + 1, 3))

    @pl.when(jnp.logical_not(middle))
    def _():
        project_far()

    def both(act, j):
        def run():
            for p in range(1, packs):
                act(p, j)

        return run

    between = {
        (0, 0): both(begin, 3),
        (0, 1): both(relay_second, 1),
        (0, 2): both(relay_first, 2),
        (0, 5): both(relay_second, 2),
        (1, 0): both(relay_first, 3),
        (1, 4): both(relay_second, 3),
    }
    late = lax.broadcasted_iota(jnp.int32, (8, own), 1) + z * own >= first_len
    sub = lax.broadcasted_iota(jnp.int32, (8, own), 0)
    away = jnp.where(sub == 0, jnp.where(late, MASKED, 0.0), jnp.where(sub == 1, jnp.where(late, 0.0, MASKED), 0.0))
    ma[...] = away
    outs = [
        pltpu.make_async_copy(a, b, out_sem.at[1 + i])
        for i, (a, b) in enumerate(
            ((xt, xt_out), (q, q_out), (qt, qt_out), (k, k_out), (v, v_out), (kt, kt_out), (ka, ka_out))
        )
    ]
    pairs = width // 128
    for part, (row0, n, start) in enumerate(parts_of(z, own)):
        if part == 1:

            @pl.when(middle)
            def _():
                project_far()

            for copy in outs:
                copy.start()
        cols = pl.ds(pl.multiple_of(row0, 128), n)
        late = lax.broadcasted_iota(jnp.int32, (1, n), 1) + (z * own + row0) >= first_len
        masks = (jnp.where(late, MASKED, 0.0), jnp.where(late, 0.0, MASKED))
        aug = aug_rows(pick_rows(masks, n), n)

        def one_pair(pair, carry):
            for (at, i), run in between.items():
                if at == part:

                    @pl.when(pair == i)
                    def _():
                        run()

            attend_pair(z, part, start, pair, cols, n, aug, qt, k, vt, ka, mixed_t, lse, sc, m, l, acc)
            return carry

        lax.fori_loop(0, pairs, one_pair, 0)

    for p in range(1, packs):
        from_pal(p)
    for stage in range(3):
        for copy in small(stage):
            copy.wait_send()
    for hop in range(2):
        for step in (1, -1):
            tokens(hop, step, lambda c: c.wait_send())
    for p in range(packs):
        sent(p)
    keep.wait()
    wd_copy.wait()
    for copy in outs:
        copy.wait()


def attend_pair(z, part, start, pair, cols, n, aug, qt, k, vt, ka, mixed_t, lse, s, m, l, acc):
    total = k.shape[0]
    lanes = pl.ds(pl.multiple_of(pair * 128, 128), 128)
    for half in range(2):
        m[half, :, :n] = jnp.full((1, n), MASKED, F32)
        l[half, :, :n] = jnp.zeros((1, n), F32)
        acc[half, :, :n] = jnp.zeros((HD, n), F32)
    qs = [padded(qt[pl.ds(pl.multiple_of(pair * 128 + half * HD, HD), HD), cols], half, aug, n) for half in range(2)]

    def scores(key0):
        keys = pl.ds(key0, KEYS)
        left = jnp.concatenate([k[keys, lanes], ka[keys, :]], axis=1)
        for half in range(2):
            score = dot(left, qs[half])
            s[half, keys, :n] = score
            m[half, :, :n] = jnp.maximum(m[half, :, :n], jnp.max(score, axis=0, keepdims=True))

    over_keys(z, part, start, total, scores)
    tops = [m[half, :, :n] for half in range(2)]

    def mix(key0):
        keys = pl.ds(key0, KEYS)
        for half in range(2):
            raised = jnp.exp(s[half, keys, :n] - tops[half])
            l[half, :, :n] += jnp.sum(raised, axis=0, keepdims=True)
            values = vt[pl.ds(pl.multiple_of(pair * 128 + half * HD, HD), HD), keys]
            acc[half, :, :n] += dot(values, raised.astype(BF16))

    over_keys(z, part, start, total, mix)
    for half in range(2):
        sums = l[half, :, :n]
        rows = pl.ds(pl.multiple_of(pair * 128 + half * HD, HD), HD)
        mixed_t[rows, cols] = acc[half, :, :n] / sums
        lse[pair, half : half + 1, cols] = tops[half] + jnp.log(sums)


def forward_all(lengths, deal, own_w, own_s, own_t):
    packs, r, c = own_w.shape
    own, width = own_t.shape
    total = 4 * own
    chunks = own // ROWS
    widest = max(SHORT - own, own - (SHORT - own))
    dma, vm = pltpu.SemaphoreType.DMA, pltpu.VMEM
    any_ = pl.BlockSpec(memory_space=pl.ANY)
    vmem = pl.BlockSpec(memory_space=pltpu.VMEM)
    smem = pl.BlockSpec(memory_space=pltpu.SMEM)
    shape = jax.ShapeDtypeStruct
    return pl.pallas_call(
        forward_kernel,
        out_shape=(
            shape((packs - 1, 4, 8, r, c), BF16),
            shape((8, width), F32),
            shape((1, 4 * c), F32),
            shape((width, total), BF16),
            shape((own, width), BF16),
            shape((width, own), BF16),
            shape((total, width), BF16),
            shape((total, width), BF16),
            shape((width, total), BF16),
            shape((4, width, width), BF16),
            shape((total, 128), BF16),
            shape((width, own), F32),
            shape((width // 128, 8, own), F32),
            shape((8, own), F32),
        ),
        in_specs=[smem, smem, vmem, vmem, vmem],
        out_specs=(any_, vmem, vmem) + (any_,) * 8 + (vmem, vmem, vmem),
        scratch_shapes=[
            vm((4, 8, r, c), BF16),
            vm((8, 16, 128), BF16),
            vm((total, width), BF16),
            vm((width, total), BF16),
            vm((own, width), BF16),
            vm((width, own), BF16),
            vm((total, width), BF16),
            vm((total, width), BF16),
            vm((width, total), BF16),
            vm((width, total), BF16),
            vm((4, width, width), BF16),
            vm((total, 128), BF16),
            vm((2, total, widest), F32),
            vm((2, 1, widest), F32),
            vm((2, 1, widest), F32),
            vm((2, HD, widest), F32),
            dma((2, packs, 4)),
            dma((packs, 4)),
            dma((packs, 4)),
            dma((packs, 4)),
            dma((packs, 4, 2)),
            dma((packs, 4, 2)),
            dma((packs, 4, 4)),
            dma((packs, 4, 4)),
            dma((2, 2, chunks)),
            dma((2, 2, chunks)),
            dma((7,)),
            dma((7,)),
            dma(()),
            dma(()),
            dma((8,)),
        ],
        compiler_params=pltpu.CompilerParams(
            collective_id=0, has_side_effects=True, vmem_limit_bytes=VMEM_MAX
        ),
        name="forward_all",
    )(lengths, deal, own_w, own_s, own_t)


def up(ref):
    return ref[...].astype(F32)


class Sums:
    def __init__(self, z, d, core, e_mask, f_mask, give, mine, ready, bufs, sems):
        self.z, self.d, self.give, self.mine, self.ready = z, d, give, mine, ready
        self.r1, self.b2, self.r2, self.b3, self.r3, self.s3, self.b4, self.r4 = bufs
        self.sems = sems
        self.xy = d // 2
        self.e, self.f = xor(d, e_mask) // 2, xor(d, f_mask) // 2
        self.ef = xor(xor(d, e_mask), f_mask) // 2
        self.d_e, self.d_f, self.pal = xor(d, e_mask), xor(d, f_mask), xor(d, 1)

    def one(self, p, t):
        return put(self.give(p, t), self.r1.at[p, t], self.sems[0].at[p, t], self.sems[1].at[p, t], self.pal, self.z)

    def two(self, p, t):
        return put(self.b2.at[p, t], self.r2.at[p, t], self.sems[2].at[p, t], self.sems[3].at[p, t], self.d_e, self.z)

    def three(self, p, t):
        return put(self.b3.at[p, t], self.r3.at[p, t], self.sems[4].at[p, t], self.sems[5].at[p, t], self.d_f, self.z)

    def four(self, p, t, way):
        to = jnp.minimum(self.z + 1, 3) if way == 0 else jnp.maximum(self.z - 1, 0)
        return put(
            self.b4.at[p, way, t], self.r4.at[p, way, t],
            self.sems[6].at[p, way, t], self.sems[7].at[p, way, t], self.d, to,
        )

    def at_two(self, p, t):
        self.ready(p, t)
        self.one(p, t).wait_recv()
        for i, x in enumerate((self.e, self.ef)):
            self.b2[p, t, i] = (self.mine(p, t, x) + up(self.r1.at[p, t, x])).astype(BF16)
        self.two(p, t).start()

    def at_three(self, p, t):
        self.two(p, t).wait_recv()
        f = self.f
        self.b3[p, t] = (self.mine(p, t, f) + up(self.r1.at[p, t, f]) + up(self.r2.at[p, t, 1])).astype(BF16)
        self.three(p, t).start()

    def at_kept(self, p, t):
        self.three(p, t).wait_recv()
        xy = self.xy
        self.s3[p, t] = self.mine(p, t, xy) + up(self.r1.at[p, t, xy]) + up(self.r2.at[p, t, 0]) + up(self.r3.at[p, t])

    def at_four(self, p, step, kept=()):
        kept = list(kept)
        for i in range(3):
            for t, way in ((3 - i, 0), (i, 1)):
                if t in kept:
                    self.at_kept(p, t)
                    kept.remove(t)
            for t, way in ((3 - i, 0), (i, 1)):
                pos = step if way == 0 else 3 - step
                if not (t > pos if way == 0 else t < pos):
                    continue

                @pl.when(self.z == pos)
                def _():
                    if step == 0:
                        self.b4[p, way, t] = self.s3[p, t].astype(BF16)
                    else:
                        self.four(p, t, way).wait_recv()
                        self.b4[p, way, t] = (self.s3[p, t] + up(self.r4.at[p, way, t])).astype(BF16)
                    self.four(p, t, way).start()

    def result(self, p, out):
        z = self.z
        out[...] = self.s3[p, z]

        @pl.when(z > 0)
        def _():
            self.four(p, z, 0).wait_recv()
            out[...] += up(self.r4.at[p, 0, z])

        @pl.when(z < 3)
        def _():
            self.four(p, z, 1).wait_recv()
            out[...] += up(self.r4.at[p, 1, z])

    def drain(self, p):
        for t in range(4):
            self.one(p, t).wait_send()
            self.two(p, t).wait_send()
            self.three(p, t).wait_send()
            for way in range(2):

                @pl.when((t > self.z) if way == 0 else (t < self.z))
                def _():
                    self.four(p, t, way).wait_send()


def sum_buffers(packs, block):
    vm = pltpu.VMEM
    return [
        vm((packs, 4, 4) + block, BF16),
        vm((packs, 4, 2) + block, BF16),
        vm((packs, 4, 2) + block, BF16),
        vm((packs, 4) + block, BF16),
        vm((packs, 4) + block, BF16),
        vm((packs, 4) + block, F32),
        vm((packs, 2, 4) + block, BF16),
        vm((packs, 2, 4) + block, BF16),
    ]


def sum_semaphores(packs):
    dma = pltpu.SemaphoreType.DMA
    return [dma((packs, 4))] * 6 + [dma((packs, 2, 4))] * 2


def finish_kernel(
    dqt, dk, dv, xt, dar, mixed_t, wd, dr1, vecs, bup,
    out_w, out_s, out_t,
    dart, dq, mixed, gp, sv, ds, dr, sk, q1, q2, q3, c2, c3, q4,
    r1, b2, r2, b3, r3, s3, b4, r4,
    p1_s, p1_r, p2_s, p2_r, p3_s, p3_r, p4_s, p4_r, t_s, t_r, v_s, v_r,
):
    z, d, core, first, second = position()
    own, width = out_t.shape
    chunks = own // ROWS
    total = 4 * chunks
    edge = SHORT // ROWS
    hw = width // 4
    r = width // 8
    greet(z, d)

    def token(k, way):
        to = jnp.minimum(z + 1, 3) if way == 0 else jnp.maximum(z - 1, 0)
        slot = k if way == 0 else jnp.where(k // chunks == to, total + k % chunks, k)
        return put(ds.at[k], dr.at[slot], t_s.at[k], t_r.at[slot], d, to)

    def token_in(k, way):
        slot = k if way == 0 else jnp.where(k // chunks == z, total + k % chunks, k)
        return put(ds.at[k], dr.at[slot], t_s.at[k], t_r.at[slot], d, z), slot

    def sends(k, way):
        o = k // chunks
        if way == 0:
            low = jnp.where(k < total - edge, 0, 1)
            return (z >= low) & (z < o) & (o > low)
        high = jnp.where(k >= edge, 3, 2)
        return (z <= high) & (z > o) & (o < high)

    def starts(k, way):
        if way == 0:
            return z == jnp.where(k < total - edge, 0, 1)
        return z == jnp.where(k >= edge, 3, 2)

    def pick(a, b, c, e):
        return jnp.where(z == 0, a, jnp.where(z == 1, b, jnp.where(z == 2, c, e)))

    tile = 256

    def far_shard(o, mine):
        rows = pl.ds(pl.multiple_of(o * own, ROWS), own)

        def one_tile(n, carry):
            lanes = pl.ds(pl.multiple_of(n * tile, tile), tile)
            far = contract_last(dk[rows, :], wd[1, lanes, :]) + contract_last(dv[rows, :], wd[2, lanes, :])
            if mine:
                out_t[:, lanes] = dr1[:, lanes] + far
            else:
                ds[pl.ds(o * chunks, chunks), :, lanes] = far.reshape(chunks, ROWS, tile).astype(BF16)
            return carry

        lax.fori_loop(0, width // tile, one_tile, 0)

    def far_and_send(j):
        o = pick(*((2, 3, 0, 1), (1, 2, 1, 2), (3, 0, 3, 0))[j])

        @pl.when((j < 2) | (z == 1) | (z == 2))
        def _():
            far_shard(o, False)

        for i in range(chunks):
            for way in range(2):
                k = o * chunks + i

                @pl.when(sends(k, way) & starts(k, way))
                def _():
                    token(k, way).start()

    far_and_send(0)

    right_order = [k for o in (3, 2, 1) for k in range(o * chunks, (o + 1) * chunks)]
    left_order = [total - 1 - k for k in right_order]

    def forward_tokens(at):
        for k, way in [(k, 0) for k in right_order] + [(k, 1) for k in left_order]:
            pos = at if way == 0 else 3 - at
            passes = (at < k // chunks) if way == 0 else (3 - at > k // chunks)
            begins = (0 if k < total - edge else 1) if way == 0 else (3 if k >= edge else 2)
            if not passes or (begins >= pos if way == 0 else begins <= pos):
                continue

            @pl.when(z == pos)
            def _():
                got, slot = token_in(k, way)
                got.wait_recv()
                ds[k] = (ds[k].astype(F32) + dr[slot].astype(F32)).astype(BF16)
                token(k, way).start()

    def flip_own(i, carry):
        cols = pl.ds(pl.multiple_of(i * ROWS, ROWS), ROWS)
        dart[:, cols] = dar[cols, :].T
        dq[cols, :] = dqt[:, cols].T
        mixed[cols, :] = mixed_t[:, cols].T.astype(BF16)
        return carry

    lax.fori_loop(0, chunks, flip_own, 0)

    def give(p, t):
        return gp.at[t, :, 1 - core]

    def mine(p, t, at):
        return gp[t, at, core].astype(F32)

    sums = Sums(
        z, d, core, second, first, give, mine, lambda p, t: None,
        (r1, b2, r2, b3, r3, s3, b4, r4), (p1_s, p1_r, p2_s, p2_r, p3_s, p3_r, p4_s, p4_r),
    )
    here = pl.ds(pl.multiple_of(z * own, ROWS), own)
    half = width // 2

    def weights(th):
        lanes = pl.ds(th * half, half)

        def rows_of(m, carry):
            rows = pl.ds(pl.multiple_of(m * half, ROWS), half)
            parts = (
                lambda: dot(xt[rows, here], dq[:, lanes]),
                lambda: dot(xt[rows, :], dk[:, lanes]),
                lambda: dot(xt[rows, :], dv[:, lanes]),
                lambda: dot(dart[rows, :], mixed[:, lanes]),
            )
            for i, part in enumerate(parts):
                got = part().astype(BF16)
                for h in range(2):
                    block = got[:, h * hw : (h + 1) * hw].reshape(2, 2, r, hw)
                    gp[2 * th + h, pl.ds(2 * m, 2), :, :, i * hw : (i + 1) * hw] = block
            return carry

        lax.fori_loop(0, 2, rows_of, 0)
        for t in (2 * th, 2 * th + 1):
            sums.one(0, t).start()

    weights(1)
    weights(0)
    for t in (3, 2):
        sums.at_two(0, t)
    far_and_send(1)
    forward_tokens(1)
    for t in (0, 1):
        sums.at_two(0, t)
    far_and_send(2)
    forward_tokens(2)

    ones = jnp.ones((8, 4 * own), BF16)
    index = lax.broadcasted_iota(jnp.int32, (8, width), 0)
    small_rows = jnp.where(index == 0, dot(ones[:, :own], dq[...]), jnp.where(index == 1, dot(ones, dv[...]), vecs[...]))
    pad = jnp.zeros((8, 128 - r), F32)
    for i in range(8):
        sv[i // 2, i % 2, 0:8, :] = jnp.concatenate([small_rows[:, i * r : (i + 1) * r], pad], axis=1)
        wide = [bup[:, (i * 3 + j) * 128 : (i * 3 + j + 1) * 128] for j in range(3)]
        sv[i // 2, i % 2, 8:16, :] = jnp.concatenate(wide + [jnp.zeros((5, 128), F32)], axis=0)
    small = [
        put(sv.at[:, 1 - core], q1, v_s.at[0], v_r.at[0], sums.pal, z),
        put(c2, q2, v_s.at[1], v_r.at[1], sums.d_e, z),
        put(c3, q3, v_s.at[2], v_r.at[2], sums.d_f, z),
    ]
    small_z = [
        put(sk, q4.at[j - 1], v_s.at[2 + j], v_r.at[2 + j], d, lax.rem(z + j, 4)) for j in range(1, 4)
    ]
    small[0].start()
    far_shard(z, True)

    def query_tile(n, carry):
        lanes = pl.ds(pl.multiple_of(n * tile, tile), tile)
        out_t[:, lanes] += contract_last(dq[...], wd[0, lanes, :])
        return carry

    lax.fori_loop(0, width // tile, query_tile, 0)
    small[0].wait_recv()
    for i, at in enumerate((sums.e, sums.ef)):
        c2[i] = sv[at, core] + q1[at]
    small[1].start()
    for t in (3, 2, 0, 1):
        sums.at_three(0, t)
    small[1].wait_recv()
    c3[...] = sv[sums.f, core] + q1[sums.f] + q2[1]
    small[2].start()
    for step in range(3):
        sums.at_four(0, step, range(4) if step == 0 else ())
        if step == 0:
            small[2].wait_recv()
            sk[...] = sv[sums.xy, core] + q1[sums.xy] + q2[0] + q3[...]
            for copy in small_z:
                copy.start()
    for i in range(chunks):
        k = z * chunks + i
        rows = pl.ds(i * ROWS, ROWS)
        from_left = (z > 0) & ((z == 1) & (k < total - edge) | (z > 1))
        from_right = (z < 3) & ((z == 2) & (k >= edge) | (z < 2))

        @pl.when(from_left)
        def _():
            put(ds.at[k], dr.at[k], t_s.at[k], t_r.at[k], d, z).wait_recv()
            out_t[rows, :] += dr[k].astype(F32)

        @pl.when(from_right)
        def _():
            put(ds.at[k], dr.at[total + i], t_s.at[k], t_r.at[total + i], d, z).wait_recv()
            out_t[rows, :] += dr[total + i].astype(F32)

    for copy in small_z:
        copy.wait_recv()
    out_s[...] = sk[...] + q4[0] + q4[1] + q4[2]
    sums.result(0, out_w)
    for copy in small + small_z:
        copy.wait_send()
    sums.drain(0)
    for k in range(total):
        for way in range(2):

            @pl.when(sends(k, way))
            def _():
                token(k, way).wait_send()


def finish(dqt, dk, dv, xt, dar, mixed_t, wd, dr1, vecs, bup):
    own, width = dr1.shape
    r = width // 8
    chunks = own // ROWS
    dma, vm = pltpu.SemaphoreType.DMA, pltpu.VMEM
    vmem = pl.BlockSpec(memory_space=pltpu.VMEM)
    block, sb = (r, width), (16, 128)
    return pl.pallas_call(
        finish_kernel,
        out_shape=(
            jax.ShapeDtypeStruct(block, F32),
            jax.ShapeDtypeStruct(sb, F32),
            jax.ShapeDtypeStruct((own, width), F32),
        ),
        in_specs=[vmem] * 10,
        out_specs=(vmem, vmem, vmem),
        scratch_shapes=[
            vm((width, own), BF16),
            vm((own, width), BF16),
            vm((own, width), BF16),
            vm((4, 4, 2) + block, BF16),
            vm((4, 2) + sb, F32),
            vm((4 * chunks, ROWS, width), BF16),
            vm((5 * chunks, ROWS, width), BF16),
            vm(sb, F32),
            vm((4,) + sb, F32),
            vm((2,) + sb, F32),
            vm(sb, F32),
            vm((2,) + sb, F32),
            vm(sb, F32),
            vm((3,) + sb, F32),
            *sum_buffers(1, block),
            *sum_semaphores(1),
            dma((4 * chunks,)),
            dma((5 * chunks,)),
            dma((6,)),
            dma((6,)),
        ],
        compiler_params=pltpu.CompilerParams(
            collective_id=1, has_side_effects=True, vmem_limit_bytes=VMEM_MAX
        ),
        name="finish",
    )(dqt, dk, dv, xt, dar, mixed_t, wd, dr1, vecs, bup)


def parts_of(z, own):
    sure = SHORT - own
    low = z < 2
    return (
        (jnp.where(low, 0, own - sure), sure, jnp.where(low, 0, SHORT)),
        (jnp.where(low, sure, 0), own - sure, jnp.where(z == 3, SHORT, 0)),
    )


def over_keys(z, part, start, total, act):
    window = total - SHORT
    for c in range(window // KEYS):
        act(pl.multiple_of(start + c * KEYS, KEYS))
    if part == 1:

        @pl.when((z == 1) | (z == 2))
        def _():
            for c in range(window // KEYS, total // KEYS):
                act(c * KEYS)


def aug_rows(top, r):
    return jnp.concatenate([top.astype(BF16), jnp.zeros((128 - 16, r), BF16)], axis=0)


def pick_rows(rows, r):
    index = lax.broadcasted_iota(jnp.int32, (16, r), 0)
    out = jnp.zeros((16, r), F32)
    for i, row in enumerate(rows):
        out = jnp.where(index == i, jnp.broadcast_to(row, (16, r)), out)
    return out


def split3(x):
    hi = x.astype(BF16).astype(F32)
    mid = (x - hi).astype(BF16).astype(F32)
    return hi, mid, x - hi - mid


def padded(head_rows, half, aug, r):
    zero = jnp.zeros((HD, r), BF16)
    pair = [head_rows, zero] if half == 0 else [zero, head_rows]
    return jnp.concatenate(pair + [aug], axis=0)


def attention_kernel(qt, k, vt, ka, ma, mixed_t, lse, s, m, l, acc):
    z = lax.axis_index("tp")
    own = qt.shape[1]
    for part, (row0, n, start) in enumerate(parts_of(z, own)):
        cols = pl.ds(pl.multiple_of(row0, 128), n)
        aug = aug_rows(pick_rows((ma[0:1, cols], ma[1:2, cols]), n), n)

        def one_pair(pair, carry):
            attend_pair(z, part, start, pair, cols, n, aug, qt, k, vt, ka, mixed_t, lse, s, m, l, acc)
            return carry

        lax.fori_loop(0, k.shape[1] // 128, one_pair, 0)


def attention(qt, k, vt, ka, ma):
    width, own = qt.shape
    total = k.shape[0]
    widest = max(SHORT - own, own - (SHORT - own))
    vm = pltpu.VMEM
    return pl.pallas_call(
        attention_kernel,
        out_shape=(
            jax.ShapeDtypeStruct((width, own), F32),
            jax.ShapeDtypeStruct((width // 128, 8, own), F32),
        ),
        in_specs=[pl.BlockSpec(memory_space=pltpu.VMEM)] * 5,
        out_specs=(pl.BlockSpec(memory_space=pltpu.VMEM),) * 2,
        scratch_shapes=[
            vm((2, total, widest), F32),
            vm((2, 1, widest), F32),
            vm((2, 1, widest), F32),
            vm((2, HD, widest), F32),
        ],
        compiler_params=pltpu.CompilerParams(vmem_limit_bytes=VMEM_MAX),
        name="attention",
    )(qt, k, vt, ka, ma)


def back_pair(z, pair, pause, qt, q, k, kt, v, ka, ma, mixed_t, lse, dmt, dm, dqt, dk, dv, dka, dva, dqa):
    own, total = qt.shape[1], k.shape[0]
    lanes = pl.ds(pl.multiple_of(pair * 128, 128), 128)
    dka[...] = jnp.zeros_like(dka)
    dva[...] = jnp.zeros_like(dva)
    for part, (row0, r, start) in enumerate(parts_of(z, own)):
        pause(part)
        cols = pl.ds(pl.multiple_of(row0, 128), r)
        qs, gs, qm, gm = [], [], [], []
        low = lax.broadcasted_iota(jnp.int32, (r, 128), 1) < HD
        for half in range(2):
            rows = pl.ds(pl.multiple_of(pair * 128 + half * HD, HD), HD)
            delta = jnp.sum(dmt[rows, cols].astype(F32) * mixed_t[rows, cols], axis=0, keepdims=True)
            total_log = lse[pair, half : half + 1, cols]
            q_aug = pick_rows((ma[0:1, cols], ma[1:2, cols]) + split3(-total_log), r)
            zero = jnp.zeros((1, r), F32)
            g_aug = pick_rows((zero, zero) + split3(-delta), r)
            qs.append(padded(qt[rows, cols], half, aug_rows(q_aug, r), r))
            gs.append(padded(dmt[rows, cols], half, aug_rows(g_aug, r), r))
            mine = low if half == 0 else jnp.logical_not(low)
            here = pl.ds(pl.multiple_of(row0, 128), r)
            qm.append(jnp.where(mine, q[here, lanes], jnp.zeros((), BF16)))
            gm.append(jnp.where(mine, dm[here, lanes], jnp.zeros((), BF16)))
            dqa[half, :, :r] = jnp.zeros((HD, r), F32)

        def step(key0):
            keys = pl.ds(key0, KEYS)
            k_left = jnp.concatenate([k[keys, lanes], ka[keys, :]], axis=1)
            v_left = jnp.concatenate([v[keys, lanes], ka[keys, :]], axis=1)
            for half in range(2):
                share = jnp.exp(dot(k_left, qs[half]))
                slope = (share * dot(v_left, gs[half])).astype(BF16)
                dva[keys, :] += dot(share.astype(BF16), gm[half])
                dka[keys, :] += dot(slope, qm[half])
                rows = pl.ds(pl.multiple_of(pair * 128 + half * HD, HD), HD)
                dqa[half, :, :r] += dot(kt[rows, keys], slope)

        over_keys(z, part, start, total, step)
        for half in range(2):
            rows = pl.ds(pl.multiple_of(pair * 128 + half * HD, HD), HD)
            dqt[rows, cols] = (dqa[half, :, :r] * HD ** (-0.5)).astype(BF16)
    dk[:, lanes] = dka[...].astype(BF16)
    dv[:, lanes] = dva[...].astype(BF16)


def attention_back_kernel(*refs):
    z = lax.axis_index("tp")

    def one_pair(pair, carry):
        back_pair(z, pair, lambda part: None, *refs)
        return carry

    lax.fori_loop(0, refs[2].shape[1] // 128, one_pair, 0)


def back_sums_kernel(qt, q, k, kt, v, ka, ma, mixed_t, lse, dmt, dm, *refs):
    g = (refs[0:4], refs[4:8])
    dqt, dk, dv, out_u, out_d, dka, dva, dqa, gk, *bufs = refs[8:]
    bufs, (gk_sem, *sems) = bufs[:8], bufs[8:]
    z, d, core, first, second = position()
    greet(z, d)

    def fetch(p, t):
        return pltpu.make_async_copy(g[p][t].at[:, core], gk.at[p, t], gk_sem.at[p, t])

    sums = Sums(
        z, d, core, second, first,
        lambda p, t: g[p][t].at[:, 1 - core],
        lambda p, t, at: up(gk.at[p, t, at]),
        lambda p, t: fetch(p, t).wait(),
        bufs, sems,
    )
    for p in range(2):
        for t in (3, 0, 2, 1):
            sums.one(p, t).start()
            fetch(p, t).start()

    def each(act, *units):
        def run():
            for p, t in units:
                act(p, t)

        return run

    def four(p, step):
        sums.at_four(p, step, range(4) if step == 0 else ())

    packs = [[(p, t) for t in (3, 0, 2, 1)] for p in range(2)]
    between = {
        (0, 1): each(sums.at_two, *packs[0]),
        (1, 0): each(sums.at_two, *packs[1]),
        (2, 1): each(sums.at_three, *packs[0][:2]),
        (3, 0): each(sums.at_three, *packs[0][2:]),
        (4, 1): lambda: four(0, 0),
        (5, 0): lambda: (each(sums.at_three, *packs[1][:2])(), four(0, 1)),
        (5, 1): lambda: (each(sums.at_three, *packs[1][2:])(), four(0, 2)),
    }

    def one_pair(pair, carry):
        def pause(part):
            for (i, at), run in between.items():
                if at == part:

                    @pl.when(pair == i)
                    def _():
                        run()

        back_pair(z, pair, pause, qt, q, k, kt, v, ka, ma, mixed_t, lse, dmt, dm, dqt, dk, dv, dka, dva, dqa)
        return carry

    lax.fori_loop(0, k.shape[1] // 128, one_pair, 0)
    for step in range(3):
        four(1, step)
    sums.result(0, out_u)
    sums.result(1, out_d)
    for p in range(2):
        sums.drain(p)


def back_shapes(own, total, width):
    widest = max(SHORT - own, own - (SHORT - own))
    vm = pltpu.VMEM
    outs = (
        jax.ShapeDtypeStruct((width, own), BF16),
        jax.ShapeDtypeStruct((total, width), BF16),
        jax.ShapeDtypeStruct((total, width), BF16),
    )
    return outs, [vm((total, 128), F32), vm((total, 128), F32), vm((2, HD, widest), F32)]


def attention_back(*args):
    (width, own), total = args[0].shape, args[2].shape[0]
    outs, scratch = back_shapes(own, total, width)
    return pl.pallas_call(
        attention_back_kernel,
        out_shape=outs,
        in_specs=[pl.BlockSpec(memory_space=pltpu.VMEM)] * 11,
        out_specs=(pl.BlockSpec(memory_space=pltpu.VMEM),) * 3,
        scratch_shapes=scratch,
        compiler_params=pltpu.CompilerParams(vmem_limit_bytes=VMEM_MAX),
        name="attention_back",
    )(*args)


def back_sums(args, gu, gd):
    (width, own), total = args[0].shape, args[2].shape[0]
    outs, scratch = back_shapes(own, total, width)
    block = (width // 8, gu[0].shape[1])
    g = [a.reshape((4, 2) + block) for a in (*gu, *gd)]
    vmem = pl.BlockSpec(memory_space=pltpu.VMEM)
    return pl.pallas_call(
        back_sums_kernel,
        out_shape=outs + (jax.ShapeDtypeStruct(block, F32),) * 2,
        in_specs=[vmem] * 11 + [pl.BlockSpec(memory_space=pl.ANY)] * 8,
        out_specs=(vmem,) * 5,
        scratch_shapes=[
            *scratch,
            pltpu.VMEM((2, 4, 4) + block, BF16),
            *sum_buffers(2, block),
            pltpu.SemaphoreType.DMA((2, 4)),
            *sum_semaphores(2),
        ],
        compiler_params=pltpu.CompilerParams(
            collective_id=2, has_side_effects=True, vmem_limit_bytes=VMEM_MAX
        ),
        name="back_sums",
    )(*args, *g)


def norms_kernel(
    tok, mixed_t, vec, bu, cot, wd, w,
    enc, dr1, dar, dm, dmt, vecs, wide, *refs,
):
    gu, gd = refs[0:4], refs[4:8]
    wo, wu, wn, mixed, y1r, hr, slope, du, dfr, y1t, dft, stage, w_sem, o_sem = refs[8:]
    own, width = tok.shape
    n_tp = wu.shape[0]
    loads = [[pltpu.make_async_copy(w.at[i, t], b.at[t], w_sem.at[i, t]) for t in range(n_tp)] for i, b in enumerate((wu, wn))]
    load_o = pltpu.make_async_copy(wd.at[3], wo, w_sem.at[2, 0])
    load_o.start()
    for t in range(n_tp):
        for i in range(2):
            loads[i][t].start()
    vecs[...] = jnp.zeros_like(vecs)
    half = own // 2

    def flip_mixed(i, carry):
        cols = pl.ds(pl.multiple_of(i * ROWS, ROWS), ROWS)
        mixed[cols, :] = mixed_t[:, cols].T.astype(BF16)
        return carry

    lax.fori_loop(0, own // ROWS, flip_mixed, 0)
    load_o.wait()
    for t in range(n_tp):
        for i in range(2):
            loads[i][t].wait()

    def row_tile(i, carry):
        rows = pl.ds(pl.multiple_of(i * half, 64), half)

        def add(index, value):
            vecs[index : index + 1, :] += jnp.sum(value, axis=0, keepdims=True)

        xhat1, inv1 = normalize_layer(tok[rows, :].astype(F32) + contract_last(mixed[rows, :], wo[...]) + vec[2:3, :])
        y1 = xhat1 * vec[3:4, :] + vec[4:5, :]
        y1b = y1.astype(BF16)
        y1r[rows, :] = y1b
        total = y1 + vec[5:6, :]
        for t in range(n_tp):
            u = dot(y1b, wu[t]) + bu[:, t * width : (t + 1) * width]
            below = 0.5 * (1.0 + lax.erf(u * SQRT_HALF))
            h = (u * below).astype(BF16)
            hr[t, rows, :] = h
            slope[t] = below + u * jnp.exp(-0.5 * u * u) * INV_ROOT_TAU
            total = total + contract_last(h, wn[t])
        xhat2, inv2 = normalize_layer(total)
        enc[rows, :] = (xhat2 * vec[6:7, :] + vec[7:8, :]).astype(BF16)
        grad = cot[rows, :].astype(F32)
        add(6, grad * xhat2)
        add(7, grad)
        dr2 = normalize_backward(grad, xhat2, inv2, vec[6:7, :])
        dfb = dr2.astype(BF16)
        dfr[rows, :] = dfb
        add(5, dfb.astype(F32))
        dy1 = dr2
        for t in range(n_tp):
            back = (dot(dfb, wn[t]) * slope[t]).astype(BF16)
            du[t, rows, :] = back
            dy1 = dy1 + contract_last(back, wu[t])
        add(3, dy1 * xhat1)
        add(4, dy1)
        first = normalize_backward(dy1, xhat1, inv1, vec[3:4, :])
        dr1[rows, :] = first
        dab = first.astype(BF16)
        dar[rows, :] = dab
        add(2, dab.astype(F32))
        dm[rows, :] = dot(dab, wo[...]).astype(BF16)
        return carry

    lax.fori_loop(0, 2, row_tile, 0)

    def flip(i, carry):
        cols = pl.ds(pl.multiple_of(i * ROWS, ROWS), ROWS)
        dft[:, cols] = dfr[cols, :].T
        y1t[:, cols] = y1r[cols, :].T
        dmt[:, cols] = dm[cols, :].T
        return carry

    lax.fori_loop(0, own // ROWS, flip, 0)
    tile = 256
    ones = jnp.ones((8, own), BF16)

    def store(i, t):
        return pltpu.make_async_copy(stage.at[i, t], (gd, gu)[i][t], o_sem.at[i, t])

    for t in range(n_tp):

        def one_tile(n, carry):
            lanes = pl.ds(pl.multiple_of(n * tile, tile), tile)
            stage[0, t, :, lanes] = dot(dft[...], hr[t, :, lanes]).astype(BF16)
            stage[1, t, :, lanes] = dot(y1t[...], du[t, :, lanes]).astype(BF16)
            wide[0:1, pl.ds(pl.multiple_of(t * width + n * tile, tile), tile)] = dot(ones, du[t, :, lanes])[0:1, :]
            return carry

        lax.fori_loop(0, width // tile, one_tile, 0)
        for i in range(2):
            store(i, t).start()
    for t in range(n_tp):
        for i in range(2):
            store(i, t).wait()


def norms(tok, mixed_t, vec, bu, cot, wd, w):
    own, width = tok.shape
    dma, vm = pltpu.SemaphoreType.DMA, pltpu.VMEM
    any_ = pl.BlockSpec(memory_space=pl.ANY)
    vmem = pl.BlockSpec(memory_space=pltpu.VMEM)
    shape = jax.ShapeDtypeStruct
    square = (width, width)
    return pl.pallas_call(
        norms_kernel,
        out_shape=(
            shape((own, width), BF16),
            shape((own, width), F32),
            shape((own, width), BF16),
            shape((own, width), BF16),
            shape((width, own), BF16),
            shape((8, width), F32),
            shape((1, 4 * width), F32),
        )
        + (shape(square, BF16),) * 8,
        in_specs=[vmem] * 5 + [any_] * 2,
        out_specs=(vmem,) * 7 + (any_,) * 8,
        scratch_shapes=[
            vm(square, BF16),
            vm((4,) + square, BF16),
            vm((4,) + square, BF16),
            vm((own, width), BF16),
            vm((own, width), BF16),
            vm((4, own, width), BF16),
            vm((4, own // 2, width), F32),
            vm((4, own, width), BF16),
            vm((own, width), BF16),
            vm((width, own), BF16),
            vm((width, own), BF16),
            vm((2, 4) + square, BF16),
            dma((3, 4)),
            dma((2, 4)),
        ],
        compiler_params=pltpu.CompilerParams(vmem_limit_bytes=VMEM_MAX),
        name="norms",
    )(tok, mixed_t, vec, bu, cot, wd, w)


def body(
    tokens, w_query, w_key, w_value, b_query, b_value, w_out, b_out, gain_attn, shift_attn,
    w_up, b_up, w_down, b_down, gain_ffn, shift_ffn, lengths, deal_order, cotangent,
):
    own, width = tokens.shape
    n_tp, n_dp = lax.axis_size("tp"), lax.axis_size("dp")
    z, g = lax.axis_index("tp"), lax.axis_index("dp")
    total = own * n_tp
    r, hw = w_query.shape
    direct = n_tp == 4 and n_dp == 8 and r % 16 == 0

    own_w = jnp.stack([jnp.concatenate([w_query, w_key, w_value, w_out], axis=1), w_up, w_down])
    vectors = (b_query, b_value, b_out, gain_attn, shift_attn, b_down, gain_ffn, shift_ffn, b_up)
    n_small = 8 * r + b_up.shape[0]
    if direct:
        line = jnp.arange(8, dtype=jnp.int32)[:, None]
        narrow = jnp.zeros((8, r), BF16)
        for i, a in enumerate(vectors[:8]):
            narrow = jnp.where(line == i, a[None, :], narrow)
        narrow = jnp.pad(narrow, ((0, 0), (0, 128 - r)))
        own_s = jnp.concatenate([narrow, jnp.pad(b_up.reshape(-1, 128), ((0, 5), (0, 0)))])
        w, vec, bu, xt, q, qt, k, v, kt, wd, ka, mixed_t, lse, ma = forward_all(lengths, deal_order, own_w, own_s, tokens)
        w = w.reshape(2, n_tp, width, w_up.shape[1])
        encoder_output, dr1, dar, dm, dmt, vecs, wide_sum, *gw = norms(tokens, mixed_t, vec, bu, cotangent, wd, w)
        args = (qt, q, k, kt, v, ka, ma, mixed_t, lse, dmt, dm)
        dqt, dk, dv, g_up, g_down = back_sums(args, gw[:4], gw[4:])
        a, gs, grad_tokens = finish(dqt, dk, dv, xt, dar, mixed_t, wd, dr1, vecs, wide_sum)
        gs = [gs[i, :r] for i in range(8)] + [gs[8:11].reshape(-1)]
    else:
        w = lax.all_gather(own_w, ("tp", "dp"), axis=0).reshape((n_tp, n_dp) + own_w.shape)
        w = jnp.moveaxis(w, 2, 0).reshape(3, n_tp, width, w_up.shape[1])
        s = lax.all_gather(jnp.concatenate(vectors), "dp", axis=0)
        x = lax.all_gather(tokens, "tp", axis=0, tiled=True)
        small = [s[:, i * r : (i + 1) * r].reshape(width).astype(F32) for i in range(8)]
        bq, bv, bo, g1, h1, bd, g2, h2 = small
        bu = s[:, 8 * r : n_small].reshape(-1).astype(F32)
        wq, wk, wv, wo = (
            w[0, :, :, i * hw : (i + 1) * hw].transpose(1, 0, 2).reshape(width, width) for i in range(4)
        )
        w = w[1:]
        q = (dot(tokens, wq) + bq).astype(BF16) * jnp.asarray(HD ** (-0.5), BF16)
        k = dot(x, wk).astype(BF16)
        v = (dot(x, wv) + bv).astype(BF16)
        qt, kt = q.T, k.T

        pair = lax.dynamic_slice_in_dim(deal_order, 2 * g, 1)
        first_len = jnp.sum(jnp.where(jnp.arange(lengths.shape[0], dtype=jnp.int32) == pair[0], lengths, 0))
        key_seg = jnp.arange(total, dtype=jnp.int32)[:, None] >= first_len
        lane = jnp.arange(128, dtype=jnp.int32)[None, :]
        ka = jnp.where(lane == 0, ~key_seg, jnp.where(lane == 1, key_seg, (lane >= 2) & (lane < 5))).astype(BF16)
        row_seg = (z * own + jnp.arange(own, dtype=jnp.int32))[None, :] >= first_len
        sub = jnp.arange(8, dtype=jnp.int32)[:, None]
        ma = jnp.where(((sub == 0) & row_seg) | ((sub == 1) & ~row_seg), MASKED, 0.0).astype(F32)

        mixed_t, lse = attention(qt, k, v.T, ka, ma)
        mixed = mixed_t.T.astype(BF16)
        first_residual = tokens.astype(F32) + contract_last(mixed, wo) + bo
        xhat1, inv1 = normalize_layer(first_residual)
        y1 = xhat1 * g1 + h1
        y1r = y1.astype(BF16)

        u = [dot(y1r, w[0, t]) + bu.reshape(n_tp, -1)[t] for t in range(n_tp)]
        hr = [jax.nn.gelu(a, approximate=False).astype(BF16) for a in u]
        ffn = sum(contract_last(hr[t], w[1, t]) for t in range(n_tp))
        xhat2, inv2 = normalize_layer(y1 + ffn + bd)
        encoder_output = (xhat2 * g2 + h2).astype(BF16)

        grad = cotangent.astype(F32)
        dr2 = normalize_backward(grad, xhat2, inv2, g2)
        dfr = dr2.astype(BF16)
        du = [(dot(dfr, w[1, t]) * gelu_slope(u[t])).astype(BF16) for t in range(n_tp)]
        dy1 = dr2 + sum(contract_last(du[t], w[0, t]) for t in range(n_tp))
        dr1 = normalize_backward(dy1, xhat1, inv1, g1)
        dar = dr1.astype(BF16)
        dm = dot(dar, wo).astype(BF16)
        gu = [contract_first(y1r, du[t]) for t in range(n_tp)]
        gd = [contract_first(dfr, hr[t]) for t in range(n_tp)]
        row_sums = [
            jnp.sum(dar, axis=0, dtype=F32),
            jnp.sum(dy1 * xhat1, axis=0),
            jnp.sum(dy1, axis=0),
            jnp.sum(dfr, axis=0, dtype=F32),
            jnp.sum(grad * xhat2, axis=0),
            jnp.sum(grad, axis=0),
        ]
        wide_sum = jnp.concatenate([jnp.sum(a, axis=0, dtype=F32) for a in du])
        back_args = (qt, q, k, kt, v, ka, ma, mixed_t, lse, dm.T, dm)
        dqt, dk, dv = attention_back(*back_args)
        dq = dqt.T
        base = dr1 + contract_last(dq, wq)
        far = contract_last(dk, wk) + contract_last(dv, wv)
        base = base + lax.dynamic_slice_in_dim(far, z * own, own)
        dt = far.astype(BF16)
        gq, gk, gv = contract_first(tokens, dq), contract_first(x, dk), contract_first(x, dv)
        go = contract_first(dar, mixed)
        ga = jnp.stack(
            [
                jnp.concatenate([m[:, t * hw : (t + 1) * hw] for m in (gq, gk, gv, go)], axis=1)
                for t in range(n_tp)
            ]
        )
        sums = [jnp.sum(dq, axis=0, dtype=F32), jnp.sum(dv, axis=0, dtype=F32)] + row_sums
        sums = [a.reshape(n_dp, r) for a in sums]
        sv = jnp.concatenate(sums + [wide_sum.reshape(n_dp, -1)], axis=1)
        grads = jnp.stack([ga, jnp.stack(gu), jnp.stack(gd)], axis=1).reshape(n_tp, 3, n_dp, r, -1)
        grads = jnp.moveaxis(grads, 1, 2).reshape(n_tp * n_dp, 3, r, -1)
        gw = lax.psum_scatter(grads, ("tp", "dp"), scatter_dimension=0, tiled=True)[0]
        gs = lax.psum_scatter(lax.psum(sv, "tp"), "dp", scatter_dimension=0, tiled=True)[0]
        others = jnp.where(jnp.arange(total)[:, None] // own == z, jnp.zeros((), BF16), dt)
        grad_tokens = base + lax.psum_scatter(others, "tp", scatter_dimension=0, tiled=True).astype(F32)
        gs = [gs[i * r : (i + 1) * r] for i in range(8)] + [gs[8 * r : n_small]]
        a, g_up, g_down = gw[0], gw[1], gw[2]
    return (
        encoder_output, grad_tokens,
        a[:, :hw], a[:, hw : 2 * hw], a[:, 2 * hw : 3 * hw], gs[0], gs[1],
        a[:, 3 * hw :], gs[2], gs[3], gs[4],
        g_up, gs[8], g_down, gs[5], gs[6], gs[7],
    )


def solution(mesh):
    rows, block, vector = P(("dp", "tp"), None), P("dp", "tp"), P("dp")
    in_specs = (
        rows, block, block, block, vector, vector, block, vector, vector, vector,
        block, vector, block, vector, vector, vector, P(), P(), rows,
    )
    out_specs = (
        rows, rows, block, block, block, vector, vector, block, vector, vector, vector,
        block, vector, block, vector, vector, vector,
    )
    return jax.shard_map(body, mesh=mesh, in_specs=in_specs, out_specs=out_specs, check_vma=False)
```

```python
import functools

import jax
import jax.numpy as jnp
from jax import lax
from jax.experimental import pallas as pl
from jax.experimental.pallas import tpu as pltpu
from jax.sharding import PartitionSpec as P

HD = 64
SHORT = 1024
EPS = 1e-05
SQRT_HALF = 0.7071067811865476
INV_ROOT_TAU = 0.3989422804014327
MASKED = -1e30
KEYS = 512
ROWS = 128
VMEM_MAX = 67043328
MESH = pl.DeviceIdType.MESH
F32 = jnp.float32
BF16 = jnp.bfloat16


def dot(left, right):
    return jnp.dot(left, right, preferred_element_type=F32)


def contract_last(left, right):
    return lax.dot_general(left, right, (((1,), (1,)), ((), ())), preferred_element_type=F32)


def contract_first(left, right):
    return lax.dot_general(left, right, (((0,), (0,)), ((), ())), preferred_element_type=F32)


def normalize_layer(resid):
    center = resid - jnp.mean(resid, axis=-1, keepdims=True)
    inverse_deviation = lax.rsqrt(jnp.mean(center * center, axis=-1, keepdims=True) + EPS)
    return (center * inverse_deviation, inverse_deviation)


def normalize_backward(output_gradient, xhat, inverse_deviation, gain):
    scaled_rows = output_gradient * gain
    return inverse_deviation * (
        scaled_rows
        - jnp.mean(scaled_rows, axis=-1, keepdims=True)
        - xhat * jnp.mean(scaled_rows * xhat, axis=-1, keepdims=True)
    )


def gelu_slope(pre_act):
    return (
        0.5 * (1.0 + lax.erf(pre_act * SQRT_HALF))
        + pre_act * jnp.exp(-0.5 * pre_act * pre_act) * INV_ROOT_TAU
    )


def position():
    z = lax.axis_index("tp")
    d = lax.axis_index("dp")
    core = lax.rem(d, 2)
    first = 2 + 2 * core
    second = 4 - 2 * core
    return z, d, core, first, second


def xor(d, mask):
    return d + mask * (1 - 2 * lax.rem(d // mask, 2))


def greet(z, d):
    barrier = pltpu.get_barrier_semaphore()
    for mask in (1, 2, 4):
        pl.semaphore_signal(barrier, inc=1, device_id=(xor(d, mask), z), device_id_type=MESH)
    for j in range(1, 4):
        pl.semaphore_signal(barrier, inc=1, device_id=(d, lax.rem(z + j, 4)), device_id_type=MESH)
    pl.semaphore_wait(barrier, 6)


def by_distance(z):
    low = z <= 1
    near = jnp.where(z == 0, 1, jnp.where(z == 1, 0, jnp.where(z == 2, 3, 2)))
    mid = jnp.where(low, 2, 1)
    far = jnp.where(low, 3, 0)
    return (z, near, mid, far)


def put(src, dst, send, recv, dp, tp):
    return pltpu.make_async_remote_copy(
        src_ref=src, dst_ref=dst, send_sem=send, recv_sem=recv, device_id=(dp, tp), device_id_type=MESH
    )


def forward_kernel(
    lengths, deal, own_w, own_s, own_t,
    w, vec, bu, xt_out, q_out, qt_out, k_out, v_out, kt_out, wd_out, ka_out, mixed_t, lse, ma,
    wa, s, x, xt, q, qt, k, v, kt, vt, wd, ka, sc, m, l, acc,
    wz_s, wz_r, wa_s, wa_r, wb_s, wb_r, wc_s, wc_r, tk_s, tk_r, sm_s, sm_r, lo_sem, arr_sem, out_sem,
):
    z, d, core, first, second = position()
    packs = own_w.shape[0]
    own, width = own_t.shape
    total = 4 * own
    hw = width // 4
    chunks = own // ROWS
    d1, d2 = xor(d, first), xor(d, second)
    d12 = xor(d1, second)
    pal = xor(d, 1)
    pd, pd1, pd2, pd12 = (xor(e, 1) for e in (d, d1, d2, d12))
    order = by_distance(z)
    first_len = lengths[deal[2 * d]]

    greet(z, d)

    def block(p, tt, e):
        return wa.at[tt, e] if p == 0 else w.at[p - 1, tt, e]

    def along_z(p, tt, src, act):
        dst = block(p, tt, d)
        right = put(src, dst, wz_s.at[0, p, tt], wz_r.at[p, tt], d, jnp.minimum(z + 1, 3))
        left = put(src, dst, wz_s.at[1, p, tt], wz_r.at[p, tt], d, jnp.maximum(z - 1, 0))

        @pl.when((tt <= z) & (z < 3))
        def _():
            act(right)

        @pl.when((tt >= z) & (z > 0))
        def _():
            act(left)

    def across(p, tt, src):
        dst = block(p, tt, d)
        return (
            put(src, dst, wa_s.at[p, tt], wa_r.at[p, tt], d1, z),
            put(src, dst, wb_s.at[p, tt, 0], wb_r.at[p, tt, 0], d2, z),
            put(src, dst, wc_s.at[p, tt, 0], wc_r.at[p, tt, 0], pal, z),
        )

    def after_first(p, tt):
        src = block(p, tt, d1)
        return (
            put(src, src, wb_s.at[p, tt, 1], wb_r.at[p, tt, 1], d2, z),
            put(src, src, wc_s.at[p, tt, 1], wc_r.at[p, tt, 1], pal, z),
        )

    def after_second(p, tt, i):
        src = block(p, tt, d2 if i == 0 else d12)
        return put(src, src, wc_s.at[p, tt, 2 + i], wc_r.at[p, tt, 2 + i], pal, z)

    def source(p, j):
        return own_w.at[p] if j == 0 else block(p, order[j], d)

    def arrive(ref, sem):
        put(ref, ref, arr_sem, sem, pal, z).wait_recv()

    def begin_z(p, j):
        if j > 0:
            arrive(block(p, order[j], d), wz_r.at[p, order[j]])
        along_z(p, order[j], source(p, j), lambda c: c.start())

    def begin_xy(p, j):
        for copy in across(p, order[j], source(p, j)):
            copy.start()

    def begin(p, j):
        begin_z(p, j)
        begin_xy(p, j)

    def relay_first(p, j):
        tt = order[j]
        arrive(block(p, tt, d1), wa_r.at[p, tt])
        for copy in after_first(p, tt):
            copy.start()

    def relay_second(p, j):
        tt = order[j]
        for i in range(2):
            arrive(block(p, tt, d2 if i == 0 else d12), wb_r.at[p, tt, i])
            after_second(p, tt, i).start()

    def from_pal(p):
        for tt in range(4):
            for i, e in enumerate((pd, pd2, pd1, pd12)):
                arrive(block(p, tt, e), wc_r.at[p, tt, i])

    def sent(p):
        for j in range(4):
            tt = order[j]
            along_z(p, tt, source(p, j), lambda c: c.wait_send())
            for copy in across(p, tt, source(p, j)) + after_first(p, tt):
                copy.wait_send()
            for i in range(2):
                after_second(p, tt, i).wait_send()

    def token_slice(o, i):
        return x.at[pl.ds(pl.multiple_of((o * chunks + i) * ROWS, ROWS), ROWS)]

    def token_hop(o, i, hop, step):
        src = own_t.at[pl.ds(i * ROWS, ROWS)] if hop == 0 else token_slice(o, i)
        way = 0 if step > 0 else 1
        return put(src, token_slice(o, i), tk_s.at[way, hop, i], tk_r.at[way, hop, i], d, jnp.clip(z + step, 0, 3))

    last = SHORT // ROWS

    def wanted(o, i, target, step):
        n = o * chunks + i
        if step > 0:
            return (target <= 2) | (n >= last)
        return (target >= 1) | (n < 4 * chunks - last)

    def chunk_ids(step):
        return list(range(chunks))[:: -step]

    def tokens(hop, step, act, which=slice(None)):
        o, target = z - step * hop, z + step
        valid = (o >= 0) & (o <= 3) & (target >= 0) & (target <= 3)
        for i in chunk_ids(step)[which]:

            @pl.when(valid & wanted(o, i, target, step))
            def _():
                act(token_hop(o, i, hop, step))

    def tokens_on(hop, step, onward):
        o, target = z - step * (hop + 1), z + step
        valid = (o >= 0) & (o <= 3) & (z - step >= 0) & (z - step <= 3)
        way = 0 if step > 0 else 1
        for i in chunk_ids(step):

            @pl.when(valid & wanted(o, i, z, step))
            def _():
                arrive(token_slice(jnp.clip(o, 0, 3), i), tk_r.at[way, hop, i])

            if onward:

                @pl.when(valid & (target >= 0) & (target <= 3) & wanted(o, i, target, step))
                def _():
                    token_hop(o, i, hop + 1, step).start()

    def small(stage):
        if stage == 0:
            return [
                put(own_s, s.at[d], sm_s.at[0], sm_r.at[0], d1, z),
                put(own_s, s.at[d], sm_s.at[1], sm_r.at[1], d2, z),
                put(own_s, s.at[d], sm_s.at[3], sm_r.at[3], pal, z),
            ]
        if stage == 1:
            return [
                put(s.at[d1], s.at[d1], sm_s.at[2], sm_r.at[2], d2, z),
                put(s.at[d1], s.at[d1], sm_s.at[4], sm_r.at[4], pal, z),
            ]
        return [
            put(s.at[d2], s.at[d2], sm_s.at[5], sm_r.at[5], pal, z),
            put(s.at[d12], s.at[d12], sm_s.at[6], sm_r.at[6], pal, z),
        ]

    def own_tokens(*which):
        for step in (1, -1):
            tokens(0, step, lambda c: c.start(), slice(*which))

    begin(0, 0)
    for copy in small(0):
        copy.start()
    own_tokens(0, 1)
    s[d] = own_s[...]
    wa[z, d] = own_w[0]
    mine = pl.ds(pl.multiple_of(z * own, ROWS), own)
    x[mine, :] = own_t[...]
    keep = pltpu.make_async_copy(own_w.at[pl.ds(1, packs - 1)], w.at[:, z, d], lo_sem)
    keep.start()

    @pl.when(z == 0)
    def _():
        x[total - SHORT :, :] = jnp.zeros((SHORT, width), BF16)
        xt[:, total - SHORT :] = jnp.zeros((width, SHORT), BF16)

    @pl.when(z == 3)
    def _():
        x[:SHORT, :] = jnp.zeros((SHORT, width), BF16)
        xt[:, :SHORT] = jnp.zeros((width, SHORT), BF16)

    middle = (z == 1) | (z == 2)
    begin(0, 1)
    relay_first(0, 0)
    for p in range(1, packs):
        begin_z(p, 0)
    begin(0, 2)
    relay_second(0, 0)
    relay_first(0, 1)
    own_tokens(1, 2)
    begin(0, 3)
    own_tokens(2, 3)
    relay_second(0, 1)
    relay_first(0, 2)
    begin_xy(1, 0)
    arrive(s.at[d1], sm_r.at[0])
    for copy in small(1):
        copy.start()
    relay_second(0, 2)
    relay_first(0, 3)
    for p in range(2, packs):
        begin_xy(p, 0)
    arrive(s.at[d2], sm_r.at[1])
    arrive(s.at[d12], sm_r.at[2])
    for copy in small(2):
        copy.start()
    for p in range(1, packs):
        begin(p, 1)

    @pl.when(middle)
    def _():
        for p in range(1, packs):
            begin(p, 2)

    own_tokens(3, chunks)
    lane = lax.broadcasted_iota(jnp.int32, (own, 128), 1)
    for i in range(4):
        late = lax.broadcasted_iota(jnp.int32, (own, 128), 0) + i * own >= first_len
        ones = jnp.where((lane >= 2) & (lane < 5), 1.0, 0.0)
        flags = jnp.where(lane == 0, jnp.where(late, 0.0, 1.0), jnp.where(lane == 1, jnp.where(late, 1.0, 0.0), ones))
        ka[pl.ds(i * own, own), :] = flags.astype(BF16)

    relay_second(0, 3)
    for i, e in enumerate((pd, pd2, pd1, pd12)):
        arrive(s.at[e], sm_r.at[3 + i])
    r = width // 8
    for e in range(8):
        piece = s[e].astype(F32)
        vec[0:8, e * r : (e + 1) * r] = piece[0:8, 0:r]
        for j in range(hw * 2 // 128):
            col = e * hw * 2 + j * 128
            bu[0:1, col : col + 128] = piece[8 + j : 9 + j, :]
    from_pal(0)
    for tt in range(4):
        rows = wa[tt].reshape(width, width)
        for i in range(4):
            wd[i, :, tt * hw : (tt + 1) * hw] = rows[:, i * hw : (i + 1) * hw]
    wd_copy = pltpu.make_async_copy(wd, wd_out, out_sem.at[0])
    wd_copy.start()

    tile = 256

    def q_tile(n, carry):
        lanes = pl.ds(pl.multiple_of(n * tile, tile), tile)
        rows = (dot(own_t[...], wd[0, :, lanes]) + vec[0:1, lanes]).astype(BF16) * jnp.asarray(HD ** (-0.5), BF16)
        q[:, lanes] = rows
        qt[lanes, :] = rows.T
        return carry

    def project(o):
        rows = pl.ds(pl.multiple_of(o * own, ROWS), own)

        def kv_tile(n, carry):
            lanes = pl.ds(pl.multiple_of(n * tile, tile), tile)
            keys = dot(x[rows, :], wd[1, :, lanes]).astype(BF16)
            k[rows, lanes] = keys
            kt[lanes, rows] = keys.T
            values = (dot(x[rows, :], wd[2, :, lanes]) + vec[1:2, lanes]).astype(BF16)
            v[rows, lanes] = values
            vt[lanes, rows] = values.T
            xt[lanes, rows] = x[rows, lanes].T
            return carry

        lax.fori_loop(0, width // tile, kv_tile, 0)

    def project_far():
        for step in (1, -1):
            tokens_on(1, step, False)
        project(jnp.where(z == 0, 2, jnp.where(z == 1, 3, z - 2)))

    lax.fori_loop(0, width // tile, q_tile, 0)
    project(z)
    for p in range(1, packs):
        relay_first(p, 0)
    for step in (1, -1):
        tokens_on(0, step, True)

    @pl.when(z > 0)
    def _():
        project(jnp.maximum(z - 1, 0))

    @pl.when(jnp.logical_not(middle))
    def _():
        for p in range(1, packs):
            begin(p, 2)

    for p in range(1, packs):
        relay_second(p, 0)
        relay_first(p, 1)

    @pl.when(z < 3)
    def _():
        project(jnp.minimum(z + 1, 3))

    @pl.when(jnp.logical_not(middle))
    def _():
        project_far()

    def both(act, j):
        def run():
            for p in range(1, packs):
                act(p, j)

        return run

    def last_block(inner):
        def run():
            @pl.when(middle if inner else jnp.logical_not(middle))
            def _():
                for p in range(1, packs):
                    begin(p, 3)

        return run

    between = {
        (0, 0): last_block(True),
        (0, 1): both(relay_second, 1),
        (0, 2): both(relay_first, 2),
        (0, 4): last_block(False),
        (0, 5): both(relay_second, 2),
        (1, 0): both(relay_first, 3),
        (1, 4): both(relay_second, 3),
    }
    late = lax.broadcasted_iota(jnp.int32, (8, own), 1) + z * own >= first_len
    sub = lax.broadcasted_iota(jnp.int32, (8, own), 0)
    away = jnp.where(sub == 0, jnp.where(late, MASKED, 0.0), jnp.where(sub == 1, jnp.where(late, 0.0, MASKED), 0.0))
    ma[...] = away
    outs = [
        pltpu.make_async_copy(a, b, out_sem.at[1 + i])
        for i, (a, b) in enumerate(
            ((xt, xt_out), (q, q_out), (qt, qt_out), (k, k_out), (v, v_out), (kt, kt_out), (ka, ka_out))
        )
    ]
    pairs = width // 128
    for part, (row0, n, start) in enumerate(parts_of(z, own)):
        if part == 1:

            @pl.when(middle)
            def _():
                project_far()

            for copy in outs:
                copy.start()
        cols = pl.ds(pl.multiple_of(row0, 128), n)
        late = lax.broadcasted_iota(jnp.int32, (1, n), 1) + (z * own + row0) >= first_len
        masks = (jnp.where(late, MASKED, 0.0), jnp.where(late, 0.0, MASKED))
        aug = aug_rows(pick_rows(masks, n), n)

        def one_pair(pair, carry):
            for (at, i), run in between.items():
                if at == part:

                    @pl.when(pair == i)
                    def _():
                        run()

            attend_pair(z, part, start, pair, cols, n, aug, qt, k, vt, ka, mixed_t, lse, sc, m, l, acc)
            return carry

        lax.fori_loop(0, pairs, one_pair, 0)

    for p in range(1, packs):
        from_pal(p)
    for stage in range(3):
        for copy in small(stage):
            copy.wait_send()
    for hop in range(2):
        for step in (1, -1):
            tokens(hop, step, lambda c: c.wait_send())
    for p in range(packs):
        sent(p)
    keep.wait()
    wd_copy.wait()
    for copy in outs:
        copy.wait()


def attend_pair(z, part, start, pair, cols, n, aug, qt, k, vt, ka, mixed_t, lse, s, m, l, acc):
    total = k.shape[0]
    lanes = pl.ds(pl.multiple_of(pair * 128, 128), 128)
    for half in range(2):
        m[half, :, :n] = jnp.full((1, n), MASKED, F32)
        l[half, :, :n] = jnp.zeros((1, n), F32)
        acc[half, :, :n] = jnp.zeros((HD, n), F32)
    qs = [padded(qt[pl.ds(pl.multiple_of(pair * 128 + half * HD, HD), HD), cols], half, aug, n) for half in range(2)]

    def scores(key0):
        keys = pl.ds(key0, KEYS)
        left = jnp.concatenate([k[keys, lanes], ka[keys, :]], axis=1)
        for half in range(2):
            score = dot(left, qs[half])
            s[half, keys, :n] = score
            m[half, :, :n] = jnp.maximum(m[half, :, :n], jnp.max(score, axis=0, keepdims=True))

    over_keys(z, part, start, total, scores)
    tops = [m[half, :, :n] for half in range(2)]

    def mix(key0):
        keys = pl.ds(key0, KEYS)
        for half in range(2):
            raised = jnp.exp(s[half, keys, :n] - tops[half])
            l[half, :, :n] += jnp.sum(raised, axis=0, keepdims=True)
            values = vt[pl.ds(pl.multiple_of(pair * 128 + half * HD, HD), HD), keys]
            acc[half, :, :n] += dot(values, raised.astype(BF16))

    over_keys(z, part, start, total, mix)
    for half in range(2):
        sums = l[half, :, :n]
        rows = pl.ds(pl.multiple_of(pair * 128 + half * HD, HD), HD)
        mixed_t[rows, cols] = acc[half, :, :n] / sums
        lse[pair, half : half + 1, cols] = tops[half] + jnp.log(sums)


def forward_all(lengths, deal, own_w, own_s, own_t):
    packs, r, c = own_w.shape
    own, width = own_t.shape
    total = 4 * own
    chunks = own // ROWS
    widest = max(SHORT - own, own - (SHORT - own))
    dma, vm = pltpu.SemaphoreType.DMA, pltpu.VMEM
    any_ = pl.BlockSpec(memory_space=pl.ANY)
    vmem = pl.BlockSpec(memory_space=pltpu.VMEM)
    smem = pl.BlockSpec(memory_space=pltpu.SMEM)
    shape = jax.ShapeDtypeStruct
    return pl.pallas_call(
        forward_kernel,
        out_shape=(
            shape((packs - 1, 4, 8, r, c), BF16),
            shape((8, width), F32),
            shape((1, 4 * c), F32),
            shape((width, total), BF16),
            shape((own, width), BF16),
            shape((width, own), BF16),
            shape((total, width), BF16),
            shape((total, width), BF16),
            shape((width, total), BF16),
            shape((4, width, width), BF16),
            shape((total, 128), BF16),
            shape((width, own), F32),
            shape((width // 128, 8, own), F32),
            shape((8, own), F32),
        ),
        in_specs=[smem, smem, vmem, vmem, vmem],
        out_specs=(any_, vmem, vmem) + (any_,) * 8 + (vmem, vmem, vmem),
        scratch_shapes=[
            vm((4, 8, r, c), BF16),
            vm((8, 16, 128), BF16),
            vm((total, width), BF16),
            vm((width, total), BF16),
            vm((own, width), BF16),
            vm((width, own), BF16),
            vm((total, width), BF16),
            vm((total, width), BF16),
            vm((width, total), BF16),
            vm((width, total), BF16),
            vm((4, width, width), BF16),
            vm((total, 128), BF16),
            vm((2, total, widest), F32),
            vm((2, 1, widest), F32),
            vm((2, 1, widest), F32),
            vm((2, HD, widest), F32),
            dma((2, packs, 4)),
            dma((packs, 4)),
            dma((packs, 4)),
            dma((packs, 4)),
            dma((packs, 4, 2)),
            dma((packs, 4, 2)),
            dma((packs, 4, 4)),
            dma((packs, 4, 4)),
            dma((2, 2, chunks)),
            dma((2, 2, chunks)),
            dma((7,)),
            dma((7,)),
            dma(()),
            dma(()),
            dma((8,)),
        ],
        compiler_params=pltpu.CompilerParams(
            collective_id=0, has_side_effects=True, vmem_limit_bytes=VMEM_MAX
        ),
        name="forward_all",
    )(lengths, deal, own_w, own_s, own_t)


def up(ref):
    return ref[...].astype(F32)


class Sums:
    def __init__(self, z, d, core, e_mask, f_mask, give, mine, ready, bufs, sems):
        self.z, self.d, self.give, self.mine, self.ready = z, d, give, mine, ready
        self.r1, self.b2, self.r2, self.b3, self.r3, self.s3, self.b4, self.r4 = bufs
        self.sems = sems
        self.xy = d // 2
        self.e, self.f = xor(d, e_mask) // 2, xor(d, f_mask) // 2
        self.ef = xor(xor(d, e_mask), f_mask) // 2
        self.d_e, self.d_f, self.pal = xor(d, e_mask), xor(d, f_mask), xor(d, 1)

    def one(self, p, t):
        return put(self.give(p, t), self.r1.at[p, t], self.sems[0].at[p, t], self.sems[1].at[p, t], self.pal, self.z)

    def two(self, p, t):
        return put(self.b2.at[p, t], self.r2.at[p, t], self.sems[2].at[p, t], self.sems[3].at[p, t], self.d_e, self.z)

    def three(self, p, t):
        return put(self.b3.at[p, t], self.r3.at[p, t], self.sems[4].at[p, t], self.sems[5].at[p, t], self.d_f, self.z)

    def four(self, p, t, way):
        to = jnp.minimum(self.z + 1, 3) if way == 0 else jnp.maximum(self.z - 1, 0)
        return put(
            self.b4.at[p, way, t], self.r4.at[p, way, t],
            self.sems[6].at[p, way, t], self.sems[7].at[p, way, t], self.d, to,
        )

    def at_two(self, p, t):
        self.ready(p, t)
        self.one(p, t).wait_recv()
        for i, x in enumerate((self.e, self.ef)):
            self.b2[p, t, i] = (self.mine(p, t, x) + up(self.r1.at[p, t, x])).astype(BF16)
        self.two(p, t).start()

    def at_three(self, p, t):
        self.two(p, t).wait_recv()
        f = self.f
        self.b3[p, t] = (self.mine(p, t, f) + up(self.r1.at[p, t, f]) + up(self.r2.at[p, t, 1])).astype(BF16)
        self.three(p, t).start()

    def at_kept(self, p, t):
        self.three(p, t).wait_recv()
        xy = self.xy
        self.s3[p, t] = self.mine(p, t, xy) + up(self.r1.at[p, t, xy]) + up(self.r2.at[p, t, 0]) + up(self.r3.at[p, t])

    def at_four(self, p, step, kept=(), ids=range(3)):
        kept = list(kept)
        for i in ids:
            for t, way in ((3 - i, 0), (i, 1)):
                if t in kept:
                    self.at_kept(p, t)
                    kept.remove(t)
            for t, way in ((3 - i, 0), (i, 1)):
                pos = step if way == 0 else 3 - step
                if not (t > pos if way == 0 else t < pos):
                    continue

                @pl.when(self.z == pos)
                def _():
                    if step == 0:
                        self.b4[p, way, t] = self.s3[p, t].astype(BF16)
                    else:
                        self.four(p, t, way).wait_recv()
                        self.b4[p, way, t] = (self.s3[p, t] + up(self.r4.at[p, way, t])).astype(BF16)
                    self.four(p, t, way).start()

    def result(self, p, out):
        z = self.z
        out[...] = self.s3[p, z]

        @pl.when(z > 0)
        def _():
            self.four(p, z, 0).wait_recv()
            out[...] += up(self.r4.at[p, 0, z])

        @pl.when(z < 3)
        def _():
            self.four(p, z, 1).wait_recv()
            out[...] += up(self.r4.at[p, 1, z])

    def drain(self, p):
        for t in range(4):
            self.one(p, t).wait_send()
            self.two(p, t).wait_send()
            self.three(p, t).wait_send()
            for way in range(2):

                @pl.when((t > self.z) if way == 0 else (t < self.z))
                def _():
                    self.four(p, t, way).wait_send()


def sum_buffers(packs, block):
    vm = pltpu.VMEM
    return [
        vm((packs, 4, 4) + block, BF16),
        vm((packs, 4, 2) + block, BF16),
        vm((packs, 4, 2) + block, BF16),
        vm((packs, 4) + block, BF16),
        vm((packs, 4) + block, BF16),
        vm((packs, 4) + block, F32),
        vm((packs, 2, 4) + block, BF16),
        vm((packs, 2, 4) + block, BF16),
    ]


def sum_semaphores(packs):
    dma = pltpu.SemaphoreType.DMA
    return [dma((packs, 4))] * 6 + [dma((packs, 2, 4))] * 2


def finish_kernel(
    dqt, dk_all, dv_all, xt_all, dar, mixed_all, wd_all, dr1_all, vecs, bup,
    out_w, out_s, out_t,
    xt, wd, dk, dv, mixed_t, dr1, ld_sem, sh_sem, dart, dq, mixed, gp, sv, ds, dr, sk, q1, q2, q3, c2, c3, q4,
    r1, b2, r2, b3, r3, s3, b4, r4,
    p1_s, p1_r, p2_s, p2_r, p3_s, p3_r, p4_s, p4_r, t_s, t_r, v_s, v_r,
):
    z, d, core, first, second = position()
    own, width = out_t.shape
    chunks = own // ROWS
    total = 4 * chunks
    edge = SHORT // ROWS
    hw = width // 4
    r = width // 8
    load_w = pltpu.make_async_copy(wd_all.at[pl.ds(0, 3)], wd, ld_sem.at[0])
    load_x = pltpu.make_async_copy(xt_all, xt, ld_sem.at[1])
    load_m = pltpu.make_async_copy(mixed_all, mixed_t, ld_sem.at[2])
    load_r = pltpu.make_async_copy(dr1_all, dr1, ld_sem.at[3])

    def pick(a, b, c, e):
        return jnp.where(z == 0, a, jnp.where(z == 1, b, jnp.where(z == 2, c, e)))

    shards = [pick(*o) for o in ((2, 3, 0, 1), (1, 2, 1, 2), (3, 0, 3, 0), (0, 1, 2, 3))]
    load_s = []
    for j, o in enumerate(shards):
        rows = pl.ds(pl.multiple_of(o * own, ROWS), own)
        load_s.append(
            [
                pltpu.make_async_copy(a.at[rows], b.at[rows], sh_sem.at[i, j])
                for i, (a, b) in enumerate(((dk_all, dk), (dv_all, dv)))
            ]
        )
    for copy in [load_w] + load_s[0] + [load_m, load_x] + load_s[1] + load_s[2] + load_s[3] + [load_r]:
        copy.start()
    greet(z, d)

    def token(k, way):
        to = jnp.minimum(z + 1, 3) if way == 0 else jnp.maximum(z - 1, 0)
        slot = k if way == 0 else jnp.where(k // chunks == to, total + k % chunks, k)
        return put(ds.at[k], dr.at[slot], t_s.at[k], t_r.at[slot], d, to)

    def token_in(k, way):
        slot = k if way == 0 else jnp.where(k // chunks == z, total + k % chunks, k)
        return put(ds.at[k], dr.at[slot], t_s.at[k], t_r.at[slot], d, z), slot

    def sends(k, way):
        o = k // chunks
        if way == 0:
            low = jnp.where(k < total - edge, 0, 1)
            return (z >= low) & (z < o) & (o > low)
        high = jnp.where(k >= edge, 3, 2)
        return (z <= high) & (z > o) & (o < high)

    def starts(k, way):
        if way == 0:
            return z == jnp.where(k < total - edge, 0, 1)
        return z == jnp.where(k >= edge, 3, 2)

    tile = 256

    def far_shard(o, mine):
        rows = pl.ds(pl.multiple_of(o * own, ROWS), own)

        def one_tile(n, carry):
            lanes = pl.ds(pl.multiple_of(n * tile, tile), tile)
            far = contract_last(dk[rows, :], wd[1, lanes, :]) + contract_last(dv[rows, :], wd[2, lanes, :])
            if mine:
                out_t[:, lanes] = dr1[:, lanes] + far
            else:
                ds[pl.ds(o * chunks, chunks), :, lanes] = far.reshape(chunks, ROWS, tile).astype(BF16)
            return carry

        lax.fori_loop(0, width // tile, one_tile, 0)

    def far_and_send(j):
        o = shards[j]

        @pl.when((j < 2) | (z == 1) | (z == 2))
        def _():
            far_shard(o, False)

        for i in range(chunks):
            for way in range(2):
                k = o * chunks + i

                @pl.when(sends(k, way) & starts(k, way))
                def _():
                    token(k, way).start()

    for copy in [load_w] + load_s[0]:
        copy.wait()
    far_and_send(0)
    load_m.wait()

    right_order = [k for o in (3, 2, 1) for k in range(o * chunks, (o + 1) * chunks)]
    left_order = [total - 1 - k for k in right_order]

    def forward_tokens(at):
        for k, way in [(k, 0) for k in right_order] + [(k, 1) for k in left_order]:
            pos = at if way == 0 else 3 - at
            passes = (at < k // chunks) if way == 0 else (3 - at > k // chunks)
            begins = (0 if k < total - edge else 1) if way == 0 else (3 if k >= edge else 2)
            if not passes or (begins >= pos if way == 0 else begins <= pos):
                continue

            @pl.when(z == pos)
            def _():
                got, slot = token_in(k, way)
                got.wait_recv()
                ds[k] = (ds[k].astype(F32) + dr[slot].astype(F32)).astype(BF16)
                token(k, way).start()

    def flip_own(i, carry):
        cols = pl.ds(pl.multiple_of(i * ROWS, ROWS), ROWS)
        dart[:, cols] = dar[cols, :].T
        dq[cols, :] = dqt[:, cols].T
        mixed[cols, :] = mixed_t[:, cols].T.astype(BF16)
        return carry

    lax.fori_loop(0, chunks, flip_own, 0)

    def give(p, t):
        return gp.at[t, :, 1 - core]

    def mine(p, t, at):
        return gp[t, at, core].astype(F32)

    sums = Sums(
        z, d, core, second, first, give, mine, lambda p, t: None,
        (r1, b2, r2, b3, r3, s3, b4, r4), (p1_s, p1_r, p2_s, p2_r, p3_s, p3_r, p4_s, p4_r),
    )
    here = pl.ds(pl.multiple_of(z * own, ROWS), own)
    half = width // 2

    def weights(th):
        lanes = pl.ds(th * half, half)

        def rows_of(m, carry):
            rows = pl.ds(pl.multiple_of(m * half, ROWS), half)
            parts = (
                lambda: dot(xt[rows, here], dq[:, lanes]),
                lambda: dot(xt[rows, :], dk[:, lanes]),
                lambda: dot(xt[rows, :], dv[:, lanes]),
                lambda: dot(dart[rows, :], mixed[:, lanes]),
            )
            for i, part in enumerate(parts):
                got = part().astype(BF16)
                for h in range(2):
                    block = got[:, h * hw : (h + 1) * hw].reshape(2, 2, r, hw)
                    gp[2 * th + h, pl.ds(2 * m, 2), :, :, i * hw : (i + 1) * hw] = block
            return carry

        lax.fori_loop(0, 2, rows_of, 0)
        for t in (2 * th, 2 * th + 1):
            sums.one(0, t).start()

    for copy in [load_x, load_r] + load_s[1] + load_s[2] + load_s[3]:
        copy.wait()
    weights(1)
    weights(0)
    for t in (3, 2):
        sums.at_two(0, t)
    far_and_send(1)
    forward_tokens(1)
    for t in (0, 1):
        sums.at_two(0, t)
    far_and_send(2)
    forward_tokens(2)

    ones = jnp.ones((8, 4 * own), BF16)
    index = lax.broadcasted_iota(jnp.int32, (8, width), 0)
    small_rows = jnp.where(index == 0, dot(ones[:, :own], dq[...]), jnp.where(index == 1, dot(ones, dv[...]), vecs[...]))
    pad = jnp.zeros((8, 128 - r), F32)
    for i in range(8):
        sv[i // 2, i % 2, 0:8, :] = jnp.concatenate([small_rows[:, i * r : (i + 1) * r], pad], axis=1)
        wide = [bup[:, (i * 3 + j) * 128 : (i * 3 + j + 1) * 128] for j in range(3)]
        sv[i // 2, i % 2, 8:16, :] = jnp.concatenate(wide + [jnp.zeros((5, 128), F32)], axis=0)
    small = [
        put(sv.at[:, 1 - core], q1, v_s.at[0], v_r.at[0], sums.pal, z),
        put(c2, q2, v_s.at[1], v_r.at[1], sums.d_e, z),
        put(c3, q3, v_s.at[2], v_r.at[2], sums.d_f, z),
    ]
    small_z = [
        put(sk, q4.at[j - 1], v_s.at[2 + j], v_r.at[2 + j], d, lax.rem(z + j, 4)) for j in range(1, 4)
    ]
    small[0].start()
    far_shard(z, True)

    def query_tile(n, carry):
        lanes = pl.ds(pl.multiple_of(n * tile, tile), tile)
        out_t[:, lanes] += contract_last(dq[...], wd[0, lanes, :])
        return carry

    lax.fori_loop(0, width // tile, query_tile, 0)
    small[0].wait_recv()
    for i, at in enumerate((sums.e, sums.ef)):
        c2[i] = sv[at, core] + q1[at]
    small[1].start()
    for t in (3, 2, 0, 1):
        sums.at_three(0, t)
    small[1].wait_recv()
    c3[...] = sv[sums.f, core] + q1[sums.f] + q2[1]
    small[2].start()
    for step in range(3):
        sums.at_four(0, step, range(4) if step == 0 else ())
        if step == 0:
            small[2].wait_recv()
            sk[...] = sv[sums.xy, core] + q1[sums.xy] + q2[0] + q3[...]
            for copy in small_z:
                copy.start()
    for i in range(chunks):
        k = z * chunks + i
        rows = pl.ds(i * ROWS, ROWS)
        from_left = (z > 0) & ((z == 1) & (k < total - edge) | (z > 1))
        from_right = (z < 3) & ((z == 2) & (k >= edge) | (z < 2))

        @pl.when(from_left)
        def _():
            put(ds.at[k], dr.at[k], t_s.at[k], t_r.at[k], d, z).wait_recv()
            out_t[rows, :] += dr[k].astype(F32)

        @pl.when(from_right)
        def _():
            put(ds.at[k], dr.at[total + i], t_s.at[k], t_r.at[total + i], d, z).wait_recv()
            out_t[rows, :] += dr[total + i].astype(F32)

    for copy in small_z:
        copy.wait_recv()
    out_s[...] = sk[...] + q4[0] + q4[1] + q4[2]
    sums.result(0, out_w)
    for copy in small + small_z:
        copy.wait_send()
    sums.drain(0)
    for k in range(total):
        for way in range(2):

            @pl.when(sends(k, way))
            def _():
                token(k, way).wait_send()


def finish(dqt, dk, dv, xt, dar, mixed_t, wd, dr1, vecs, bup):
    own, width = dr1.shape
    r = width // 8
    chunks = own // ROWS
    dma, vm = pltpu.SemaphoreType.DMA, pltpu.VMEM
    vmem = pl.BlockSpec(memory_space=pltpu.VMEM)
    any_ = pl.BlockSpec(memory_space=pl.ANY)
    block, sb = (r, width), (16, 128)
    return pl.pallas_call(
        finish_kernel,
        out_shape=(
            jax.ShapeDtypeStruct(block, F32),
            jax.ShapeDtypeStruct(sb, F32),
            jax.ShapeDtypeStruct((own, width), F32),
        ),
        in_specs=[vmem] + [any_] * 3 + [vmem] + [any_] * 3 + [vmem] * 2,
        out_specs=(vmem, vmem, vmem),
        scratch_shapes=[
            vm((width, 4 * own), BF16),
            vm((3, width, width), BF16),
            vm((4 * own, width), BF16),
            vm((4 * own, width), BF16),
            vm((width, own), F32),
            vm((own, width), F32),
            dma((4,)),
            dma((2, 4)),
            vm((width, own), BF16),
            vm((own, width), BF16),
            vm((own, width), BF16),
            vm((4, 4, 2) + block, BF16),
            vm((4, 2) + sb, F32),
            vm((4 * chunks, ROWS, width), BF16),
            vm((5 * chunks, ROWS, width), BF16),
            vm(sb, F32),
            vm((4,) + sb, F32),
            vm((2,) + sb, F32),
            vm(sb, F32),
            vm((2,) + sb, F32),
            vm(sb, F32),
            vm((3,) + sb, F32),
            *sum_buffers(1, block),
            *sum_semaphores(1),
            dma((4 * chunks,)),
            dma((5 * chunks,)),
            dma((6,)),
            dma((6,)),
        ],
        compiler_params=pltpu.CompilerParams(
            collective_id=1, has_side_effects=True, vmem_limit_bytes=VMEM_MAX
        ),
        name="finish",
    )(dqt, dk, dv, xt, dar, mixed_t, wd, dr1, vecs, bup)


def parts_of(z, own):
    sure = SHORT - own
    low = z < 2
    return (
        (jnp.where(low, 0, own - sure), sure, jnp.where(low, 0, SHORT)),
        (jnp.where(low, sure, 0), own - sure, jnp.where(z == 3, SHORT, 0)),
    )


def over_keys(z, part, start, total, act):
    window = total - SHORT
    for c in range(window // KEYS):
        act(pl.multiple_of(start + c * KEYS, KEYS))
    if part == 1:

        @pl.when((z == 1) | (z == 2))
        def _():
            for c in range(window // KEYS, total // KEYS):
                act(c * KEYS)


def aug_rows(top, r):
    return jnp.concatenate([top.astype(BF16), jnp.zeros((128 - 16, r), BF16)], axis=0)


def pick_rows(rows, r):
    index = lax.broadcasted_iota(jnp.int32, (16, r), 0)
    out = jnp.zeros((16, r), F32)
    for i, row in enumerate(rows):
        out = jnp.where(index == i, jnp.broadcast_to(row, (16, r)), out)
    return out


def split3(x):
    hi = x.astype(BF16).astype(F32)
    mid = (x - hi).astype(BF16).astype(F32)
    return hi, mid, x - hi - mid


def padded(head_rows, half, aug, r):
    zero = jnp.zeros((HD, r), BF16)
    pair = [head_rows, zero] if half == 0 else [zero, head_rows]
    return jnp.concatenate(pair + [aug], axis=0)


def attention_kernel(qt, k, vt, ka, ma, mixed_t, lse, s, m, l, acc):
    z = lax.axis_index("tp")
    own = qt.shape[1]
    for part, (row0, n, start) in enumerate(parts_of(z, own)):
        cols = pl.ds(pl.multiple_of(row0, 128), n)
        aug = aug_rows(pick_rows((ma[0:1, cols], ma[1:2, cols]), n), n)

        def one_pair(pair, carry):
            attend_pair(z, part, start, pair, cols, n, aug, qt, k, vt, ka, mixed_t, lse, s, m, l, acc)
            return carry

        lax.fori_loop(0, k.shape[1] // 128, one_pair, 0)


def attention(qt, k, vt, ka, ma):
    width, own = qt.shape
    total = k.shape[0]
    widest = max(SHORT - own, own - (SHORT - own))
    vm = pltpu.VMEM
    return pl.pallas_call(
        attention_kernel,
        out_shape=(
            jax.ShapeDtypeStruct((width, own), F32),
            jax.ShapeDtypeStruct((width // 128, 8, own), F32),
        ),
        in_specs=[pl.BlockSpec(memory_space=pltpu.VMEM)] * 5,
        out_specs=(pl.BlockSpec(memory_space=pltpu.VMEM),) * 2,
        scratch_shapes=[
            vm((2, total, widest), F32),
            vm((2, 1, widest), F32),
            vm((2, 1, widest), F32),
            vm((2, HD, widest), F32),
        ],
        compiler_params=pltpu.CompilerParams(vmem_limit_bytes=VMEM_MAX),
        name="attention",
    )(qt, k, vt, ka, ma)


def back_pair(z, pair, pause, qt, q, k, kt, v, ka, ma, mixed_t, lse, dmt, dm, dqt, dk, dv, dka, dva, dqa):
    own, total = qt.shape[1], k.shape[0]
    lanes = pl.ds(pl.multiple_of(pair * 128, 128), 128)
    dka[...] = jnp.zeros_like(dka)
    dva[...] = jnp.zeros_like(dva)
    for part, (row0, r, start) in enumerate(parts_of(z, own)):
        pause(part)
        cols = pl.ds(pl.multiple_of(row0, 128), r)
        qs, gs, qm, gm = [], [], [], []
        low = lax.broadcasted_iota(jnp.int32, (r, 128), 1) < HD
        for half in range(2):
            rows = pl.ds(pl.multiple_of(pair * 128 + half * HD, HD), HD)
            delta = jnp.sum(dmt[rows, cols].astype(F32) * mixed_t[rows, cols], axis=0, keepdims=True)
            total_log = lse[pair, half : half + 1, cols]
            q_aug = pick_rows((ma[0:1, cols], ma[1:2, cols]) + split3(-total_log), r)
            zero = jnp.zeros((1, r), F32)
            g_aug = pick_rows((zero, zero) + split3(-delta), r)
            qs.append(padded(qt[rows, cols], half, aug_rows(q_aug, r), r))
            gs.append(padded(dmt[rows, cols], half, aug_rows(g_aug, r), r))
            mine = low if half == 0 else jnp.logical_not(low)
            here = pl.ds(pl.multiple_of(row0, 128), r)
            qm.append(jnp.where(mine, q[here, lanes], jnp.zeros((), BF16)))
            gm.append(jnp.where(mine, dm[here, lanes], jnp.zeros((), BF16)))
            dqa[half, :, :r] = jnp.zeros((HD, r), F32)

        def step(key0):
            keys = pl.ds(key0, KEYS)
            k_left = jnp.concatenate([k[keys, lanes], ka[keys, :]], axis=1)
            v_left = jnp.concatenate([v[keys, lanes], ka[keys, :]], axis=1)
            for half in range(2):
                share = jnp.exp(dot(k_left, qs[half]))
                slope = (share * dot(v_left, gs[half])).astype(BF16)
                dva[keys, :] += dot(share.astype(BF16), gm[half])
                dka[keys, :] += dot(slope, qm[half])
                rows = pl.ds(pl.multiple_of(pair * 128 + half * HD, HD), HD)
                dqa[half, :, :r] += dot(kt[rows, keys], slope)

        over_keys(z, part, start, total, step)
        for half in range(2):
            rows = pl.ds(pl.multiple_of(pair * 128 + half * HD, HD), HD)
            dqt[rows, cols] = (dqa[half, :, :r] * HD ** (-0.5)).astype(BF16)
    dk[:, lanes] = dka[...].astype(BF16)
    dv[:, lanes] = dva[...].astype(BF16)


def attention_back_kernel(*refs):
    z = lax.axis_index("tp")

    def one_pair(pair, carry):
        back_pair(z, pair, lambda part: None, *refs)
        return carry

    lax.fori_loop(0, refs[2].shape[1] // 128, one_pair, 0)


def back_sums_kernel(qt, q, k_all, kt_all, v_all, ka, ma, mixed_t, lse, dmt, dm, *refs):
    g = (refs[0:4], refs[4:8])
    dqt, dk_out, dv_out, out_u, out_d, dka, dva, dqa, k, kt, v, dk, dv, kv_sem, gk, *bufs = refs[8:]
    bufs, (gk_sem, *sems) = bufs[:8], bufs[8:]
    z, d, core, first, second = position()
    pairs = k.shape[1] // 128

    def operands(pair):
        lanes = pl.ds(pl.multiple_of(pair * 128, 128), 128)
        return (
            pltpu.make_async_copy(k_all.at[:, lanes], k.at[:, lanes], kv_sem.at[0, pair]),
            pltpu.make_async_copy(v_all.at[:, lanes], v.at[:, lanes], kv_sem.at[1, pair]),
            pltpu.make_async_copy(kt_all.at[lanes, :], kt.at[lanes, :], kv_sem.at[2, pair]),
        )

    def results(pair):
        lanes = pl.ds(pl.multiple_of(pair * 128, 128), 128)
        return (
            pltpu.make_async_copy(dk.at[:, lanes], dk_out.at[:, lanes], kv_sem.at[3, pair]),
            pltpu.make_async_copy(dv.at[:, lanes], dv_out.at[:, lanes], kv_sem.at[4, pair]),
        )

    for copy in operands(0):
        copy.start()
    greet(z, d)

    def fetch(p, t):
        return pltpu.make_async_copy(g[p][t].at[:, core], gk.at[p, t], gk_sem.at[p, t])

    sums = Sums(
        z, d, core, second, first,
        lambda p, t: g[p][t].at[:, 1 - core],
        lambda p, t, at: up(gk.at[p, t, at]),
        lambda p, t: fetch(p, t).wait(),
        bufs, sems,
    )
    for p in range(2):
        for t in (3, 0, 2, 1):
            sums.one(p, t).start()
            fetch(p, t).start()
    for pair in range(1, pairs):
        for copy in operands(pair):
            copy.start()

    def each(act, *units):
        def run():
            for p, t in units:
                act(p, t)

        return run

    def four(p, step, ids=range(3)):
        sums.at_four(p, step, range(4) if step == 0 else (), ids)

    packs = [[(p, t) for t in (3, 0, 2, 1)] for p in range(2)]
    between = {
        (0, 1): each(sums.at_two, *packs[0]),
        (1, 0): each(sums.at_two, *packs[1]),
        (2, 0): each(sums.at_three, *packs[0][:2]),
        (2, 1): each(sums.at_three, *packs[0][2:]),
        (3, 1): lambda: four(0, 0),
        (4, 0): each(sums.at_three, *packs[1][:2]),
        (4, 1): lambda: four(0, 1),
        (5, 0): each(sums.at_three, *packs[1][2:]),
        (5, 1): lambda: (four(0, 2), four(1, 0, (0,))),
    }

    def one_pair(pair, carry):
        def pause(part):
            for (i, at), run in between.items():
                if at == part:

                    @pl.when(pair == i)
                    def _():
                        run()

        for copy in operands(pair):
            copy.wait()
        back_pair(z, pair, pause, qt, q, k, kt, v, ka, ma, mixed_t, lse, dmt, dm, dqt, dk, dv, dka, dva, dqa)
        for copy in results(pair):
            copy.start()
        return carry

    lax.fori_loop(0, k.shape[1] // 128, one_pair, 0)
    for step, ids in ((1, (0,)), (0, (1, 2)), (1, (1, 2)), (2, (0, 1, 2))):
        sums.at_four(1, step, (2, 1) if step == 0 else (), ids)
    for pair in range(pairs):
        for copy in results(pair):
            copy.wait()
    sums.result(0, out_u)
    sums.result(1, out_d)
    for p in range(2):
        sums.drain(p)


def back_shapes(own, total, width):
    widest = max(SHORT - own, own - (SHORT - own))
    vm = pltpu.VMEM
    outs = (
        jax.ShapeDtypeStruct((width, own), BF16),
        jax.ShapeDtypeStruct((total, width), BF16),
        jax.ShapeDtypeStruct((total, width), BF16),
    )
    return outs, [vm((total, 128), F32), vm((total, 128), F32), vm((2, HD, widest), F32)]


def attention_back(*args):
    (width, own), total = args[0].shape, args[2].shape[0]
    outs, scratch = back_shapes(own, total, width)
    return pl.pallas_call(
        attention_back_kernel,
        out_shape=outs,
        in_specs=[pl.BlockSpec(memory_space=pltpu.VMEM)] * 11,
        out_specs=(pl.BlockSpec(memory_space=pltpu.VMEM),) * 3,
        scratch_shapes=scratch,
        compiler_params=pltpu.CompilerParams(vmem_limit_bytes=VMEM_MAX),
        name="attention_back",
    )(*args)


def back_sums(args, gu, gd):
    (width, own), total = args[0].shape, args[2].shape[0]
    outs, scratch = back_shapes(own, total, width)
    block = (width // 8, gu[0].shape[1])
    g = [a.reshape((4, 2) + block) for a in (*gu, *gd)]
    vmem = pl.BlockSpec(memory_space=pltpu.VMEM)
    any_ = pl.BlockSpec(memory_space=pl.ANY)
    return pl.pallas_call(
        back_sums_kernel,
        out_shape=outs + (jax.ShapeDtypeStruct(block, F32),) * 2,
        in_specs=[vmem] * 2 + [any_] * 3 + [vmem] * 6 + [any_] * 8,
        out_specs=(vmem, any_, any_, vmem, vmem),
        scratch_shapes=[
            *scratch,
            pltpu.VMEM((total, width), BF16),
            pltpu.VMEM((width, total), BF16),
            pltpu.VMEM((total, width), BF16),
            pltpu.VMEM((total, width), BF16),
            pltpu.VMEM((total, width), BF16),
            pltpu.SemaphoreType.DMA((5, width // 128)),
            pltpu.VMEM((2, 4, 4) + block, BF16),
            *sum_buffers(2, block),
            pltpu.SemaphoreType.DMA((2, 4)),
            *sum_semaphores(2),
        ],
        compiler_params=pltpu.CompilerParams(
            collective_id=2, has_side_effects=True, vmem_limit_bytes=VMEM_MAX
        ),
        name="back_sums",
    )(*args, *g)


def norms_kernel(
    tok, mixed_t, vec, bu, cot, wd, w,
    enc, dr1, dar, dm, dmt, vecs, wide, *refs,
):
    gu, gd = refs[0:4], refs[4:8]
    wo, wu, wn, mixed, y1r, hr, slope, du, dfr, y1t, dft, stage, w_sem, o_sem = refs[8:]
    own, width = tok.shape
    n_tp = wu.shape[0]
    loads = [[pltpu.make_async_copy(w.at[i, t], b.at[t], w_sem.at[i, t]) for t in range(n_tp)] for i, b in enumerate((wu, wn))]
    load_o = pltpu.make_async_copy(wd.at[3], wo, w_sem.at[2, 0])
    load_o.start()
    for t in range(n_tp):
        for i in range(2):
            loads[i][t].start()
    vecs[...] = jnp.zeros_like(vecs)
    half = own // 2

    def flip_mixed(i, carry):
        cols = pl.ds(pl.multiple_of(i * ROWS, ROWS), ROWS)
        mixed[cols, :] = mixed_t[:, cols].T.astype(BF16)
        return carry

    lax.fori_loop(0, own // ROWS, flip_mixed, 0)
    load_o.wait()

    def row_tile(i, carry):
        rows = pl.ds(pl.multiple_of(i * half, 64), half)

        def add(index, value):
            vecs[index : index + 1, :] += jnp.sum(value, axis=0, keepdims=True)

        xhat1, inv1 = normalize_layer(tok[rows, :].astype(F32) + contract_last(mixed[rows, :], wo[...]) + vec[2:3, :])
        y1 = xhat1 * vec[3:4, :] + vec[4:5, :]
        y1b = y1.astype(BF16)
        y1r[rows, :] = y1b
        total = y1 + vec[5:6, :]

        @pl.when(i == 0)
        def _():
            for t in range(n_tp):
                for j in range(2):
                    loads[j][t].wait()

        for t in range(n_tp):
            u = dot(y1b, wu[t]) + bu[:, t * width : (t + 1) * width]
            below = 0.5 * (1.0 + lax.erf(u * SQRT_HALF))
            h = (u * below).astype(BF16)
            hr[t, rows, :] = h
            slope[t] = below + u * jnp.exp(-0.5 * u * u) * INV_ROOT_TAU
            total = total + contract_last(h, wn[t])
        xhat2, inv2 = normalize_layer(total)
        enc[rows, :] = (xhat2 * vec[6:7, :] + vec[7:8, :]).astype(BF16)
        grad = cot[rows, :].astype(F32)
        add(6, grad * xhat2)
        add(7, grad)
        dr2 = normalize_backward(grad, xhat2, inv2, vec[6:7, :])
        dfb = dr2.astype(BF16)
        dfr[rows, :] = dfb
        add(5, dfb.astype(F32))
        dy1 = dr2
        for t in range(n_tp):
            back = (dot(dfb, wn[t]) * slope[t]).astype(BF16)
            du[t, rows, :] = back
            dy1 = dy1 + contract_last(back, wu[t])
        add(3, dy1 * xhat1)
        add(4, dy1)
        first = normalize_backward(dy1, xhat1, inv1, vec[3:4, :])
        dr1[rows, :] = first
        dab = first.astype(BF16)
        dar[rows, :] = dab
        add(2, dab.astype(F32))
        dm[rows, :] = dot(dab, wo[...]).astype(BF16)
        return carry

    lax.fori_loop(0, 2, row_tile, 0)

    def flip(i, carry):
        cols = pl.ds(pl.multiple_of(i * ROWS, ROWS), ROWS)
        dft[:, cols] = dfr[cols, :].T
        y1t[:, cols] = y1r[cols, :].T
        dmt[:, cols] = dm[cols, :].T
        return carry

    lax.fori_loop(0, own // ROWS, flip, 0)
    tile = 256
    ones = jnp.ones((8, own), BF16)

    def store(i, t):
        return pltpu.make_async_copy(stage.at[i, t], (gd, gu)[i][t], o_sem.at[i, t])

    for t in range(n_tp):

        def one_tile(n, carry):
            lanes = pl.ds(pl.multiple_of(n * tile, tile), tile)
            stage[0, t, :, lanes] = dot(dft[...], hr[t, :, lanes]).astype(BF16)
            stage[1, t, :, lanes] = dot(y1t[...], du[t, :, lanes]).astype(BF16)
            wide[0:1, pl.ds(pl.multiple_of(t * width + n * tile, tile), tile)] = dot(ones, du[t, :, lanes])[0:1, :]
            return carry

        lax.fori_loop(0, width // tile, one_tile, 0)
        for i in range(2):
            store(i, t).start()
    for t in range(n_tp):
        for i in range(2):
            store(i, t).wait()


def norms(tok, mixed_t, vec, bu, cot, wd, w):
    own, width = tok.shape
    dma, vm = pltpu.SemaphoreType.DMA, pltpu.VMEM
    any_ = pl.BlockSpec(memory_space=pl.ANY)
    vmem = pl.BlockSpec(memory_space=pltpu.VMEM)
    shape = jax.ShapeDtypeStruct
    square = (width, width)
    return pl.pallas_call(
        norms_kernel,
        out_shape=(
            shape((own, width), BF16),
            shape((own, width), F32),
            shape((own, width), BF16),
            shape((own, width), BF16),
            shape((width, own), BF16),
            shape((8, width), F32),
            shape((1, 4 * width), F32),
        )
        + (shape(square, BF16),) * 8,
        in_specs=[vmem] * 5 + [any_] * 2,
        out_specs=(vmem,) * 7 + (any_,) * 8,
        scratch_shapes=[
            vm(square, BF16),
            vm((4,) + square, BF16),
            vm((4,) + square, BF16),
            vm((own, width), BF16),
            vm((own, width), BF16),
            vm((4, own, width), BF16),
            vm((4, own // 2, width), F32),
            vm((4, own, width), BF16),
            vm((own, width), BF16),
            vm((width, own), BF16),
            vm((width, own), BF16),
            vm((2, 4) + square, BF16),
            dma((3, 4)),
            dma((2, 4)),
        ],
        compiler_params=pltpu.CompilerParams(vmem_limit_bytes=VMEM_MAX),
        name="norms",
    )(tok, mixed_t, vec, bu, cot, wd, w)


def body(
    tokens, w_query, w_key, w_value, b_query, b_value, w_out, b_out, gain_attn, shift_attn,
    w_up, b_up, w_down, b_down, gain_ffn, shift_ffn, lengths, deal_order, cotangent,
):
    own, width = tokens.shape
    n_tp, n_dp = lax.axis_size("tp"), lax.axis_size("dp")
    z, g = lax.axis_index("tp"), lax.axis_index("dp")
    total = own * n_tp
    r, hw = w_query.shape
    direct = n_tp == 4 and n_dp == 8 and r % 16 == 0

    own_w = jnp.stack([jnp.concatenate([w_query, w_key, w_value, w_out], axis=1), w_up, w_down])
    vectors = (b_query, b_value, b_out, gain_attn, shift_attn, b_down, gain_ffn, shift_ffn, b_up)
    n_small = 8 * r + b_up.shape[0]
    if direct:
        line = jnp.arange(8, dtype=jnp.int32)[:, None]
        narrow = jnp.zeros((8, r), BF16)
        for i, a in enumerate(vectors[:8]):
            narrow = jnp.where(line == i, a[None, :], narrow)
        narrow = jnp.pad(narrow, ((0, 0), (0, 128 - r)))
        own_s = jnp.concatenate([narrow, jnp.pad(b_up.reshape(-1, 128), ((0, 5), (0, 0)))])
        w, vec, bu, xt, q, qt, k, v, kt, wd, ka, mixed_t, lse, ma = forward_all(lengths, deal_order, own_w, own_s, tokens)
        w = w.reshape(2, n_tp, width, w_up.shape[1])
        encoder_output, dr1, dar, dm, dmt, vecs, wide_sum, *gw = norms(tokens, mixed_t, vec, bu, cotangent, wd, w)
        args = (qt, q, k, kt, v, ka, ma, mixed_t, lse, dmt, dm)
        dqt, dk, dv, g_up, g_down = back_sums(args, gw[:4], gw[4:])
        a, gs, grad_tokens = finish(dqt, dk, dv, xt, dar, mixed_t, wd, dr1, vecs, wide_sum)
        gs = [gs[i, :r] for i in range(8)] + [gs[8:11].reshape(-1)]
    else:
        w = lax.all_gather(own_w, ("tp", "dp"), axis=0).reshape((n_tp, n_dp) + own_w.shape)
        w = jnp.moveaxis(w, 2, 0).reshape(3, n_tp, width, w_up.shape[1])
        s = lax.all_gather(jnp.concatenate(vectors), "dp", axis=0)
        x = lax.all_gather(tokens, "tp", axis=0, tiled=True)
        small = [s[:, i * r : (i + 1) * r].reshape(width).astype(F32) for i in range(8)]
        bq, bv, bo, g1, h1, bd, g2, h2 = small
        bu = s[:, 8 * r : n_small].reshape(-1).astype(F32)
        wq, wk, wv, wo = (
            w[0, :, :, i * hw : (i + 1) * hw].transpose(1, 0, 2).reshape(width, width) for i in range(4)
        )
        w = w[1:]
        q = (dot(tokens, wq) + bq).astype(BF16) * jnp.asarray(HD ** (-0.5), BF16)
        k = dot(x, wk).astype(BF16)
        v = (dot(x, wv) + bv).astype(BF16)
        qt, kt = q.T, k.T

        pair = lax.dynamic_slice_in_dim(deal_order, 2 * g, 1)
        first_len = jnp.sum(jnp.where(jnp.arange(lengths.shape[0], dtype=jnp.int32) == pair[0], lengths, 0))
        key_seg = jnp.arange(total, dtype=jnp.int32)[:, None] >= first_len
        lane = jnp.arange(128, dtype=jnp.int32)[None, :]
        ka = jnp.where(lane == 0, ~key_seg, jnp.where(lane == 1, key_seg, (lane >= 2) & (lane < 5))).astype(BF16)
        row_seg = (z * own + jnp.arange(own, dtype=jnp.int32))[None, :] >= first_len
        sub = jnp.arange(8, dtype=jnp.int32)[:, None]
        ma = jnp.where(((sub == 0) & row_seg) | ((sub == 1) & ~row_seg), MASKED, 0.0).astype(F32)

        mixed_t, lse = attention(qt, k, v.T, ka, ma)
        mixed = mixed_t.T.astype(BF16)
        first_residual = tokens.astype(F32) + contract_last(mixed, wo) + bo
        xhat1, inv1 = normalize_layer(first_residual)
        y1 = xhat1 * g1 + h1
        y1r = y1.astype(BF16)

        u = [dot(y1r, w[0, t]) + bu.reshape(n_tp, -1)[t] for t in range(n_tp)]
        hr = [jax.nn.gelu(a, approximate=False).astype(BF16) for a in u]
        ffn = sum(contract_last(hr[t], w[1, t]) for t in range(n_tp))
        xhat2, inv2 = normalize_layer(y1 + ffn + bd)
        encoder_output = (xhat2 * g2 + h2).astype(BF16)

        grad = cotangent.astype(F32)
        dr2 = normalize_backward(grad, xhat2, inv2, g2)
        dfr = dr2.astype(BF16)
        du = [(dot(dfr, w[1, t]) * gelu_slope(u[t])).astype(BF16) for t in range(n_tp)]
        dy1 = dr2 + sum(contract_last(du[t], w[0, t]) for t in range(n_tp))
        dr1 = normalize_backward(dy1, xhat1, inv1, g1)
        dar = dr1.astype(BF16)
        dm = dot(dar, wo).astype(BF16)
        gu = [contract_first(y1r, du[t]) for t in range(n_tp)]
        gd = [contract_first(dfr, hr[t]) for t in range(n_tp)]
        row_sums = [
            jnp.sum(dar, axis=0, dtype=F32),
            jnp.sum(dy1 * xhat1, axis=0),
            jnp.sum(dy1, axis=0),
            jnp.sum(dfr, axis=0, dtype=F32),
            jnp.sum(grad * xhat2, axis=0),
            jnp.sum(grad, axis=0),
        ]
        wide_sum = jnp.concatenate([jnp.sum(a, axis=0, dtype=F32) for a in du])
        back_args = (qt, q, k, kt, v, ka, ma, mixed_t, lse, dm.T, dm)
        dqt, dk, dv = attention_back(*back_args)
        dq = dqt.T
        base = dr1 + contract_last(dq, wq)
        far = contract_last(dk, wk) + contract_last(dv, wv)
        base = base + lax.dynamic_slice_in_dim(far, z * own, own)
        dt = far.astype(BF16)
        gq, gk, gv = contract_first(tokens, dq), contract_first(x, dk), contract_first(x, dv)
        go = contract_first(dar, mixed)
        ga = jnp.stack(
            [
                jnp.concatenate([m[:, t * hw : (t + 1) * hw] for m in (gq, gk, gv, go)], axis=1)
                for t in range(n_tp)
            ]
        )
        sums = [jnp.sum(dq, axis=0, dtype=F32), jnp.sum(dv, axis=0, dtype=F32)] + row_sums
        sums = [a.reshape(n_dp, r) for a in sums]
        sv = jnp.concatenate(sums + [wide_sum.reshape(n_dp, -1)], axis=1)
        grads = jnp.stack([ga, jnp.stack(gu), jnp.stack(gd)], axis=1).reshape(n_tp, 3, n_dp, r, -1)
        grads = jnp.moveaxis(grads, 1, 2).reshape(n_tp * n_dp, 3, r, -1)
        gw = lax.psum_scatter(grads, ("tp", "dp"), scatter_dimension=0, tiled=True)[0]
        gs = lax.psum_scatter(lax.psum(sv, "tp"), "dp", scatter_dimension=0, tiled=True)[0]
        others = jnp.where(jnp.arange(total)[:, None] // own == z, jnp.zeros((), BF16), dt)
        grad_tokens = base + lax.psum_scatter(others, "tp", scatter_dimension=0, tiled=True).astype(F32)
        gs = [gs[i * r : (i + 1) * r] for i in range(8)] + [gs[8 * r : n_small]]
        a, g_up, g_down = gw[0], gw[1], gw[2]
    return (
        encoder_output, grad_tokens,
        a[:, :hw], a[:, hw : 2 * hw], a[:, 2 * hw : 3 * hw], gs[0], gs[1],
        a[:, 3 * hw :], gs[2], gs[3], gs[4],
        g_up, gs[8], g_down, gs[5], gs[6], gs[7],
    )


def solution(mesh):
    rows, block, vector = P(("dp", "tp"), None), P("dp", "tp"), P("dp")
    in_specs = (
        rows, block, block, block, vector, vector, block, vector, vector, vector,
        block, vector, block, vector, vector, vector, P(), P(), rows,
    )
    out_specs = (
        rows, rows, block, block, block, vector, vector, block, vector, vector, vector,
        block, vector, block, vector, vector, vector,
    )
    return jax.shard_map(body, mesh=mesh, in_specs=in_specs, out_specs=out_specs, check_vma=False)
```

```python
import functools

import jax
import jax.numpy as jnp
from jax import lax
from jax.experimental import pallas as pl
from jax.experimental.pallas import tpu as pltpu
from jax.sharding import PartitionSpec as P

HD = 64
SHORT = 1024
EPS = 1e-05
SQRT_HALF = 0.7071067811865476
INV_ROOT_TAU = 0.3989422804014327
MASKED = -1e30
KEYS = 512
ROWS = 128
VMEM_MAX = 67043328
MESH = pl.DeviceIdType.MESH
F32 = jnp.float32
BF16 = jnp.bfloat16


def dot(left, right):
    return jnp.dot(left, right, preferred_element_type=F32)


def contract_last(left, right):
    return lax.dot_general(left, right, (((1,), (1,)), ((), ())), preferred_element_type=F32)


def contract_first(left, right):
    return lax.dot_general(left, right, (((0,), (0,)), ((), ())), preferred_element_type=F32)


def normalize_layer(resid):
    center = resid - jnp.mean(resid, axis=-1, keepdims=True)
    inverse_deviation = lax.rsqrt(jnp.mean(center * center, axis=-1, keepdims=True) + EPS)
    return (center * inverse_deviation, inverse_deviation)


def normalize_backward(output_gradient, xhat, inverse_deviation, gain):
    scaled_rows = output_gradient * gain
    return inverse_deviation * (
        scaled_rows
        - jnp.mean(scaled_rows, axis=-1, keepdims=True)
        - xhat * jnp.mean(scaled_rows * xhat, axis=-1, keepdims=True)
    )


def gelu_slope(pre_act):
    return (
        0.5 * (1.0 + lax.erf(pre_act * SQRT_HALF))
        + pre_act * jnp.exp(-0.5 * pre_act * pre_act) * INV_ROOT_TAU
    )


def position():
    z = lax.axis_index("tp")
    d = lax.axis_index("dp")
    core = lax.rem(d, 2)
    first = 2 + 2 * core
    second = 4 - 2 * core
    return z, d, core, first, second


def xor(d, mask):
    return d + mask * (1 - 2 * lax.rem(d // mask, 2))


def greet(z, d):
    barrier = pltpu.get_barrier_semaphore()
    for mask in (1, 2, 4):
        pl.semaphore_signal(barrier, inc=1, device_id=(xor(d, mask), z), device_id_type=MESH)
    for j in range(1, 4):
        pl.semaphore_signal(barrier, inc=1, device_id=(d, lax.rem(z + j, 4)), device_id_type=MESH)
    pl.semaphore_wait(barrier, 6)


def by_distance(z):
    low = z <= 1
    near = jnp.where(z == 0, 1, jnp.where(z == 1, 0, jnp.where(z == 2, 3, 2)))
    mid = jnp.where(low, 2, 1)
    far = jnp.where(low, 3, 0)
    return (z, near, mid, far)


def put(src, dst, send, recv, dp, tp):
    return pltpu.make_async_remote_copy(
        src_ref=src, dst_ref=dst, send_sem=send, recv_sem=recv, device_id=(dp, tp), device_id_type=MESH
    )


def forward_kernel(
    lengths, deal, own_w, own_s, own_t,
    w, vec, bu, xt_out, q_out, qt_out, k_out, v_out, kt_out, wd_out, ka_out, mixed_t, lse, ma,
    wa, s, x, xt, q, qt, k, v, kt, vt, wd, ka, sc, m, l, acc,
    wz_s, wz_r, wa_s, wa_r, wb_s, wb_r, wc_s, wc_r, tk_s, tk_r, sm_s, sm_r, lo_sem, arr_sem, out_sem,
):
    z, d, core, first, second = position()
    packs = own_w.shape[0]
    own, width = own_t.shape
    total = 4 * own
    hw = width // 4
    chunks = own // ROWS
    d1, d2 = xor(d, first), xor(d, second)
    d12 = xor(d1, second)
    pal = xor(d, 1)
    pd, pd1, pd2, pd12 = (xor(e, 1) for e in (d, d1, d2, d12))
    order = by_distance(z)
    first_len = lengths[deal[2 * d]]

    greet(z, d)

    def block(p, tt, e):
        return wa.at[tt, e] if p == 0 else w.at[p - 1, tt, e]

    def along_z(p, tt, src, act):
        dst = block(p, tt, d)
        right = put(src, dst, wz_s.at[0, p, tt], wz_r.at[p, tt], d, jnp.minimum(z + 1, 3))
        left = put(src, dst, wz_s.at[1, p, tt], wz_r.at[p, tt], d, jnp.maximum(z - 1, 0))

        @pl.when((tt <= z) & (z < 3))
        def _():
            act(right)

        @pl.when((tt >= z) & (z > 0))
        def _():
            act(left)

    def across(p, tt, src):
        dst = block(p, tt, d)
        return (
            put(src, dst, wa_s.at[p, tt], wa_r.at[p, tt], d1, z),
            put(src, dst, wb_s.at[p, tt, 0], wb_r.at[p, tt, 0], d2, z),
            put(src, dst, wc_s.at[p, tt, 0], wc_r.at[p, tt, 0], pal, z),
        )

    def after_first(p, tt):
        src = block(p, tt, d1)
        return (
            put(src, src, wb_s.at[p, tt, 1], wb_r.at[p, tt, 1], d2, z),
            put(src, src, wc_s.at[p, tt, 1], wc_r.at[p, tt, 1], pal, z),
        )

    def after_second(p, tt, i):
        src = block(p, tt, d2 if i == 0 else d12)
        return put(src, src, wc_s.at[p, tt, 2 + i], wc_r.at[p, tt, 2 + i], pal, z)

    def source(p, j):
        return own_w.at[p] if j == 0 else block(p, order[j], d)

    def arrive(ref, sem):
        put(ref, ref, arr_sem, sem, pal, z).wait_recv()

    def begin_z(p, j):
        if j > 0:
            arrive(block(p, order[j], d), wz_r.at[p, order[j]])
        along_z(p, order[j], source(p, j), lambda c: c.start())

    def begin_xy(p, j):
        for copy in across(p, order[j], source(p, j)):
            copy.start()

    def begin(p, j):
        begin_z(p, j)
        begin_xy(p, j)

    def relay_first(p, j):
        tt = order[j]
        arrive(block(p, tt, d1), wa_r.at[p, tt])
        for copy in after_first(p, tt):
            copy.start()

    def relay_second(p, j):
        tt = order[j]
        for i in range(2):
            arrive(block(p, tt, d2 if i == 0 else d12), wb_r.at[p, tt, i])
            after_second(p, tt, i).start()

    def from_pal(p):
        for tt in range(4):
            for i, e in enumerate((pd, pd2, pd1, pd12)):
                arrive(block(p, tt, e), wc_r.at[p, tt, i])

    def sent(p):
        for j in range(4):
            tt = order[j]
            along_z(p, tt, source(p, j), lambda c: c.wait_send())
            for copy in across(p, tt, source(p, j)) + after_first(p, tt):
                copy.wait_send()
            for i in range(2):
                after_second(p, tt, i).wait_send()

    def token_slice(o, i):
        return x.at[pl.ds(pl.multiple_of((o * chunks + i) * ROWS, ROWS), ROWS)]

    def token_hop(o, i, hop, step):
        src = own_t.at[pl.ds(i * ROWS, ROWS)] if hop == 0 else token_slice(o, i)
        way = 0 if step > 0 else 1
        return put(src, token_slice(o, i), tk_s.at[way, hop, i], tk_r.at[way, hop, i], d, jnp.clip(z + step, 0, 3))

    last = SHORT // ROWS

    def wanted(o, i, target, step):
        n = o * chunks + i
        if step > 0:
            return (target <= 2) | (n >= last)
        return (target >= 1) | (n < 4 * chunks - last)

    def chunk_ids(step):
        return list(range(chunks))[:: -step]

    def tokens(hop, step, act, which=slice(None)):
        o, target = z - step * hop, z + step
        valid = (o >= 0) & (o <= 3) & (target >= 0) & (target <= 3)
        for i in chunk_ids(step)[which]:

            @pl.when(valid & wanted(o, i, target, step))
            def _():
                act(token_hop(o, i, hop, step))

    def tokens_on(hop, step, onward):
        o, target = z - step * (hop + 1), z + step
        valid = (o >= 0) & (o <= 3) & (z - step >= 0) & (z - step <= 3)
        way = 0 if step > 0 else 1
        for i in chunk_ids(step):

            @pl.when(valid & wanted(o, i, z, step))
            def _():
                arrive(token_slice(jnp.clip(o, 0, 3), i), tk_r.at[way, hop, i])

            if onward:

                @pl.when(valid & (target >= 0) & (target <= 3) & wanted(o, i, target, step))
                def _():
                    token_hop(o, i, hop + 1, step).start()

    def small(stage):
        if stage == 0:
            return [
                put(own_s, s.at[d], sm_s.at[0], sm_r.at[0], d1, z),
                put(own_s, s.at[d], sm_s.at[1], sm_r.at[1], d2, z),
                put(own_s, s.at[d], sm_s.at[3], sm_r.at[3], pal, z),
            ]
        if stage == 1:
            return [
                put(s.at[d1], s.at[d1], sm_s.at[2], sm_r.at[2], d2, z),
                put(s.at[d1], s.at[d1], sm_s.at[4], sm_r.at[4], pal, z),
            ]
        return [
            put(s.at[d2], s.at[d2], sm_s.at[5], sm_r.at[5], pal, z),
            put(s.at[d12], s.at[d12], sm_s.at[6], sm_r.at[6], pal, z),
        ]

    def own_tokens(*which):
        for step in (1, -1):
            tokens(0, step, lambda c: c.start(), slice(*which))

    begin(0, 0)
    for copy in small(0):
        copy.start()
    own_tokens(0, 1)
    s[d] = own_s[...]
    wa[z, d] = own_w[0]
    mine = pl.ds(pl.multiple_of(z * own, ROWS), own)
    x[mine, :] = own_t[...]
    keep = pltpu.make_async_copy(own_w.at[pl.ds(1, packs - 1)], w.at[:, z, d], lo_sem)
    keep.start()

    @pl.when(z == 0)
    def _():
        x[total - SHORT :, :] = jnp.zeros((SHORT, width), BF16)
        xt[:, total - SHORT :] = jnp.zeros((width, SHORT), BF16)

    @pl.when(z == 3)
    def _():
        x[:SHORT, :] = jnp.zeros((SHORT, width), BF16)
        xt[:, :SHORT] = jnp.zeros((width, SHORT), BF16)

    middle = (z == 1) | (z == 2)
    begin(0, 1)
    relay_first(0, 0)
    for p in range(1, packs):
        begin_z(p, 0)
    begin(0, 2)
    relay_second(0, 0)
    relay_first(0, 1)
    own_tokens(1, 2)
    begin(0, 3)
    own_tokens(2, 3)
    relay_second(0, 1)
    relay_first(0, 2)
    begin_xy(1, 0)
    arrive(s.at[d1], sm_r.at[0])
    for copy in small(1):
        copy.start()
    relay_second(0, 2)
    relay_first(0, 3)
    for p in range(2, packs):
        begin_xy(p, 0)
    arrive(s.at[d2], sm_r.at[1])
    arrive(s.at[d12], sm_r.at[2])
    for copy in small(2):
        copy.start()
    for p in range(1, packs):
        begin(p, 1)

    @pl.when(middle)
    def _():
        for p in range(1, packs):
            begin(p, 2)

    own_tokens(3, chunks)
    lane = lax.broadcasted_iota(jnp.int32, (own, 128), 1)
    for i in range(4):
        late = lax.broadcasted_iota(jnp.int32, (own, 128), 0) + i * own >= first_len
        ones = jnp.where((lane >= 2) & (lane < 5), 1.0, 0.0)
        flags = jnp.where(lane == 0, jnp.where(late, 0.0, 1.0), jnp.where(lane == 1, jnp.where(late, 1.0, 0.0), ones))
        ka[pl.ds(i * own, own), :] = flags.astype(BF16)

    relay_second(0, 3)
    for i, e in enumerate((pd, pd2, pd1, pd12)):
        arrive(s.at[e], sm_r.at[3 + i])
    r = width // 8
    for e in range(8):
        piece = s[e].astype(F32)
        vec[0:8, e * r : (e + 1) * r] = piece[0:8, 0:r]
        for j in range(hw * 2 // 128):
            col = e * hw * 2 + j * 128
            bu[0:1, col : col + 128] = piece[8 + j : 9 + j, :]
    from_pal(0)
    for tt in range(4):
        rows = wa[tt].reshape(width, width)
        for i in range(4):
            wd[i, :, tt * hw : (tt + 1) * hw] = rows[:, i * hw : (i + 1) * hw]
    wd_copy = pltpu.make_async_copy(wd, wd_out, out_sem.at[0])
    wd_copy.start()

    tile = 256

    def q_tile(n, carry):
        lanes = pl.ds(pl.multiple_of(n * tile, tile), tile)
        rows = (dot(own_t[...], wd[0, :, lanes]) + vec[0:1, lanes]).astype(BF16) * jnp.asarray(HD ** (-0.5), BF16)
        q[:, lanes] = rows
        qt[lanes, :] = rows.T
        return carry

    def project(o):
        rows = pl.ds(pl.multiple_of(o * own, ROWS), own)

        def kv_tile(n, carry):
            lanes = pl.ds(pl.multiple_of(n * tile, tile), tile)
            keys = dot(x[rows, :], wd[1, :, lanes]).astype(BF16)
            k[rows, lanes] = keys
            kt[lanes, rows] = keys.T
            values = (dot(x[rows, :], wd[2, :, lanes]) + vec[1:2, lanes]).astype(BF16)
            v[rows, lanes] = values
            vt[lanes, rows] = values.T
            xt[lanes, rows] = x[rows, lanes].T
            return carry

        lax.fori_loop(0, width // tile, kv_tile, 0)

    def project_far():
        for step in (1, -1):
            tokens_on(1, step, False)
        project(jnp.where(z == 0, 2, jnp.where(z == 1, 3, z - 2)))

    lax.fori_loop(0, width // tile, q_tile, 0)
    project(z)
    for p in range(1, packs):
        relay_first(p, 0)
    for step in (1, -1):
        tokens_on(0, step, True)

    @pl.when(z > 0)
    def _():
        project(jnp.maximum(z - 1, 0))

    @pl.when(jnp.logical_not(middle))
    def _():
        for p in range(1, packs):
            begin(p, 2)

    for p in range(1, packs):
        relay_second(p, 0)
        relay_first(p, 1)

    @pl.when(z < 3)
    def _():
        project(jnp.minimum(z + 1, 3))

    @pl.when(jnp.logical_not(middle))
    def _():
        project_far()

    def both(act, j):
        def run():
            for p in range(1, packs):
                act(p, j)

        return run

    def last_block(inner):
        def run():
            @pl.when(middle if inner else jnp.logical_not(middle))
            def _():
                for p in range(1, packs):
                    begin(p, 3)

        return run

    between = {
        (0, 0): last_block(True),
        (0, 1): both(relay_second, 1),
        (0, 2): both(relay_first, 2),
        (0, 4): last_block(False),
        (0, 5): both(relay_second, 2),
        (1, 0): both(relay_first, 3),
        (1, 4): both(relay_second, 3),
    }
    late = lax.broadcasted_iota(jnp.int32, (8, own), 1) + z * own >= first_len
    sub = lax.broadcasted_iota(jnp.int32, (8, own), 0)
    away = jnp.where(sub == 0, jnp.where(late, MASKED, 0.0), jnp.where(sub == 1, jnp.where(late, 0.0, MASKED), 0.0))
    ma[...] = away
    outs = [
        pltpu.make_async_copy(a, b, out_sem.at[1 + i])
        for i, (a, b) in enumerate(
            ((xt, xt_out), (q, q_out), (qt, qt_out), (k, k_out), (v, v_out), (kt, kt_out), (ka, ka_out))
        )
    ]
    pairs = width // 128
    for part, (row0, n, start) in enumerate(parts_of(z, own)):
        if part == 1:

            @pl.when(middle)
            def _():
                project_far()

            for copy in outs:
                copy.start()
        cols = pl.ds(pl.multiple_of(row0, 128), n)
        late = lax.broadcasted_iota(jnp.int32, (1, n), 1) + (z * own + row0) >= first_len
        masks = (jnp.where(late, MASKED, 0.0), jnp.where(late, 0.0, MASKED))
        aug = aug_rows(pick_rows(masks, n), n)

        def one_pair(pair, carry):
            for (at, i), run in between.items():
                if at == part:

                    @pl.when(pair == i)
                    def _():
                        run()

            attend_pair(z, part, start, pair, cols, n, aug, qt, k, vt, ka, mixed_t, lse, sc, m, l, acc)
            return carry

        lax.fori_loop(0, pairs, one_pair, 0)

    for p in range(1, packs):
        from_pal(p)
    for stage in range(3):
        for copy in small(stage):
            copy.wait_send()
    for hop in range(2):
        for step in (1, -1):
            tokens(hop, step, lambda c: c.wait_send())
    for p in range(packs):
        sent(p)
    keep.wait()
    wd_copy.wait()
    for copy in outs:
        copy.wait()


def attend_pair(z, part, start, pair, cols, n, aug, qt, k, vt, ka, mixed_t, lse, s, m, l, acc):
    total = k.shape[0]
    lanes = pl.ds(pl.multiple_of(pair * 128, 128), 128)
    for half in range(2):
        m[half, :, :n] = jnp.full((1, n), MASKED, F32)
        l[half, :, :n] = jnp.zeros((1, n), F32)
        acc[half, :, :n] = jnp.zeros((HD, n), F32)
    qs = [padded(qt[pl.ds(pl.multiple_of(pair * 128 + half * HD, HD), HD), cols], half, aug, n) for half in range(2)]

    def scores(key0):
        keys = pl.ds(key0, KEYS)
        left = jnp.concatenate([k[keys, lanes], ka[keys, :]], axis=1)
        for half in range(2):
            score = dot(left, qs[half])
            s[half, keys, :n] = score
            m[half, :, :n] = jnp.maximum(m[half, :, :n], jnp.max(score, axis=0, keepdims=True))

    over_keys(z, part, start, total, scores)
    tops = [m[half, :, :n] for half in range(2)]

    def mix(key0):
        keys = pl.ds(key0, KEYS)
        for half in range(2):
            raised = jnp.exp(s[half, keys, :n] - tops[half])
            l[half, :, :n] += jnp.sum(raised, axis=0, keepdims=True)
            values = vt[pl.ds(pl.multiple_of(pair * 128 + half * HD, HD), HD), keys]
            acc[half, :, :n] += dot(values, raised.astype(BF16))

    over_keys(z, part, start, total, mix)
    for half in range(2):
        sums = l[half, :, :n]
        rows = pl.ds(pl.multiple_of(pair * 128 + half * HD, HD), HD)
        mixed_t[rows, cols] = acc[half, :, :n] / sums
        lse[pair, half : half + 1, cols] = tops[half] + jnp.log(sums)


def forward_all(lengths, deal, own_w, own_s, own_t):
    packs, r, c = own_w.shape
    own, width = own_t.shape
    total = 4 * own
    chunks = own // ROWS
    widest = max(SHORT - own, own - (SHORT - own))
    dma, vm = pltpu.SemaphoreType.DMA, pltpu.VMEM
    any_ = pl.BlockSpec(memory_space=pl.ANY)
    vmem = pl.BlockSpec(memory_space=pltpu.VMEM)
    smem = pl.BlockSpec(memory_space=pltpu.SMEM)
    shape = jax.ShapeDtypeStruct
    return pl.pallas_call(
        forward_kernel,
        out_shape=(
            shape((packs - 1, 4, 8, r, c), BF16),
            shape((8, width), F32),
            shape((1, 4 * c), F32),
            shape((width, total), BF16),
            shape((own, width), BF16),
            shape((width, own), BF16),
            shape((total, width), BF16),
            shape((total, width), BF16),
            shape((width, total), BF16),
            shape((4, width, width), BF16),
            shape((total, 128), BF16),
            shape((width, own), F32),
            shape((width // 128, 8, own), F32),
            shape((8, own), F32),
        ),
        in_specs=[smem, smem, vmem, vmem, vmem],
        out_specs=(any_, vmem, vmem) + (any_,) * 8 + (vmem, vmem, vmem),
        scratch_shapes=[
            vm((4, 8, r, c), BF16),
            vm((8, 16, 128), BF16),
            vm((total, width), BF16),
            vm((width, total), BF16),
            vm((own, width), BF16),
            vm((width, own), BF16),
            vm((total, width), BF16),
            vm((total, width), BF16),
            vm((width, total), BF16),
            vm((width, total), BF16),
            vm((4, width, width), BF16),
            vm((total, 128), BF16),
            vm((2, total, widest), F32),
            vm((2, 1, widest), F32),
            vm((2, 1, widest), F32),
            vm((2, HD, widest), F32),
            dma((2, packs, 4)),
            dma((packs, 4)),
            dma((packs, 4)),
            dma((packs, 4)),
            dma((packs, 4, 2)),
            dma((packs, 4, 2)),
            dma((packs, 4, 4)),
            dma((packs, 4, 4)),
            dma((2, 2, chunks)),
            dma((2, 2, chunks)),
            dma((7,)),
            dma((7,)),
            dma(()),
            dma(()),
            dma((8,)),
        ],
        compiler_params=pltpu.CompilerParams(
            collective_id=0, has_side_effects=True, vmem_limit_bytes=VMEM_MAX
        ),
        name="forward_all",
    )(lengths, deal, own_w, own_s, own_t)


def up(ref):
    return ref[...].astype(F32)


class Sums:
    def __init__(self, z, d, core, e_mask, f_mask, give, mine, ready, bufs, sems):
        self.z, self.d, self.give, self.mine, self.ready = z, d, give, mine, ready
        self.r1, self.b2, self.r2, self.b3, self.r3, self.s3, self.b4, self.r4 = bufs
        self.sems = sems
        self.xy = d // 2
        self.e, self.f = xor(d, e_mask) // 2, xor(d, f_mask) // 2
        self.ef = xor(xor(d, e_mask), f_mask) // 2
        self.d_e, self.d_f, self.pal = xor(d, e_mask), xor(d, f_mask), xor(d, 1)

    def one(self, p, t):
        return put(self.give(p, t), self.r1.at[p, t], self.sems[0].at[p, t], self.sems[1].at[p, t], self.pal, self.z)

    def two(self, p, t):
        return put(self.b2.at[p, t], self.r2.at[p, t], self.sems[2].at[p, t], self.sems[3].at[p, t], self.d_e, self.z)

    def three(self, p, t):
        return put(self.b3.at[p, t], self.r3.at[p, t], self.sems[4].at[p, t], self.sems[5].at[p, t], self.d_f, self.z)

    def four(self, p, t, way):
        to = jnp.minimum(self.z + 1, 3) if way == 0 else jnp.maximum(self.z - 1, 0)
        return put(
            self.b4.at[p, way, t], self.r4.at[p, way, t],
            self.sems[6].at[p, way, t], self.sems[7].at[p, way, t], self.d, to,
        )

    def at_two(self, p, t):
        self.ready(p, t)
        self.one(p, t).wait_recv()
        for i, x in enumerate((self.e, self.ef)):
            self.b2[p, t, i] = (self.mine(p, t, x) + up(self.r1.at[p, t, x])).astype(BF16)
        self.two(p, t).start()

    def at_three(self, p, t):
        self.two(p, t).wait_recv()
        f = self.f
        self.b3[p, t] = (self.mine(p, t, f) + up(self.r1.at[p, t, f]) + up(self.r2.at[p, t, 1])).astype(BF16)
        self.three(p, t).start()

    def at_kept(self, p, t):
        self.three(p, t).wait_recv()
        xy = self.xy
        self.s3[p, t] = self.mine(p, t, xy) + up(self.r1.at[p, t, xy]) + up(self.r2.at[p, t, 0]) + up(self.r3.at[p, t])

    def at_four(self, p, step, kept=(), ids=range(3)):
        kept = list(kept)
        for i in ids:
            for t, way in ((3 - i, 0), (i, 1)):
                if t in kept:
                    self.at_kept(p, t)
                    kept.remove(t)
            for t, way in ((3 - i, 0), (i, 1)):
                pos = step if way == 0 else 3 - step
                if not (t > pos if way == 0 else t < pos):
                    continue

                @pl.when(self.z == pos)
                def _():
                    if step == 0:
                        self.b4[p, way, t] = self.s3[p, t].astype(BF16)
                    else:
                        self.four(p, t, way).wait_recv()
                        self.b4[p, way, t] = (self.s3[p, t] + up(self.r4.at[p, way, t])).astype(BF16)
                    self.four(p, t, way).start()

    def result(self, p, out):
        z = self.z
        out[...] = self.s3[p, z]

        @pl.when(z > 0)
        def _():
            self.four(p, z, 0).wait_recv()
            out[...] += up(self.r4.at[p, 0, z])

        @pl.when(z < 3)
        def _():
            self.four(p, z, 1).wait_recv()
            out[...] += up(self.r4.at[p, 1, z])

    def drain(self, p):
        for t in range(4):
            self.one(p, t).wait_send()
            self.two(p, t).wait_send()
            self.three(p, t).wait_send()
            for way in range(2):

                @pl.when((t > self.z) if way == 0 else (t < self.z))
                def _():
                    self.four(p, t, way).wait_send()


def sum_buffers(packs, block):
    vm = pltpu.VMEM
    return [
        vm((packs, 4, 4) + block, BF16),
        vm((packs, 4, 2) + block, BF16),
        vm((packs, 4, 2) + block, BF16),
        vm((packs, 4) + block, BF16),
        vm((packs, 4) + block, BF16),
        vm((packs, 4) + block, F32),
        vm((packs, 2, 4) + block, BF16),
        vm((packs, 2, 4) + block, BF16),
    ]


def sum_semaphores(packs):
    dma = pltpu.SemaphoreType.DMA
    return [dma((packs, 4))] * 6 + [dma((packs, 2, 4))] * 2


def finish_kernel(
    dqt, dk_all, dv_all, xt_all, dar, mixed_all, wd_all, dr1_all, vecs, bup,
    out_w, out_s, out_t,
    xt, wd, dk, dv, mixed_t, dr1, ld_sem, sh_sem, dart, dq, mixed, gp, sv, ds, dr, sk, q1, q2, q3, c2, c3, q4,
    r1, b2, r2, b3, r3, s3, b4, r4,
    p1_s, p1_r, p2_s, p2_r, p3_s, p3_r, p4_s, p4_r, t_s, t_r, v_s, v_r,
):
    z, d, core, first, second = position()
    own, width = out_t.shape
    chunks = own // ROWS
    total = 4 * chunks
    edge = SHORT // ROWS
    hw = width // 4
    r = width // 8
    load_w = pltpu.make_async_copy(wd_all.at[pl.ds(0, 3)], wd, ld_sem.at[0])
    load_x = pltpu.make_async_copy(xt_all, xt, ld_sem.at[1])
    load_m = pltpu.make_async_copy(mixed_all, mixed_t, ld_sem.at[2])
    load_r = pltpu.make_async_copy(dr1_all, dr1, ld_sem.at[3])

    def pick(a, b, c, e):
        return jnp.where(z == 0, a, jnp.where(z == 1, b, jnp.where(z == 2, c, e)))

    shards = [pick(*o) for o in ((2, 3, 0, 1), (1, 2, 1, 2), (3, 0, 3, 0), (0, 1, 2, 3))]
    load_s = []
    for j, o in enumerate(shards):
        rows = pl.ds(pl.multiple_of(o * own, ROWS), own)
        load_s.append(
            [
                pltpu.make_async_copy(a.at[rows], b.at[rows], sh_sem.at[i, j])
                for i, (a, b) in enumerate(((dk_all, dk), (dv_all, dv)))
            ]
        )
    for copy in [load_w] + load_s[0] + [load_m, load_x] + load_s[1] + load_s[2] + load_s[3] + [load_r]:
        copy.start()
    greet(z, d)

    def token(k, way):
        to = jnp.minimum(z + 1, 3) if way == 0 else jnp.maximum(z - 1, 0)
        slot = k if way == 0 else jnp.where(k // chunks == to, total + k % chunks, k)
        return put(ds.at[k], dr.at[slot], t_s.at[k], t_r.at[slot], d, to)

    def token_in(k, way):
        slot = k if way == 0 else jnp.where(k // chunks == z, total + k % chunks, k)
        return put(ds.at[k], dr.at[slot], t_s.at[k], t_r.at[slot], d, z), slot

    def sends(k, way):
        o = k // chunks
        if way == 0:
            low = jnp.where(k < total - edge, 0, 1)
            return (z >= low) & (z < o) & (o > low)
        high = jnp.where(k >= edge, 3, 2)
        return (z <= high) & (z > o) & (o < high)

    def starts(k, way):
        if way == 0:
            return z == jnp.where(k < total - edge, 0, 1)
        return z == jnp.where(k >= edge, 3, 2)

    tile = 256

    def far_shard(o, mine):
        rows = pl.ds(pl.multiple_of(o * own, ROWS), own)

        def one_tile(n, carry):
            lanes = pl.ds(pl.multiple_of(n * tile, tile), tile)
            far = contract_last(dk[rows, :], wd[1, lanes, :]) + contract_last(dv[rows, :], wd[2, lanes, :])
            if mine:
                out_t[:, lanes] = dr1[:, lanes] + far
            else:
                ds[pl.ds(o * chunks, chunks), :, lanes] = far.reshape(chunks, ROWS, tile).astype(BF16)
            return carry

        lax.fori_loop(0, width // tile, one_tile, 0)

    def far_and_send(j):
        o = shards[j]

        @pl.when((j < 2) | (z == 1) | (z == 2))
        def _():
            far_shard(o, False)

        for i in range(chunks):
            for way in range(2):
                k = o * chunks + i

                @pl.when(sends(k, way) & starts(k, way))
                def _():
                    token(k, way).start()

    for copy in [load_w] + load_s[0]:
        copy.wait()
    far_and_send(0)
    load_m.wait()

    right_order = [k for o in (3, 2, 1) for k in range(o * chunks, (o + 1) * chunks)]
    left_order = [total - 1 - k for k in right_order]

    def forward_tokens(at):
        for k, way in [(k, 0) for k in right_order] + [(k, 1) for k in left_order]:
            pos = at if way == 0 else 3 - at
            passes = (at < k // chunks) if way == 0 else (3 - at > k // chunks)
            begins = (0 if k < total - edge else 1) if way == 0 else (3 if k >= edge else 2)
            if not passes or (begins >= pos if way == 0 else begins <= pos):
                continue

            @pl.when(z == pos)
            def _():
                got, slot = token_in(k, way)
                got.wait_recv()
                ds[k] = (ds[k].astype(F32) + dr[slot].astype(F32)).astype(BF16)
                token(k, way).start()

    def flip_own(i, carry):
        cols = pl.ds(pl.multiple_of(i * ROWS, ROWS), ROWS)
        dart[:, cols] = dar[cols, :].T
        dq[cols, :] = dqt[:, cols].T
        mixed[cols, :] = mixed_t[:, cols].T.astype(BF16)
        return carry

    lax.fori_loop(0, chunks, flip_own, 0)

    def give(p, t):
        return gp.at[t, :, 1 - core]

    def mine(p, t, at):
        return gp[t, at, core].astype(F32)

    sums = Sums(
        z, d, core, second, first, give, mine, lambda p, t: None,
        (r1, b2, r2, b3, r3, s3, b4, r4), (p1_s, p1_r, p2_s, p2_r, p3_s, p3_r, p4_s, p4_r),
    )
    here = pl.ds(pl.multiple_of(z * own, ROWS), own)
    half = width // 2

    def weights(th):
        lanes = pl.ds(th * half, half)

        def rows_of(m, carry):
            rows = pl.ds(pl.multiple_of(m * half, ROWS), half)
            parts = (
                lambda: dot(xt[rows, here], dq[:, lanes]),
                lambda: dot(xt[rows, :], dk[:, lanes]),
                lambda: dot(xt[rows, :], dv[:, lanes]),
                lambda: dot(dart[rows, :], mixed[:, lanes]),
            )
            for i, part in enumerate(parts):
                got = part().astype(BF16)
                for h in range(2):
                    block = got[:, h * hw : (h + 1) * hw].reshape(2, 2, r, hw)
                    gp[2 * th + h, pl.ds(2 * m, 2), :, :, i * hw : (i + 1) * hw] = block
            return carry

        lax.fori_loop(0, 2, rows_of, 0)
        for t in (2 * th, 2 * th + 1):
            sums.one(0, t).start()

    for copy in [load_x, load_r] + load_s[1] + load_s[2] + load_s[3]:
        copy.wait()
    weights(1)
    weights(0)
    for t in (3, 2):
        sums.at_two(0, t)
    far_and_send(1)
    forward_tokens(1)
    for t in (0, 1):
        sums.at_two(0, t)
    far_and_send(2)
    forward_tokens(2)

    ones = jnp.ones((8, 4 * own), BF16)
    index = lax.broadcasted_iota(jnp.int32, (8, width), 0)
    small_rows = jnp.where(index == 0, dot(ones[:, :own], dq[...]), jnp.where(index == 1, dot(ones, dv[...]), vecs[...]))
    pad = jnp.zeros((8, 128 - r), F32)
    for i in range(8):
        sv[i // 2, i % 2, 0:8, :] = jnp.concatenate([small_rows[:, i * r : (i + 1) * r], pad], axis=1)
        wide = [bup[:, (i * 3 + j) * 128 : (i * 3 + j + 1) * 128] for j in range(3)]
        sv[i // 2, i % 2, 8:16, :] = jnp.concatenate(wide + [jnp.zeros((5, 128), F32)], axis=0)
    small = [
        put(sv.at[:, 1 - core], q1, v_s.at[0], v_r.at[0], sums.pal, z),
        put(c2, q2, v_s.at[1], v_r.at[1], sums.d_e, z),
        put(c3, q3, v_s.at[2], v_r.at[2], sums.d_f, z),
    ]
    small_z = [
        put(sk, q4.at[j - 1], v_s.at[2 + j], v_r.at[2 + j], d, lax.rem(z + j, 4)) for j in range(1, 4)
    ]
    small[0].start()
    far_shard(z, True)

    def query_tile(n, carry):
        lanes = pl.ds(pl.multiple_of(n * tile, tile), tile)
        out_t[:, lanes] += contract_last(dq[...], wd[0, lanes, :])
        return carry

    lax.fori_loop(0, width // tile, query_tile, 0)
    small[0].wait_recv()
    for i, at in enumerate((sums.e, sums.ef)):
        c2[i] = sv[at, core] + q1[at]
    small[1].start()
    for t in (3, 2, 0, 1):
        sums.at_three(0, t)
    small[1].wait_recv()
    c3[...] = sv[sums.f, core] + q1[sums.f] + q2[1]
    small[2].start()
    for step in range(3):
        sums.at_four(0, step, range(4) if step == 0 else ())
        if step == 0:
            small[2].wait_recv()
            sk[...] = sv[sums.xy, core] + q1[sums.xy] + q2[0] + q3[...]
            for copy in small_z:
                copy.start()
    for i in range(chunks):
        k = z * chunks + i
        rows = pl.ds(i * ROWS, ROWS)
        from_left = (z > 0) & ((z == 1) & (k < total - edge) | (z > 1))
        from_right = (z < 3) & ((z == 2) & (k >= edge) | (z < 2))

        @pl.when(from_left)
        def _():
            put(ds.at[k], dr.at[k], t_s.at[k], t_r.at[k], d, z).wait_recv()
            out_t[rows, :] += dr[k].astype(F32)

        @pl.when(from_right)
        def _():
            put(ds.at[k], dr.at[total + i], t_s.at[k], t_r.at[total + i], d, z).wait_recv()
            out_t[rows, :] += dr[total + i].astype(F32)

    for copy in small_z:
        copy.wait_recv()
    out_s[...] = sk[...] + q4[0] + q4[1] + q4[2]
    sums.result(0, out_w)
    for copy in small + small_z:
        copy.wait_send()
    sums.drain(0)
    for k in range(total):
        for way in range(2):

            @pl.when(sends(k, way))
            def _():
                token(k, way).wait_send()


def finish(dqt, dk, dv, xt, dar, mixed_t, wd, dr1, vecs, bup):
    own, width = dr1.shape
    r = width // 8
    chunks = own // ROWS
    dma, vm = pltpu.SemaphoreType.DMA, pltpu.VMEM
    vmem = pl.BlockSpec(memory_space=pltpu.VMEM)
    any_ = pl.BlockSpec(memory_space=pl.ANY)
    block, sb = (r, width), (16, 128)
    return pl.pallas_call(
        finish_kernel,
        out_shape=(
            jax.ShapeDtypeStruct(block, F32),
            jax.ShapeDtypeStruct(sb, F32),
            jax.ShapeDtypeStruct((own, width), F32),
        ),
        in_specs=[vmem] + [any_] * 3 + [vmem] + [any_] * 3 + [vmem] * 2,
        out_specs=(vmem, vmem, vmem),
        scratch_shapes=[
            vm((width, 4 * own), BF16),
            vm((3, width, width), BF16),
            vm((4 * own, width), BF16),
            vm((4 * own, width), BF16),
            vm((width, own), F32),
            vm((own, width), F32),
            dma((4,)),
            dma((2, 4)),
            vm((width, own), BF16),
            vm((own, width), BF16),
            vm((own, width), BF16),
            vm((4, 4, 2) + block, BF16),
            vm((4, 2) + sb, F32),
            vm((4 * chunks, ROWS, width), BF16),
            vm((5 * chunks, ROWS, width), BF16),
            vm(sb, F32),
            vm((4,) + sb, F32),
            vm((2,) + sb, F32),
            vm(sb, F32),
            vm((2,) + sb, F32),
            vm(sb, F32),
            vm((3,) + sb, F32),
            *sum_buffers(1, block),
            *sum_semaphores(1),
            dma((4 * chunks,)),
            dma((5 * chunks,)),
            dma((6,)),
            dma((6,)),
        ],
        compiler_params=pltpu.CompilerParams(
            collective_id=1, has_side_effects=True, vmem_limit_bytes=VMEM_MAX
        ),
        name="finish",
    )(dqt, dk, dv, xt, dar, mixed_t, wd, dr1, vecs, bup)


def parts_of(z, own):
    sure = SHORT - own
    low = z < 2
    return (
        (jnp.where(low, 0, own - sure), sure, jnp.where(low, 0, SHORT)),
        (jnp.where(low, sure, 0), own - sure, jnp.where(z == 3, SHORT, 0)),
    )


def over_keys(z, part, start, total, act):
    window = total - SHORT
    for c in range(window // KEYS):
        act(pl.multiple_of(start + c * KEYS, KEYS))
    if part == 1:

        @pl.when((z == 1) | (z == 2))
        def _():
            for c in range(window // KEYS, total // KEYS):
                act(c * KEYS)


def aug_rows(top, r):
    return jnp.concatenate([top.astype(BF16), jnp.zeros((128 - 16, r), BF16)], axis=0)


def pick_rows(rows, r):
    index = lax.broadcasted_iota(jnp.int32, (16, r), 0)
    out = jnp.zeros((16, r), F32)
    for i, row in enumerate(rows):
        out = jnp.where(index == i, jnp.broadcast_to(row, (16, r)), out)
    return out


def split3(x):
    hi = x.astype(BF16).astype(F32)
    mid = (x - hi).astype(BF16).astype(F32)
    return hi, mid, x - hi - mid


def padded(head_rows, half, aug, r):
    zero = jnp.zeros((HD, r), BF16)
    pair = [head_rows, zero] if half == 0 else [zero, head_rows]
    return jnp.concatenate(pair + [aug], axis=0)


def attention_kernel(qt, k, vt, ka, ma, mixed_t, lse, s, m, l, acc):
    z = lax.axis_index("tp")
    own = qt.shape[1]
    for part, (row0, n, start) in enumerate(parts_of(z, own)):
        cols = pl.ds(pl.multiple_of(row0, 128), n)
        aug = aug_rows(pick_rows((ma[0:1, cols], ma[1:2, cols]), n), n)

        def one_pair(pair, carry):
            attend_pair(z, part, start, pair, cols, n, aug, qt, k, vt, ka, mixed_t, lse, s, m, l, acc)
            return carry

        lax.fori_loop(0, k.shape[1] // 128, one_pair, 0)


def attention(qt, k, vt, ka, ma):
    width, own = qt.shape
    total = k.shape[0]
    widest = max(SHORT - own, own - (SHORT - own))
    vm = pltpu.VMEM
    return pl.pallas_call(
        attention_kernel,
        out_shape=(
            jax.ShapeDtypeStruct((width, own), F32),
            jax.ShapeDtypeStruct((width // 128, 8, own), F32),
        ),
        in_specs=[pl.BlockSpec(memory_space=pltpu.VMEM)] * 5,
        out_specs=(pl.BlockSpec(memory_space=pltpu.VMEM),) * 2,
        scratch_shapes=[
            vm((2, total, widest), F32),
            vm((2, 1, widest), F32),
            vm((2, 1, widest), F32),
            vm((2, HD, widest), F32),
        ],
        compiler_params=pltpu.CompilerParams(vmem_limit_bytes=VMEM_MAX),
        name="attention",
    )(qt, k, vt, ka, ma)


def back_pair(z, pair, pause, qt, q, k, kt, v, ka, ma, mixed_t, lse, dmt, dm, dqt, dk, dv, dka, dva, dqa):
    own, total = qt.shape[1], k.shape[0]
    lanes = pl.ds(pl.multiple_of(pair * 128, 128), 128)
    dka[...] = jnp.zeros_like(dka)
    dva[...] = jnp.zeros_like(dva)
    for part, (row0, r, start) in enumerate(parts_of(z, own)):
        pause(part)
        cols = pl.ds(pl.multiple_of(row0, 128), r)
        qs, gs, qm, gm = [], [], [], []
        low = lax.broadcasted_iota(jnp.int32, (r, 128), 1) < HD
        for half in range(2):
            rows = pl.ds(pl.multiple_of(pair * 128 + half * HD, HD), HD)
            delta = jnp.sum(dmt[rows, cols].astype(F32) * mixed_t[rows, cols], axis=0, keepdims=True)
            total_log = lse[pair, half : half + 1, cols]
            q_aug = pick_rows((ma[0:1, cols], ma[1:2, cols]) + split3(-total_log), r)
            zero = jnp.zeros((1, r), F32)
            g_aug = pick_rows((zero, zero) + split3(-delta), r)
            qs.append(padded(qt[rows, cols], half, aug_rows(q_aug, r), r))
            gs.append(padded(dmt[rows, cols], half, aug_rows(g_aug, r), r))
            mine = low if half == 0 else jnp.logical_not(low)
            here = pl.ds(pl.multiple_of(row0, 128), r)
            qm.append(jnp.where(mine, q[here, lanes], jnp.zeros((), BF16)))
            gm.append(jnp.where(mine, dm[here, lanes], jnp.zeros((), BF16)))
            dqa[half, :, :r] = jnp.zeros((HD, r), F32)

        def step(key0):
            keys = pl.ds(key0, KEYS)
            k_left = jnp.concatenate([k[keys, lanes], ka[keys, :]], axis=1)
            v_left = jnp.concatenate([v[keys, lanes], ka[keys, :]], axis=1)
            for half in range(2):
                share = jnp.exp(dot(k_left, qs[half]))
                slope = (share * dot(v_left, gs[half])).astype(BF16)
                dva[keys, :] += dot(share.astype(BF16), gm[half])
                dka[keys, :] += dot(slope, qm[half])
                rows = pl.ds(pl.multiple_of(pair * 128 + half * HD, HD), HD)
                dqa[half, :, :r] += dot(kt[rows, keys], slope)

        over_keys(z, part, start, total, step)
        for half in range(2):
            rows = pl.ds(pl.multiple_of(pair * 128 + half * HD, HD), HD)
            dqt[rows, cols] = (dqa[half, :, :r] * HD ** (-0.5)).astype(BF16)
    dk[:, lanes] = dka[...].astype(BF16)
    dv[:, lanes] = dva[...].astype(BF16)


def attention_back_kernel(*refs):
    z = lax.axis_index("tp")

    def one_pair(pair, carry):
        back_pair(z, pair, lambda part: None, *refs)
        return carry

    lax.fori_loop(0, refs[2].shape[1] // 128, one_pair, 0)


def back_sums_kernel(qt_all, q_all, k_all, kt_all, v_all, ka_all, ma, mixed_all, lse, dmt_all, dm_all, *refs):
    g = (refs[0:4], refs[4:8])
    dqt, dk_out, dv_out, out_u, out_d, dka, dva, dqa, *bufs = refs[8:]
    qt, q, ka, mixed_t, dmt, dm, in_sem, k, kt, v, dk, dv, kv_sem, gk, *bufs = bufs
    bufs, (gk_sem, *sems) = bufs[:8], bufs[8:]
    z, d, core, first, second = position()
    pairs = k.shape[1] // 128

    def operands(pair):
        lanes = pl.ds(pl.multiple_of(pair * 128, 128), 128)
        return (
            pltpu.make_async_copy(k_all.at[:, lanes], k.at[:, lanes], kv_sem.at[0, pair]),
            pltpu.make_async_copy(v_all.at[:, lanes], v.at[:, lanes], kv_sem.at[1, pair]),
            pltpu.make_async_copy(kt_all.at[lanes, :], kt.at[lanes, :], kv_sem.at[2, pair]),
        )

    def results(pair):
        lanes = pl.ds(pl.multiple_of(pair * 128, 128), 128)
        return (
            pltpu.make_async_copy(dk.at[:, lanes], dk_out.at[:, lanes], kv_sem.at[3, pair]),
            pltpu.make_async_copy(dv.at[:, lanes], dv_out.at[:, lanes], kv_sem.at[4, pair]),
        )

    pieces = ((qt_all, qt), (dmt_all, dmt), (mixed_all, mixed_t), (q_all, q), (dm_all, dm), (ka_all, ka))
    early = [pltpu.make_async_copy(a, b, in_sem.at[i]) for i, (a, b) in enumerate(pieces)]
    for copy in early:
        copy.start()
    for copy in operands(0):
        copy.start()
    greet(z, d)

    def fetch(p, t):
        return pltpu.make_async_copy(g[p][t].at[:, core], gk.at[p, t], gk_sem.at[p, t])

    sums = Sums(
        z, d, core, second, first,
        lambda p, t: g[p][t].at[:, 1 - core],
        lambda p, t, at: up(gk.at[p, t, at]),
        lambda p, t: fetch(p, t).wait(),
        bufs, sems,
    )
    for p in range(2):
        for t in (3, 0, 2, 1):
            sums.one(p, t).start()
            fetch(p, t).start()
    for pair in range(1, pairs):
        for copy in operands(pair):
            copy.start()
    for copy in early:
        copy.wait()

    def each(act, *units):
        def run():
            for p, t in units:
                act(p, t)

        return run

    def four(p, step, ids=range(3)):
        sums.at_four(p, step, range(4) if step == 0 else (), ids)

    packs = [[(p, t) for t in (3, 0, 2, 1)] for p in range(2)]
    between = {
        (0, 1): each(sums.at_two, *packs[0]),
        (1, 0): each(sums.at_two, *packs[1]),
        (2, 0): each(sums.at_three, *packs[0][:2]),
        (2, 1): each(sums.at_three, *packs[0][2:]),
        (3, 1): lambda: four(0, 0),
        (4, 0): each(sums.at_three, *packs[1][:2]),
        (4, 1): lambda: four(0, 1),
        (5, 0): each(sums.at_three, *packs[1][2:]),
        (5, 1): lambda: (four(0, 2), four(1, 0, (0,))),
    }

    def one_pair(pair, carry):
        def pause(part):
            for (i, at), run in between.items():
                if at == part:

                    @pl.when(pair == i)
                    def _():
                        run()

        for copy in operands(pair):
            copy.wait()
        back_pair(z, pair, pause, qt, q, k, kt, v, ka, ma, mixed_t, lse, dmt, dm, dqt, dk, dv, dka, dva, dqa)
        for copy in results(pair):
            copy.start()
        return carry

    lax.fori_loop(0, k.shape[1] // 128, one_pair, 0)
    for step, ids in ((1, (0,)), (0, (1, 2)), (1, (1, 2)), (2, (0, 1, 2))):
        sums.at_four(1, step, (2, 1) if step == 0 else (), ids)
    for pair in range(pairs):
        for copy in results(pair):
            copy.wait()
    sums.result(0, out_u)
    sums.result(1, out_d)
    for p in range(2):
        sums.drain(p)


def back_shapes(own, total, width):
    widest = max(SHORT - own, own - (SHORT - own))
    vm = pltpu.VMEM
    outs = (
        jax.ShapeDtypeStruct((width, own), BF16),
        jax.ShapeDtypeStruct((total, width), BF16),
        jax.ShapeDtypeStruct((total, width), BF16),
    )
    return outs, [vm((total, 128), F32), vm((total, 128), F32), vm((2, HD, widest), F32)]


def attention_back(*args):
    (width, own), total = args[0].shape, args[2].shape[0]
    outs, scratch = back_shapes(own, total, width)
    return pl.pallas_call(
        attention_back_kernel,
        out_shape=outs,
        in_specs=[pl.BlockSpec(memory_space=pltpu.VMEM)] * 11,
        out_specs=(pl.BlockSpec(memory_space=pltpu.VMEM),) * 3,
        scratch_shapes=scratch,
        compiler_params=pltpu.CompilerParams(vmem_limit_bytes=VMEM_MAX),
        name="attention_back",
    )(*args)


def back_sums(args, gu, gd):
    (width, own), total = args[0].shape, args[2].shape[0]
    outs, scratch = back_shapes(own, total, width)
    block = (width // 8, gu[0].shape[1])
    g = [a.reshape((4, 2) + block) for a in (*gu, *gd)]
    vmem = pl.BlockSpec(memory_space=pltpu.VMEM)
    any_ = pl.BlockSpec(memory_space=pl.ANY)
    return pl.pallas_call(
        back_sums_kernel,
        out_shape=outs + (jax.ShapeDtypeStruct(block, F32),) * 2,
        in_specs=[any_] * 6 + [vmem, any_, vmem] + [any_] * 10,
        out_specs=(vmem, any_, any_, vmem, vmem),
        scratch_shapes=[
            *scratch,
            pltpu.VMEM((width, own), BF16),
            pltpu.VMEM((own, width), BF16),
            pltpu.VMEM((total, 128), BF16),
            pltpu.VMEM((width, own), F32),
            pltpu.VMEM((width, own), BF16),
            pltpu.VMEM((own, width), BF16),
            pltpu.SemaphoreType.DMA((6,)),
            pltpu.VMEM((total, width), BF16),
            pltpu.VMEM((width, total), BF16),
            pltpu.VMEM((total, width), BF16),
            pltpu.VMEM((total, width), BF16),
            pltpu.VMEM((total, width), BF16),
            pltpu.SemaphoreType.DMA((5, width // 128)),
            pltpu.VMEM((2, 4, 4) + block, BF16),
            *sum_buffers(2, block),
            pltpu.SemaphoreType.DMA((2, 4)),
            *sum_semaphores(2),
        ],
        compiler_params=pltpu.CompilerParams(
            collective_id=2, has_side_effects=True, vmem_limit_bytes=VMEM_MAX
        ),
        name="back_sums",
    )(*args, *g)


def norms_kernel(
    tok, mixed_t, vec, bu, cot, wd, w,
    enc_out, dr1_out, dar_out, dm_out, dmt_out, vecs, wide, *refs,
):
    gu, gd = refs[0:4], refs[4:8]
    wo, wu, wn, mixed, y1r, hr, slope, du, dfr, y1t, dft, stage, enc, dr1, dar, dm, dmt, w_sem, o_sem, r_sem = refs[8:]
    own, width = tok.shape
    n_tp = wu.shape[0]
    loads = [[pltpu.make_async_copy(w.at[i, t], b.at[t], w_sem.at[i, t]) for t in range(n_tp)] for i, b in enumerate((wu, wn))]
    load_o = pltpu.make_async_copy(wd.at[3], wo, w_sem.at[2, 0])
    load_o.start()
    for t in range(n_tp):
        for i in range(2):
            loads[i][t].start()
    vecs[...] = jnp.zeros_like(vecs)
    half = own // 2

    def flip_mixed(i, carry):
        cols = pl.ds(pl.multiple_of(i * ROWS, ROWS), ROWS)
        mixed[cols, :] = mixed_t[:, cols].T.astype(BF16)
        return carry

    lax.fori_loop(0, own // ROWS, flip_mixed, 0)
    load_o.wait()

    def row_tile(i, carry):
        rows = pl.ds(pl.multiple_of(i * half, 64), half)

        def add(index, value):
            vecs[index : index + 1, :] += jnp.sum(value, axis=0, keepdims=True)

        xhat1, inv1 = normalize_layer(tok[rows, :].astype(F32) + contract_last(mixed[rows, :], wo[...]) + vec[2:3, :])
        y1 = xhat1 * vec[3:4, :] + vec[4:5, :]
        y1b = y1.astype(BF16)
        y1r[rows, :] = y1b
        total = y1 + vec[5:6, :]

        @pl.when(i == 0)
        def _():
            for t in range(n_tp):
                for j in range(2):
                    loads[j][t].wait()

        for t in range(n_tp):
            u = dot(y1b, wu[t]) + bu[:, t * width : (t + 1) * width]
            below = 0.5 * (1.0 + lax.erf(u * SQRT_HALF))
            h = (u * below).astype(BF16)
            hr[t, rows, :] = h
            slope[t] = below + u * jnp.exp(-0.5 * u * u) * INV_ROOT_TAU
            total = total + contract_last(h, wn[t])
        xhat2, inv2 = normalize_layer(total)
        enc[rows, :] = (xhat2 * vec[6:7, :] + vec[7:8, :]).astype(BF16)
        grad = cot[rows, :].astype(F32)
        add(6, grad * xhat2)
        add(7, grad)
        dr2 = normalize_backward(grad, xhat2, inv2, vec[6:7, :])
        dfb = dr2.astype(BF16)
        dfr[rows, :] = dfb
        add(5, dfb.astype(F32))
        dy1 = dr2
        for t in range(n_tp):
            back = (dot(dfb, wn[t]) * slope[t]).astype(BF16)
            du[t, rows, :] = back
            dy1 = dy1 + contract_last(back, wu[t])
        add(3, dy1 * xhat1)
        add(4, dy1)
        first = normalize_backward(dy1, xhat1, inv1, vec[3:4, :])
        dr1[rows, :] = first
        dab = first.astype(BF16)
        dar[rows, :] = dab
        add(2, dab.astype(F32))
        dm[rows, :] = dot(dab, wo[...]).astype(BF16)
        return carry

    lax.fori_loop(0, 2, row_tile, 0)
    pieces = ((enc, enc_out), (dr1, dr1_out), (dar, dar_out), (dm, dm_out), (dmt, dmt_out))
    outs = [pltpu.make_async_copy(a, b, r_sem.at[i]) for i, (a, b) in enumerate(pieces)]
    for copy in outs[:4]:
        copy.start()

    def flip(i, carry):
        cols = pl.ds(pl.multiple_of(i * ROWS, ROWS), ROWS)
        dft[:, cols] = dfr[cols, :].T
        y1t[:, cols] = y1r[cols, :].T
        dmt[:, cols] = dm[cols, :].T
        return carry

    lax.fori_loop(0, own // ROWS, flip, 0)
    outs[4].start()
    tile = 256
    ones = jnp.ones((8, own), BF16)

    def store(i, t):
        return pltpu.make_async_copy(stage.at[i, t], (gd, gu)[i][t], o_sem.at[i, t])

    for t in range(n_tp):

        def one_tile(n, carry):
            lanes = pl.ds(pl.multiple_of(n * tile, tile), tile)
            stage[0, t, :, lanes] = dot(dft[...], hr[t, :, lanes]).astype(BF16)
            stage[1, t, :, lanes] = dot(y1t[...], du[t, :, lanes]).astype(BF16)
            wide[0:1, pl.ds(pl.multiple_of(t * width + n * tile, tile), tile)] = dot(ones, du[t, :, lanes])[0:1, :]
            return carry

        lax.fori_loop(0, width // tile, one_tile, 0)
        for i in range(2):
            store(i, t).start()
    for t in range(n_tp):
        for i in range(2):
            store(i, t).wait()
    for copy in outs:
        copy.wait()


def norms(tok, mixed_t, vec, bu, cot, wd, w):
    own, width = tok.shape
    dma, vm = pltpu.SemaphoreType.DMA, pltpu.VMEM
    any_ = pl.BlockSpec(memory_space=pl.ANY)
    vmem = pl.BlockSpec(memory_space=pltpu.VMEM)
    shape = jax.ShapeDtypeStruct
    square = (width, width)
    return pl.pallas_call(
        norms_kernel,
        out_shape=(
            shape((own, width), BF16),
            shape((own, width), F32),
            shape((own, width), BF16),
            shape((own, width), BF16),
            shape((width, own), BF16),
            shape((8, width), F32),
            shape((1, 4 * width), F32),
        )
        + (shape(square, BF16),) * 8,
        in_specs=[vmem] * 5 + [any_] * 2,
        out_specs=(any_,) * 5 + (vmem,) * 2 + (any_,) * 8,
        scratch_shapes=[
            vm(square, BF16),
            vm((4,) + square, BF16),
            vm((4,) + square, BF16),
            vm((own, width), BF16),
            vm((own, width), BF16),
            vm((4, own, width), BF16),
            vm((4, own // 2, width), F32),
            vm((4, own, width), BF16),
            vm((own, width), BF16),
            vm((width, own), BF16),
            vm((width, own), BF16),
            vm((2, 4) + square, BF16),
            vm((own, width), BF16),
            vm((own, width), F32),
            vm((own, width), BF16),
            vm((own, width), BF16),
            vm((width, own), BF16),
            dma((3, 4)),
            dma((2, 4)),
            dma((5,)),
        ],
        compiler_params=pltpu.CompilerParams(vmem_limit_bytes=VMEM_MAX),
        name="norms",
    )(tok, mixed_t, vec, bu, cot, wd, w)


def body(
    tokens, w_query, w_key, w_value, b_query, b_value, w_out, b_out, gain_attn, shift_attn,
    w_up, b_up, w_down, b_down, gain_ffn, shift_ffn, lengths, deal_order, cotangent,
):
    own, width = tokens.shape
    n_tp, n_dp = lax.axis_size("tp"), lax.axis_size("dp")
    z, g = lax.axis_index("tp"), lax.axis_index("dp")
    total = own * n_tp
    r, hw = w_query.shape
    direct = n_tp == 4 and n_dp == 8 and r % 16 == 0

    own_w = jnp.stack([jnp.concatenate([w_query, w_key, w_value, w_out], axis=1), w_up, w_down])
    vectors = (b_query, b_value, b_out, gain_attn, shift_attn, b_down, gain_ffn, shift_ffn, b_up)
    n_small = 8 * r + b_up.shape[0]
    if direct:
        line = jnp.arange(8, dtype=jnp.int32)[:, None]
        narrow = jnp.zeros((8, r), BF16)
        for i, a in enumerate(vectors[:8]):
            narrow = jnp.where(line == i, a[None, :], narrow)
        narrow = jnp.pad(narrow, ((0, 0), (0, 128 - r)))
        own_s = jnp.concatenate([narrow, jnp.pad(b_up.reshape(-1, 128), ((0, 5), (0, 0)))])
        w, vec, bu, xt, q, qt, k, v, kt, wd, ka, mixed_t, lse, ma = forward_all(lengths, deal_order, own_w, own_s, tokens)
        w = w.reshape(2, n_tp, width, w_up.shape[1])
        encoder_output, dr1, dar, dm, dmt, vecs, wide_sum, *gw = norms(tokens, mixed_t, vec, bu, cotangent, wd, w)
        args = (qt, q, k, kt, v, ka, ma, mixed_t, lse, dmt, dm)
        dqt, dk, dv, g_up, g_down = back_sums(args, gw[:4], gw[4:])
        a, gs, grad_tokens = finish(dqt, dk, dv, xt, dar, mixed_t, wd, dr1, vecs, wide_sum)
        gs = [gs[i, :r] for i in range(8)] + [gs[8:11].reshape(-1)]
    else:
        w = lax.all_gather(own_w, ("tp", "dp"), axis=0).reshape((n_tp, n_dp) + own_w.shape)
        w = jnp.moveaxis(w, 2, 0).reshape(3, n_tp, width, w_up.shape[1])
        s = lax.all_gather(jnp.concatenate(vectors), "dp", axis=0)
        x = lax.all_gather(tokens, "tp", axis=0, tiled=True)
        small = [s[:, i * r : (i + 1) * r].reshape(width).astype(F32) for i in range(8)]
        bq, bv, bo, g1, h1, bd, g2, h2 = small
        bu = s[:, 8 * r : n_small].reshape(-1).astype(F32)
        wq, wk, wv, wo = (
            w[0, :, :, i * hw : (i + 1) * hw].transpose(1, 0, 2).reshape(width, width) for i in range(4)
        )
        w = w[1:]
        q = (dot(tokens, wq) + bq).astype(BF16) * jnp.asarray(HD ** (-0.5), BF16)
        k = dot(x, wk).astype(BF16)
        v = (dot(x, wv) + bv).astype(BF16)
        qt, kt = q.T, k.T

        pair = lax.dynamic_slice_in_dim(deal_order, 2 * g, 1)
        first_len = jnp.sum(jnp.where(jnp.arange(lengths.shape[0], dtype=jnp.int32) == pair[0], lengths, 0))
        key_seg = jnp.arange(total, dtype=jnp.int32)[:, None] >= first_len
        lane = jnp.arange(128, dtype=jnp.int32)[None, :]
        ka = jnp.where(lane == 0, ~key_seg, jnp.where(lane == 1, key_seg, (lane >= 2) & (lane < 5))).astype(BF16)
        row_seg = (z * own + jnp.arange(own, dtype=jnp.int32))[None, :] >= first_len
        sub = jnp.arange(8, dtype=jnp.int32)[:, None]
        ma = jnp.where(((sub == 0) & row_seg) | ((sub == 1) & ~row_seg), MASKED, 0.0).astype(F32)

        mixed_t, lse = attention(qt, k, v.T, ka, ma)
        mixed = mixed_t.T.astype(BF16)
        first_residual = tokens.astype(F32) + contract_last(mixed, wo) + bo
        xhat1, inv1 = normalize_layer(first_residual)
        y1 = xhat1 * g1 + h1
        y1r = y1.astype(BF16)

        u = [dot(y1r, w[0, t]) + bu.reshape(n_tp, -1)[t] for t in range(n_tp)]
        hr = [jax.nn.gelu(a, approximate=False).astype(BF16) for a in u]
        ffn = sum(contract_last(hr[t], w[1, t]) for t in range(n_tp))
        xhat2, inv2 = normalize_layer(y1 + ffn + bd)
        encoder_output = (xhat2 * g2 + h2).astype(BF16)

        grad = cotangent.astype(F32)
        dr2 = normalize_backward(grad, xhat2, inv2, g2)
        dfr = dr2.astype(BF16)
        du = [(dot(dfr, w[1, t]) * gelu_slope(u[t])).astype(BF16) for t in range(n_tp)]
        dy1 = dr2 + sum(contract_last(du[t], w[0, t]) for t in range(n_tp))
        dr1 = normalize_backward(dy1, xhat1, inv1, g1)
        dar = dr1.astype(BF16)
        dm = dot(dar, wo).astype(BF16)
        gu = [contract_first(y1r, du[t]) for t in range(n_tp)]
        gd = [contract_first(dfr, hr[t]) for t in range(n_tp)]
        row_sums = [
            jnp.sum(dar, axis=0, dtype=F32),
            jnp.sum(dy1 * xhat1, axis=0),
            jnp.sum(dy1, axis=0),
            jnp.sum(dfr, axis=0, dtype=F32),
            jnp.sum(grad * xhat2, axis=0),
            jnp.sum(grad, axis=0),
        ]
        wide_sum = jnp.concatenate([jnp.sum(a, axis=0, dtype=F32) for a in du])
        back_args = (qt, q, k, kt, v, ka, ma, mixed_t, lse, dm.T, dm)
        dqt, dk, dv = attention_back(*back_args)
        dq = dqt.T
        base = dr1 + contract_last(dq, wq)
        far = contract_last(dk, wk) + contract_last(dv, wv)
        base = base + lax.dynamic_slice_in_dim(far, z * own, own)
        dt = far.astype(BF16)
        gq, gk, gv = contract_first(tokens, dq), contract_first(x, dk), contract_first(x, dv)
        go = contract_first(dar, mixed)
        ga = jnp.stack(
            [
                jnp.concatenate([m[:, t * hw : (t + 1) * hw] for m in (gq, gk, gv, go)], axis=1)
                for t in range(n_tp)
            ]
        )
        sums = [jnp.sum(dq, axis=0, dtype=F32), jnp.sum(dv, axis=0, dtype=F32)] + row_sums
        sums = [a.reshape(n_dp, r) for a in sums]
        sv = jnp.concatenate(sums + [wide_sum.reshape(n_dp, -1)], axis=1)
        grads = jnp.stack([ga, jnp.stack(gu), jnp.stack(gd)], axis=1).reshape(n_tp, 3, n_dp, r, -1)
        grads = jnp.moveaxis(grads, 1, 2).reshape(n_tp * n_dp, 3, r, -1)
        gw = lax.psum_scatter(grads, ("tp", "dp"), scatter_dimension=0, tiled=True)[0]
        gs = lax.psum_scatter(lax.psum(sv, "tp"), "dp", scatter_dimension=0, tiled=True)[0]
        others = jnp.where(jnp.arange(total)[:, None] // own == z, jnp.zeros((), BF16), dt)
        grad_tokens = base + lax.psum_scatter(others, "tp", scatter_dimension=0, tiled=True).astype(F32)
        gs = [gs[i * r : (i + 1) * r] for i in range(8)] + [gs[8 * r : n_small]]
        a, g_up, g_down = gw[0], gw[1], gw[2]
    return (
        encoder_output, grad_tokens,
        a[:, :hw], a[:, hw : 2 * hw], a[:, 2 * hw : 3 * hw], gs[0], gs[1],
        a[:, 3 * hw :], gs[2], gs[3], gs[4],
        g_up, gs[8], g_down, gs[5], gs[6], gs[7],
    )


def solution(mesh):
    rows, block, vector = P(("dp", "tp"), None), P("dp", "tp"), P("dp")
    in_specs = (
        rows, block, block, block, vector, vector, block, vector, vector, vector,
        block, vector, block, vector, vector, vector, P(), P(), rows,
    )
    out_specs = (
        rows, rows, block, block, block, vector, vector, block, vector, vector, vector,
        block, vector, block, vector, vector, vector,
    )
    return jax.shard_map(body, mesh=mesh, in_specs=in_specs, out_specs=out_specs, check_vma=False)
```

```python
import functools

import jax
import jax.numpy as jnp
from jax import lax
from jax.experimental import pallas as pl
from jax.experimental.pallas import tpu as pltpu
from jax.sharding import PartitionSpec as P

HD = 64
SHORT = 1024
EPS = 1e-05
SQRT_HALF = 0.7071067811865476
INV_ROOT_TAU = 0.3989422804014327
MASKED = -1e30
KEYS = 512
ROWS = 128
VMEM_MAX = 67043328
MESH = pl.DeviceIdType.MESH
F32 = jnp.float32
BF16 = jnp.bfloat16


def dot(left, right):
    return jnp.dot(left, right, preferred_element_type=F32)


def contract_last(left, right):
    return lax.dot_general(left, right, (((1,), (1,)), ((), ())), preferred_element_type=F32)


def contract_first(left, right):
    return lax.dot_general(left, right, (((0,), (0,)), ((), ())), preferred_element_type=F32)


def normalize_layer(resid):
    center = resid - jnp.mean(resid, axis=-1, keepdims=True)
    inverse_deviation = lax.rsqrt(jnp.mean(center * center, axis=-1, keepdims=True) + EPS)
    return (center * inverse_deviation, inverse_deviation)


def normalize_backward(output_gradient, xhat, inverse_deviation, gain):
    scaled_rows = output_gradient * gain
    return inverse_deviation * (
        scaled_rows
        - jnp.mean(scaled_rows, axis=-1, keepdims=True)
        - xhat * jnp.mean(scaled_rows * xhat, axis=-1, keepdims=True)
    )


def gelu_slope(pre_act):
    return (
        0.5 * (1.0 + lax.erf(pre_act * SQRT_HALF))
        + pre_act * jnp.exp(-0.5 * pre_act * pre_act) * INV_ROOT_TAU
    )


def position():
    z = lax.axis_index("tp")
    d = lax.axis_index("dp")
    core = lax.rem(d, 2)
    first = 2 + 2 * core
    second = 4 - 2 * core
    return z, d, core, first, second


def xor(d, mask):
    return d + mask * (1 - 2 * lax.rem(d // mask, 2))


def greet(z, d):
    barrier = pltpu.get_barrier_semaphore()
    for mask in (1, 2, 4):
        pl.semaphore_signal(barrier, inc=1, device_id=(xor(d, mask), z), device_id_type=MESH)
    for j in range(1, 4):
        pl.semaphore_signal(barrier, inc=1, device_id=(d, lax.rem(z + j, 4)), device_id_type=MESH)
    pl.semaphore_wait(barrier, 6)


def by_distance(z):
    low = z <= 1
    near = jnp.where(z == 0, 1, jnp.where(z == 1, 0, jnp.where(z == 2, 3, 2)))
    mid = jnp.where(low, 2, 1)
    far = jnp.where(low, 3, 0)
    return (z, near, mid, far)


def put(src, dst, send, recv, dp, tp):
    return pltpu.make_async_remote_copy(
        src_ref=src, dst_ref=dst, send_sem=send, recv_sem=recv, device_id=(dp, tp), device_id_type=MESH
    )


def forward_kernel(
    lengths, deal, own_w, own_s, own_t,
    w, vec, bu, xt_out, q_out, qt_out, k_out, v_out, kt_out, wd_out, ka_out, mixed_t, lse, ma,
    wa, s, x, xt, q, qt, k, v, kt, vt, wd, ka, sc, m, l, acc,
    wz_s, wz_r, wa_s, wa_r, wb_s, wb_r, wc_s, wc_r, tk_s, tk_r, sm_s, sm_r, lo_sem, arr_sem, out_sem,
):
    z, d, core, first, second = position()
    packs = own_w.shape[0]
    own, width = own_t.shape
    total = 4 * own
    hw = width // 4
    chunks = own // ROWS
    d1, d2 = xor(d, first), xor(d, second)
    d12 = xor(d1, second)
    pal = xor(d, 1)
    pd, pd1, pd2, pd12 = (xor(e, 1) for e in (d, d1, d2, d12))
    order = by_distance(z)
    first_len = lengths[deal[2 * d]]

    greet(z, d)

    def block(p, tt, e):
        return wa.at[tt, e] if p == 0 else w.at[p - 1, tt, e]

    def along_z(p, tt, src, act):
        dst = block(p, tt, d)
        right = put(src, dst, wz_s.at[0, p, tt], wz_r.at[p, tt], d, jnp.minimum(z + 1, 3))
        left = put(src, dst, wz_s.at[1, p, tt], wz_r.at[p, tt], d, jnp.maximum(z - 1, 0))

        @pl.when((tt <= z) & (z < 3))
        def _():
            act(right)

        @pl.when((tt >= z) & (z > 0))
        def _():
            act(left)

    def across(p, tt, src):
        dst = block(p, tt, d)
        return (
            put(src, dst, wa_s.at[p, tt], wa_r.at[p, tt], d1, z),
            put(src, dst, wb_s.at[p, tt, 0], wb_r.at[p, tt, 0], d2, z),
            put(src, dst, wc_s.at[p, tt, 0], wc_r.at[p, tt, 0], pal, z),
        )

    def after_first(p, tt):
        src = block(p, tt, d1)
        return (
            put(src, src, wb_s.at[p, tt, 1], wb_r.at[p, tt, 1], d2, z),
            put(src, src, wc_s.at[p, tt, 1], wc_r.at[p, tt, 1], pal, z),
        )

    def after_second(p, tt, i):
        src = block(p, tt, d2 if i == 0 else d12)
        return put(src, src, wc_s.at[p, tt, 2 + i], wc_r.at[p, tt, 2 + i], pal, z)

    def source(p, j):
        return own_w.at[p] if j == 0 else block(p, order[j], d)

    def arrive(ref, sem):
        put(ref, ref, arr_sem, sem, pal, z).wait_recv()

    def begin_z(p, j):
        if j > 0:
            arrive(block(p, order[j], d), wz_r.at[p, order[j]])
        along_z(p, order[j], source(p, j), lambda c: c.start())

    def begin_xy(p, j):
        for copy in across(p, order[j], source(p, j)):
            copy.start()

    def begin(p, j):
        begin_z(p, j)
        begin_xy(p, j)

    def relay_first(p, j):
        tt = order[j]
        arrive(block(p, tt, d1), wa_r.at[p, tt])
        for copy in after_first(p, tt):
            copy.start()

    def relay_second(p, j):
        tt = order[j]
        for i in range(2):
            arrive(block(p, tt, d2 if i == 0 else d12), wb_r.at[p, tt, i])
            after_second(p, tt, i).start()

    def from_pal(p):
        for tt in range(4):
            for i, e in enumerate((pd, pd2, pd1, pd12)):
                arrive(block(p, tt, e), wc_r.at[p, tt, i])

    def sent(p):
        for j in range(4):
            tt = order[j]
            along_z(p, tt, source(p, j), lambda c: c.wait_send())
            for copy in across(p, tt, source(p, j)) + after_first(p, tt):
                copy.wait_send()
            for i in range(2):
                after_second(p, tt, i).wait_send()

    def token_slice(o, i):
        return x.at[pl.ds(pl.multiple_of((o * chunks + i) * ROWS, ROWS), ROWS)]

    def token_hop(o, i, hop, step):
        src = own_t.at[pl.ds(i * ROWS, ROWS)] if hop == 0 else token_slice(o, i)
        way = 0 if step > 0 else 1
        return put(src, token_slice(o, i), tk_s.at[way, hop, i], tk_r.at[way, hop, i], d, jnp.clip(z + step, 0, 3))

    last = SHORT // ROWS

    def wanted(o, i, target, step):
        n = o * chunks + i
        if step > 0:
            return (target <= 2) | (n >= last)
        return (target >= 1) | (n < 4 * chunks - last)

    def chunk_ids(step):
        return list(range(chunks))[:: -step]

    def tokens(hop, step, act, which=slice(None)):
        o, target = z - step * hop, z + step
        valid = (o >= 0) & (o <= 3) & (target >= 0) & (target <= 3)
        for i in chunk_ids(step)[which]:

            @pl.when(valid & wanted(o, i, target, step))
            def _():
                act(token_hop(o, i, hop, step))

    def tokens_on(hop, step, onward):
        o, target = z - step * (hop + 1), z + step
        valid = (o >= 0) & (o <= 3) & (z - step >= 0) & (z - step <= 3)
        way = 0 if step > 0 else 1
        for i in chunk_ids(step):

            @pl.when(valid & wanted(o, i, z, step))
            def _():
                arrive(token_slice(jnp.clip(o, 0, 3), i), tk_r.at[way, hop, i])

            if onward:

                @pl.when(valid & (target >= 0) & (target <= 3) & wanted(o, i, target, step))
                def _():
                    token_hop(o, i, hop + 1, step).start()

    def small(stage):
        if stage == 0:
            return [
                put(own_s, s.at[d], sm_s.at[0], sm_r.at[0], d1, z),
                put(own_s, s.at[d], sm_s.at[1], sm_r.at[1], d2, z),
                put(own_s, s.at[d], sm_s.at[3], sm_r.at[3], pal, z),
            ]
        if stage == 1:
            return [
                put(s.at[d1], s.at[d1], sm_s.at[2], sm_r.at[2], d2, z),
                put(s.at[d1], s.at[d1], sm_s.at[4], sm_r.at[4], pal, z),
            ]
        return [
            put(s.at[d2], s.at[d2], sm_s.at[5], sm_r.at[5], pal, z),
            put(s.at[d12], s.at[d12], sm_s.at[6], sm_r.at[6], pal, z),
        ]

    def own_tokens(*which):
        for step in (1, -1):
            tokens(0, step, lambda c: c.start(), slice(*which))

    begin(0, 0)
    for copy in small(0):
        copy.start()
    own_tokens(0, 1)
    s[d] = own_s[...]
    wa[z, d] = own_w[0]
    mine = pl.ds(pl.multiple_of(z * own, ROWS), own)
    x[mine, :] = own_t[...]
    keep = pltpu.make_async_copy(own_w.at[pl.ds(1, packs - 1)], w.at[:, z, d], lo_sem)
    keep.start()

    @pl.when(z == 0)
    def _():
        x[total - SHORT :, :] = jnp.zeros((SHORT, width), BF16)
        xt[:, total - SHORT :] = jnp.zeros((width, SHORT), BF16)

    @pl.when(z == 3)
    def _():
        x[:SHORT, :] = jnp.zeros((SHORT, width), BF16)
        xt[:, :SHORT] = jnp.zeros((width, SHORT), BF16)

    middle = (z == 1) | (z == 2)
    begin(0, 1)
    relay_first(0, 0)
    for p in range(1, packs):
        begin_z(p, 0)
    begin(0, 2)
    relay_second(0, 0)
    relay_first(0, 1)
    own_tokens(1, 2)
    begin(0, 3)
    own_tokens(2, 3)
    relay_second(0, 1)
    relay_first(0, 2)
    begin_xy(1, 0)
    arrive(s.at[d1], sm_r.at[0])
    for copy in small(1):
        copy.start()
    relay_second(0, 2)
    relay_first(0, 3)
    for p in range(2, packs):
        begin_xy(p, 0)
    arrive(s.at[d2], sm_r.at[1])
    arrive(s.at[d12], sm_r.at[2])
    for copy in small(2):
        copy.start()
    for p in range(1, packs):
        begin(p, 1)

    @pl.when(middle)
    def _():
        for p in range(1, packs):
            begin(p, 2)

    own_tokens(3, chunks)
    lane = lax.broadcasted_iota(jnp.int32, (own, 128), 1)
    for i in range(4):
        late = lax.broadcasted_iota(jnp.int32, (own, 128), 0) + i * own >= first_len
        ones = jnp.where((lane >= 2) & (lane < 5), 1.0, 0.0)
        flags = jnp.where(lane == 0, jnp.where(late, 0.0, 1.0), jnp.where(lane == 1, jnp.where(late, 1.0, 0.0), ones))
        ka[pl.ds(i * own, own), :] = flags.astype(BF16)

    relay_second(0, 3)
    for i, e in enumerate((pd, pd2, pd1, pd12)):
        arrive(s.at[e], sm_r.at[3 + i])
    r = width // 8
    for e in range(8):
        piece = s[e].astype(F32)
        vec[0:8, e * r : (e + 1) * r] = piece[0:8, 0:r]
        for j in range(hw * 2 // 128):
            col = e * hw * 2 + j * 128
            bu[0:1, col : col + 128] = piece[8 + j : 9 + j, :]
    from_pal(0)
    for tt in range(4):
        rows = wa[tt].reshape(width, width)
        for i in range(4):
            wd[i, :, tt * hw : (tt + 1) * hw] = rows[:, i * hw : (i + 1) * hw]
    wd_copy = pltpu.make_async_copy(wd, wd_out, out_sem.at[0])
    wd_copy.start()

    tile = 256

    def q_tile(n, carry):
        lanes = pl.ds(pl.multiple_of(n * tile, tile), tile)
        rows = (dot(own_t[...], wd[0, :, lanes]) + vec[0:1, lanes]).astype(BF16) * jnp.asarray(HD ** (-0.5), BF16)
        q[:, lanes] = rows
        qt[lanes, :] = rows.T
        return carry

    def project(o):
        rows = pl.ds(pl.multiple_of(o * own, ROWS), own)

        def kv_tile(n, carry):
            lanes = pl.ds(pl.multiple_of(n * tile, tile), tile)
            keys = dot(x[rows, :], wd[1, :, lanes]).astype(BF16)
            k[rows, lanes] = keys
            kt[lanes, rows] = keys.T
            values = (dot(x[rows, :], wd[2, :, lanes]) + vec[1:2, lanes]).astype(BF16)
            v[rows, lanes] = values
            vt[lanes, rows] = values.T
            xt[lanes, rows] = x[rows, lanes].T
            return carry

        lax.fori_loop(0, width // tile, kv_tile, 0)

    def project_far():
        for step in (1, -1):
            tokens_on(1, step, False)
        project(jnp.where(z == 0, 2, jnp.where(z == 1, 3, z - 2)))

    lax.fori_loop(0, width // tile, q_tile, 0)
    project(z)
    for p in range(1, packs):
        relay_first(p, 0)
    for step in (1, -1):
        tokens_on(0, step, True)

    @pl.when(z > 0)
    def _():
        project(jnp.maximum(z - 1, 0))

    @pl.when(jnp.logical_not(middle))
    def _():
        for p in range(1, packs):
            begin(p, 2)

    for p in range(1, packs):
        relay_second(p, 0)
        relay_first(p, 1)

    @pl.when(z < 3)
    def _():
        project(jnp.minimum(z + 1, 3))

    @pl.when(jnp.logical_not(middle))
    def _():
        project_far()

    def both(act, j):
        def run():
            for p in range(1, packs):
                act(p, j)

        return run

    def last_block(inner):
        def run():
            @pl.when(middle if inner else jnp.logical_not(middle))
            def _():
                for p in range(1, packs):
                    begin(p, 3)

        return run

    between = {
        (0, 0): last_block(True),
        (0, 1): both(relay_second, 1),
        (0, 2): both(relay_first, 2),
        (0, 4): last_block(False),
        (0, 5): both(relay_second, 2),
        (1, 0): both(relay_first, 3),
        (1, 4): both(relay_second, 3),
    }
    late = lax.broadcasted_iota(jnp.int32, (8, own), 1) + z * own >= first_len
    sub = lax.broadcasted_iota(jnp.int32, (8, own), 0)
    away = jnp.where(sub == 0, jnp.where(late, MASKED, 0.0), jnp.where(sub == 1, jnp.where(late, 0.0, MASKED), 0.0))
    ma[...] = away
    outs = [
        pltpu.make_async_copy(a, b, out_sem.at[1 + i])
        for i, (a, b) in enumerate(
            ((xt, xt_out), (q, q_out), (qt, qt_out), (k, k_out), (v, v_out), (kt, kt_out), (ka, ka_out))
        )
    ]
    pairs = width // 128
    for part, (row0, n, start) in enumerate(parts_of(z, own)):
        if part == 1:

            @pl.when(middle)
            def _():
                project_far()

            for copy in outs:
                copy.start()
        cols = pl.ds(pl.multiple_of(row0, 128), n)
        late = lax.broadcasted_iota(jnp.int32, (1, n), 1) + (z * own + row0) >= first_len
        masks = (jnp.where(late, MASKED, 0.0), jnp.where(late, 0.0, MASKED))
        aug = aug_rows(pick_rows(masks, n), n)

        def one_pair(pair, carry):
            for (at, i), run in between.items():
                if at == part:

                    @pl.when(pair == i)
                    def _():
                        run()

            attend_pair(z, part, start, pair, cols, n, aug, qt, k, vt, ka, mixed_t, lse, sc, m, l, acc)
            return carry

        lax.fori_loop(0, pairs, one_pair, 0)

    for p in range(1, packs):
        from_pal(p)
    for stage in range(3):
        for copy in small(stage):
            copy.wait_send()
    for hop in range(2):
        for step in (1, -1):
            tokens(hop, step, lambda c: c.wait_send())
    for p in range(packs):
        sent(p)
    keep.wait()
    wd_copy.wait()
    for copy in outs:
        copy.wait()


def attend_pair(z, part, start, pair, cols, n, aug, qt, k, vt, ka, mixed_t, lse, s, m, l, acc):
    total = k.shape[0]
    lanes = pl.ds(pl.multiple_of(pair * 128, 128), 128)
    for half in range(2):
        m[half, :, :n] = jnp.full((1, n), MASKED, F32)
        l[half, :, :n] = jnp.zeros((1, n), F32)
        acc[half, :, :n] = jnp.zeros((HD, n), F32)
    qs = [padded(qt[pl.ds(pl.multiple_of(pair * 128 + half * HD, HD), HD), cols], half, aug, n) for half in range(2)]

    def scores(key0):
        keys = pl.ds(key0, KEYS)
        left = jnp.concatenate([k[keys, lanes], ka[keys, :]], axis=1)
        for half in range(2):
            score = dot(left, qs[half])
            s[half, keys, :n] = score
            m[half, :, :n] = jnp.maximum(m[half, :, :n], jnp.max(score, axis=0, keepdims=True))

    over_keys(z, part, start, total, scores)
    tops = [m[half, :, :n] for half in range(2)]

    def mix(key0):
        keys = pl.ds(key0, KEYS)
        for half in range(2):
            raised = jnp.exp(s[half, keys, :n] - tops[half])
            l[half, :, :n] += jnp.sum(raised, axis=0, keepdims=True)
            values = vt[pl.ds(pl.multiple_of(pair * 128 + half * HD, HD), HD), keys]
            acc[half, :, :n] += dot(values, raised.astype(BF16))

    over_keys(z, part, start, total, mix)
    for half in range(2):
        sums = l[half, :, :n]
        rows = pl.ds(pl.multiple_of(pair * 128 + half * HD, HD), HD)
        mixed_t[rows, cols] = acc[half, :, :n] / sums
        lse[pair, half : half + 1, cols] = tops[half] + jnp.log(sums)


def forward_all(lengths, deal, own_w, own_s, own_t):
    packs, r, c = own_w.shape
    own, width = own_t.shape
    total = 4 * own
    chunks = own // ROWS
    widest = max(SHORT - own, own - (SHORT - own))
    dma, vm = pltpu.SemaphoreType.DMA, pltpu.VMEM
    any_ = pl.BlockSpec(memory_space=pl.ANY)
    vmem = pl.BlockSpec(memory_space=pltpu.VMEM)
    smem = pl.BlockSpec(memory_space=pltpu.SMEM)
    shape = jax.ShapeDtypeStruct
    return pl.pallas_call(
        forward_kernel,
        out_shape=(
            shape((packs - 1, 4, 8, r, c), BF16),
            shape((8, width), F32),
            shape((1, 4 * c), F32),
            shape((width, total), BF16),
            shape((own, width), BF16),
            shape((width, own), BF16),
            shape((total, width), BF16),
            shape((total, width), BF16),
            shape((width, total), BF16),
            shape((4, width, width), BF16),
            shape((total, 128), BF16),
            shape((width, own), F32),
            shape((width // 128, 8, own), F32),
            shape((8, own), F32),
        ),
        in_specs=[smem, smem, vmem, vmem, vmem],
        out_specs=(any_, vmem, vmem) + (any_,) * 8 + (vmem, vmem, vmem),
        scratch_shapes=[
            vm((4, 8, r, c), BF16),
            vm((8, 16, 128), BF16),
            vm((total, width), BF16),
            vm((width, total), BF16),
            vm((own, width), BF16),
            vm((width, own), BF16),
            vm((total, width), BF16),
            vm((total, width), BF16),
            vm((width, total), BF16),
            vm((width, total), BF16),
            vm((4, width, width), BF16),
            vm((total, 128), BF16),
            vm((2, total, widest), F32),
            vm((2, 1, widest), F32),
            vm((2, 1, widest), F32),
            vm((2, HD, widest), F32),
            dma((2, packs, 4)),
            dma((packs, 4)),
            dma((packs, 4)),
            dma((packs, 4)),
            dma((packs, 4, 2)),
            dma((packs, 4, 2)),
            dma((packs, 4, 4)),
            dma((packs, 4, 4)),
            dma((2, 2, chunks)),
            dma((2, 2, chunks)),
            dma((7,)),
            dma((7,)),
            dma(()),
            dma(()),
            dma((8,)),
        ],
        compiler_params=pltpu.CompilerParams(
            collective_id=0, has_side_effects=True, vmem_limit_bytes=VMEM_MAX
        ),
        name="forward_all",
    )(lengths, deal, own_w, own_s, own_t)


def up(ref):
    return ref[...].astype(F32)


class Sums:
    def __init__(self, z, d, core, e_mask, f_mask, give, mine, ready, bufs, sems):
        self.z, self.d, self.give, self.mine, self.ready = z, d, give, mine, ready
        self.r1, self.b2, self.r2, self.b3, self.r3, self.s3, self.b4, self.r4 = bufs
        self.sems = sems
        self.xy = d // 2
        self.e, self.f = xor(d, e_mask) // 2, xor(d, f_mask) // 2
        self.ef = xor(xor(d, e_mask), f_mask) // 2
        self.d_e, self.d_f, self.pal = xor(d, e_mask), xor(d, f_mask), xor(d, 1)

    def one(self, p, t):
        return put(self.give(p, t), self.r1.at[p, t], self.sems[0].at[p, t], self.sems[1].at[p, t], self.pal, self.z)

    def two(self, p, t):
        return put(self.b2.at[p, t], self.r2.at[p, t], self.sems[2].at[p, t], self.sems[3].at[p, t], self.d_e, self.z)

    def three(self, p, t):
        return put(self.b3.at[p, t], self.r3.at[p, t], self.sems[4].at[p, t], self.sems[5].at[p, t], self.d_f, self.z)

    def four(self, p, t, way):
        to = jnp.minimum(self.z + 1, 3) if way == 0 else jnp.maximum(self.z - 1, 0)
        return put(
            self.b4.at[p, way, t], self.r4.at[p, way, t],
            self.sems[6].at[p, way, t], self.sems[7].at[p, way, t], self.d, to,
        )

    def at_two(self, p, t):
        self.ready(p, t)
        self.one(p, t).wait_recv()
        for i, x in enumerate((self.e, self.ef)):
            self.b2[p, t, i] = (self.mine(p, t, x) + up(self.r1.at[p, t, x])).astype(BF16)
        self.two(p, t).start()

    def at_three(self, p, t):
        self.two(p, t).wait_recv()
        f = self.f
        self.b3[p, t] = (self.mine(p, t, f) + up(self.r1.at[p, t, f]) + up(self.r2.at[p, t, 1])).astype(BF16)
        self.three(p, t).start()

    def at_kept(self, p, t):
        self.three(p, t).wait_recv()
        xy = self.xy
        self.s3[p, t] = self.mine(p, t, xy) + up(self.r1.at[p, t, xy]) + up(self.r2.at[p, t, 0]) + up(self.r3.at[p, t])

    def at_four(self, p, step, kept=(), ids=range(3)):
        kept = list(kept)
        for i in ids:
            for t, way in ((3 - i, 0), (i, 1)):
                if t in kept:
                    self.at_kept(p, t)
                    kept.remove(t)
            for t, way in ((3 - i, 0), (i, 1)):
                pos = step if way == 0 else 3 - step
                if not (t > pos if way == 0 else t < pos):
                    continue

                @pl.when(self.z == pos)
                def _():
                    if step == 0:
                        self.b4[p, way, t] = self.s3[p, t].astype(BF16)
                    else:
                        self.four(p, t, way).wait_recv()
                        self.b4[p, way, t] = (self.s3[p, t] + up(self.r4.at[p, way, t])).astype(BF16)
                    self.four(p, t, way).start()

    def result(self, p, out):
        z = self.z
        out[...] = self.s3[p, z]

        @pl.when(z > 0)
        def _():
            self.four(p, z, 0).wait_recv()
            out[...] += up(self.r4.at[p, 0, z])

        @pl.when(z < 3)
        def _():
            self.four(p, z, 1).wait_recv()
            out[...] += up(self.r4.at[p, 1, z])

    def drain(self, p):
        for t in range(4):
            self.one(p, t).wait_send()
            self.two(p, t).wait_send()
            self.three(p, t).wait_send()
            for way in range(2):

                @pl.when((t > self.z) if way == 0 else (t < self.z))
                def _():
                    self.four(p, t, way).wait_send()


def sum_buffers(packs, block):
    vm = pltpu.VMEM
    return [
        vm((packs, 4, 4) + block, BF16),
        vm((packs, 4, 2) + block, BF16),
        vm((packs, 4, 2) + block, BF16),
        vm((packs, 4) + block, BF16),
        vm((packs, 4) + block, BF16),
        vm((packs, 4) + block, F32),
        vm((packs, 2, 4) + block, BF16),
        vm((packs, 2, 4) + block, BF16),
    ]


def sum_semaphores(packs):
    dma = pltpu.SemaphoreType.DMA
    return [dma((packs, 4))] * 6 + [dma((packs, 2, 4))] * 2


def finish_kernel(
    dqt, dk_all, dv_all, xt_all, dar, mixed_all, wd_all, dr1_all, vecs, bup,
    out_w, out_s, out_t,
    xt, wd, dk, dv, mixed_t, dr1, ld_sem, sh_sem, dart, dq, mixed, gp, sv, ds, dr, sk, q1, q2, q3, c2, c3, q4,
    r1, b2, r2, b3, r3, s3, b4, r4,
    p1_s, p1_r, p2_s, p2_r, p3_s, p3_r, p4_s, p4_r, t_s, t_r, v_s, v_r,
):
    z, d, core, first, second = position()
    own, width = out_t.shape
    chunks = own // ROWS
    total = 4 * chunks
    edge = SHORT // ROWS
    hw = width // 4
    r = width // 8
    load_w = pltpu.make_async_copy(wd_all.at[pl.ds(0, 3)], wd, ld_sem.at[0])
    load_x = pltpu.make_async_copy(xt_all, xt, ld_sem.at[1])
    load_m = pltpu.make_async_copy(mixed_all, mixed_t, ld_sem.at[2])
    load_r = pltpu.make_async_copy(dr1_all, dr1, ld_sem.at[3])

    def pick(a, b, c, e):
        return jnp.where(z == 0, a, jnp.where(z == 1, b, jnp.where(z == 2, c, e)))

    shards = [pick(*o) for o in ((2, 3, 0, 1), (1, 2, 1, 2), (3, 0, 3, 0), (0, 1, 2, 3))]
    load_s = []
    for j, o in enumerate(shards):
        rows = pl.ds(pl.multiple_of(o * own, ROWS), own)
        load_s.append(
            [
                pltpu.make_async_copy(a.at[rows], b.at[rows], sh_sem.at[i, j])
                for i, (a, b) in enumerate(((dk_all, dk), (dv_all, dv)))
            ]
        )
    for copy in [load_w] + load_s[0] + [load_m, load_x] + load_s[1] + load_s[2] + load_s[3] + [load_r]:
        copy.start()
    greet(z, d)

    def token(k, way):
        to = jnp.minimum(z + 1, 3) if way == 0 else jnp.maximum(z - 1, 0)
        slot = k if way == 0 else jnp.where(k // chunks == to, total + k % chunks, k)
        return put(ds.at[k], dr.at[slot], t_s.at[k], t_r.at[slot], d, to)

    def token_in(k, way):
        slot = k if way == 0 else jnp.where(k // chunks == z, total + k % chunks, k)
        return put(ds.at[k], dr.at[slot], t_s.at[k], t_r.at[slot], d, z), slot

    def sends(k, way):
        o = k // chunks
        if way == 0:
            low = jnp.where(k < total - edge, 0, 1)
            return (z >= low) & (z < o) & (o > low)
        high = jnp.where(k >= edge, 3, 2)
        return (z <= high) & (z > o) & (o < high)

    def starts(k, way):
        if way == 0:
            return z == jnp.where(k < total - edge, 0, 1)
        return z == jnp.where(k >= edge, 3, 2)

    tile = 256

    def far_shard(o, mine):
        rows = pl.ds(pl.multiple_of(o * own, ROWS), own)

        def one_tile(n, carry):
            lanes = pl.ds(pl.multiple_of(n * tile, tile), tile)
            far = contract_last(dk[rows, :], wd[1, lanes, :]) + contract_last(dv[rows, :], wd[2, lanes, :])
            if mine:
                out_t[:, lanes] = dr1[:, lanes] + far
            else:
                ds[pl.ds(o * chunks, chunks), :, lanes] = far.reshape(chunks, ROWS, tile).astype(BF16)
            return carry

        lax.fori_loop(0, width // tile, one_tile, 0)

    def far_and_send(j):
        o = shards[j]

        @pl.when((j < 2) | (z == 1) | (z == 2))
        def _():
            far_shard(o, False)

        for i in range(chunks):
            for way in range(2):
                k = o * chunks + i

                @pl.when(sends(k, way) & starts(k, way))
                def _():
                    token(k, way).start()

    for copy in [load_w] + load_s[0]:
        copy.wait()
    far_and_send(0)
    load_m.wait()

    right_order = [k for o in (3, 2, 1) for k in range(o * chunks, (o + 1) * chunks)]
    left_order = [total - 1 - k for k in right_order]

    def forward_tokens(at):
        for k, way in [(k, 0) for k in right_order] + [(k, 1) for k in left_order]:
            pos = at if way == 0 else 3 - at
            passes = (at < k // chunks) if way == 0 else (3 - at > k // chunks)
            begins = (0 if k < total - edge else 1) if way == 0 else (3 if k >= edge else 2)
            if not passes or (begins >= pos if way == 0 else begins <= pos):
                continue

            @pl.when(z == pos)
            def _():
                got, slot = token_in(k, way)
                got.wait_recv()
                ds[k] = (ds[k].astype(F32) + dr[slot].astype(F32)).astype(BF16)
                token(k, way).start()

    def flip_own(i, carry):
        cols = pl.ds(pl.multiple_of(i * ROWS, ROWS), ROWS)
        dart[:, cols] = dar[cols, :].T
        dq[cols, :] = dqt[:, cols].T
        mixed[cols, :] = mixed_t[:, cols].T.astype(BF16)
        return carry

    lax.fori_loop(0, chunks, flip_own, 0)

    def give(p, t):
        return gp.at[t, :, 1 - core]

    def mine(p, t, at):
        return gp[t, at, core].astype(F32)

    sums = Sums(
        z, d, core, second, first, give, mine, lambda p, t: None,
        (r1, b2, r2, b3, r3, s3, b4, r4), (p1_s, p1_r, p2_s, p2_r, p3_s, p3_r, p4_s, p4_r),
    )
    here = pl.ds(pl.multiple_of(z * own, ROWS), own)
    half = width // 2

    def weights(th):
        lanes = pl.ds(th * half, half)

        def rows_of(m, carry):
            rows = pl.ds(pl.multiple_of(m * half, ROWS), half)
            parts = (
                lambda: dot(xt[rows, here], dq[:, lanes]),
                lambda: dot(xt[rows, :], dk[:, lanes]),
                lambda: dot(xt[rows, :], dv[:, lanes]),
                lambda: dot(dart[rows, :], mixed[:, lanes]),
            )
            for i, part in enumerate(parts):
                got = part().astype(BF16)
                for h in range(2):
                    block = got[:, h * hw : (h + 1) * hw].reshape(2, 2, r, hw)
                    gp[2 * th + h, pl.ds(2 * m, 2), :, :, i * hw : (i + 1) * hw] = block
            return carry

        lax.fori_loop(0, 2, rows_of, 0)
        for t in (2 * th, 2 * th + 1):
            sums.one(0, t).start()

    for copy in [load_x, load_r] + load_s[1] + load_s[2] + load_s[3]:
        copy.wait()
    weights(1)
    weights(0)
    for t in (3, 2):
        sums.at_two(0, t)
    far_and_send(1)
    forward_tokens(1)
    for t in (0, 1):
        sums.at_two(0, t)
    far_and_send(2)
    forward_tokens(2)

    ones = jnp.ones((8, 4 * own), BF16)
    index = lax.broadcasted_iota(jnp.int32, (8, width), 0)
    small_rows = jnp.where(index == 0, dot(ones[:, :own], dq[...]), jnp.where(index == 1, dot(ones, dv[...]), vecs[...]))
    pad = jnp.zeros((8, 128 - r), F32)
    for i in range(8):
        sv[i // 2, i % 2, 0:8, :] = jnp.concatenate([small_rows[:, i * r : (i + 1) * r], pad], axis=1)
        wide = [bup[:, (i * 3 + j) * 128 : (i * 3 + j + 1) * 128] for j in range(3)]
        sv[i // 2, i % 2, 8:16, :] = jnp.concatenate(wide + [jnp.zeros((5, 128), F32)], axis=0)
    small = [
        put(sv.at[:, 1 - core], q1, v_s.at[0], v_r.at[0], sums.pal, z),
        put(c2, q2, v_s.at[1], v_r.at[1], sums.d_e, z),
        put(c3, q3, v_s.at[2], v_r.at[2], sums.d_f, z),
    ]
    small_z = [
        put(sk, q4.at[j - 1], v_s.at[2 + j], v_r.at[2 + j], d, lax.rem(z + j, 4)) for j in range(1, 4)
    ]
    small[0].start()
    far_shard(z, True)

    def query_tile(n, carry):
        lanes = pl.ds(pl.multiple_of(n * tile, tile), tile)
        out_t[:, lanes] += contract_last(dq[...], wd[0, lanes, :])
        return carry

    lax.fori_loop(0, width // tile, query_tile, 0)
    small[0].wait_recv()
    for i, at in enumerate((sums.e, sums.ef)):
        c2[i] = sv[at, core] + q1[at]
    small[1].start()
    for t in (3, 2, 0, 1):
        sums.at_three(0, t)
    small[1].wait_recv()
    c3[...] = sv[sums.f, core] + q1[sums.f] + q2[1]
    small[2].start()
    for step in range(3):
        sums.at_four(0, step, range(4) if step == 0 else ())
        if step == 0:
            small[2].wait_recv()
            sk[...] = sv[sums.xy, core] + q1[sums.xy] + q2[0] + q3[...]
            for copy in small_z:
                copy.start()
    for i in range(chunks):
        k = z * chunks + i
        rows = pl.ds(i * ROWS, ROWS)
        from_left = (z > 0) & ((z == 1) & (k < total - edge) | (z > 1))
        from_right = (z < 3) & ((z == 2) & (k >= edge) | (z < 2))

        @pl.when(from_left)
        def _():
            put(ds.at[k], dr.at[k], t_s.at[k], t_r.at[k], d, z).wait_recv()
            out_t[rows, :] += dr[k].astype(F32)

        @pl.when(from_right)
        def _():
            put(ds.at[k], dr.at[total + i], t_s.at[k], t_r.at[total + i], d, z).wait_recv()
            out_t[rows, :] += dr[total + i].astype(F32)

    for copy in small_z:
        copy.wait_recv()
    out_s[...] = sk[...] + q4[0] + q4[1] + q4[2]
    sums.result(0, out_w)
    for copy in small + small_z:
        copy.wait_send()
    sums.drain(0)
    for k in range(total):
        for way in range(2):

            @pl.when(sends(k, way))
            def _():
                token(k, way).wait_send()


def finish(dqt, dk, dv, xt, dar, mixed_t, wd, dr1, vecs, bup):
    own, width = dr1.shape
    r = width // 8
    chunks = own // ROWS
    dma, vm = pltpu.SemaphoreType.DMA, pltpu.VMEM
    vmem = pl.BlockSpec(memory_space=pltpu.VMEM)
    any_ = pl.BlockSpec(memory_space=pl.ANY)
    block, sb = (r, width), (16, 128)
    return pl.pallas_call(
        finish_kernel,
        out_shape=(
            jax.ShapeDtypeStruct(block, F32),
            jax.ShapeDtypeStruct(sb, F32),
            jax.ShapeDtypeStruct((own, width), F32),
        ),
        in_specs=[vmem] + [any_] * 3 + [vmem] + [any_] * 3 + [vmem] * 2,
        out_specs=(vmem, vmem, vmem),
        scratch_shapes=[
            vm((width, 4 * own), BF16),
            vm((3, width, width), BF16),
            vm((4 * own, width), BF16),
            vm((4 * own, width), BF16),
            vm((width, own), F32),
            vm((own, width), F32),
            dma((4,)),
            dma((2, 4)),
            vm((width, own), BF16),
            vm((own, width), BF16),
            vm((own, width), BF16),
            vm((4, 4, 2) + block, BF16),
            vm((4, 2) + sb, F32),
            vm((4 * chunks, ROWS, width), BF16),
            vm((5 * chunks, ROWS, width), BF16),
            vm(sb, F32),
            vm((4,) + sb, F32),
            vm((2,) + sb, F32),
            vm(sb, F32),
            vm((2,) + sb, F32),
            vm(sb, F32),
            vm((3,) + sb, F32),
            *sum_buffers(1, block),
            *sum_semaphores(1),
            dma((4 * chunks,)),
            dma((5 * chunks,)),
            dma((6,)),
            dma((6,)),
        ],
        compiler_params=pltpu.CompilerParams(
            collective_id=1, has_side_effects=True, vmem_limit_bytes=VMEM_MAX
        ),
        name="finish",
    )(dqt, dk, dv, xt, dar, mixed_t, wd, dr1, vecs, bup)


def parts_of(z, own):
    sure = SHORT - own
    low = z < 2
    return (
        (jnp.where(low, 0, own - sure), sure, jnp.where(low, 0, SHORT)),
        (jnp.where(low, sure, 0), own - sure, jnp.where(z == 3, SHORT, 0)),
    )


def over_keys(z, part, start, total, act):
    window = total - SHORT
    for c in range(window // KEYS):
        act(pl.multiple_of(start + c * KEYS, KEYS))
    if part == 1:

        @pl.when((z == 1) | (z == 2))
        def _():
            for c in range(window // KEYS, total // KEYS):
                act(c * KEYS)


def aug_rows(top, r):
    return jnp.concatenate([top.astype(BF16), jnp.zeros((128 - 16, r), BF16)], axis=0)


def pick_rows(rows, r):
    index = lax.broadcasted_iota(jnp.int32, (16, r), 0)
    out = jnp.zeros((16, r), F32)
    for i, row in enumerate(rows):
        out = jnp.where(index == i, jnp.broadcast_to(row, (16, r)), out)
    return out


def split3(x):
    hi = x.astype(BF16).astype(F32)
    mid = (x - hi).astype(BF16).astype(F32)
    return hi, mid, x - hi - mid


def padded(head_rows, half, aug, r):
    zero = jnp.zeros((HD, r), BF16)
    pair = [head_rows, zero] if half == 0 else [zero, head_rows]
    return jnp.concatenate(pair + [aug], axis=0)


def attention_kernel(qt, k, vt, ka, ma, mixed_t, lse, s, m, l, acc):
    z = lax.axis_index("tp")
    own = qt.shape[1]
    for part, (row0, n, start) in enumerate(parts_of(z, own)):
        cols = pl.ds(pl.multiple_of(row0, 128), n)
        aug = aug_rows(pick_rows((ma[0:1, cols], ma[1:2, cols]), n), n)

        def one_pair(pair, carry):
            attend_pair(z, part, start, pair, cols, n, aug, qt, k, vt, ka, mixed_t, lse, s, m, l, acc)
            return carry

        lax.fori_loop(0, k.shape[1] // 128, one_pair, 0)


def attention(qt, k, vt, ka, ma):
    width, own = qt.shape
    total = k.shape[0]
    widest = max(SHORT - own, own - (SHORT - own))
    vm = pltpu.VMEM
    return pl.pallas_call(
        attention_kernel,
        out_shape=(
            jax.ShapeDtypeStruct((width, own), F32),
            jax.ShapeDtypeStruct((width // 128, 8, own), F32),
        ),
        in_specs=[pl.BlockSpec(memory_space=pltpu.VMEM)] * 5,
        out_specs=(pl.BlockSpec(memory_space=pltpu.VMEM),) * 2,
        scratch_shapes=[
            vm((2, total, widest), F32),
            vm((2, 1, widest), F32),
            vm((2, 1, widest), F32),
            vm((2, HD, widest), F32),
        ],
        compiler_params=pltpu.CompilerParams(vmem_limit_bytes=VMEM_MAX),
        name="attention",
    )(qt, k, vt, ka, ma)


def back_pair(z, pair, pause, qt, q, k, kt, v, ka, ma, mixed_t, lse, dmt, dm, dqt, dk, dv, dka, dva, dqa):
    own, total = qt.shape[1], k.shape[0]
    lanes = pl.ds(pl.multiple_of(pair * 128, 128), 128)
    dka[...] = jnp.zeros_like(dka)
    dva[...] = jnp.zeros_like(dva)
    for part, (row0, r, start) in enumerate(parts_of(z, own)):
        pause(part)
        cols = pl.ds(pl.multiple_of(row0, 128), r)
        qs, gs, qm, gm = [], [], [], []
        low = lax.broadcasted_iota(jnp.int32, (r, 128), 1) < HD
        for half in range(2):
            rows = pl.ds(pl.multiple_of(pair * 128 + half * HD, HD), HD)
            delta = jnp.sum(dmt[rows, cols].astype(F32) * mixed_t[rows, cols], axis=0, keepdims=True)
            total_log = lse[pair, half : half + 1, cols]
            q_aug = pick_rows((ma[0:1, cols], ma[1:2, cols]) + split3(-total_log), r)
            zero = jnp.zeros((1, r), F32)
            g_aug = pick_rows((zero, zero) + split3(-delta), r)
            qs.append(padded(qt[rows, cols], half, aug_rows(q_aug, r), r))
            gs.append(padded(dmt[rows, cols], half, aug_rows(g_aug, r), r))
            mine = low if half == 0 else jnp.logical_not(low)
            here = pl.ds(pl.multiple_of(row0, 128), r)
            qm.append(jnp.where(mine, q[here, lanes], jnp.zeros((), BF16)))
            gm.append(jnp.where(mine, dm[here, lanes], jnp.zeros((), BF16)))
            dqa[half, :, :r] = jnp.zeros((HD, r), F32)

        def step(key0):
            keys = pl.ds(key0, KEYS)
            k_left = jnp.concatenate([k[keys, lanes], ka[keys, :]], axis=1)
            v_left = jnp.concatenate([v[keys, lanes], ka[keys, :]], axis=1)
            for half in range(2):
                share = jnp.exp(dot(k_left, qs[half]))
                slope = (share * dot(v_left, gs[half])).astype(BF16)
                dva[keys, :] += dot(share.astype(BF16), gm[half])
                dka[keys, :] += dot(slope, qm[half])
                rows = pl.ds(pl.multiple_of(pair * 128 + half * HD, HD), HD)
                dqa[half, :, :r] += dot(kt[rows, keys], slope)

        over_keys(z, part, start, total, step)
        for half in range(2):
            rows = pl.ds(pl.multiple_of(pair * 128 + half * HD, HD), HD)
            dqt[rows, cols] = (dqa[half, :, :r] * HD ** (-0.5)).astype(BF16)
    dk[:, lanes] = dka[...].astype(BF16)
    dv[:, lanes] = dva[...].astype(BF16)


def attention_back_kernel(*refs):
    z = lax.axis_index("tp")

    def one_pair(pair, carry):
        back_pair(z, pair, lambda part: None, *refs)
        return carry

    lax.fori_loop(0, refs[2].shape[1] // 128, one_pair, 0)


def back_sums_kernel(qt_all, q_all, k_all, kt_all, v_all, ka_all, ma, mixed_all, lse, dmt_all, dm_all, *refs):
    g = (refs[0:4], refs[4:8])
    dqt, dk_out, dv_out, out_u, out_d, dka, dva, dqa, *bufs = refs[8:]
    qt, q, ka, mixed_t, dmt, dm, in_sem, k, kt, v, dk, dv, kv_sem, gk, *bufs = bufs
    bufs, (gk_sem, *sems) = bufs[:8], bufs[8:]
    z, d, core, first, second = position()
    pairs = k.shape[1] // 128

    def operands(pair):
        lanes = pl.ds(pl.multiple_of(pair * 128, 128), 128)
        return (
            pltpu.make_async_copy(k_all.at[:, lanes], k.at[:, lanes], kv_sem.at[0, pair]),
            pltpu.make_async_copy(v_all.at[:, lanes], v.at[:, lanes], kv_sem.at[1, pair]),
            pltpu.make_async_copy(kt_all.at[lanes, :], kt.at[lanes, :], kv_sem.at[2, pair]),
        )

    def results(pair):
        lanes = pl.ds(pl.multiple_of(pair * 128, 128), 128)
        return (
            pltpu.make_async_copy(dk.at[:, lanes], dk_out.at[:, lanes], kv_sem.at[3, pair]),
            pltpu.make_async_copy(dv.at[:, lanes], dv_out.at[:, lanes], kv_sem.at[4, pair]),
        )

    pieces = ((qt_all, qt), (dmt_all, dmt), (mixed_all, mixed_t), (q_all, q), (dm_all, dm), (ka_all, ka))
    early = [pltpu.make_async_copy(a, b, in_sem.at[i]) for i, (a, b) in enumerate(pieces)]
    for copy in early:
        copy.start()
    for copy in operands(0):
        copy.start()
    greet(z, d)

    def fetch(p, t):
        return pltpu.make_async_copy(g[p][t].at[:, core], gk.at[p, t], gk_sem.at[p, t])

    sums = Sums(
        z, d, core, second, first,
        lambda p, t: g[p][t].at[:, 1 - core],
        lambda p, t, at: up(gk.at[p, t, at]),
        lambda p, t: fetch(p, t).wait(),
        bufs, sems,
    )
    for p in range(2):
        for t in (3, 0, 2, 1):
            sums.one(p, t).start()
            fetch(p, t).start()
    for pair in range(1, pairs):
        for copy in operands(pair):
            copy.start()
    for copy in early:
        copy.wait()

    def each(act, *units):
        def run():
            for p, t in units:
                act(p, t)

        return run

    def four(p, step, ids=range(3)):
        sums.at_four(p, step, range(4) if step == 0 else (), ids)

    packs = [[(p, t) for t in (3, 0, 2, 1)] for p in range(2)]
    between = {
        (0, 1): each(sums.at_two, *packs[0]),
        (1, 0): each(sums.at_two, *packs[1]),
        (2, 0): each(sums.at_three, *packs[0][:2]),
        (2, 1): each(sums.at_three, *packs[0][2:]),
        (3, 1): each(sums.at_three, *packs[1][:2]),
        (4, 0): lambda: four(0, 0),
        (4, 1): each(sums.at_three, *packs[1][2:]),
        (5, 0): lambda: four(0, 1),
        (5, 1): lambda: four(1, 0, (0,)),
    }

    def one_pair(pair, carry):
        def pause(part):
            for (i, at), run in between.items():
                if at == part:

                    @pl.when(pair == i)
                    def _():
                        run()

        for copy in operands(pair):
            copy.wait()
        back_pair(z, pair, pause, qt, q, k, kt, v, ka, ma, mixed_t, lse, dmt, dm, dqt, dk, dv, dka, dva, dqa)
        for copy in results(pair):
            copy.start()
        return carry

    lax.fori_loop(0, k.shape[1] // 128, one_pair, 0)
    four(0, 2)
    for step, ids in ((1, (0,)), (0, (1, 2)), (1, (1, 2)), (2, (0, 1, 2))):
        sums.at_four(1, step, (2, 1) if step == 0 else (), ids)
    for pair in range(pairs):
        for copy in results(pair):
            copy.wait()
    sums.result(0, out_u)
    sums.result(1, out_d)
    for p in range(2):
        sums.drain(p)


def back_shapes(own, total, width):
    widest = max(SHORT - own, own - (SHORT - own))
    vm = pltpu.VMEM
    outs = (
        jax.ShapeDtypeStruct((width, own), BF16),
        jax.ShapeDtypeStruct((total, width), BF16),
        jax.ShapeDtypeStruct((total, width), BF16),
    )
    return outs, [vm((total, 128), F32), vm((total, 128), F32), vm((2, HD, widest), F32)]


def attention_back(*args):
    (width, own), total = args[0].shape, args[2].shape[0]
    outs, scratch = back_shapes(own, total, width)
    return pl.pallas_call(
        attention_back_kernel,
        out_shape=outs,
        in_specs=[pl.BlockSpec(memory_space=pltpu.VMEM)] * 11,
        out_specs=(pl.BlockSpec(memory_space=pltpu.VMEM),) * 3,
        scratch_shapes=scratch,
        compiler_params=pltpu.CompilerParams(vmem_limit_bytes=VMEM_MAX),
        name="attention_back",
    )(*args)


def back_sums(args, gu, gd):
    (width, own), total = args[0].shape, args[2].shape[0]
    outs, scratch = back_shapes(own, total, width)
    block = (width // 8, gu[0].shape[1])
    g = [a.reshape((4, 2) + block) for a in (*gu, *gd)]
    vmem = pl.BlockSpec(memory_space=pltpu.VMEM)
    any_ = pl.BlockSpec(memory_space=pl.ANY)
    return pl.pallas_call(
        back_sums_kernel,
        out_shape=outs + (jax.ShapeDtypeStruct(block, F32),) * 2,
        in_specs=[any_] * 6 + [vmem, any_, vmem] + [any_] * 10,
        out_specs=(vmem, any_, any_, vmem, vmem),
        scratch_shapes=[
            *scratch,
            pltpu.VMEM((width, own), BF16),
            pltpu.VMEM((own, width), BF16),
            pltpu.VMEM((total, 128), BF16),
            pltpu.VMEM((width, own), F32),
            pltpu.VMEM((width, own), BF16),
            pltpu.VMEM((own, width), BF16),
            pltpu.SemaphoreType.DMA((6,)),
            pltpu.VMEM((total, width), BF16),
            pltpu.VMEM((width, total), BF16),
            pltpu.VMEM((total, width), BF16),
            pltpu.VMEM((total, width), BF16),
            pltpu.VMEM((total, width), BF16),
            pltpu.SemaphoreType.DMA((5, width // 128)),
            pltpu.VMEM((2, 4, 4) + block, BF16),
            *sum_buffers(2, block),
            pltpu.SemaphoreType.DMA((2, 4)),
            *sum_semaphores(2),
        ],
        compiler_params=pltpu.CompilerParams(
            collective_id=2, has_side_effects=True, vmem_limit_bytes=VMEM_MAX
        ),
        name="back_sums",
    )(*args, *g)


def norms_kernel(
    tok, mixed_t, vec, bu, cot, wd, w,
    enc_out, dr1_out, dar_out, dm_out, dmt_out, vecs, wide, *refs,
):
    gu, gd = refs[0:4], refs[4:8]
    wo, wu, wn, mixed, y1r, hr, slope, du, dfr, y1t, dft, stage, enc, dr1, dar, dm, dmt, w_sem, o_sem, r_sem = refs[8:]
    own, width = tok.shape
    n_tp = wu.shape[0]
    loads = [[pltpu.make_async_copy(w.at[i, t], b.at[t], w_sem.at[i, t]) for t in range(n_tp)] for i, b in enumerate((wu, wn))]
    load_o = pltpu.make_async_copy(wd.at[3], wo, w_sem.at[2, 0])
    load_o.start()
    for t in range(n_tp):
        for i in range(2):
            loads[i][t].start()
    vecs[...] = jnp.zeros_like(vecs)
    half = own // 2

    def flip_mixed(i, carry):
        cols = pl.ds(pl.multiple_of(i * ROWS, ROWS), ROWS)
        mixed[cols, :] = mixed_t[:, cols].T.astype(BF16)
        return carry

    lax.fori_loop(0, own // ROWS, flip_mixed, 0)
    load_o.wait()

    def row_tile(i, carry):
        rows = pl.ds(pl.multiple_of(i * half, 64), half)

        def add(index, value):
            vecs[index : index + 1, :] += jnp.sum(value, axis=0, keepdims=True)

        xhat1, inv1 = normalize_layer(tok[rows, :].astype(F32) + contract_last(mixed[rows, :], wo[...]) + vec[2:3, :])
        y1 = xhat1 * vec[3:4, :] + vec[4:5, :]
        y1b = y1.astype(BF16)
        y1r[rows, :] = y1b
        total = y1 + vec[5:6, :]

        @pl.when(i == 0)
        def _():
            for t in range(n_tp):
                for j in range(2):
                    loads[j][t].wait()

        for t in range(n_tp):
            u = dot(y1b, wu[t]) + bu[:, t * width : (t + 1) * width]
            below = 0.5 * (1.0 + lax.erf(u * SQRT_HALF))
            h = (u * below).astype(BF16)
            hr[t, rows, :] = h
            slope[t] = below + u * jnp.exp(-0.5 * u * u) * INV_ROOT_TAU
            total = total + contract_last(h, wn[t])
        xhat2, inv2 = normalize_layer(total)
        enc[rows, :] = (xhat2 * vec[6:7, :] + vec[7:8, :]).astype(BF16)
        grad = cot[rows, :].astype(F32)
        add(6, grad * xhat2)
        add(7, grad)
        dr2 = normalize_backward(grad, xhat2, inv2, vec[6:7, :])
        dfb = dr2.astype(BF16)
        dfr[rows, :] = dfb
        add(5, dfb.astype(F32))
        dy1 = dr2
        for t in range(n_tp):
            back = (dot(dfb, wn[t]) * slope[t]).astype(BF16)
            du[t, rows, :] = back
            dy1 = dy1 + contract_last(back, wu[t])
        add(3, dy1 * xhat1)
        add(4, dy1)
        first = normalize_backward(dy1, xhat1, inv1, vec[3:4, :])
        dr1[rows, :] = first
        dab = first.astype(BF16)
        dar[rows, :] = dab
        add(2, dab.astype(F32))
        dm[rows, :] = dot(dab, wo[...]).astype(BF16)
        return carry

    lax.fori_loop(0, 2, row_tile, 0)
    pieces = ((enc, enc_out), (dr1, dr1_out), (dar, dar_out), (dm, dm_out), (dmt, dmt_out))
    outs = [pltpu.make_async_copy(a, b, r_sem.at[i]) for i, (a, b) in enumerate(pieces)]
    for copy in outs[:4]:
        copy.start()

    def flip(i, carry):
        cols = pl.ds(pl.multiple_of(i * ROWS, ROWS), ROWS)
        dft[:, cols] = dfr[cols, :].T
        y1t[:, cols] = y1r[cols, :].T
        dmt[:, cols] = dm[cols, :].T
        return carry

    lax.fori_loop(0, own // ROWS, flip, 0)
    outs[4].start()
    tile = 256
    ones = jnp.ones((8, own), BF16)

    def store(i, t):
        return pltpu.make_async_copy(stage.at[i, t], (gd, gu)[i][t], o_sem.at[i, t])

    for t in range(n_tp):

        def one_tile(n, carry):
            lanes = pl.ds(pl.multiple_of(n * tile, tile), tile)
            stage[0, t, :, lanes] = dot(dft[...], hr[t, :, lanes]).astype(BF16)
            stage[1, t, :, lanes] = dot(y1t[...], du[t, :, lanes]).astype(BF16)
            wide[0:1, pl.ds(pl.multiple_of(t * width + n * tile, tile), tile)] = dot(ones, du[t, :, lanes])[0:1, :]
            return carry

        lax.fori_loop(0, width // tile, one_tile, 0)
        for i in range(2):
            store(i, t).start()
    for t in range(n_tp):
        for i in range(2):
            store(i, t).wait()
    for copy in outs:
        copy.wait()


def norms(tok, mixed_t, vec, bu, cot, wd, w):
    own, width = tok.shape
    dma, vm = pltpu.SemaphoreType.DMA, pltpu.VMEM
    any_ = pl.BlockSpec(memory_space=pl.ANY)
    vmem = pl.BlockSpec(memory_space=pltpu.VMEM)
    shape = jax.ShapeDtypeStruct
    square = (width, width)
    return pl.pallas_call(
        norms_kernel,
        out_shape=(
            shape((own, width), BF16),
            shape((own, width), F32),
            shape((own, width), BF16),
            shape((own, width), BF16),
            shape((width, own), BF16),
            shape((8, width), F32),
            shape((1, 4 * width), F32),
        )
        + (shape(square, BF16),) * 8,
        in_specs=[vmem] * 5 + [any_] * 2,
        out_specs=(any_,) * 5 + (vmem,) * 2 + (any_,) * 8,
        scratch_shapes=[
            vm(square, BF16),
            vm((4,) + square, BF16),
            vm((4,) + square, BF16),
            vm((own, width), BF16),
            vm((own, width), BF16),
            vm((4, own, width), BF16),
            vm((4, own // 2, width), F32),
            vm((4, own, width), BF16),
            vm((own, width), BF16),
            vm((width, own), BF16),
            vm((width, own), BF16),
            vm((2, 4) + square, BF16),
            vm((own, width), BF16),
            vm((own, width), F32),
            vm((own, width), BF16),
            vm((own, width), BF16),
            vm((width, own), BF16),
            dma((3, 4)),
            dma((2, 4)),
            dma((5,)),
        ],
        compiler_params=pltpu.CompilerParams(vmem_limit_bytes=VMEM_MAX),
        name="norms",
    )(tok, mixed_t, vec, bu, cot, wd, w)


def body(
    tokens, w_query, w_key, w_value, b_query, b_value, w_out, b_out, gain_attn, shift_attn,
    w_up, b_up, w_down, b_down, gain_ffn, shift_ffn, lengths, deal_order, cotangent,
):
    own, width = tokens.shape
    n_tp, n_dp = lax.axis_size("tp"), lax.axis_size("dp")
    z, g = lax.axis_index("tp"), lax.axis_index("dp")
    total = own * n_tp
    r, hw = w_query.shape
    direct = n_tp == 4 and n_dp == 8 and r % 16 == 0

    own_w = jnp.stack([jnp.concatenate([w_query, w_key, w_value, w_out], axis=1), w_up, w_down])
    vectors = (b_query, b_value, b_out, gain_attn, shift_attn, b_down, gain_ffn, shift_ffn, b_up)
    n_small = 8 * r + b_up.shape[0]
    if direct:
        line = jnp.arange(8, dtype=jnp.int32)[:, None]
        narrow = jnp.zeros((8, r), BF16)
        for i, a in enumerate(vectors[:8]):
            narrow = jnp.where(line == i, a[None, :], narrow)
        narrow = jnp.pad(narrow, ((0, 0), (0, 128 - r)))
        own_s = jnp.concatenate([narrow, jnp.pad(b_up.reshape(-1, 128), ((0, 5), (0, 0)))])
        w, vec, bu, xt, q, qt, k, v, kt, wd, ka, mixed_t, lse, ma = forward_all(lengths, deal_order, own_w, own_s, tokens)
        w = w.reshape(2, n_tp, width, w_up.shape[1])
        encoder_output, dr1, dar, dm, dmt, vecs, wide_sum, *gw = norms(tokens, mixed_t, vec, bu, cotangent, wd, w)
        args = (qt, q, k, kt, v, ka, ma, mixed_t, lse, dmt, dm)
        dqt, dk, dv, g_up, g_down = back_sums(args, gw[:4], gw[4:])
        a, gs, grad_tokens = finish(dqt, dk, dv, xt, dar, mixed_t, wd, dr1, vecs, wide_sum)
        gs = [gs[i, :r] for i in range(8)] + [gs[8:11].reshape(-1)]
    else:
        w = lax.all_gather(own_w, ("tp", "dp"), axis=0).reshape((n_tp, n_dp) + own_w.shape)
        w = jnp.moveaxis(w, 2, 0).reshape(3, n_tp, width, w_up.shape[1])
        s = lax.all_gather(jnp.concatenate(vectors), "dp", axis=0)
        x = lax.all_gather(tokens, "tp", axis=0, tiled=True)
        small = [s[:, i * r : (i + 1) * r].reshape(width).astype(F32) for i in range(8)]
        bq, bv, bo, g1, h1, bd, g2, h2 = small
        bu = s[:, 8 * r : n_small].reshape(-1).astype(F32)
        wq, wk, wv, wo = (
            w[0, :, :, i * hw : (i + 1) * hw].transpose(1, 0, 2).reshape(width, width) for i in range(4)
        )
        w = w[1:]
        q = (dot(tokens, wq) + bq).astype(BF16) * jnp.asarray(HD ** (-0.5), BF16)
        k = dot(x, wk).astype(BF16)
        v = (dot(x, wv) + bv).astype(BF16)
        qt, kt = q.T, k.T

        pair = lax.dynamic_slice_in_dim(deal_order, 2 * g, 1)
        first_len = jnp.sum(jnp.where(jnp.arange(lengths.shape[0], dtype=jnp.int32) == pair[0], lengths, 0))
        key_seg = jnp.arange(total, dtype=jnp.int32)[:, None] >= first_len
        lane = jnp.arange(128, dtype=jnp.int32)[None, :]
        ka = jnp.where(lane == 0, ~key_seg, jnp.where(lane == 1, key_seg, (lane >= 2) & (lane < 5))).astype(BF16)
        row_seg = (z * own + jnp.arange(own, dtype=jnp.int32))[None, :] >= first_len
        sub = jnp.arange(8, dtype=jnp.int32)[:, None]
        ma = jnp.where(((sub == 0) & row_seg) | ((sub == 1) & ~row_seg), MASKED, 0.0).astype(F32)

        mixed_t, lse = attention(qt, k, v.T, ka, ma)
        mixed = mixed_t.T.astype(BF16)
        first_residual = tokens.astype(F32) + contract_last(mixed, wo) + bo
        xhat1, inv1 = normalize_layer(first_residual)
        y1 = xhat1 * g1 + h1
        y1r = y1.astype(BF16)

        u = [dot(y1r, w[0, t]) + bu.reshape(n_tp, -1)[t] for t in range(n_tp)]
        hr = [jax.nn.gelu(a, approximate=False).astype(BF16) for a in u]
        ffn = sum(contract_last(hr[t], w[1, t]) for t in range(n_tp))
        xhat2, inv2 = normalize_layer(y1 + ffn + bd)
        encoder_output = (xhat2 * g2 + h2).astype(BF16)

        grad = cotangent.astype(F32)
        dr2 = normalize_backward(grad, xhat2, inv2, g2)
        dfr = dr2.astype(BF16)
        du = [(dot(dfr, w[1, t]) * gelu_slope(u[t])).astype(BF16) for t in range(n_tp)]
        dy1 = dr2 + sum(contract_last(du[t], w[0, t]) for t in range(n_tp))
        dr1 = normalize_backward(dy1, xhat1, inv1, g1)
        dar = dr1.astype(BF16)
        dm = dot(dar, wo).astype(BF16)
        gu = [contract_first(y1r, du[t]) for t in range(n_tp)]
        gd = [contract_first(dfr, hr[t]) for t in range(n_tp)]
        row_sums = [
            jnp.sum(dar, axis=0, dtype=F32),
            jnp.sum(dy1 * xhat1, axis=0),
            jnp.sum(dy1, axis=0),
            jnp.sum(dfr, axis=0, dtype=F32),
            jnp.sum(grad * xhat2, axis=0),
            jnp.sum(grad, axis=0),
        ]
        wide_sum = jnp.concatenate([jnp.sum(a, axis=0, dtype=F32) for a in du])
        back_args = (qt, q, k, kt, v, ka, ma, mixed_t, lse, dm.T, dm)
        dqt, dk, dv = attention_back(*back_args)
        dq = dqt.T
        base = dr1 + contract_last(dq, wq)
        far = contract_last(dk, wk) + contract_last(dv, wv)
        base = base + lax.dynamic_slice_in_dim(far, z * own, own)
        dt = far.astype(BF16)
        gq, gk, gv = contract_first(tokens, dq), contract_first(x, dk), contract_first(x, dv)
        go = contract_first(dar, mixed)
        ga = jnp.stack(
            [
                jnp.concatenate([m[:, t * hw : (t + 1) * hw] for m in (gq, gk, gv, go)], axis=1)
                for t in range(n_tp)
            ]
        )
        sums = [jnp.sum(dq, axis=0, dtype=F32), jnp.sum(dv, axis=0, dtype=F32)] + row_sums
        sums = [a.reshape(n_dp, r) for a in sums]
        sv = jnp.concatenate(sums + [wide_sum.reshape(n_dp, -1)], axis=1)
        grads = jnp.stack([ga, jnp.stack(gu), jnp.stack(gd)], axis=1).reshape(n_tp, 3, n_dp, r, -1)
        grads = jnp.moveaxis(grads, 1, 2).reshape(n_tp * n_dp, 3, r, -1)
        gw = lax.psum_scatter(grads, ("tp", "dp"), scatter_dimension=0, tiled=True)[0]
        gs = lax.psum_scatter(lax.psum(sv, "tp"), "dp", scatter_dimension=0, tiled=True)[0]
        others = jnp.where(jnp.arange(total)[:, None] // own == z, jnp.zeros((), BF16), dt)
        grad_tokens = base + lax.psum_scatter(others, "tp", scatter_dimension=0, tiled=True).astype(F32)
        gs = [gs[i * r : (i + 1) * r] for i in range(8)] + [gs[8 * r : n_small]]
        a, g_up, g_down = gw[0], gw[1], gw[2]
    return (
        encoder_output, grad_tokens,
        a[:, :hw], a[:, hw : 2 * hw], a[:, 2 * hw : 3 * hw], gs[0], gs[1],
        a[:, 3 * hw :], gs[2], gs[3], gs[4],
        g_up, gs[8], g_down, gs[5], gs[6], gs[7],
    )


def solution(mesh):
    rows, block, vector = P(("dp", "tp"), None), P("dp", "tp"), P("dp")
    in_specs = (
        rows, block, block, block, vector, vector, block, vector, vector, vector,
        block, vector, block, vector, vector, vector, P(), P(), rows,
    )
    out_specs = (
        rows, rows, block, block, block, vector, vector, block, vector, vector, vector,
        block, vector, block, vector, vector, vector,
    )
    return jax.shard_map(body, mesh=mesh, in_specs=in_specs, out_specs=out_specs, check_vma=False)
```
